32 devices in a mesh: ctx: 8 (over z, y), shard: 4 (over x, core).
Axes of the slice: x: 2, y: 2, z: 4, core: 2. Of those that a mesh axis runs over, the one named last changes fastest.
Arguments:
- tokens: bfloat16 [4, 1024, 768], P('shard', 'ctx'), may hold values from -6 to 6
- cotangent: bfloat16 [4, 1024, 768], P('shard', 'ctx'), may hold values from -6 to 6
- seq_ids: int32 [4, 1024], P('shard', 'ctx'), may hold values from 0 to 2, never falling along the last dimension, each value on 1 to 512 neighbouring positions
- w_query: bfloat16 [768, 768], P('shard'), may hold values from -0.3125 to 0.3125
- b_query: bfloat16 [768], P('shard'), may hold values from -3 to 3
- w_key: bfloat16 [768, 768], P('shard'), may hold values from -0.3125 to 0.3125
- w_value: bfloat16 [768, 768], P('shard'), may hold values from -0.21875 to 0.21875
- b_value: bfloat16 [768], P('shard'), may hold values from -3 to 3
- w_out: bfloat16 [768, 768], P('shard'), may hold values from -0.875 to 0.875
- b_out: bfloat16 [768], P('shard'), may hold values from -1.75 to 1.75
- attn_gain: bfloat16 [768], P('shard'), may hold values from 0.099609375 to 1.8984375
- attn_shift: bfloat16 [768], P('shard'), may hold values from -3 to 3
- w_up: bfloat16 [768, 3072], P('shard'), may hold values from -0.21875 to 0.21875
- b_up: bfloat16 [3072], P('shard'), may hold values from -3 to 3
- w_down: bfloat16 [3072, 768], P('shard'), may hold values from -0.15625 to 0.15625
- b_down: bfloat16 [768], P('shard'), may hold values from -3 to 3
- ffn_gain: bfloat16 [768], P('shard'), may hold values from 0.099609375 to 1.8984375
- ffn_shift: bfloat16 [768], P('shard'), may hold values from -3 to 3
Outputs:
- hidden_out: bfloat16 [4, 1024, 768], P('shard', 'ctx')
- tokens_grad: bfloat16 [4, 1024, 768], P('shard', 'ctx')
- w_query_grad: float32 [768, 768], P('shard')
- b_query_grad: float32 [768], P('shard')
- w_key_grad: float32 [768, 768], P('shard')
- w_value_grad: float32 [768, 768], P('shard')
- b_value_grad: float32 [768], P('shard')
- w_out_grad: float32 [768, 768], P('shard')
- b_out_grad: float32 [768], P('shard')
- attn_gain_grad: float32 [768], P('shard')
- attn_shift_grad: float32 [768], P('shard')
- w_up_grad: float32 [768, 3072], P('shard')
- b_up_grad: float32 [3072], P('shard')
- w_down_grad: float32 [3072, 768], P('shard')
- b_down_grad: float32 [768], P('shard')
- ffn_gain_grad: float32 [768], P('shard')
- ffn_shift_grad: float32 [768], P('shard')
The draws below stay inside these ranges and needn't reach their ends.
Inputs may be any that keep to these rules, and one draw needn't show every extreme that they name: `seq_ids`: in each group ids never fall along the tokens; each sequence has 1 to 512 tokens, one exactly 512.
All inputs are finite; a program needn't handle non-finite values.
Results may differ from the reference program's by a relative error of at most 0.035.
Values may be sent and summed in bfloat16 or wider, within the bound.
No kernel may reach another device: no remote copies, remote signals or barrier semaphores. Data moves between devices by JAX's collectives and lax.ppermute only.
A program may use at most 128 MiB of HBM per device.

```python
import math
import jax
import jax.numpy as jnp
import numpy as np
from jax import lax

D = 768
FF = 3072
HEAD_DIM = 64
GROUPS = 4
GTOK = 1024
SEQ_MAX = 512
SEQS = 3


def block_scale(rng, extent, shards, low, top_value):
    level = 1.0
    for dim, shards_of in shards:
        heights = jax.random.uniform(jax.random.fold_in(jax.random.fold_in(rng, 6), dim), (shards_of,), jnp.float32, low / len(shards), top_value / len(shards))
        level = level * jnp.repeat(jnp.exp(heights), extent[dim] // shards_of).reshape((-1,) + (1,) * (len(extent) - 1 - dim))
    return level


def profile(amount, total, most, skew):
    weights = [(1 << 20) // math.isqrt(rank ** skew) + 1 for rank in range(2, amount + 1)]
    spare, given = total - most - (amount - 1), [1] * (amount - 1)
    while spare > 0:
        candidates = [i for i in range(amount - 1) if given[i] < most]
        mass, left = sum([weights[i] for i in candidates]), spare
        for i in candidates:
            addition = min(most - given[i], max(1, left * weights[i] // mass), spare)
            given[i] = given[i] + addition
            spare = spare - addition
    return np.array([most] + given)


def ragged(key, number_of, total, reach, slope):
    if number_of == 2:
        one = jax.random.randint(key, (), max(1, total - reach), min(reach, total - 1) + 1)
        return jnp.stack([one, total - one])
    tallies = jnp.asarray(profile(number_of, total, reach, slope), jnp.int32)
    pairs = (number_of - 1) // 2
    donor, taker = tallies[1:1 + 2 * pairs:2], tallies[2:2 + 2 * pairs:2]
    margin = jnp.minimum(donor - 1, reach - taker)
    passed = jax.random.randint(jax.random.fold_in(key, 1), (pairs,), 0, 1 << 20) % (margin + 1)
    tallies = tallies.at[1:1 + 2 * pairs:2].set(donor - passed).at[2:2 + 2 * pairs:2].set(taker + passed)
    return tallies[jax.random.permutation(jax.random.fold_in(key, 2), number_of)]


def centred(rng, dims, scale, most, split=(), held_as=jnp.bfloat16):
    result = jax.random.normal(rng, dims, jnp.float32) * scale
    if len(split) > 0:
        result = block_scale(rng, dims, split, -0.22, 0.18) * result
    return jnp.clip(result, min=-most, max=most).astype(held_as)


def setup_inputs(seed: int = 0) -> dict:
    key_list = jax.random.split(jax.random.key(seed), 19)
    return {
        "tokens": centred(key_list[0], (GROUPS, GTOK, D), 1.0, 6.0, ((0, 4), (1, 8))),
        "cotangent": centred(key_list[1], (GROUPS, GTOK, D), 1.0, 6.0, ((0, 4), (1, 8))),
        "seq_ids": jax.vmap(lambda own: jnp.searchsorted(jnp.cumsum(ragged(own, SEQS, GTOK, SEQ_MAX, 2)), jnp.arange(GTOK), side="right"))(jax.random.split(key_list[2], GROUPS)).reshape((GROUPS, GTOK)).astype(jnp.int32),
        "w_query": centred(key_list[3], (D, D), (D // 2) ** -0.5, 0.3125, ((0, 4),)),
        "b_query": centred(key_list[4], (D,), 0.5, 3.0, ((0, 4),)),
        "w_key": centred(key_list[5], (D, D), (D // 2) ** -0.5, 0.3125, ((0, 4),)),
        "w_value": centred(key_list[6], (D, D), D ** -0.5, 0.21875, ((0, 4),)),
        "b_value": centred(key_list[7], (D,), 0.5, 3.0, ((0, 4),)),
        "w_out": centred(key_list[8], (D, D), (D // 16) ** -0.5, 0.875, ((0, 4),)),
        "b_out": centred(key_list[9], (D,), 0.3, 1.75, ((0, 4),)),
        "attn_gain": jnp.clip(1.0 + 0.18 * jax.random.normal(key_list[10], (D,), jnp.float32), 0.099609375, 1.8984375).astype(jnp.bfloat16),
        "attn_shift": centred(key_list[11], (D,), 0.5, 3.0, ((0, 4),)),
        "w_up": centred(key_list[12], (D, FF), D ** -0.5, 0.21875, ((0, 4),)),
        "b_up": centred(key_list[13], (FF,), 0.5, 3.0, ((0, 4),)),
        "w_down": centred(key_list[14], (FF, D), (FF // 2) ** -0.5, 0.15625, ((0, 4),)),
        "b_down": centred(key_list[15], (D,), 0.5, 3.0, ((0, 4),)),
        "ffn_gain": jnp.clip(1.0 + 0.18 * jax.random.normal(key_list[16], (D,), jnp.float32), 0.099609375, 1.8984375).astype(jnp.bfloat16),
        "ffn_shift": centred(key_list[17], (D,), 0.5, 3.0, ((0, 4),)),
    }


@jax.custom_vjp
def low(v):
    return lax.optimization_barrier(v.astype(jnp.bfloat16)).astype(jnp.float32)

@jax.custom_vjp
def low_back(v):
    return v

def low_keep(v):
    return (low(v), None)

def low_pass(kept, grad):
    return (grad,)

def back_keep(v):
    return (v, None)

def back_low(kept, grad):
    return (low(grad),)
low.defvjp(low_keep, low_pass)
low_back.defvjp(back_keep, back_low)
ln_eps = 1e-12
masked_fill = -1e+30

def matmul(left, right):
    return jnp.dot(left, right, precision=lax.Precision.HIGHEST, preferred_element_type=jnp.float32)

def apply_layer_norm(value, gain, shift):
    mean = lax.optimization_barrier(jnp.mean(value, axis=-1, keepdims=True))
    centered = value - mean
    return centered * lax.rsqrt(lax.optimization_barrier(jnp.mean(centered * centered, axis=-1, keepdims=True)) + ln_eps) * gain + shift

def group_layer(inputs, params):
    tokens_f, ident = inputs
    query_mat, query_bias, key_mat, value_mat, value_bias, out_mat, out_bias, attention_norm_gain, first_shift, up_mat, up_bias, down_mat, down_bias, feedforward_norm_gain, second_shift = params
    rows = tokens_f.shape[0]
    heads = tokens_f.shape[1] // HEAD_DIM
    scale = 1.0 / math.sqrt(HEAD_DIM)
    block_rows = min(512, rows)
    query = low_back(low(matmul(tokens_f, query_mat) + query_bias))
    keys = low_back(low(matmul(tokens_f, key_mat)))
    values = low_back(low(matmul(tokens_f, value_mat) + value_bias))
    key_heads = keys.reshape(rows, heads, HEAD_DIM)
    value_heads = values.reshape(rows, heads, HEAD_DIM)

    def one_block(piece):
        q_block, id_block = piece
        raw = jnp.einsum('qhd,khd->hqk', q_block, key_heads, precision=lax.Precision.HIGHEST)
        scores = low_back(raw * scale)
        match = (id_block[:, None] == ident[None, :])[None, :, :]
        probs = low(jax.nn.softmax(jnp.where(match, scores, masked_fill), axis=-1))
        return jnp.einsum('hqk,khd->qhd', probs, value_heads, precision=lax.Precision.HIGHEST)
    attn = lax.map(jax.checkpoint(one_block), (query.reshape(rows // block_rows, block_rows, heads, HEAD_DIM), ident.reshape(rows // block_rows, block_rows)))
    attn = low_back(low(attn.reshape(rows, heads * HEAD_DIM)))
    attn_proj = low_back(matmul(attn, out_mat) + out_bias)
    first_normalized_rows = apply_layer_norm(tokens_f + attn_proj, attention_norm_gain, first_shift)
    up_pre = low_back(matmul(low(first_normalized_rows), up_mat) + up_bias)
    up_act = low(jax.nn.gelu(up_pre, approximate=False))
    down_pre = low_back(matmul(up_act, down_mat) + down_bias)
    return apply_layer_norm(first_normalized_rows + down_pre, feedforward_norm_gain, second_shift)

def reference(tokens, cotangent, seq_ids, w_query, b_query, w_key, w_value, b_value, w_out, b_out, attn_gain, attn_shift, w_up, b_up, w_down, b_down, ffn_gain, ffn_shift):
    params = tuple((p.astype(jnp.float32) for p in (w_query, b_query, w_key, w_value, b_value, w_out, b_out, attn_gain, attn_shift, w_up, b_up, w_down, b_down, ffn_gain, ffn_shift)))

    def forward(tokens_f, *param_list):

        def per_group(piece):
            return group_layer(piece, param_list)
        return lax.map(per_group, (tokens_f, seq_ids))
    layer_output, pull = jax.vjp(forward, tokens.astype(jnp.float32), *params)
    grads = pull(cotangent.astype(jnp.float32))
    return (layer_output.astype(jnp.bfloat16), grads[0].astype(jnp.bfloat16), grads[1], grads[2], grads[3], grads[4], grads[5], grads[6], grads[7], grads[8], grads[9], grads[10], grads[11], grads[12], grads[13], grads[14], grads[15])
```

```python
import math

import jax
import jax.numpy as jnp
from jax import lax
from jax.experimental import pallas as pl
from jax.experimental.pallas import tpu as pltpu
from jax.sharding import Mesh
from jax.sharding import PartitionSpec as P

HEAD_DIM = 64


ln_eps = 1e-12
masked_fill = -1e30


def from_behind(block, axis, distance):
    devices = range(lax.axis_size(axis))
    route = [((i - distance) % len(devices), i) for i in devices]
    return lax.ppermute(block, axis, route)


def matmul(left, right):
    return jnp.dot(left, right, preferred_element_type=jnp.float32)


def matmul_tn(left, right):
    return lax.dot_general(
        left, right, (((0,), (0,)), ((), ())), preferred_element_type=jnp.float32
    )


def matmul_nt(left, right):
    return lax.dot_general(
        left, right, (((1,), (1,)), ((), ())), preferred_element_type=jnp.float32
    )


def apply_layer_norm(value, gain, shift):
    mean = jnp.mean(value, axis=-1, keepdims=True)
    centered = value - mean
    rstd = lax.rsqrt(jnp.mean(centered * centered, axis=-1, keepdims=True) + ln_eps)
    normed = centered * rstd
    return (normed * gain + shift, normed, rstd)


def norm_back(grad, normed, rstd, gain):
    d_gain = jnp.sum(grad * normed, axis=0)
    d_shift = jnp.sum(grad, axis=0)
    scaled = grad * gain
    d_value = rstd * (
        scaled
        - jnp.mean(scaled, axis=-1, keepdims=True)
        - normed * jnp.mean(scaled * normed, axis=-1, keepdims=True)
    )
    return (d_value, d_gain, d_shift)


def gelu_slope(value):
    normal_cdf = 0.5 * (1.0 + lax.erf(value * (1.0 / math.sqrt(2.0))))
    density = jnp.exp(-0.5 * value * value) * (1.0 / math.sqrt(2.0 * math.pi))
    return normal_cdf + value * density


def scores_of(query, keys, q_ids, k_ids, scale):
    raw = jnp.einsum("qhd,khd->hqk", query, keys, preferred_element_type=jnp.float32) * scale
    match = (q_ids[:, None] == k_ids[None, :])[None, :, :]
    return (raw, match)


def attend(query, q_ids, keys, values, k_ids, stats, scale):
    top, total, accum = stats
    raw, match = scores_of(query, keys, q_ids, k_ids, scale)
    masked = jnp.where(match, raw, masked_fill)
    new_top = jnp.maximum(top, jnp.max(masked, axis=-1))
    weights = jnp.where(match, jnp.exp(masked - new_top[:, :, None]), 0.0)
    factor = jnp.exp(top - new_top)
    total = total * factor + jnp.sum(weights, axis=-1)
    accum = accum * factor[:, :, None] + jnp.einsum(
        "hqk,khd->hqd", weights.astype(jnp.bfloat16), values, preferred_element_type=jnp.float32
    )
    return (new_top, total, accum)


def block_grads(query, q_ids, d_out, log_total, delta, keys, values, k_ids, scale):
    raw, match = scores_of(query, keys, q_ids, k_ids, scale)
    probs = jnp.exp(jnp.where(match, raw - log_total[:, :, None], masked_fill))
    d_values = jnp.einsum(
        "hqk,qhd->khd", probs.astype(jnp.bfloat16), d_out, preferred_element_type=jnp.float32
    )
    d_probs = jnp.einsum("qhd,khd->hqk", d_out, values, preferred_element_type=jnp.float32)
    d_scores = (probs * (d_probs - delta[:, :, None])).astype(jnp.bfloat16)
    d_query = jnp.einsum("hqk,khd->qhd", d_scores, keys, preferred_element_type=jnp.float32) * scale
    d_keys = jnp.einsum("hqk,qhd->khd", d_scores, query, preferred_element_type=jnp.float32) * scale
    return (d_query, d_keys, d_values)


def ring_local(
    tokens,
    cotangent,
    seq_ids,
    w_query,
    b_query,
    w_key,
    w_value,
    b_value,
    w_out,
    b_out,
    attn_gain,
    attn_shift,
    w_up,
    b_up,
    w_down,
    b_down,
    ffn_gain,
    ffn_shift,
):
    cycle = lax.axis_size("ctx")
    tok_rows = tokens.shape[1]
    width = tokens.shape[2]
    heads = width // HEAD_DIM
    scale = 1.0 / math.sqrt(HEAD_DIM)
    share = tok_rows // cycle
    got_tokens, got_grads, got_ids = (
        lax.all_to_all(
            tokens[0].reshape(share, cycle, width), "ctx", split_axis=1, concat_axis=1, tiled=True
        ),
        lax.all_to_all(
            cotangent[0].reshape(share, cycle, width),
            "ctx",
            split_axis=1,
            concat_axis=1,
            tiled=True,
        ),
        lax.all_to_all(
            seq_ids[0].reshape(share, cycle), "ctx", split_axis=1, concat_axis=1, tiled=True
        ),
    )
    x_local = got_tokens.reshape(tok_rows, width)
    local_gradient = got_grads.reshape(tok_rows, width).astype(jnp.float32)
    local_ids = got_ids.reshape(tok_rows)
    (
        query_mat,
        query_bias,
        key_mat,
        value_mat,
        value_bias,
        out_mat,
        out_bias,
        attention_norm_gain,
        first_shift,
        up_mat,
        up_bias,
        down_mat,
        down_bias,
        feedforward_norm_gain,
        second_shift,
    ) = (
        lax.all_gather(w_query, "shard", axis=0, tiled=True),
        lax.all_gather(b_query, "shard", axis=0, tiled=True),
        lax.all_gather(w_key, "shard", axis=0, tiled=True),
        lax.all_gather(w_value, "shard", axis=0, tiled=True),
        lax.all_gather(b_value, "shard", axis=0, tiled=True),
        lax.all_gather(w_out, "shard", axis=0, tiled=True),
        lax.all_gather(b_out, "shard", axis=0, tiled=True),
        lax.all_gather(attn_gain, "shard", axis=0, tiled=True),
        lax.all_gather(attn_shift, "shard", axis=0, tiled=True),
        lax.all_gather(w_up, "shard", axis=0, tiled=True),
        lax.all_gather(b_up, "shard", axis=0, tiled=True),
        lax.all_gather(w_down, "shard", axis=0, tiled=True),
        lax.all_gather(b_down, "shard", axis=0, tiled=True),
        lax.all_gather(ffn_gain, "shard", axis=0, tiled=True),
        lax.all_gather(ffn_shift, "shard", axis=0, tiled=True),
    )
    query = (matmul(x_local, query_mat) + query_bias.astype(jnp.float32)).astype(jnp.bfloat16)
    keys = matmul(x_local, key_mat).astype(jnp.bfloat16)
    values = (matmul(x_local, value_mat) + value_bias.astype(jnp.float32)).astype(jnp.bfloat16)
    q_heads = query.reshape(tok_rows, heads, HEAD_DIM)
    start_stats = (
        jnp.full((heads, tok_rows), masked_fill, jnp.float32),
        jnp.zeros((heads, tok_rows), jnp.float32),
        jnp.zeros((heads, tok_rows, HEAD_DIM), jnp.float32),
    )

    def forward_step(step, carry):
        block, stats = carry
        stats = attend(
            q_heads,
            local_ids,
            block[0].reshape(tok_rows, heads, HEAD_DIM),
            block[1].reshape(tok_rows, heads, HEAD_DIM),
            block[2],
            stats,
            scale,
        )
        block = from_behind((block[0], block[1], block[2]), "ctx", 1)
        return (block, stats)

    block, stats = lax.fori_loop(
        0, cycle - 1, forward_step, ((keys, values, local_ids), start_stats)
    )
    top, total, accum = attend(
        q_heads,
        local_ids,
        block[0].reshape(tok_rows, heads, HEAD_DIM),
        block[1].reshape(tok_rows, heads, HEAD_DIM),
        block[2],
        stats,
        scale,
    )
    attn_out = (
        (accum / total[:, :, None]).transpose(1, 0, 2).reshape(tok_rows, width).astype(jnp.bfloat16)
    )
    log_total = top + jnp.log(total)
    attn_proj = matmul(attn_out, out_mat) + out_bias.astype(jnp.float32)
    first_sum = x_local.astype(jnp.float32) + attn_proj
    first_normalized_rows, first_centered_scaled, first_inverse_deviation = apply_layer_norm(
        first_sum, attention_norm_gain.astype(jnp.float32), first_shift.astype(jnp.float32)
    )
    normed_low = first_normalized_rows.astype(jnp.bfloat16)
    up_pre = matmul(normed_low, up_mat) + up_bias.astype(jnp.float32)
    up_act = jax.nn.gelu(up_pre, approximate=False).astype(jnp.bfloat16)
    down_pre = matmul(up_act, down_mat) + down_bias.astype(jnp.float32)
    layer_output, second_centered_scaled, second_inverse_deviation = apply_layer_norm(
        first_normalized_rows + down_pre,
        feedforward_norm_gain.astype(jnp.float32),
        second_shift.astype(jnp.float32),
    )
    (
        query_mat,
        key_mat,
        value_mat,
        out_mat,
        attention_norm_gain,
        up_mat,
        down_mat,
        feedforward_norm_gain,
    ) = (
        lax.all_gather(w_query, "shard", axis=0, tiled=True),
        lax.all_gather(w_key, "shard", axis=0, tiled=True),
        lax.all_gather(w_value, "shard", axis=0, tiled=True),
        lax.all_gather(w_out, "shard", axis=0, tiled=True),
        lax.all_gather(attn_gain, "shard", axis=0, tiled=True),
        lax.all_gather(w_up, "shard", axis=0, tiled=True),
        lax.all_gather(w_down, "shard", axis=0, tiled=True),
        lax.all_gather(ffn_gain, "shard", axis=0, tiled=True),
    )
    grad_two, d_second_gain, d_second_shift = norm_back(
        local_gradient,
        second_centered_scaled,
        second_inverse_deviation,
        feedforward_norm_gain.astype(jnp.float32),
    )
    grad_down = grad_two.astype(jnp.bfloat16)
    d_down_bias = jnp.sum(grad_down, axis=0, dtype=jnp.float32)
    d_down_mat = matmul_tn(up_act, grad_down)
    grad_up = (matmul_nt(grad_down, down_mat) * gelu_slope(up_pre)).astype(jnp.bfloat16)
    d_up_bias = jnp.sum(grad_up, axis=0, dtype=jnp.float32)
    d_up_mat = matmul_tn(normed_low, grad_up)
    first_norm_gradient = grad_two + matmul_nt(grad_up, up_mat)
    grad_first, d_first_gain, d_first_shift = norm_back(
        first_norm_gradient,
        first_centered_scaled,
        first_inverse_deviation,
        attention_norm_gain.astype(jnp.float32),
    )
    grad_proj = grad_first.astype(jnp.bfloat16)
    d_out_bias = jnp.sum(grad_proj, axis=0, dtype=jnp.float32)
    d_out_mat = matmul_tn(attn_out, grad_proj)
    grad_attn = matmul_nt(grad_proj, out_mat).astype(jnp.bfloat16)
    grad_heads = grad_attn.reshape(tok_rows, heads, HEAD_DIM)
    delta = jnp.einsum(
        "qhd,qhd->hq",
        grad_heads,
        attn_out.reshape(tok_rows, heads, HEAD_DIM),
        preferred_element_type=jnp.float32,
    )
    zero_rows = jnp.zeros((tok_rows, width), jnp.float32)

    def key_step(step, carry):
        block, sums, acc_query = carry
        d_query, d_keys, d_values = block_grads(
            q_heads,
            local_ids,
            grad_heads,
            log_total,
            delta,
            block[0].reshape(tok_rows, heads, HEAD_DIM),
            block[1].reshape(tok_rows, heads, HEAD_DIM),
            block[2],
            scale,
        )
        sums = (
            sums[0] + d_keys.reshape(tok_rows, width),
            sums[1] + d_values.reshape(tok_rows, width),
        )
        block = from_behind((block[0], block[1], block[2]), "ctx", 1)
        sums = (
            from_behind(sums[0].astype(jnp.bfloat16), "ctx", 1).astype(jnp.float32),
            from_behind(sums[1].astype(jnp.bfloat16), "ctx", 1).astype(jnp.float32),
        )
        return (block, sums, acc_query + d_query.reshape(tok_rows, width))

    block, sums, d_query_sum = lax.fori_loop(
        0, cycle, key_step, ((keys, values, local_ids), (zero_rows, zero_rows), zero_rows)
    )
    d_keys_sum, d_values_sum = sums
    grad_query = d_query_sum.astype(jnp.bfloat16)
    grad_keys = d_keys_sum.astype(jnp.bfloat16)
    grad_values = d_values_sum.astype(jnp.bfloat16)
    d_query_bias = jnp.sum(grad_query, axis=0, dtype=jnp.float32)
    d_value_bias = jnp.sum(grad_values, axis=0, dtype=jnp.float32)
    d_query_mat = matmul_tn(x_local, grad_query)
    d_key_mat = matmul_tn(x_local, grad_keys)
    d_value_mat = matmul_tn(x_local, grad_values)
    grad_input = (
        grad_first
        + matmul_nt(grad_query, query_mat)
        + matmul_nt(grad_keys, key_mat)
        + matmul_nt(grad_values, value_mat)
    )
    home_hidden, home_grad = (
        lax.all_to_all(
            layer_output.astype(jnp.bfloat16).reshape(share, cycle, width),
            "ctx",
            split_axis=1,
            concat_axis=1,
            tiled=True,
        ),
        lax.all_to_all(
            grad_input.astype(jnp.bfloat16).reshape(share, cycle, width),
            "ctx",
            split_axis=1,
            concat_axis=1,
            tiled=True,
        ),
    )
    hidden_out = home_hidden.reshape(tok_rows, width)[None]
    tokens_grad = home_grad.reshape(tok_rows, width)[None]
    shares = (
        lax.psum_scatter(
            d_query_mat.astype(jnp.bfloat16), "shard", scatter_dimension=0, tiled=True
        ).astype(jnp.float32),
        lax.psum_scatter(
            d_query_bias.astype(jnp.bfloat16), "shard", scatter_dimension=0, tiled=True
        ).astype(jnp.float32),
        lax.psum_scatter(
            d_key_mat.astype(jnp.bfloat16), "shard", scatter_dimension=0, tiled=True
        ).astype(jnp.float32),
        lax.psum_scatter(
            d_value_mat.astype(jnp.bfloat16), "shard", scatter_dimension=0, tiled=True
        ).astype(jnp.float32),
        lax.psum_scatter(
            d_value_bias.astype(jnp.bfloat16), "shard", scatter_dimension=0, tiled=True
        ).astype(jnp.float32),
        lax.psum_scatter(
            d_out_mat.astype(jnp.bfloat16), "shard", scatter_dimension=0, tiled=True
        ).astype(jnp.float32),
        lax.psum_scatter(
            d_out_bias.astype(jnp.bfloat16), "shard", scatter_dimension=0, tiled=True
        ).astype(jnp.float32),
        lax.psum_scatter(
            d_first_gain.astype(jnp.bfloat16), "shard", scatter_dimension=0, tiled=True
        ).astype(jnp.float32),
        lax.psum_scatter(
            d_first_shift.astype(jnp.bfloat16), "shard", scatter_dimension=0, tiled=True
        ).astype(jnp.float32),
        lax.psum_scatter(
            d_up_mat.astype(jnp.bfloat16), "shard", scatter_dimension=0, tiled=True
        ).astype(jnp.float32),
        lax.psum_scatter(
            d_up_bias.astype(jnp.bfloat16), "shard", scatter_dimension=0, tiled=True
        ).astype(jnp.float32),
        lax.psum_scatter(
            d_down_mat.astype(jnp.bfloat16), "shard", scatter_dimension=0, tiled=True
        ).astype(jnp.float32),
        lax.psum_scatter(
            d_down_bias.astype(jnp.bfloat16), "shard", scatter_dimension=0, tiled=True
        ).astype(jnp.float32),
        lax.psum_scatter(
            d_second_gain.astype(jnp.bfloat16), "shard", scatter_dimension=0, tiled=True
        ).astype(jnp.float32),
        lax.psum_scatter(
            d_second_shift.astype(jnp.bfloat16), "shard", scatter_dimension=0, tiled=True
        ).astype(jnp.float32),
    )
    totals = lax.psum(
        (
            shares[0],
            shares[1],
            shares[2],
            shares[3],
            shares[4],
            shares[5],
            shares[6],
            shares[7],
            shares[8],
            shares[9],
            shares[10],
            shares[11],
            shares[12],
            shares[13],
            shares[14],
        ),
        "ctx",
    )
    return (hidden_out, tokens_grad) + tuple(totals)


def ring_solution(mesh):
    return jax.shard_map(
        ring_local,
        mesh=mesh,
        in_specs=(
            P("shard", "ctx", None),
            P("shard", "ctx", None),
            P("shard", "ctx"),
            P("shard", None),
            P("shard"),
            P("shard", None),
            P("shard", None),
            P("shard"),
            P("shard", None),
            P("shard"),
            P("shard"),
            P("shard"),
            P("shard", None),
            P("shard"),
            P("shard", None),
            P("shard"),
            P("shard"),
            P("shard"),
        ),
        out_specs=(
            P("shard", "ctx", None),
            P("shard", "ctx", None),
            P("shard", None),
            P("shard"),
            P("shard", None),
            P("shard", None),
            P("shard"),
            P("shard", None),
            P("shard"),
            P("shard"),
            P("shard"),
            P("shard", None),
            P("shard"),
            P("shard", None),
            P("shard"),
            P("shard"),
            P("shard"),
        ),
        check_vma=False,
    )


AXES = ("q", "r", "x", "c")
ANY = pl.BlockSpec(memory_space=pl.ANY)
WHOLE = pl.BlockSpec(memory_space=pltpu.VMEM)


def moved(block, move):
    sizes = [lax.axis_size(a) for a in AXES]

    def number(spot):
        place = 0
        for size, at in zip(sizes, spot):
            place = place * size + at
        return place

    spots = [
        (q, r, x, c)
        for q in range(sizes[0])
        for r in range(sizes[1])
        for x in range(sizes[2])
        for c in range(sizes[3])
    ]
    return lax.ppermute(block, AXES, [(number(s), number(move(*s))) for s in spots])


def swap_x(block):
    return moved(block, lambda q, r, x, c: (q, r, 1 - x, c))


def swap_c(block):
    return moved(block, lambda q, r, x, c: (q, r, x, 1 - c))


def swap_r(block):
    return moved(block, lambda q, r, x, c: (q, r ^ 1, x, c))


def swap_rc(block):
    return moved(block, lambda q, r, x, c: (q, r ^ 1, x, 1 - c))


def swap_near(block):
    return moved(block, lambda q, r, x, c: (q ^ 1, r, x, c))


def swap_far(block):
    return moved(block, lambda q, r, x, c: (q ^ 2, r, x, c))


def regroup(block):
    return moved(block, lambda q, r, x, c: (2 * c + x, r, q & 1, q >> 1))


def in_order(mine, theirs, bit):
    first, second = jnp.stack([mine, theirs]), jnp.stack([theirs, mine])
    return jnp.where(bit == 0, first, second)


def take(stacked, at):
    return lax.dynamic_index_in_dim(stacked, at, 0, keepdims=False)


def dot(left, right):
    return jnp.dot(left, right, preferred_element_type=jnp.float32)


def dot_nt(left, right):
    return lax.dot_general(
        left, right, (((1,), (1,)), ((), ())), preferred_element_type=jnp.float32
    )


class Copies:
    def __init__(self, sems):
        self.sems = sems
        self.count = 0
        self.held = []

    def start(self, source, target):
        copy = pltpu.make_async_copy(source, target, self.sems.at[self.count])
        copy.start()
        self.count += 1
        self.held.append(copy)

    def wait(self):
        for copy in self.held:
            copy.wait()
        self.held = []


def spot():
    return tuple(lax.axis_index(a) for a in AXES)


def fill_mask(ids, mask, own):
    blocks, rows = ids.shape
    mine = jnp.concatenate([ids[pl.ds(own, 1), :], ids[pl.ds(own + 1, 1), :]], axis=1)
    across = jnp.transpose(ids[...])
    for b in range(blocks):
        mask[rows * b : rows * (b + 1), :] = jnp.where(across[:, b : b + 1] == mine, 0.0, masked_fill)


def attend_kernel(
    b0, b1, b2, b3, b4, b5, b6, b7, w_q, w_k, w_v, w_x, w_m, w_mx, w_o, w_om, bias,
    x_out, w_out, wo_out, k_out, v_out, q_out, o_out, lse_out, ids_out, a_out, a_low,
    xs, raw, w, wo, k3, v3, vt, q3, ot, mask, sems, outs,
):
    q, r, x, c = spot()
    rows = xs.shape[0] // 8
    part = w.shape[0] // 4
    half = wo.shape[0]
    width = w.shape[0]
    me, shard = 4 * r + 2 * c + x, 2 * x + c
    ins = Copies(sems)
    for j, block in enumerate((b0, b1, b2, b3, b4, b5, b6, b7)):
        at = me ^ j
        ins.start(block.at[pl.ds(0, rows)], xs.at[pl.ds(pl.multiple_of(rows * at, rows), rows)])
        ins.start(block.at[pl.ds(rows, 16)], raw.at[at])
    columns = pl.ds(pl.multiple_of(half * x, 128), half)
    for t, own in enumerate((w_q, w_k, w_v)):
        place = pl.ds(half * t, half)
        ins.start(own.at[:, columns], w.at[pl.ds(pl.multiple_of(part * shard, 64), part), place])
        for flip, piece in ((2, w_x), (1, w_m), (3, w_mx)):
            at = pl.ds(pl.multiple_of(part * (shard ^ flip), 64), part)
            ins.start(piece.at[t], w.at[at, place])
    ins.start(w_o, wo.at[pl.ds(pl.multiple_of(part * c, 64), part)])
    ins.start(w_om, wo.at[pl.ds(pl.multiple_of(part * (1 - c), 64), part)])
    ins.wait()
    backs = Copies(outs)
    backs.start(xs, x_out)
    backs.start(w, w_out)
    backs.start(wo, wo_out)
    for b in range(8):
        ids_out[b : b + 1, :] = raw[b, 0:1, 0:rows].astype(jnp.float32)
    fill_mask(ids_out, mask, 4 * r + 2 * c)
    keyed = dot(xs[...], w[:, half : 2 * half]).astype(jnp.bfloat16)
    valued = dot(xs[...], w[:, 2 * half : 3 * half]) + bias[1:2, :]
    own = pl.ds(pl.multiple_of(rows * (4 * r + 2 * c), rows), 2 * rows)
    asked = (dot(xs[own, :], w[:, 0:half]) + bias[0:1, :]).astype(jnp.bfloat16)
    turned = jnp.transpose(valued).astype(jnp.bfloat16)
    valued = valued.astype(jnp.bfloat16)
    pairs = half // 128
    for p in range(pairs):
        k3[p] = keyed[:, 128 * p : 128 * (p + 1)]
        v3[p] = valued[:, 128 * p : 128 * (p + 1)]
        q3[p] = asked[:, 128 * p : 128 * (p + 1)]
    for h in range(2 * pairs):
        vt[h] = turned[64 * h : 64 * (h + 1), :]
    backs.start(k3, k_out)
    backs.start(v3, v_out)
    q_out[...] = q3[...]
    lane = lax.broadcasted_iota(jnp.int32, (2 * rows, 128), 1) // 64

    def head(h, carry):
        query = jnp.where(lane == h % 2, q3[h // 2], 0) * 0.125
        scores = dot_nt(k3[h // 2], query.astype(jnp.bfloat16)) + mask[...]
        top = jnp.max(scores, axis=0, keepdims=True)
        weights = jnp.exp(scores - top)
        total = jnp.sum(weights, axis=0, keepdims=True)
        ot[h] = dot(vt[h], weights.astype(jnp.bfloat16)) / total
        lse_out[pl.ds(h, 1), :] = top + jnp.log(total)
        return carry

    lax.fori_loop(0, 2 * pairs, head, 0)
    mixed = jnp.transpose(ot[...].reshape(half, 2 * rows)).astype(jnp.bfloat16)
    o_out[...] = mixed
    partial = dot(mixed, wo[...])
    a_out[...] = partial
    a_low[...] = partial.astype(jnp.bfloat16)
    backs.wait()


def load_feedforward(copies, up, down, u_own, u_x, u_m, u_mx, d_own, d_m):
    q, r, x, c = spot()
    part = up.shape[0] // 4
    wide = up.shape[1] // 4
    shard = 2 * x + c
    for j in range(4):
        at = pl.ds(wide * j, wide)
        slot = (2 * c + r) ^ j
        pieces = ((0, u_own, 4 * wide * x), (2, u_x, 0), (1, u_m, 0), (3, u_mx, 0))
        for flip, piece, base in pieces:
            rows = pl.ds(pl.multiple_of(part * (shard ^ flip), 64), part)
            columns = pl.ds(pl.multiple_of(base + wide * slot, 128), wide)
            copies.start(piece.at[:, columns], up.at[rows, at])
        source = d_own if j < 2 else d_m
        copies.start(source.at[pl.ds(pl.multiple_of(wide * (r ^ (j & 1)), 128), wide)], down.at[at])


def norm_of(value):
    mean = jnp.mean(value, axis=-1, keepdims=True)
    centered = value - mean
    rstd = lax.rsqrt(jnp.mean(centered * centered, axis=-1, keepdims=True) + ln_eps)
    return centered * rstd, rstd


def norm_pull(scaled, normed, rstd):
    return rstd * (
        scaled
        - jnp.mean(scaled, axis=-1, keepdims=True)
        - normed * jnp.mean(scaled * normed, axis=-1, keepdims=True)
    )


def forward_kernel(
    a_own, a_got, xs, vecs, b_up, u_own, u_x, u_m, u_mx, d_own, d_m,
    h_out, n_out, r_out, z_out, slope_out, y_out, y_low,
    up, down, x_own, sems, more,
):
    q, r, x, c = spot()
    rows = x_own.shape[0]
    first = Copies(more)
    first.start(xs.at[pl.ds(pl.multiple_of(rows * (2 * r + c), rows), rows)], x_own)
    copies = Copies(sems)
    load_feedforward(copies, up, down, u_own, u_x, u_m, u_mx, d_own, d_m)
    first.wait()
    total = x_own[...].astype(jnp.float32) + (a_own[...] + a_got[...].astype(jnp.float32) + vecs[0:1, :])
    normed, rstd = norm_of(total)
    n_out[...] = normed
    r_out[...] = jnp.broadcast_to(rstd, r_out.shape)
    low = (normed * vecs[1:2, :] + vecs[2:3, :]).astype(jnp.bfloat16)
    h_out[...] = low
    copies.wait()
    wide = up.shape[1] // 4
    for j in range(4):
        pre = dot(low, up[:, wide * j : wide * (j + 1)]) + b_up[(2 * c + r) ^ j, 0:1, :]
        cdf = 0.5 * (1.0 + lax.erf(pre * (1.0 / math.sqrt(2.0))))
        density = jnp.exp(-0.5 * pre * pre) * (1.0 / math.sqrt(2.0 * math.pi))
        z_out[j] = (pre * cdf).astype(jnp.bfloat16)
        slope_out[j] = cdf + pre * density
    result = dot(z_out[0], down[0:wide, :])
    for j in range(1, 4):
        result += dot(z_out[j], down[wide * j : wide * (j + 1), :])
    y_out[...] = result
    y_low[...] = result.astype(jnp.bfloat16)


def backward_kernel(
    y_own, y_got, normed1, g_own, g_x, slope, vecs, u_own, u_x, u_m, u_mx, d_own, d_m,
    hid_out, dy_out, du_out, s_out, p_low, sums, up_sums,
    up, down, grad, hid, sems, more,
):
    q, r, x, c = spot()
    rows = grad.shape[0] // 2
    first = Copies(more)
    first.start(g_own, grad.at[pl.ds(pl.multiple_of(rows * x, rows), rows)])
    first.start(g_x, grad.at[pl.ds(pl.multiple_of(rows * (1 - x), rows), rows)])
    copies = Copies(sems)
    load_feedforward(copies, up, down, u_own, u_x, u_m, u_mx, d_own, d_m)
    first.wait()
    h1 = normed1[...] * vecs[1:2, :] + vecs[2:3, :]
    normed, rstd = norm_of(h1 + (y_own[...] + y_got[...].astype(jnp.float32) + vecs[3:4, :]))
    hid[...] = (normed * vecs[4:5, :] + vecs[5:6, :]).astype(jnp.bfloat16)
    hid_out[...] = hid[pl.ds(pl.multiple_of(rows * x, rows), rows), :]
    cot = grad[...].astype(jnp.float32)
    dy = norm_pull(cot * vecs[4:5, :], normed, rstd)
    low = dy.astype(jnp.bfloat16)
    dy_out[...] = low
    sums[...] = jnp.zeros_like(sums)
    sums[0:1, :] = jnp.sum(low.astype(jnp.float32), axis=0, keepdims=True)
    sums[1:2, :] = jnp.sum(cot * normed, axis=0, keepdims=True)
    sums[2:3, :] = jnp.sum(cot, axis=0, keepdims=True)
    copies.wait()
    wide = up.shape[1] // 4
    result = jnp.zeros(dy.shape, jnp.float32)
    for j in range(4):
        du = (dot_nt(low, down[wide * j : wide * (j + 1), :]) * slope[j]).astype(jnp.bfloat16)
        du_out[j] = du
        total = jnp.sum(du.astype(jnp.float32), axis=0, keepdims=True)
        up_sums[j] = jnp.broadcast_to(total, up_sums.shape[1:])
        result += dot_nt(du, up[:, wide * j : wide * (j + 1)])
    s_out[...] = dy + result
    p_low[...] = result.astype(jnp.bfloat16)


def attend_back_kernel(
    s_own, p_got, normed1, rstd1, vecs, wo, mixed, q3, k3, v3, kt, lse, ids,
    dr_out, da_out, dq_out, dkv_out, sums, qv_sums,
    mask, do3, delta, dk, dv, dqt, whole,
):
    q, r, x, c = spot()
    rows = dr_out.shape[0]
    pairs = q3.shape[0]
    half = 128 * pairs
    fill_mask(ids, mask, 4 * r + 2 * c)
    dh = s_own[...] + p_got[...].astype(jnp.float32)
    normed = normed1[...]
    dr = norm_pull(dh * vecs[1:2, :], normed, rstd1[:, 0:1])
    whole[...] = dr
    dr_out[...] = whole[pl.ds(pl.multiple_of(rows * x, rows), rows), :]
    low = dr.astype(jnp.bfloat16)
    da_out[...] = low
    sums[...] = jnp.zeros_like(sums)
    sums[0:1, :] = jnp.sum(low.astype(jnp.float32), axis=0, keepdims=True)
    sums[1:2, :] = jnp.sum(dh * normed, axis=0, keepdims=True)
    sums[2:3, :] = jnp.sum(dh, axis=0, keepdims=True)
    d_o = dot_nt(low, wo[...]).astype(jnp.bfloat16)
    products = jnp.transpose(d_o.astype(jnp.float32) * mixed[...].astype(jnp.float32))
    for h in range(2 * pairs):
        delta[h : h + 1, :] = jnp.sum(products[64 * h : 64 * (h + 1), :], axis=0, keepdims=True)
    for p in range(pairs):
        do3[p] = d_o[:, 128 * p : 128 * (p + 1)]
    dk[...] = jnp.zeros_like(dk)
    dv[...] = jnp.zeros_like(dv)
    lane = lax.broadcasted_iota(jnp.int32, (2 * rows, 128), 1) // 64

    def head(h, carry):
        p = h // 2
        here = lane == h % 2
        query = (jnp.where(here, q3[p], 0) * 0.125).astype(jnp.bfloat16)
        d_here = jnp.where(here, do3[p], 0).astype(jnp.bfloat16)
        probs = jnp.exp(dot_nt(k3[p], query) + mask[...] - lse[pl.ds(h, 1), :])
        d_probs = dot_nt(v3[p], d_here)
        d_scores = (probs * (d_probs - delta[pl.ds(h, 1), :])).astype(jnp.bfloat16)
        dv[p] += dot(probs.astype(jnp.bfloat16), d_here)
        dk[p] += dot(d_scores, query)
        dqt[h] = dot(kt[h], d_scores)
        return carry

    lax.fori_loop(0, 2 * pairs, head, 0)
    dq = (jnp.transpose(dqt[...].reshape(half, 2 * rows)) * 0.125).astype(jnp.bfloat16)
    dq_out[...] = dq
    qv_sums[...] = jnp.zeros_like(qv_sums)
    qv_sums[0:1, :] = jnp.sum(dq.astype(jnp.float32), axis=0, keepdims=True)
    for p in range(pairs):
        at = slice(128 * p, 128 * (p + 1))
        dkv_out[:, at] = dk[p].astype(jnp.bfloat16)
        value = dv[p].astype(jnp.bfloat16)
        dkv_out[:, half + 128 * p : half + 128 * (p + 1)] = value
        qv_sums[1:2, at] = jnp.sum(value.astype(jnp.float32), axis=0, keepdims=True)


def input_grad_kernel(dq, dkv, w, send, keep, whole):
    q, r, x, c = spot()
    half = dq.shape[1]
    rows = dq.shape[0] // 2
    whole[...] = dot_nt(dkv[...], w[:, half:])
    own = pl.ds(pl.multiple_of(rows * (4 * r + 2 * c), rows), 2 * rows)
    whole[own, :] += dot_nt(dq[...], w[:, 0:half])
    for b in range(2):
        mine = pl.ds(pl.multiple_of(rows * (4 * b + 2 * c), rows), 2 * rows)
        keep[b] = whole[mine, :]
        theirs = pl.ds(pl.multiple_of(rows * (4 * b + 2 * (1 - c)), rows), 2 * rows)
        send[b] = whole[theirs, :].astype(jnp.bfloat16)


def kernel_call(body, name, ins, outs, scratch, cost, args):
    return pl.pallas_call(
        body,
        name=name,
        out_shape=[jax.ShapeDtypeStruct(shape, dtype) for shape, dtype, _ in outs],
        in_specs=ins,
        out_specs=[spec for _, _, spec in outs],
        scratch_shapes=scratch,
        cost_estimate=pl.CostEstimate(flops=cost, bytes_accessed=8 << 20, transcendentals=0),
    )(*args)


def plane_local(
    tokens, cotangent, seq_ids, w_query, b_query, w_key, w_value, b_value, w_out, b_out,
    attn_gain, attn_shift, w_up, b_up, w_down, b_down, ffn_gain, ffn_shift,
):
    q, r, x, c = spot()
    q1, q0 = q // 2, q % 2
    low, wide_type = jnp.bfloat16, jnp.float32
    rows, width = tokens.shape[1:]
    part = w_query.shape[0]
    half = width // 2
    inner = w_up.shape[1]
    wide = inner // 8
    keys = 8 * rows
    pairs = half // 128

    ids_rows = jnp.pad(seq_ids.astype(low), ((0, 15), (0, width - rows)))
    blocks = [regroup(jnp.concatenate([tokens[0], ids_rows]))]
    blocks.append(swap_x(blocks[0]))
    blocks.append(swap_c(blocks[0]))
    blocks.append(swap_c(blocks[1]))
    blocks.append(swap_r(blocks[0]))
    blocks.append(swap_r(blocks[1]))
    blocks.append(swap_c(blocks[4]))
    blocks.append(swap_c(blocks[5]))

    def cut(w, side, size):
        return lax.dynamic_slice_in_dim(w, side * size, size, 1)

    qkv = (w_query, w_key, w_value)
    qkv_x = swap_x(jnp.stack([cut(w, 1 - x, half) for w in qkv]))
    qkv_m = swap_c(jnp.stack([cut(w, x, half) for w in qkv]))
    qkv_mx = swap_c(qkv_x)
    out_m = swap_c(w_out)
    small = jnp.concatenate(
        [b_query, b_value, b_out, attn_gain, attn_shift, b_down, ffn_gain, ffn_shift, b_up]
    ).reshape(-1, half)
    small = jnp.pad(small, ((0, 8 - small.shape[0]), (0, 0)))
    small_x = swap_x(small)
    small_m = swap_c(small)
    small_mx = swap_c(small_x)
    up_x = swap_x(cut(w_up, 1 - x, 4 * wide))
    up_m = swap_c(cut(w_up, x, 4 * wide))
    up_mx = swap_c(up_x)
    down_m = swap_c(w_down)

    chip = in_order(small, small_m, c).astype(wide_type)
    other = in_order(small_x, small_mx, c).astype(wide_type)
    every = in_order(chip, other, x).reshape(4, -1)
    mine = chip.reshape(2, -1)
    names = ("b_q", "b_v", "b_out", "gain1", "shift1", "b_down", "gain2", "shift2")
    vec = {n: every[:, part * i : part * (i + 1)].reshape(1, width) for i, n in enumerate(names)}
    vecs = jnp.concatenate(
        [vec[n] for n in names[2:]] + [jnp.zeros((2, width), wide_type)]
    )
    bias = jnp.concatenate(
        [mine[:, part * i : part * (i + 1)].reshape(1, half) for i in range(2)]
        + [jnp.zeros((6, half), wide_type)]
    )
    up_bias = mine[:, 8 * part : 8 * part + 2 * wide].reshape(4, 1, wide)
    up_bias = jnp.broadcast_to(up_bias, (4, 8, wide))

    own = 2 * rows
    x_all, w_all, wo_all, k3, v3, q3, mixed, lse, ids, a_own, a_low = kernel_call(
        attend_kernel,
        "attend",
        [ANY] * 16 + [WHOLE],
        [
            ((keys, width), low, ANY),
            ((width, 3 * half), low, ANY),
            ((half, width), low, ANY),
            ((pairs, keys, 128), low, ANY),
            ((pairs, keys, 128), low, ANY),
            ((pairs, own, 128), low, WHOLE),
            ((own, half), low, WHOLE),
            ((8, own), wide_type, WHOLE),
            ((8, rows), wide_type, WHOLE),
            ((own, width), wide_type, WHOLE),
            ((own, width), low, WHOLE),
        ],
        [
            pltpu.VMEM((keys, width), low),
            pltpu.VMEM((8, 16, width), low),
            pltpu.VMEM((width, 3 * half), low),
            pltpu.VMEM((half, width), low),
            pltpu.VMEM((pairs, keys, 128), low),
            pltpu.VMEM((pairs, keys, 128), low),
            pltpu.VMEM((2 * pairs, 64, keys), low),
            pltpu.VMEM((pairs, own, 128), low),
            pltpu.VMEM((2 * pairs, 64, own), wide_type),
            pltpu.VMEM((keys, own), wide_type),
            pltpu.SemaphoreType.DMA((30,)),
            pltpu.SemaphoreType.DMA((5,)),
        ],
        6 * 10**9,
        (*blocks, *qkv, qkv_x, qkv_m, qkv_mx, w_out, out_m, bias),
    )
    a_got = swap_x(a_low)
    kt = jnp.swapaxes(k3, 1, 2).reshape(2 * pairs, 64, keys)

    inner_weights = (w_up, up_x, up_m, up_mx, w_down, down_m)
    inner_scratch = [
        pltpu.VMEM((width, 4 * wide), low),
        pltpu.VMEM((4 * wide, width), low),
    ]
    h_low, normed1, rstd1, z, slope, y_own, y_low = kernel_call(
        forward_kernel,
        "feedforward",
        [WHOLE, WHOLE, ANY, WHOLE, WHOLE] + [ANY] * 6,
        [
            ((own, width), low, WHOLE),
            ((own, width), wide_type, WHOLE),
            ((own, 128), wide_type, WHOLE),
            ((4, own, wide), low, WHOLE),
            ((4, own, wide), wide_type, WHOLE),
            ((own, width), wide_type, WHOLE),
            ((own, width), low, WHOLE),
        ],
        inner_scratch
        + [pltpu.VMEM((own, width), low), pltpu.SemaphoreType.DMA((20,)), pltpu.SemaphoreType.DMA((1,))],
        2 * 10**9,
        (a_own, a_got, x_all, vecs, up_bias, *inner_weights),
    )
    y_got = swap_x(y_low)

    def over_plane(pieces):
        return jnp.concatenate([pieces[0], swap_r(pieces[1]), swap_c(pieces[2]), swap_rc(pieces[3])])

    def whole_plane(block):
        beside = swap_r(block)
        return jnp.concatenate([block, beside, swap_c(block), swap_c(beside)])

    z_plane = over_plane([z[j] for j in range(4)])
    h_plane = whole_plane(h_low)

    cot = regroup(cotangent[0])
    cot_x = swap_x(cot)
    hidden, dy, du, s_own, p_low, sums2, up_sums = kernel_call(
        backward_kernel,
        "feedforward_back",
        [WHOLE, WHOLE, WHOLE, ANY, ANY, WHOLE, WHOLE] + [ANY] * 6,
        [
            ((rows, width), low, WHOLE),
            ((own, width), low, WHOLE),
            ((4, own, wide), low, WHOLE),
            ((own, width), wide_type, WHOLE),
            ((own, width), low, WHOLE),
            ((8, width), wide_type, WHOLE),
            ((4, 8, wide), wide_type, WHOLE),
        ],
        inner_scratch
        + [
            pltpu.VMEM((own, width), low),
            pltpu.VMEM((own, width), low),
            pltpu.SemaphoreType.DMA((20,)),
            pltpu.SemaphoreType.DMA((2,)),
        ],
        2 * 10**9,
        (y_own, y_got, normed1, cot, cot_x, slope, vecs, *inner_weights),
    )
    p_got = swap_x(p_low)
    hidden_out = regroup(hidden)[None]

    dr, da, dq, dkv, sums1, qv_sums = kernel_call(
        attend_back_kernel,
        "attend_back",
        [WHOLE] * 13,
        [
            ((rows, width), wide_type, WHOLE),
            ((own, width), low, WHOLE),
            ((own, half), low, WHOLE),
            ((keys, 2 * half), low, WHOLE),
            ((8, width), wide_type, WHOLE),
            ((8, half), wide_type, WHOLE),
        ],
        [
            pltpu.VMEM((keys, own), wide_type),
            pltpu.VMEM((pairs, own, 128), low),
            pltpu.VMEM((8, own), wide_type),
            pltpu.VMEM((pairs, keys, 128), wide_type),
            pltpu.VMEM((pairs, keys, 128), wide_type),
            pltpu.VMEM((2 * pairs, 64, own), wide_type),
            pltpu.VMEM((own, width), wide_type),
        ],
        6 * 10**9,
        (s_own, p_got, normed1, rstd1, vecs, wo_all, mixed, q3, k3, v3, kt, lse, ids),
    )

    send, keep = kernel_call(
        input_grad_kernel,
        "input_grad",
        [WHOLE] * 3,
        [((2, own, width), low, WHOLE), ((2, own, width), wide_type, WHOLE)],
        [pltpu.VMEM((keys, width), wide_type)],
        10**9,
        (dq, dkv, w_all),
    )

    def folded(kept, got):
        return kept + got.astype(wide_type)

    total = folded(keep, swap_c(send))
    total = folded(take(total, r), swap_r(take(total, 1 - r).astype(low))).reshape(2, rows, width)
    total = folded(take(total, x), swap_x(take(total, 1 - x).astype(low)))
    tokens_grad = regroup((total + dr).astype(low))[None]

    def swept(grad):
        total = folded(take(grad, q0), swap_near(take(grad, 1 - q0).astype(low)))
        return folded(take(total, q1), swap_far(take(total, 1 - q1).astype(low)))

    def spread(block):
        block = in_order(block, swap_far(block), q1)
        block = in_order(block, swap_near(block), q0)
        return in_order(block, swap_r(block), r)

    dy_plane = whole_plane(dy)
    du_plane = over_plane([du[j] for j in range(4)])
    d_down = matmul_tn(z_plane, dy_plane).reshape(2, 2, wide // 4, width)
    d_down = spread(swept(jnp.swapaxes(d_down, 0, 1)).astype(low))
    w_down_grad = jnp.swapaxes(d_down, 1, 2).reshape(2 * wide, width).astype(wide_type)

    d_up = matmul_tn(h_plane, du_plane).reshape(4, 2, 2, part // 4, wide)
    d_up = swept(d_up.transpose(2, 1, 0, 3, 4)).astype(low).reshape(2, 2, part // 4, wide)
    d_up = in_order(take(d_up, x), swap_x(take(d_up, 1 - x)), x)
    d_up = jnp.swapaxes(d_up, 0, 1)
    d_up = in_order(take(d_up, c), swap_c(take(d_up, 1 - c)), c)
    d_up = spread(d_up)
    w_up_grad = d_up.transpose(2, 1, 5, 4, 3, 0, 6).reshape(part, inner).astype(wide_type)

    thin = part // 8
    own_x = lax.dynamic_slice_in_dim(x_all, own * (2 * r + c), own, 0)
    d_kv = matmul_tn(x_all, dkv).reshape(2, 2, 2, 2, 2, thin, 2, half)
    d_q = matmul_tn(own_x, dq).reshape(2, 2, 2, 2, 2, thin, 1, half)
    packed = jnp.concatenate([d_q, d_kv], axis=6).transpose(1, 2, 4, 3, 0, 6, 5, 7)
    d_o = matmul_tn(mixed, da).reshape(2, 2, 2, 2, thin, 2, half).transpose(0, 1, 3, 2, 5, 4, 6)
    packed = jnp.concatenate([packed.reshape(2, 2, 2, 2, 6, thin, half), d_o], axis=4)
    packed = packed.reshape(2, 8, 8 * thin, half)

    bits = up_sums[:, 0, :].reshape(2, 2, wide)
    bits = jnp.where(c == 0, bits, bits[::-1])
    bits = jnp.where(r == 0, bits, bits[:, ::-1]).reshape(4, wide)
    wides = jnp.concatenate([sums1[:3], sums2[:3]]).reshape(6, 2, half)
    wides = jnp.where(x == 0, wides[:, 0], wides[:, 1])
    lines = jnp.concatenate([qv_sums[:2], bits, wides, jnp.zeros((4, half), wide_type)])

    def step(block, lines, swap, bit):
        block = block.reshape((2, -1, half))
        out = jnp.concatenate([take(block, 1 - bit), lines]).astype(low)
        got = swap(out).astype(wide_type)
        count = block.shape[1]
        return take(block, bit) + got[:count], lines + got[count:]

    block, lines = step(packed, lines, swap_c, c)
    block, lines = step(block, lines, swap_r, r)
    block, lines = step(block, lines, swap_near, q0)
    block, lines = step(block, lines, swap_far, q1)
    block = block.astype(low)
    sides = block[: 6 * thin].reshape(2, 3 * thin, half)
    sides = in_order(take(sides, x), swap_x(take(sides, 1 - x)), x).reshape(6 * thin, half)
    block = spread(jnp.concatenate([sides, block[6 * thin :]]).reshape(8, thin, half))
    block = block.transpose(0, 2, 1, 4, 3, 5).reshape(part, 8, half).astype(wide_type)
    w_query_grad, w_key_grad, w_value_grad = (
        jnp.concatenate([block[:, t], block[:, 3 + t]], axis=1) for t in range(3)
    )
    w_out_grad = block[:, 6:8].reshape(part, width)

    pieces = take(jnp.swapaxes(lines.reshape(-1, 2, part), 0, 1), c)
    b_up_grad = take(lines[2:6].reshape(2, 2 * wide), c)
    return (
        hidden_out,
        tokens_grad,
        w_query_grad,
        pieces[0],
        w_key_grad,
        w_value_grad,
        pieces[1],
        w_out_grad,
        pieces[6],
        pieces[7],
        pieces[8],
        w_up_grad,
        b_up_grad,
        w_down_grad,
        pieces[9],
        pieces[10],
        pieces[11],
    )


def plane_solution(mesh):
    planes, cycle = mesh.shape["shard"], mesh.shape["ctx"]
    grid = Mesh(mesh.devices.reshape(planes, cycle // planes, 2, 2), AXES)
    shard, ctx = ("x", "c"), ("q", "r")
    tokens, matrix, vector = P(shard, ctx, None), P(shard, None), P(shard)
    return jax.shard_map(
        plane_local,
        mesh=grid,
        in_specs=(
            tokens, tokens, P(shard, ctx), matrix, vector, matrix, matrix, vector, matrix, vector,
            vector, vector, matrix, vector, matrix, vector, vector, vector,
        ),
        out_specs=(
            tokens, tokens, matrix, vector, matrix, matrix, vector, matrix, vector,
            vector, vector, matrix, vector, matrix, vector, vector, vector,
        ),
        check_vma=False,
    )


def solution(mesh):
    if mesh.shape["shard"] == 4 and mesh.shape["ctx"] == 8:
        return plane_solution(mesh)
    return ring_solution(mesh)
```

```python
import math

import jax
import jax.numpy as jnp
from jax import lax
from jax.experimental import pallas as pl
from jax.experimental.pallas import tpu as pltpu
from jax.sharding import Mesh
from jax.sharding import PartitionSpec as P

HEAD_DIM = 64


ln_eps = 1e-12
masked_fill = -1e30


def from_behind(block, axis, distance):
    devices = range(lax.axis_size(axis))
    route = [((i - distance) % len(devices), i) for i in devices]
    return lax.ppermute(block, axis, route)


def matmul(left, right):
    return jnp.dot(left, right, preferred_element_type=jnp.float32)


def matmul_tn(left, right):
    return lax.dot_general(
        left, right, (((0,), (0,)), ((), ())), preferred_element_type=jnp.float32
    )


def matmul_nt(left, right):
    return lax.dot_general(
        left, right, (((1,), (1,)), ((), ())), preferred_element_type=jnp.float32
    )


def apply_layer_norm(value, gain, shift):
    mean = jnp.mean(value, axis=-1, keepdims=True)
    centered = value - mean
    rstd = lax.rsqrt(jnp.mean(centered * centered, axis=-1, keepdims=True) + ln_eps)
    normed = centered * rstd
    return (normed * gain + shift, normed, rstd)


def norm_back(grad, normed, rstd, gain):
    d_gain = jnp.sum(grad * normed, axis=0)
    d_shift = jnp.sum(grad, axis=0)
    scaled = grad * gain
    d_value = rstd * (
        scaled
        - jnp.mean(scaled, axis=-1, keepdims=True)
        - normed * jnp.mean(scaled * normed, axis=-1, keepdims=True)
    )
    return (d_value, d_gain, d_shift)


def gelu_slope(value):
    normal_cdf = 0.5 * (1.0 + lax.erf(value * (1.0 / math.sqrt(2.0))))
    density = jnp.exp(-0.5 * value * value) * (1.0 / math.sqrt(2.0 * math.pi))
    return normal_cdf + value * density


def scores_of(query, keys, q_ids, k_ids, scale):
    raw = jnp.einsum("qhd,khd->hqk", query, keys, preferred_element_type=jnp.float32) * scale
    match = (q_ids[:, None] == k_ids[None, :])[None, :, :]
    return (raw, match)


def attend(query, q_ids, keys, values, k_ids, stats, scale):
    top, total, accum = stats
    raw, match = scores_of(query, keys, q_ids, k_ids, scale)
    masked = jnp.where(match, raw, masked_fill)
    new_top = jnp.maximum(top, jnp.max(masked, axis=-1))
    weights = jnp.where(match, jnp.exp(masked - new_top[:, :, None]), 0.0)
    factor = jnp.exp(top - new_top)
    total = total * factor + jnp.sum(weights, axis=-1)
    accum = accum * factor[:, :, None] + jnp.einsum(
        "hqk,khd->hqd", weights.astype(jnp.bfloat16), values, preferred_element_type=jnp.float32
    )
    return (new_top, total, accum)


def block_grads(query, q_ids, d_out, log_total, delta, keys, values, k_ids, scale):
    raw, match = scores_of(query, keys, q_ids, k_ids, scale)
    probs = jnp.exp(jnp.where(match, raw - log_total[:, :, None], masked_fill))
    d_values = jnp.einsum(
        "hqk,qhd->khd", probs.astype(jnp.bfloat16), d_out, preferred_element_type=jnp.float32
    )
    d_probs = jnp.einsum("qhd,khd->hqk", d_out, values, preferred_element_type=jnp.float32)
    d_scores = (probs * (d_probs - delta[:, :, None])).astype(jnp.bfloat16)
    d_query = jnp.einsum("hqk,khd->qhd", d_scores, keys, preferred_element_type=jnp.float32) * scale
    d_keys = jnp.einsum("hqk,qhd->khd", d_scores, query, preferred_element_type=jnp.float32) * scale
    return (d_query, d_keys, d_values)


def ring_local(
    tokens,
    cotangent,
    seq_ids,
    w_query,
    b_query,
    w_key,
    w_value,
    b_value,
    w_out,
    b_out,
    attn_gain,
    attn_shift,
    w_up,
    b_up,
    w_down,
    b_down,
    ffn_gain,
    ffn_shift,
):
    cycle = lax.axis_size("ctx")
    tok_rows = tokens.shape[1]
    width = tokens.shape[2]
    heads = width // HEAD_DIM
    scale = 1.0 / math.sqrt(HEAD_DIM)
    share = tok_rows // cycle
    got_tokens, got_grads, got_ids = (
        lax.all_to_all(
            tokens[0].reshape(share, cycle, width), "ctx", split_axis=1, concat_axis=1, tiled=True
        ),
        lax.all_to_all(
            cotangent[0].reshape(share, cycle, width),
            "ctx",
            split_axis=1,
            concat_axis=1,
            tiled=True,
        ),
        lax.all_to_all(
            seq_ids[0].reshape(share, cycle), "ctx", split_axis=1, concat_axis=1, tiled=True
        ),
    )
    x_local = got_tokens.reshape(tok_rows, width)
    local_gradient = got_grads.reshape(tok_rows, width).astype(jnp.float32)
    local_ids = got_ids.reshape(tok_rows)
    (
        query_mat,
        query_bias,
        key_mat,
        value_mat,
        value_bias,
        out_mat,
        out_bias,
        attention_norm_gain,
        first_shift,
        up_mat,
        up_bias,
        down_mat,
        down_bias,
        feedforward_norm_gain,
        second_shift,
    ) = (
        lax.all_gather(w_query, "shard", axis=0, tiled=True),
        lax.all_gather(b_query, "shard", axis=0, tiled=True),
        lax.all_gather(w_key, "shard", axis=0, tiled=True),
        lax.all_gather(w_value, "shard", axis=0, tiled=True),
        lax.all_gather(b_value, "shard", axis=0, tiled=True),
        lax.all_gather(w_out, "shard", axis=0, tiled=True),
        lax.all_gather(b_out, "shard", axis=0, tiled=True),
        lax.all_gather(attn_gain, "shard", axis=0, tiled=True),
        lax.all_gather(attn_shift, "shard", axis=0, tiled=True),
        lax.all_gather(w_up, "shard", axis=0, tiled=True),
        lax.all_gather(b_up, "shard", axis=0, tiled=True),
        lax.all_gather(w_down, "shard", axis=0, tiled=True),
        lax.all_gather(b_down, "shard", axis=0, tiled=True),
        lax.all_gather(ffn_gain, "shard", axis=0, tiled=True),
        lax.all_gather(ffn_shift, "shard", axis=0, tiled=True),
    )
    query = (matmul(x_local, query_mat) + query_bias.astype(jnp.float32)).astype(jnp.bfloat16)
    keys = matmul(x_local, key_mat).astype(jnp.bfloat16)
    values = (matmul(x_local, value_mat) + value_bias.astype(jnp.float32)).astype(jnp.bfloat16)
    q_heads = query.reshape(tok_rows, heads, HEAD_DIM)
    start_stats = (
        jnp.full((heads, tok_rows), masked_fill, jnp.float32),
        jnp.zeros((heads, tok_rows), jnp.float32),
        jnp.zeros((heads, tok_rows, HEAD_DIM), jnp.float32),
    )

    def forward_step(step, carry):
        block, stats = carry
        stats = attend(
            q_heads,
            local_ids,
            block[0].reshape(tok_rows, heads, HEAD_DIM),
            block[1].reshape(tok_rows, heads, HEAD_DIM),
            block[2],
            stats,
            scale,
        )
        block = from_behind((block[0], block[1], block[2]), "ctx", 1)
        return (block, stats)

    block, stats = lax.fori_loop(
        0, cycle - 1, forward_step, ((keys, values, local_ids), start_stats)
    )
    top, total, accum = attend(
        q_heads,
        local_ids,
        block[0].reshape(tok_rows, heads, HEAD_DIM),
        block[1].reshape(tok_rows, heads, HEAD_DIM),
        block[2],
        stats,
        scale,
    )
    attn_out = (
        (accum / total[:, :, None]).transpose(1, 0, 2).reshape(tok_rows, width).astype(jnp.bfloat16)
    )
    log_total = top + jnp.log(total)
    attn_proj = matmul(attn_out, out_mat) + out_bias.astype(jnp.float32)
    first_sum = x_local.astype(jnp.float32) + attn_proj
    first_normalized_rows, first_centered_scaled, first_inverse_deviation = apply_layer_norm(
        first_sum, attention_norm_gain.astype(jnp.float32), first_shift.astype(jnp.float32)
    )
    normed_low = first_normalized_rows.astype(jnp.bfloat16)
    up_pre = matmul(normed_low, up_mat) + up_bias.astype(jnp.float32)
    up_act = jax.nn.gelu(up_pre, approximate=False).astype(jnp.bfloat16)
    down_pre = matmul(up_act, down_mat) + down_bias.astype(jnp.float32)
    layer_output, second_centered_scaled, second_inverse_deviation = apply_layer_norm(
        first_normalized_rows + down_pre,
        feedforward_norm_gain.astype(jnp.float32),
        second_shift.astype(jnp.float32),
    )
    (
        query_mat,
        key_mat,
        value_mat,
        out_mat,
        attention_norm_gain,
        up_mat,
        down_mat,
        feedforward_norm_gain,
    ) = (
        lax.all_gather(w_query, "shard", axis=0, tiled=True),
        lax.all_gather(w_key, "shard", axis=0, tiled=True),
        lax.all_gather(w_value, "shard", axis=0, tiled=True),
        lax.all_gather(w_out, "shard", axis=0, tiled=True),
        lax.all_gather(attn_gain, "shard", axis=0, tiled=True),
        lax.all_gather(w_up, "shard", axis=0, tiled=True),
        lax.all_gather(w_down, "shard", axis=0, tiled=True),
        lax.all_gather(ffn_gain, "shard", axis=0, tiled=True),
    )
    grad_two, d_second_gain, d_second_shift = norm_back(
        local_gradient,
        second_centered_scaled,
        second_inverse_deviation,
        feedforward_norm_gain.astype(jnp.float32),
    )
    grad_down = grad_two.astype(jnp.bfloat16)
    d_down_bias = jnp.sum(grad_down, axis=0, dtype=jnp.float32)
    d_down_mat = matmul_tn(up_act, grad_down)
    grad_up = (matmul_nt(grad_down, down_mat) * gelu_slope(up_pre)).astype(jnp.bfloat16)
    d_up_bias = jnp.sum(grad_up, axis=0, dtype=jnp.float32)
    d_up_mat = matmul_tn(normed_low, grad_up)
    first_norm_gradient = grad_two + matmul_nt(grad_up, up_mat)
    grad_first, d_first_gain, d_first_shift = norm_back(
        first_norm_gradient,
        first_centered_scaled,
        first_inverse_deviation,
        attention_norm_gain.astype(jnp.float32),
    )
    grad_proj = grad_first.astype(jnp.bfloat16)
    d_out_bias = jnp.sum(grad_proj, axis=0, dtype=jnp.float32)
    d_out_mat = matmul_tn(attn_out, grad_proj)
    grad_attn = matmul_nt(grad_proj, out_mat).astype(jnp.bfloat16)
    grad_heads = grad_attn.reshape(tok_rows, heads, HEAD_DIM)
    delta = jnp.einsum(
        "qhd,qhd->hq",
        grad_heads,
        attn_out.reshape(tok_rows, heads, HEAD_DIM),
        preferred_element_type=jnp.float32,
    )
    zero_rows = jnp.zeros((tok_rows, width), jnp.float32)

    def key_step(step, carry):
        block, sums, acc_query = carry
        d_query, d_keys, d_values = block_grads(
            q_heads,
            local_ids,
            grad_heads,
            log_total,
            delta,
            block[0].reshape(tok_rows, heads, HEAD_DIM),
            block[1].reshape(tok_rows, heads, HEAD_DIM),
            block[2],
            scale,
        )
        sums = (
            sums[0] + d_keys.reshape(tok_rows, width),
            sums[1] + d_values.reshape(tok_rows, width),
        )
        block = from_behind((block[0], block[1], block[2]), "ctx", 1)
        sums = (
            from_behind(sums[0].astype(jnp.bfloat16), "ctx", 1).astype(jnp.float32),
            from_behind(sums[1].astype(jnp.bfloat16), "ctx", 1).astype(jnp.float32),
        )
        return (block, sums, acc_query + d_query.reshape(tok_rows, width))

    block, sums, d_query_sum = lax.fori_loop(
        0, cycle, key_step, ((keys, values, local_ids), (zero_rows, zero_rows), zero_rows)
    )
    d_keys_sum, d_values_sum = sums
    grad_query = d_query_sum.astype(jnp.bfloat16)
    grad_keys = d_keys_sum.astype(jnp.bfloat16)
    grad_values = d_values_sum.astype(jnp.bfloat16)
    d_query_bias = jnp.sum(grad_query, axis=0, dtype=jnp.float32)
    d_value_bias = jnp.sum(grad_values, axis=0, dtype=jnp.float32)
    d_query_mat = matmul_tn(x_local, grad_query)
    d_key_mat = matmul_tn(x_local, grad_keys)
    d_value_mat = matmul_tn(x_local, grad_values)
    grad_input = (
        grad_first
        + matmul_nt(grad_query, query_mat)
        + matmul_nt(grad_keys, key_mat)
        + matmul_nt(grad_values, value_mat)
    )
    home_hidden, home_grad = (
        lax.all_to_all(
            layer_output.astype(jnp.bfloat16).reshape(share, cycle, width),
            "ctx",
            split_axis=1,
            concat_axis=1,
            tiled=True,
        ),
        lax.all_to_all(
            grad_input.astype(jnp.bfloat16).reshape(share, cycle, width),
            "ctx",
            split_axis=1,
            concat_axis=1,
            tiled=True,
        ),
    )
    hidden_out = home_hidden.reshape(tok_rows, width)[None]
    tokens_grad = home_grad.reshape(tok_rows, width)[None]
    shares = (
        lax.psum_scatter(
            d_query_mat.astype(jnp.bfloat16), "shard", scatter_dimension=0, tiled=True
        ).astype(jnp.float32),
        lax.psum_scatter(
            d_query_bias.astype(jnp.bfloat16), "shard", scatter_dimension=0, tiled=True
        ).astype(jnp.float32),
        lax.psum_scatter(
            d_key_mat.astype(jnp.bfloat16), "shard", scatter_dimension=0, tiled=True
        ).astype(jnp.float32),
        lax.psum_scatter(
            d_value_mat.astype(jnp.bfloat16), "shard", scatter_dimension=0, tiled=True
        ).astype(jnp.float32),
        lax.psum_scatter(
            d_value_bias.astype(jnp.bfloat16), "shard", scatter_dimension=0, tiled=True
        ).astype(jnp.float32),
        lax.psum_scatter(
            d_out_mat.astype(jnp.bfloat16), "shard", scatter_dimension=0, tiled=True
        ).astype(jnp.float32),
        lax.psum_scatter(
            d_out_bias.astype(jnp.bfloat16), "shard", scatter_dimension=0, tiled=True
        ).astype(jnp.float32),
        lax.psum_scatter(
            d_first_gain.astype(jnp.bfloat16), "shard", scatter_dimension=0, tiled=True
        ).astype(jnp.float32),
        lax.psum_scatter(
            d_first_shift.astype(jnp.bfloat16), "shard", scatter_dimension=0, tiled=True
        ).astype(jnp.float32),
        lax.psum_scatter(
            d_up_mat.astype(jnp.bfloat16), "shard", scatter_dimension=0, tiled=True
        ).astype(jnp.float32),
        lax.psum_scatter(
            d_up_bias.astype(jnp.bfloat16), "shard", scatter_dimension=0, tiled=True
        ).astype(jnp.float32),
        lax.psum_scatter(
            d_down_mat.astype(jnp.bfloat16), "shard", scatter_dimension=0, tiled=True
        ).astype(jnp.float32),
        lax.psum_scatter(
            d_down_bias.astype(jnp.bfloat16), "shard", scatter_dimension=0, tiled=True
        ).astype(jnp.float32),
        lax.psum_scatter(
            d_second_gain.astype(jnp.bfloat16), "shard", scatter_dimension=0, tiled=True
        ).astype(jnp.float32),
        lax.psum_scatter(
            d_second_shift.astype(jnp.bfloat16), "shard", scatter_dimension=0, tiled=True
        ).astype(jnp.float32),
    )
    totals = lax.psum(
        (
            shares[0],
            shares[1],
            shares[2],
            shares[3],
            shares[4],
            shares[5],
            shares[6],
            shares[7],
            shares[8],
            shares[9],
            shares[10],
            shares[11],
            shares[12],
            shares[13],
            shares[14],
        ),
        "ctx",
    )
    return (hidden_out, tokens_grad) + tuple(totals)


def ring_solution(mesh):
    return jax.shard_map(
        ring_local,
        mesh=mesh,
        in_specs=(
            P("shard", "ctx", None),
            P("shard", "ctx", None),
            P("shard", "ctx"),
            P("shard", None),
            P("shard"),
            P("shard", None),
            P("shard", None),
            P("shard"),
            P("shard", None),
            P("shard"),
            P("shard"),
            P("shard"),
            P("shard", None),
            P("shard"),
            P("shard", None),
            P("shard"),
            P("shard"),
            P("shard"),
        ),
        out_specs=(
            P("shard", "ctx", None),
            P("shard", "ctx", None),
            P("shard", None),
            P("shard"),
            P("shard", None),
            P("shard", None),
            P("shard"),
            P("shard", None),
            P("shard"),
            P("shard"),
            P("shard"),
            P("shard", None),
            P("shard"),
            P("shard", None),
            P("shard"),
            P("shard"),
            P("shard"),
        ),
        check_vma=False,
    )


AXES = ("q", "r", "x", "c")
ANY = pl.BlockSpec(memory_space=pl.ANY)
WHOLE = pl.BlockSpec(memory_space=pltpu.VMEM)


def moved(block, move):
    sizes = [lax.axis_size(a) for a in AXES]

    def number(spot):
        place = 0
        for size, at in zip(sizes, spot):
            place = place * size + at
        return place

    spots = [
        (q, r, x, c)
        for q in range(sizes[0])
        for r in range(sizes[1])
        for x in range(sizes[2])
        for c in range(sizes[3])
    ]
    return lax.ppermute(block, AXES, [(number(s), number(move(*s))) for s in spots])


def swap_x(block):
    return moved(block, lambda q, r, x, c: (q, r, 1 - x, c))


def swap_c(block):
    return moved(block, lambda q, r, x, c: (q, r, x, 1 - c))


def swap_r(block):
    return moved(block, lambda q, r, x, c: (q, r ^ 1, x, c))


def swap_rc(block):
    return moved(block, lambda q, r, x, c: (q, r ^ 1, x, 1 - c))


def swap_near(block):
    return moved(block, lambda q, r, x, c: (q ^ 1, r, x, c))


def swap_far(block):
    return moved(block, lambda q, r, x, c: (q ^ 2, r, x, c))


def regroup(block):
    return moved(block, lambda q, r, x, c: (2 * c + x, r, q & 1, q >> 1))


def swap_xc(block):
    return moved(block, lambda q, r, x, c: (q, r, 1 - x, 1 - c))


def beside(mine, got):
    return jnp.concatenate([mine, got])


def dot(left, right):
    return jnp.dot(left, right, preferred_element_type=jnp.float32)


def dot_nt(left, right):
    return lax.dot_general(
        left, right, (((1,), (1,)), ((), ())), preferred_element_type=jnp.float32
    )


def dot_tn(left, right):
    return lax.dot_general(
        left, right, (((0,), (0,)), ((), ())), preferred_element_type=jnp.float32
    )


class Copies:
    def __init__(self, sems):
        self.sems = sems
        self.count = 0
        self.held = []

    def start(self, source, target):
        copy = pltpu.make_async_copy(source, target, self.sems.at[self.count])
        copy.start()
        self.count += 1
        self.held.append(copy)

    def wait(self):
        for copy in self.held:
            copy.wait()
        self.held = []


def spot():
    return tuple(lax.axis_index(a) for a in AXES)


def fill_mask(ids, mask, own):
    blocks, rows = ids.shape
    mine = jnp.concatenate([ids[pl.ds(own, 1), :], ids[pl.ds(own + 1, 1), :]], axis=1)
    across = jnp.transpose(ids[...])
    for b in range(blocks):
        mask[rows * b : rows * (b + 1), :] = jnp.where(across[:, b : b + 1] == mine, 0.0, masked_fill)


def block_kernel(tokens, ids, block):
    rows = tokens.shape[0]
    block[0:rows, :] = tokens[...]
    block[rows:, :] = jnp.zeros((16, block.shape[1]), block.dtype)
    line = ids[...].astype(jnp.float32)
    block[rows:, 0:rows] = jnp.broadcast_to(line, (16, rows)).astype(block.dtype)


def pack_kernel(w_q, w_k, w_v, *refs):
    vectors, b_up, theirs, mine, lines = refs[:8], refs[8], refs[9], refs[10], refs[11]
    q, r, x, c = spot()
    part, width = w_q.shape
    half = width // 2
    for t, w in enumerate((w_q, w_k, w_v)):
        rows = slice(part * t, part * (t + 1))
        mine[rows, :] = w[:, pl.ds(pl.multiple_of(half * x, 128), half)]
        theirs[rows, :] = w[:, pl.ds(pl.multiple_of(half * (1 - x), 128), half)]
    lines[...] = jnp.zeros_like(lines)
    for i, vector in enumerate(vectors):
        line = vector[...].astype(jnp.float32).reshape(1, part)
        none = jnp.zeros_like(line)
        first = jnp.concatenate([line, none], axis=1)
        second = jnp.concatenate([none, line], axis=1)
        lines[i : i + 1, :] = jnp.where(c == 0, first, second)
    wide = b_up[...].astype(jnp.float32).reshape(1, width)
    lines[pl.ds(8 + 2 * c, 1), :] = wide[:, 0:half]
    lines[pl.ds(9 + 2 * c, 1), :] = wide[:, half:]
    low = lines[...].astype(jnp.bfloat16)
    mine[3 * part :, :] = low
    theirs[3 * part :, :] = low


def attend_kernel(
    b0, b1, b2, b3, b4, b5, b6, b7, w_q, w_k, w_v, w_x, w_m, w_mx, own_lines, w_o, w_om,
    x_out, w_out, wo_out, k_out, v_out, q_out, o_out, lse_out, ids_out, a_out, a_low, vecs, up_bias,
    xs, raw, w, wo, lines, k3, v3, vt, q3, ot, mask, sems, outs,
):
    q, r, x, c = spot()
    rows = xs.shape[0] // 8
    part = w.shape[0] // 4
    half = wo.shape[0]
    me, shard = 4 * r + 2 * c + x, 2 * x + c
    ins = Copies(sems)
    for j, block in enumerate((b0, b1, b2, b3, b4, b5, b6, b7)):
        at = me ^ j
        ins.start(block.at[pl.ds(0, rows)], xs.at[pl.ds(pl.multiple_of(rows * at, rows), rows)])
        ins.start(block.at[pl.ds(rows, 16)], raw.at[at])
    columns = pl.ds(pl.multiple_of(half * x, 128), half)
    for t, own in enumerate((w_q, w_k, w_v)):
        place = pl.ds(half * t, half)
        ins.start(own.at[:, columns], w.at[pl.ds(pl.multiple_of(part * shard, 64), part), place])
        for flip, piece in ((2, w_x), (1, w_m), (3, w_mx)):
            at = pl.ds(pl.multiple_of(part * (shard ^ flip), 64), part)
            ins.start(piece.at[pl.ds(part * t, part)], w.at[at, place])
    for i, piece in enumerate((own_lines, w_m, w_x, w_mx)):
        ins.start(piece.at[pl.ds(3 * part, 16)], lines.at[i])
    ins.start(w_o, wo.at[pl.ds(pl.multiple_of(part * c, 64), part)])
    ins.start(w_om, wo.at[pl.ds(pl.multiple_of(part * (1 - c), 64), part)])
    ins.wait()
    backs = Copies(outs)
    backs.start(xs, x_out)
    backs.start(w, w_out)
    backs.start(wo, wo_out)
    mine = lines[0].astype(jnp.float32) + lines[1].astype(jnp.float32)
    other = lines[2].astype(jnp.float32) + lines[3].astype(jnp.float32)
    vecs[:, columns] = mine[0:8, :]
    vecs[:, pl.ds(pl.multiple_of(half * (1 - x), 128), half)] = other[0:8, :]
    for i in range(4):
        up_bias[i] = jnp.broadcast_to(mine[8 + i : 9 + i, :], (8, half))
    for b in range(8):
        ids_out[b : b + 1, :] = raw[b, 0:1, 0:rows].astype(jnp.float32)
    fill_mask(ids_out, mask, 4 * r + 2 * c)
    keyed = dot(xs[...], w[:, half : 2 * half]).astype(jnp.bfloat16)
    valued = dot(xs[...], w[:, 2 * half : 3 * half]) + mine[1:2, :]
    own = pl.ds(pl.multiple_of(rows * (4 * r + 2 * c), rows), 2 * rows)
    asked = (dot(xs[own, :], w[:, 0:half]) + mine[0:1, :]).astype(jnp.bfloat16)
    valued = valued.astype(jnp.bfloat16)
    turned = jnp.transpose(valued)
    pairs = half // 128
    for p in range(pairs):
        k3[p] = keyed[:, 128 * p : 128 * (p + 1)]
        v3[p] = valued[:, 128 * p : 128 * (p + 1)]
        q3[p] = asked[:, 128 * p : 128 * (p + 1)]
    for h in range(2 * pairs):
        vt[h] = turned[64 * h : 64 * (h + 1), :]
    backs.start(k3, k_out)
    backs.start(v3, v_out)
    q_out[...] = q3[...]
    lane = lax.broadcasted_iota(jnp.int32, (2 * rows, 128), 1) // 64

    def head(h, carry):
        query = jnp.where(lane == h % 2, q3[h // 2], 0) * 0.125
        scores = dot_nt(k3[h // 2], query.astype(jnp.bfloat16)) + mask[...]
        top = jnp.max(scores, axis=0, keepdims=True)
        weights = jnp.exp(scores - top)
        total = jnp.sum(weights, axis=0, keepdims=True)
        ot[h] = dot(vt[h], weights.astype(jnp.bfloat16)) / total
        lse_out[pl.ds(h, 1), :] = top + jnp.log(total)
        return carry

    lax.fori_loop(0, 2 * pairs, head, 0)
    mixed = jnp.transpose(ot[...].reshape(half, 2 * rows)).astype(jnp.bfloat16)
    o_out[...] = mixed
    partial = dot(mixed, wo[...])
    a_out[...] = partial
    a_low[...] = partial.astype(jnp.bfloat16)
    backs.wait()


def load_feedforward(copies, up, down, u_own, u_x, u_m, u_mx, d_own, d_m):
    q, r, x, c = spot()
    part = up.shape[0] // 4
    wide = up.shape[1] // 4
    shard = 2 * x + c
    for j in range(4):
        at = pl.ds(wide * j, wide)
        slot = (2 * c + r) ^ j
        pieces = ((0, u_own, 4 * wide * x), (2, u_x, 0), (1, u_m, 0), (3, u_mx, 0))
        for flip, piece, base in pieces:
            rows = pl.ds(pl.multiple_of(part * (shard ^ flip), 64), part)
            columns = pl.ds(pl.multiple_of(base + wide * slot, 128), wide)
            copies.start(piece.at[:, columns], up.at[rows, at])
        source = d_own if j < 2 else d_m
        copies.start(source.at[pl.ds(pl.multiple_of(wide * (r ^ (j & 1)), 128), wide)], down.at[at])


def norm_of(value):
    mean = jnp.mean(value, axis=-1, keepdims=True)
    centered = value - mean
    rstd = lax.rsqrt(jnp.mean(centered * centered, axis=-1, keepdims=True) + ln_eps)
    return centered * rstd, rstd


def norm_pull(scaled, normed, rstd):
    return rstd * (
        scaled
        - jnp.mean(scaled, axis=-1, keepdims=True)
        - normed * jnp.mean(scaled * normed, axis=-1, keepdims=True)
    )


def forward_kernel(
    a_own, a_got, xs, vecs, b_up, u_own, u_x, u_m, u_mx, d_own, d_m,
    to_r, to_c, z_own, n_out, r_out, slope_out, y_out, y_low,
    up, down, x_own, z, sems, more,
):
    q, r, x, c = spot()
    rows = x_own.shape[0]
    first = Copies(more)
    first.start(xs.at[pl.ds(pl.multiple_of(rows * (2 * r + c), rows), rows)], x_own)
    copies = Copies(sems)
    load_feedforward(copies, up, down, u_own, u_x, u_m, u_mx, d_own, d_m)
    first.wait()
    total = x_own[...].astype(jnp.float32) + (a_own[...] + a_got[...].astype(jnp.float32) + vecs[2:3, :])
    normed, rstd = norm_of(total)
    n_out[...] = normed
    r_out[...] = jnp.broadcast_to(rstd, r_out.shape)
    low = (normed * vecs[3:4, :] + vecs[4:5, :]).astype(jnp.bfloat16)
    wide = up.shape[1] // 4
    to_r[:, 2 * wide :] = low
    to_c[:, wide:] = low
    copies.wait()
    for j in range(4):
        pre = dot(low, up[:, wide * j : wide * (j + 1)]) + b_up[(2 * c + r) ^ j, 0:1, :]
        cdf = 0.5 * (1.0 + lax.erf(pre * (1.0 / math.sqrt(2.0))))
        density = jnp.exp(-0.5 * pre * pre) * (1.0 / math.sqrt(2.0 * math.pi))
        z[:, wide * j : wide * (j + 1)] = (pre * cdf).astype(jnp.bfloat16)
        slope_out[j] = cdf + pre * density
    result = dot(z[...], down[...])
    y_out[...] = result
    y_low[...] = result.astype(jnp.bfloat16)
    z_own[...] = z[:, 0:wide]
    to_r[:, 0:wide] = z[:, wide : 2 * wide]
    to_r[:, wide : 2 * wide] = z[:, 3 * wide :]
    to_c[:, 0:wide] = z[:, 2 * wide : 3 * wide]


def backward_kernel(
    y_own, y_got, normed1, g_own, g_x, slope, vecs, u_own, u_x, u_m, u_mx, d_own, d_m,
    hid_out, to_r, to_c, du_own, s_out, p_low, sums, up_sums,
    up, down, grad, hid, sems, more,
):
    q, r, x, c = spot()
    rows = grad.shape[0] // 2
    first = Copies(more)
    first.start(g_own, grad.at[pl.ds(pl.multiple_of(rows * x, rows), rows)])
    first.start(g_x, grad.at[pl.ds(pl.multiple_of(rows * (1 - x), rows), rows)])
    copies = Copies(sems)
    load_feedforward(copies, up, down, u_own, u_x, u_m, u_mx, d_own, d_m)
    first.wait()
    h1 = normed1[...] * vecs[3:4, :] + vecs[4:5, :]
    normed, rstd = norm_of(h1 + (y_own[...] + y_got[...].astype(jnp.float32) + vecs[5:6, :]))
    hid[...] = (normed * vecs[6:7, :] + vecs[7:8, :]).astype(jnp.bfloat16)
    hid_out[...] = hid[pl.ds(pl.multiple_of(rows * x, rows), rows), :]
    cot = grad[...].astype(jnp.float32)
    dy = norm_pull(cot * vecs[6:7, :], normed, rstd)
    low = dy.astype(jnp.bfloat16)
    wide = up.shape[1] // 4
    to_r[:, 2 * wide :] = low
    to_c[:, wide:] = low
    sums[...] = jnp.zeros_like(sums)
    sums[0:1, :] = jnp.sum(low.astype(jnp.float32), axis=0, keepdims=True)
    sums[1:2, :] = jnp.sum(cot * normed, axis=0, keepdims=True)
    sums[2:3, :] = jnp.sum(cot, axis=0, keepdims=True)
    copies.wait()
    result = jnp.zeros(dy.shape, jnp.float32)
    places = (du_own.at[...], to_r.at[:, 0:wide], to_c.at[:, 0:wide], to_r.at[:, wide : 2 * wide])
    for j in range(4):
        du = (dot_nt(low, down[wide * j : wide * (j + 1), :]) * slope[j]).astype(jnp.bfloat16)
        places[j][...] = du
        total = jnp.sum(du.astype(jnp.float32), axis=0, keepdims=True)
        up_sums[j] = jnp.broadcast_to(total, up_sums.shape[1:])
        result += dot_nt(du, up[:, wide * j : wide * (j + 1)])
    s_out[...] = dy + result
    p_low[...] = result.astype(jnp.bfloat16)


def attend_back_kernel(
    s_own, p_got, normed1, rstd1, vecs, wo, mixed, q3, k3, v3, kt, lse, ids,
    dr_out, da_out, dq_out, dkv_out, sums, qv_sums,
    mask, do3, delta, dk, dv, dqt, whole,
):
    q, r, x, c = spot()
    rows = dr_out.shape[0]
    pairs = q3.shape[0]
    half = 128 * pairs
    fill_mask(ids, mask, 4 * r + 2 * c)
    dh = s_own[...] + p_got[...].astype(jnp.float32)
    normed = normed1[...]
    dr = norm_pull(dh * vecs[3:4, :], normed, rstd1[:, 0:1])
    whole[...] = dr
    dr_out[...] = whole[pl.ds(pl.multiple_of(rows * x, rows), rows), :]
    low = dr.astype(jnp.bfloat16)
    da_out[...] = low
    sums[...] = jnp.zeros_like(sums)
    sums[0:1, :] = jnp.sum(low.astype(jnp.float32), axis=0, keepdims=True)
    sums[1:2, :] = jnp.sum(dh * normed, axis=0, keepdims=True)
    sums[2:3, :] = jnp.sum(dh, axis=0, keepdims=True)
    d_o = dot_nt(low, wo[...]).astype(jnp.bfloat16)
    products = jnp.transpose(d_o.astype(jnp.float32) * mixed[...].astype(jnp.float32))
    for h in range(2 * pairs):
        delta[h : h + 1, :] = jnp.sum(products[64 * h : 64 * (h + 1), :], axis=0, keepdims=True)
    for p in range(pairs):
        do3[p] = d_o[:, 128 * p : 128 * (p + 1)]
    dk[...] = jnp.zeros_like(dk)
    dv[...] = jnp.zeros_like(dv)
    lane = lax.broadcasted_iota(jnp.int32, (2 * rows, 128), 1) // 64

    def head(h, carry):
        p = h // 2
        here = lane == h % 2
        query = (jnp.where(here, q3[p], 0) * 0.125).astype(jnp.bfloat16)
        d_here = jnp.where(here, do3[p], 0).astype(jnp.bfloat16)
        probs = jnp.exp(dot_nt(k3[p], query) + mask[...] - lse[pl.ds(h, 1), :])
        d_probs = dot_nt(v3[p], d_here)
        d_scores = (probs * (d_probs - delta[pl.ds(h, 1), :])).astype(jnp.bfloat16)
        dv[p] += dot(probs.astype(jnp.bfloat16), d_here)
        dk[p] += dot(d_scores, query)
        dqt[h] = dot(kt[h], d_scores)
        return carry

    lax.fori_loop(0, 2 * pairs, head, 0)
    dq = (jnp.transpose(dqt[...].reshape(half, 2 * rows)) * 0.125).astype(jnp.bfloat16)
    dq_out[...] = dq
    qv_sums[...] = jnp.zeros_like(qv_sums)
    qv_sums[0:1, :] = jnp.sum(dq.astype(jnp.float32), axis=0, keepdims=True)
    for p in range(pairs):
        at = slice(128 * p, 128 * (p + 1))
        dkv_out[:, at] = dk[p].astype(jnp.bfloat16)
        value = dv[p].astype(jnp.bfloat16)
        dkv_out[:, half + 128 * p : half + 128 * (p + 1)] = value
        qv_sums[1:2, at] = jnp.sum(value.astype(jnp.float32), axis=0, keepdims=True)


def input_grad_kernel(dq, dkv, w, send, keep, whole):
    q, r, x, c = spot()
    half = dq.shape[1]
    rows = dq.shape[0] // 2
    whole[...] = dot_nt(dkv[...], w[:, half:])
    own = pl.ds(pl.multiple_of(rows * (4 * r + 2 * c), rows), 2 * rows)
    whole[own, :] += dot_nt(dq[...], w[:, 0:half])
    for b in range(2):
        mine = pl.ds(pl.multiple_of(rows * (4 * b + 2 * c), rows), 2 * rows)
        keep[b] = whole[mine, :]
        theirs = pl.ds(pl.multiple_of(rows * (4 * b + 2 * (1 - c)), rows), 2 * rows)
        send[b] = whole[theirs, :].astype(jnp.bfloat16)


def down_grad_kernel(z0, r0, c0, f0, dc, dr_, df, c_own, send, keep, whole):
    q, r, x, c = spot()
    wide = z0.shape[1]
    total = dot_tn(z0[...], c_own[:, wide:])
    total += dot_tn(r0[:, 0:wide], dr_[:, 2 * wide :])
    total += dot_tn(c0[:, 0:wide], dc[:, wide:])
    total += dot_tn(f0[:, wide : 2 * wide], df[:, 2 * wide :])
    whole[...] = total
    count = wide // 4
    for b in range(2):
        theirs = pl.ds(pl.multiple_of(2 * count * b + count * (1 - q % 2), 32), count)
        mine = pl.ds(pl.multiple_of(2 * count * b + count * (q % 2), 32), count)
        send[b] = whole[theirs, :].astype(jnp.bfloat16)
        keep[b] = whole[mine, :]


def up_grad_kernel(h0, hr, hc, hf, d0, dr_, dc, df, send, keep, whole):
    q, r, x, c = spot()
    wide = d0.shape[1]
    total = dot_tn(h0[:, wide:], d0[...])
    total += dot_tn(hr[:, 2 * wide :], dr_[:, 0:wide])
    total += dot_tn(hc[:, wide:], dc[:, 0:wide])
    total += dot_tn(hf[:, 2 * wide :], df[:, wide : 2 * wide])
    whole[...] = total
    count = whole.shape[0] // 16
    for b in range(2):
        for s in range(4):
            at = 4 * count * s + 2 * count * b
            rows = slice(count * s, count * (s + 1))
            theirs = pl.ds(pl.multiple_of(at + count * (1 - q % 2), 16), count)
            mine = pl.ds(pl.multiple_of(at + count * (q % 2), 16), count)
            send[b, rows, :] = whole[theirs, :].astype(jnp.bfloat16)
            keep[b, rows, :] = whole[mine, :]


def fold_kernel(bit, keep, got, send, kept):
    at = bit(*spot())
    send[...] = (keep[1 - at] + got[1 - at].astype(jnp.float32)).astype(send.dtype)
    kept[...] = keep[at] + got[at].astype(jnp.float32)


def sum_kernel(keep, got, out):
    out[...] = (keep[...] + got[...].astype(jnp.float32)).astype(out.dtype)


def share_kernel(keep, got, *out):
    q, r, x, c = spot()
    count = keep.shape[0] // 4
    for k in range(4):
        rows = pl.ds(pl.multiple_of(count * ((2 * x + c) ^ k), 16), count)
        out[k][...] = (keep[rows, :] + got[rows, :].astype(jnp.float32)).astype(jnp.bfloat16)


def weight_grad_kernel(
    xs, dkv, dq, mixed, da, sums1, sums2, qv_sums, up_sums, send, keep, packed, sems
):
    q, r, x, c = spot()
    width = xs.shape[1]
    own, half = dq.shape
    thin = width // 32
    for_c = 64 * thin
    own_rows = pl.ds(pl.multiple_of(own * (2 * r + c), own), own)
    asked = dot_tn(xs[own_rows, :], dq[...])
    kept = dot_tn(xs[...], dkv[...])
    outer = dot_tn(mixed[...], da[...])
    for cc in range(2):
        for rr in range(2):
            for q1 in range(2):
                for q0 in range(2):
                    at = ((4 * rr + 2 * q0 + q1) * 8) * thin
                    within = (4 * rr + 2 * q1 + q0) * thin
                    for xx in range(2):
                        rows = slice((16 * xx + 8 * cc) * thin + within, (16 * xx + 8 * cc + 1) * thin + within)
                        for t, piece in enumerate((asked, kept[:, 0:half], kept[:, half:])):
                            to = at + (3 * xx + t) * thin
                            packed[cc, to : to + thin, :] = piece[rows, :]
                    rows = slice(8 * cc * thin + within, (8 * cc + 1) * thin + within)
                    for t in range(2):
                        to = at + (6 + t) * thin
                        packed[cc, to : to + thin, :] = outer[rows, half * t : half * (t + 1)]
    columns = pl.ds(pl.multiple_of(half * x, 128), half)
    for cc in range(2):
        packed[cc, for_c : for_c + 16, :] = jnp.zeros((16, half), jnp.float32)
        packed[cc, for_c : for_c + 2, :] = qv_sums[0:2, :]
        for j in range(4):
            packed[cc, pl.ds(for_c + 2 + ((2 * c + r) ^ j), 1), :] = up_sums[j, 0:1, :]
        packed[cc, for_c + 6 : for_c + 9, :] = sums1[0:3, columns]
        packed[cc, for_c + 9 : for_c + 12, :] = sums2[0:3, columns]
    send[...] = packed[1 - c].astype(jnp.bfloat16)
    copy = pltpu.make_async_copy(packed.at[c], keep, sems.at[0])
    copy.start()
    copy.wait()


def step_kernel(bit, keep, got, send, kept, whole):
    at = bit(*spot())
    count = send.shape[0] - 16
    whole[...] = keep[...] + got[...].astype(jnp.float32)
    theirs = pl.ds(pl.multiple_of(count * (1 - at), 64), count)
    mine = pl.ds(pl.multiple_of(count * at, 64), count)
    send[0:count, :] = whole[theirs, :].astype(jnp.bfloat16)
    send[count:, :] = whole[2 * count :, :].astype(jnp.bfloat16)
    kept[0:count, :] = whole[mine, :]
    kept[count:, :] = whole[2 * count :, :]


def last_step_kernel(keep, got, side, base, lines, whole):
    q, r, x, c = spot()
    count = side.shape[0]
    whole[...] = keep[...] + got[...].astype(jnp.float32)
    theirs = pl.ds(pl.multiple_of(count * (1 - x), 8), count)
    mine = pl.ds(pl.multiple_of(count * x, 8), count)
    side[...] = whole[theirs, :].astype(jnp.bfloat16)
    rest = slice(2 * count, whole.shape[0] - 16)
    base[...] = jnp.concatenate([whole[mine, :], whole[rest, :]]).astype(jnp.bfloat16)
    lines[...] = whole[whole.shape[0] - 16 :, :]


def down_out_kernel(near, far, out):
    q, r, x, c = spot()
    count = near.shape[0] // 4
    for d, piece in enumerate((near, far)):
        for k in range(4):
            at = 4 * (r ^ d) + 2 * ((q // 2) ^ (k & 1)) + ((q % 2) ^ (k >> 1))
            rows = pl.ds(pl.multiple_of(count * at, 32), count)
            out[rows, :] = piece[count * k : count * (k + 1), :].astype(jnp.float32)


def up_out_kernel(near, far, out):
    q, r, x, c = spot()
    count, wide = near.shape[0] // 16, near.shape[1]
    for d, piece in enumerate((near, far)):
        for k in range(4):
            at = 2 * ((q // 2) ^ (k & 1)) + ((q % 2) ^ (k >> 1))
            rows = pl.ds(pl.multiple_of(count * at, 16), count)
            for s in range(4):
                place = 2 * ((2 * x + c) ^ s) + (r ^ d)
                columns = pl.ds(pl.multiple_of(wide * place, 128), wide)
                first = count * (4 * k + s)
                out[rows, columns] = piece[first : first + count, :].astype(jnp.float32)


def rest_out_kernel(near, far, out_q, out_k, out_v, out_o, whole):
    q, r, x, c = spot()
    half = near.shape[1]
    thin = near.shape[0] // 32
    ours = pl.ds(pl.multiple_of(half * x, 128), half)
    other = pl.ds(pl.multiple_of(half * (1 - x), 128), half)
    for d, piece in enumerate((near, far)):
        whole[...] = piece[...].astype(jnp.float32)
        for k in range(4):
            at = 4 * (r ^ d) + 2 * ((q // 2) ^ (k & 1)) + ((q % 2) ^ (k >> 1))
            rows = pl.ds(pl.multiple_of(thin * at, 8), thin)
            first = 8 * thin * k
            for t, out in enumerate((out_q, out_k, out_v)):
                out[rows, ours] = whole[first + thin * t : first + thin * (t + 1), :]
                out[rows, other] = whole[first + thin * (5 + t) : first + thin * (6 + t), :]
            for t in range(2):
                columns = slice(half * t, half * (t + 1))
                out_o[rows, columns] = whole[first + thin * (3 + t) : first + thin * (4 + t), :]


def kernel_call(body, name, ins, outs, scratch, args, after=(), flops=10**8):
    count = len(args)

    def run(*refs):
        body(*refs[:count], *refs[count + len(after) :])

    return pl.pallas_call(
        run,
        name=name,
        out_shape=[jax.ShapeDtypeStruct(shape, dtype) for shape, dtype, _ in outs],
        in_specs=list(ins) + [ANY] * len(after),
        out_specs=[spec for _, _, spec in outs],
        scratch_shapes=scratch,
        cost_estimate=pl.CostEstimate(flops=flops, bytes_accessed=4 << 20, transcendentals=0),
    )(*args, *after)


def once(value, *after):
    return pl.pallas_call(
        lambda *refs: None,
        name="once",
        out_shape=jax.ShapeDtypeStruct(value.shape, value.dtype),
        in_specs=[ANY] * (1 + len(after)),
        out_specs=ANY,
        input_output_aliases={0: 0},
    )(value, *after)


def plane_local(
    tokens, cotangent, seq_ids, w_query, b_query, w_key, w_value, b_value, w_out, b_out,
    attn_gain, attn_shift, w_up, b_up, w_down, b_down, ffn_gain, ffn_shift,
):
    x = lax.axis_index("x")
    low, exact = jnp.bfloat16, jnp.float32
    rows, width = tokens.shape[1:]
    part = w_query.shape[0]
    half = width // 2
    inner = w_up.shape[1]
    wide = inner // 8
    keys = 8 * rows
    own = 2 * rows
    pairs = half // 128

    def call(body, name, ins, outs, scratch, args, after=(), flops=10**8):
        return kernel_call(body, name, ins, outs, scratch, args, after, flops)

    (block,) = call(
        block_kernel, "block", [WHOLE] * 2, [((rows + 16, width), low, WHOLE)], [],
        (tokens[0], seq_ids),
    )
    blocks = [regroup(block)]
    theirs, mine = call(
        pack_kernel,
        "pack",
        [WHOLE] * 12,
        [((3 * part + 16, half), low, WHOLE)] * 2,
        [pltpu.VMEM((16, half), exact)],
        (w_query, w_key, w_value, b_query, b_value, b_out, attn_gain, attn_shift, b_down, ffn_gain, ffn_shift, b_up),
    )
    qkv_x = swap_x(theirs)
    qkv_m = swap_c(mine)
    blocks.append(swap_x(blocks[0]))
    blocks.append(swap_c(blocks[0]))
    blocks.append(swap_c(blocks[1]))
    blocks.append(swap_r(blocks[0]))
    blocks.append(swap_r(blocks[1]))
    blocks.append(swap_c(blocks[4]))
    blocks.append(swap_c(blocks[5]))
    qkv_mx = swap_c(qkv_x)
    out_m = swap_c(w_out)

    def cut(w, side, size):
        return lax.dynamic_slice_in_dim(w, side * size, size, 1)

    up_x = swap_x(once(cut(w_up, 1 - x, 4 * wide), blocks[1]))
    up_m = swap_c(cut(w_up, x, 4 * wide))
    up_mx = swap_c(up_x)
    down_m = swap_c(w_down)
    cot = regroup(once(cotangent[0], blocks[5]))
    cot_x = swap_x(cot)

    (
        x_all, w_all, wo_all, k3, v3, q3, mixed, lse, ids, a_own, a_low, vecs, up_bias
    ) = call(
        attend_kernel,
        "attend",
        [ANY] * 17,
        [
            ((keys, width), low, ANY),
            ((width, 3 * half), low, ANY),
            ((half, width), low, ANY),
            ((pairs, keys, 128), low, ANY),
            ((pairs, keys, 128), low, ANY),
            ((pairs, own, 128), low, WHOLE),
            ((own, half), low, WHOLE),
            ((8, own), exact, WHOLE),
            ((8, rows), exact, WHOLE),
            ((own, width), exact, WHOLE),
            ((own, width), low, WHOLE),
            ((8, width), exact, WHOLE),
            ((4, 8, wide), exact, WHOLE),
        ],
        [
            pltpu.VMEM((keys, width), low),
            pltpu.VMEM((8, 16, width), low),
            pltpu.VMEM((width, 3 * half), low),
            pltpu.VMEM((half, width), low),
            pltpu.VMEM((4, 16, half), low),
            pltpu.VMEM((pairs, keys, 128), low),
            pltpu.VMEM((pairs, keys, 128), low),
            pltpu.VMEM((2 * pairs, 64, keys), low),
            pltpu.VMEM((pairs, own, 128), low),
            pltpu.VMEM((2 * pairs, 64, own), exact),
            pltpu.VMEM((keys, own), exact),
            pltpu.SemaphoreType.DMA((34,)),
            pltpu.SemaphoreType.DMA((5,)),
        ],
        (*blocks, w_query, w_key, w_value, qkv_x, qkv_m, qkv_mx, mine, w_out, out_m),
        flops=3 * 10**9,
    )
    a_got = swap_x(a_low)
    kt = jnp.swapaxes(k3, 1, 2).reshape(2 * pairs, 64, keys)

    inner_weights = (w_up, up_x, up_m, up_mx, w_down, down_m)
    inner_scratch = [
        pltpu.VMEM((width, 4 * wide), low),
        pltpu.VMEM((4 * wide, width), low),
    ]
    f_r, f_c, z_own, normed1, rstd1, slope, y_own, y_low = call(
        forward_kernel,
        "feedforward",
        [WHOLE, WHOLE, ANY, WHOLE, WHOLE] + [ANY] * 6,
        [
            ((own, 2 * wide + width), low, WHOLE),
            ((own, wide + width), low, WHOLE),
            ((own, wide), low, WHOLE),
            ((own, width), exact, WHOLE),
            ((own, 128), exact, WHOLE),
            ((4, own, wide), exact, WHOLE),
            ((own, width), exact, WHOLE),
            ((own, width), low, WHOLE),
        ],
        inner_scratch
        + [
            pltpu.VMEM((own, width), low),
            pltpu.VMEM((own, 4 * wide), low),
            pltpu.SemaphoreType.DMA((20,)),
            pltpu.SemaphoreType.DMA((1,)),
        ],
        (a_own, a_got, x_all, vecs, up_bias, *inner_weights),
        flops=2 * 10**9,
    )
    y_got = swap_x(y_low)
    f_from_r = swap_r(f_r)
    f_from_c = swap_c(f_c)
    f_from_rc = swap_c(f_from_r)

    hidden, b_r, b_c, du_own, s_own, p_low, sums2, up_sums = call(
        backward_kernel,
        "feedforward_back",
        [WHOLE, WHOLE, WHOLE, ANY, ANY, WHOLE, WHOLE] + [ANY] * 6,
        [
            ((rows, width), low, WHOLE),
            ((own, 2 * wide + width), low, WHOLE),
            ((own, wide + width), low, WHOLE),
            ((own, wide), low, WHOLE),
            ((own, width), exact, WHOLE),
            ((own, width), low, WHOLE),
            ((8, width), exact, WHOLE),
            ((4, 8, wide), exact, WHOLE),
        ],
        inner_scratch
        + [
            pltpu.VMEM((own, width), low),
            pltpu.VMEM((own, width), low),
            pltpu.SemaphoreType.DMA((20,)),
            pltpu.SemaphoreType.DMA((2,)),
        ],
        (y_own, y_got, normed1, cot, cot_x, slope, vecs, *inner_weights),
        flops=2 * 10**9,
    )
    p_got = swap_x(p_low)
    b_from_r = swap_r(b_r)
    b_from_c = swap_c(b_c)
    b_from_rc = swap_c(b_from_r)

    dr, da, dq, dkv, sums1, qv_sums = call(
        attend_back_kernel,
        "attend_back",
        [WHOLE] * 13,
        [
            ((rows, width), exact, WHOLE),
            ((own, width), low, WHOLE),
            ((own, half), low, WHOLE),
            ((keys, 2 * half), low, WHOLE),
            ((8, width), exact, WHOLE),
            ((8, half), exact, WHOLE),
        ],
        [
            pltpu.VMEM((keys, own), exact),
            pltpu.VMEM((pairs, own, 128), low),
            pltpu.VMEM((8, own), exact),
            pltpu.VMEM((pairs, keys, 128), exact),
            pltpu.VMEM((pairs, keys, 128), exact),
            pltpu.VMEM((2 * pairs, 64, own), exact),
            pltpu.VMEM((own, width), exact),
        ],
        (s_own, p_got, normed1, rstd1, vecs, wo_all, mixed, q3, k3, v3, kt, lse, ids),
        after=(f_from_rc, f_from_c),
        flops=3 * 10**9,
    )

    thin = part // 8
    count = 64 * thin
    send, keep = call(
        weight_grad_kernel,
        "weight_grad",
        [WHOLE] * 9,
        [((count + 16, half), low, WHOLE), ((count + 16, half), exact, ANY)],
        [pltpu.VMEM((2, count + 16, half), exact), pltpu.SemaphoreType.DMA((1,))],
        (x_all, dkv, dq, mixed, da, sums1, sums2, qv_sums, up_sums),
        flops=2 * 10**9,
    )
    rest_got = swap_c(send)
    rest_keep = keep

    quarter = wide // 4
    down_send, down_keep = call(
        down_grad_kernel,
        "down_grad",
        [WHOLE] * 8,
        [((2, quarter, width), low, WHOLE), ((2, quarter, width), exact, WHOLE)],
        [pltpu.VMEM((wide, width), exact)],
        (z_own, f_from_r, f_from_c, f_from_rc, b_from_c, b_from_r, b_from_rc, b_c),
        after=(send,),
        flops=10**9,
    )
    down_got = swap_near(down_send)
    up_send, up_keep = call(
        up_grad_kernel,
        "up_grad",
        [WHOLE] * 8,
        [((2, part, wide), low, WHOLE), ((2, part, wide), exact, WHOLE)],
        [pltpu.VMEM((width, wide), exact)],
        (f_c, f_from_r, f_from_c, f_from_rc, du_own, b_from_r, b_from_c, b_from_rc),
        after=(down_send,),
        flops=10**9,
    )
    up_got = swap_near(up_send)

    x_send, x_keep = call(
        input_grad_kernel,
        "input_grad",
        [WHOLE] * 3,
        [((2, own, width), low, WHOLE), ((2, own, width), exact, WHOLE)],
        [pltpu.VMEM((keys, width), exact)],
        (dq, dkv, w_all),
        after=(up_send,),
        flops=10**9,
    )
    x_got = swap_c(x_send)

    def fold(name, bit, keep, got):
        shape = keep.shape[1:]
        return call(
            lambda *refs: fold_kernel(bit, *refs),
            name,
            [WHOLE] * 2,
            [(shape, low, WHOLE), (shape, exact, WHOLE)],
            [],
            (keep, got),
        )

    def step(name, bit, keep, got, size):
        return call(
            lambda *refs: step_kernel(bit, *refs),
            name,
            [WHOLE] * 2,
            [((size + 16, half), low, WHOLE), ((size + 16, half), exact, WHOLE)],
            [pltpu.VMEM((2 * size + 16, half), exact)],
            (keep, got),
        )

    def spread(block):
        block = beside(block, swap_far(block))
        block = beside(block, swap_near(block))
        return block, swap_r(block)

    rest_send, rest_keep = step("rest_r", lambda q, r, x, c: r, rest_keep, rest_got, count // 2)
    rest_got = swap_r(rest_send)
    down_send, down_keep = fold("down_far", lambda q, r, x, c: q // 2, down_keep, down_got)
    down_got = swap_far(down_send)
    up_send, up_keep = fold("up_far", lambda q, r, x, c: q // 2, up_keep, up_got)
    up_got = swap_far(up_send)
    rest_send, rest_keep = step("rest_near", lambda q, r, x, c: q % 2, rest_keep, rest_got, count // 4)
    rest_got = swap_near(rest_send)
    (down_sum,) = call(
        sum_kernel, "down_sum", [WHOLE] * 2, [((quarter, width), low, WHOLE)], [], (down_keep, down_got)
    )
    down_near, down_far = spread(down_sum)
    shares = call(
        share_kernel, "up_share", [WHOLE] * 2, [((part // 4, wide), low, WHOLE)] * 4, [], (up_keep, up_got)
    )
    up_sum = jnp.concatenate([shares[0], swap_c(shares[1]), swap_x(shares[2]), swap_xc(shares[3])])
    up_near, up_far = spread(up_sum)
    rest_send, rest_keep = step("rest_far", lambda q, r, x, c: q // 2, rest_keep, rest_got, count // 8)
    rest_got = swap_far(rest_send)
    side, base, lines = call(
        last_step_kernel,
        "rest_last",
        [WHOLE] * 2,
        [((3 * thin, half), low, WHOLE), ((5 * thin, half), low, WHOLE), ((16, half), exact, WHOLE)],
        [pltpu.VMEM((8 * thin + 16, half), exact)],
        (rest_keep, rest_got),
    )
    rest_near, rest_far = spread(beside(base, swap_x(side)))

    x_send, x_keep = fold("input_r", lambda q, r, x, c: r, x_keep, x_got)
    x_got = swap_r(x_send)
    x_send, x_keep = fold(
        "input_x", lambda q, r, x, c: x, x_keep.reshape(2, rows, width), x_got.reshape(2, rows, width)
    )
    total = x_keep + swap_x(x_send).astype(exact)
    tokens_grad = regroup((total + dr).astype(low))[None]
    hidden_out = regroup(hidden)[None]

    (w_down_grad,) = call(
        down_out_kernel, "down_out", [WHOLE] * 2, [((2 * wide, width), exact, WHOLE)], [], (down_near, down_far)
    )
    (w_up_grad,) = call(
        up_out_kernel, "up_out", [WHOLE] * 2, [((part, inner), exact, WHOLE)], [], (up_near, up_far)
    )
    w_query_grad, w_key_grad, w_value_grad, w_out_grad = call(
        rest_out_kernel,
        "rest_out",
        [WHOLE] * 2,
        [((part, width), exact, WHOLE)] * 4,
        [pltpu.VMEM((32 * thin, half), exact)],
        (rest_near, rest_far),
    )

    c = lax.axis_index("c")
    pieces = jnp.where(c == 0, lines[:, :part], lines[:, part:])
    ups = jnp.where(c == 0, lines[2:4], lines[4:6])
    b_up_grad = ups.reshape(2 * wide)
    return (
        hidden_out,
        tokens_grad,
        w_query_grad,
        pieces[0],
        w_key_grad,
        w_value_grad,
        pieces[1],
        w_out_grad,
        pieces[6],
        pieces[7],
        pieces[8],
        w_up_grad,
        b_up_grad,
        w_down_grad,
        pieces[9],
        pieces[10],
        pieces[11],
    )


def plane_solution(mesh):
    planes, cycle = mesh.shape["shard"], mesh.shape["ctx"]
    grid = Mesh(mesh.devices.reshape(planes, cycle // planes, 2, 2), AXES)
    shard, ctx = ("x", "c"), ("q", "r")
    tokens, matrix, vector = P(shard, ctx, None), P(shard, None), P(shard)
    return jax.shard_map(
        plane_local,
        mesh=grid,
        in_specs=(
            tokens, tokens, P(shard, ctx), matrix, vector, matrix, matrix, vector, matrix, vector,
            vector, vector, matrix, vector, matrix, vector, vector, vector,
        ),
        out_specs=(
            tokens, tokens, matrix, vector, matrix, matrix, vector, matrix, vector,
            vector, vector, matrix, vector, matrix, vector, vector, vector,
        ),
        check_vma=False,
    )


def solution(mesh):
    if mesh.shape["shard"] == 4 and mesh.shape["ctx"] == 8:
        return plane_solution(mesh)
    return ring_solution(mesh)
```

```python
import math

import jax
import jax.numpy as jnp
from jax import lax
from jax.experimental import pallas as pl
from jax.experimental.pallas import tpu as pltpu
from jax.sharding import Mesh
from jax.sharding import PartitionSpec as P

HEAD_DIM = 64


ln_eps = 1e-12
masked_fill = -1e30


def from_behind(block, axis, distance):
    devices = range(lax.axis_size(axis))
    route = [((i - distance) % len(devices), i) for i in devices]
    return lax.ppermute(block, axis, route)


def matmul(left, right):
    return jnp.dot(left, right, preferred_element_type=jnp.float32)


def matmul_tn(left, right):
    return lax.dot_general(
        left, right, (((0,), (0,)), ((), ())), preferred_element_type=jnp.float32
    )


def matmul_nt(left, right):
    return lax.dot_general(
        left, right, (((1,), (1,)), ((), ())), preferred_element_type=jnp.float32
    )


def apply_layer_norm(value, gain, shift):
    mean = jnp.mean(value, axis=-1, keepdims=True)
    centered = value - mean
    rstd = lax.rsqrt(jnp.mean(centered * centered, axis=-1, keepdims=True) + ln_eps)
    normed = centered * rstd
    return (normed * gain + shift, normed, rstd)


def norm_back(grad, normed, rstd, gain):
    d_gain = jnp.sum(grad * normed, axis=0)
    d_shift = jnp.sum(grad, axis=0)
    scaled = grad * gain
    d_value = rstd * (
        scaled
        - jnp.mean(scaled, axis=-1, keepdims=True)
        - normed * jnp.mean(scaled * normed, axis=-1, keepdims=True)
    )
    return (d_value, d_gain, d_shift)


def gelu_slope(value):
    normal_cdf = 0.5 * (1.0 + lax.erf(value * (1.0 / math.sqrt(2.0))))
    density = jnp.exp(-0.5 * value * value) * (1.0 / math.sqrt(2.0 * math.pi))
    return normal_cdf + value * density


def scores_of(query, keys, q_ids, k_ids, scale):
    raw = jnp.einsum("qhd,khd->hqk", query, keys, preferred_element_type=jnp.float32) * scale
    match = (q_ids[:, None] == k_ids[None, :])[None, :, :]
    return (raw, match)


def attend(query, q_ids, keys, values, k_ids, stats, scale):
    top, total, accum = stats
    raw, match = scores_of(query, keys, q_ids, k_ids, scale)
    masked = jnp.where(match, raw, masked_fill)
    new_top = jnp.maximum(top, jnp.max(masked, axis=-1))
    weights = jnp.where(match, jnp.exp(masked - new_top[:, :, None]), 0.0)
    factor = jnp.exp(top - new_top)
    total = total * factor + jnp.sum(weights, axis=-1)
    accum = accum * factor[:, :, None] + jnp.einsum(
        "hqk,khd->hqd", weights.astype(jnp.bfloat16), values, preferred_element_type=jnp.float32
    )
    return (new_top, total, accum)


def block_grads(query, q_ids, d_out, log_total, delta, keys, values, k_ids, scale):
    raw, match = scores_of(query, keys, q_ids, k_ids, scale)
    probs = jnp.exp(jnp.where(match, raw - log_total[:, :, None], masked_fill))
    d_values = jnp.einsum(
        "hqk,qhd->khd", probs.astype(jnp.bfloat16), d_out, preferred_element_type=jnp.float32
    )
    d_probs = jnp.einsum("qhd,khd->hqk", d_out, values, preferred_element_type=jnp.float32)
    d_scores = (probs * (d_probs - delta[:, :, None])).astype(jnp.bfloat16)
    d_query = jnp.einsum("hqk,khd->qhd", d_scores, keys, preferred_element_type=jnp.float32) * scale
    d_keys = jnp.einsum("hqk,qhd->khd", d_scores, query, preferred_element_type=jnp.float32) * scale
    return (d_query, d_keys, d_values)


def ring_local(
    tokens,
    cotangent,
    seq_ids,
    w_query,
    b_query,
    w_key,
    w_value,
    b_value,
    w_out,
    b_out,
    attn_gain,
    attn_shift,
    w_up,
    b_up,
    w_down,
    b_down,
    ffn_gain,
    ffn_shift,
):
    cycle = lax.axis_size("ctx")
    tok_rows = tokens.shape[1]
    width = tokens.shape[2]
    heads = width // HEAD_DIM
    scale = 1.0 / math.sqrt(HEAD_DIM)
    share = tok_rows // cycle
    got_tokens, got_grads, got_ids = (
        lax.all_to_all(
            tokens[0].reshape(share, cycle, width), "ctx", split_axis=1, concat_axis=1, tiled=True
        ),
        lax.all_to_all(
            cotangent[0].reshape(share, cycle, width),
            "ctx",
            split_axis=1,
            concat_axis=1,
            tiled=True,
        ),
        lax.all_to_all(
            seq_ids[0].reshape(share, cycle), "ctx", split_axis=1, concat_axis=1, tiled=True
        ),
    )
    x_local = got_tokens.reshape(tok_rows, width)
    local_gradient = got_grads.reshape(tok_rows, width).astype(jnp.float32)
    local_ids = got_ids.reshape(tok_rows)
    (
        query_mat,
        query_bias,
        key_mat,
        value_mat,
        value_bias,
        out_mat,
        out_bias,
        attention_norm_gain,
        first_shift,
        up_mat,
        up_bias,
        down_mat,
        down_bias,
        feedforward_norm_gain,
        second_shift,
    ) = (
        lax.all_gather(w_query, "shard", axis=0, tiled=True),
        lax.all_gather(b_query, "shard", axis=0, tiled=True),
        lax.all_gather(w_key, "shard", axis=0, tiled=True),
        lax.all_gather(w_value, "shard", axis=0, tiled=True),
        lax.all_gather(b_value, "shard", axis=0, tiled=True),
        lax.all_gather(w_out, "shard", axis=0, tiled=True),
        lax.all_gather(b_out, "shard", axis=0, tiled=True),
        lax.all_gather(attn_gain, "shard", axis=0, tiled=True),
        lax.all_gather(attn_shift, "shard", axis=0, tiled=True),
        lax.all_gather(w_up, "shard", axis=0, tiled=True),
        lax.all_gather(b_up, "shard", axis=0, tiled=True),
        lax.all_gather(w_down, "shard", axis=0, tiled=True),
        lax.all_gather(b_down, "shard", axis=0, tiled=True),
        lax.all_gather(ffn_gain, "shard", axis=0, tiled=True),
        lax.all_gather(ffn_shift, "shard", axis=0, tiled=True),
    )
    query = (matmul(x_local, query_mat) + query_bias.astype(jnp.float32)).astype(jnp.bfloat16)
    keys = matmul(x_local, key_mat).astype(jnp.bfloat16)
    values = (matmul(x_local, value_mat) + value_bias.astype(jnp.float32)).astype(jnp.bfloat16)
    q_heads = query.reshape(tok_rows, heads, HEAD_DIM)
    start_stats = (
        jnp.full((heads, tok_rows), masked_fill, jnp.float32),
        jnp.zeros((heads, tok_rows), jnp.float32),
        jnp.zeros((heads, tok_rows, HEAD_DIM), jnp.float32),
    )

    def forward_step(step, carry):
        block, stats = carry
        stats = attend(
            q_heads,
            local_ids,
            block[0].reshape(tok_rows, heads, HEAD_DIM),
            block[1].reshape(tok_rows, heads, HEAD_DIM),
            block[2],
            stats,
            scale,
        )
        block = from_behind((block[0], block[1], block[2]), "ctx", 1)
        return (block, stats)

    block, stats = lax.fori_loop(
        0, cycle - 1, forward_step, ((keys, values, local_ids), start_stats)
    )
    top, total, accum = attend(
        q_heads,
        local_ids,
        block[0].reshape(tok_rows, heads, HEAD_DIM),
        block[1].reshape(tok_rows, heads, HEAD_DIM),
        block[2],
        stats,
        scale,
    )
    attn_out = (
        (accum / total[:, :, None]).transpose(1, 0, 2).reshape(tok_rows, width).astype(jnp.bfloat16)
    )
    log_total = top + jnp.log(total)
    attn_proj = matmul(attn_out, out_mat) + out_bias.astype(jnp.float32)
    first_sum = x_local.astype(jnp.float32) + attn_proj
    first_normalized_rows, first_centered_scaled, first_inverse_deviation = apply_layer_norm(
        first_sum, attention_norm_gain.astype(jnp.float32), first_shift.astype(jnp.float32)
    )
    normed_low = first_normalized_rows.astype(jnp.bfloat16)
    up_pre = matmul(normed_low, up_mat) + up_bias.astype(jnp.float32)
    up_act = jax.nn.gelu(up_pre, approximate=False).astype(jnp.bfloat16)
    down_pre = matmul(up_act, down_mat) + down_bias.astype(jnp.float32)
    layer_output, second_centered_scaled, second_inverse_deviation = apply_layer_norm(
        first_normalized_rows + down_pre,
        feedforward_norm_gain.astype(jnp.float32),
        second_shift.astype(jnp.float32),
    )
    (
        query_mat,
        key_mat,
        value_mat,
        out_mat,
        attention_norm_gain,
        up_mat,
        down_mat,
        feedforward_norm_gain,
    ) = (
        lax.all_gather(w_query, "shard", axis=0, tiled=True),
        lax.all_gather(w_key, "shard", axis=0, tiled=True),
        lax.all_gather(w_value, "shard", axis=0, tiled=True),
        lax.all_gather(w_out, "shard", axis=0, tiled=True),
        lax.all_gather(attn_gain, "shard", axis=0, tiled=True),
        lax.all_gather(w_up, "shard", axis=0, tiled=True),
        lax.all_gather(w_down, "shard", axis=0, tiled=True),
        lax.all_gather(ffn_gain, "shard", axis=0, tiled=True),
    )
    grad_two, d_second_gain, d_second_shift = norm_back(
        local_gradient,
        second_centered_scaled,
        second_inverse_deviation,
        feedforward_norm_gain.astype(jnp.float32),
    )
    grad_down = grad_two.astype(jnp.bfloat16)
    d_down_bias = jnp.sum(grad_down, axis=0, dtype=jnp.float32)
    d_down_mat = matmul_tn(up_act, grad_down)
    grad_up = (matmul_nt(grad_down, down_mat) * gelu_slope(up_pre)).astype(jnp.bfloat16)
    d_up_bias = jnp.sum(grad_up, axis=0, dtype=jnp.float32)
    d_up_mat = matmul_tn(normed_low, grad_up)
    first_norm_gradient = grad_two + matmul_nt(grad_up, up_mat)
    grad_first, d_first_gain, d_first_shift = norm_back(
        first_norm_gradient,
        first_centered_scaled,
        first_inverse_deviation,
        attention_norm_gain.astype(jnp.float32),
    )
    grad_proj = grad_first.astype(jnp.bfloat16)
    d_out_bias = jnp.sum(grad_proj, axis=0, dtype=jnp.float32)
    d_out_mat = matmul_tn(attn_out, grad_proj)
    grad_attn = matmul_nt(grad_proj, out_mat).astype(jnp.bfloat16)
    grad_heads = grad_attn.reshape(tok_rows, heads, HEAD_DIM)
    delta = jnp.einsum(
        "qhd,qhd->hq",
        grad_heads,
        attn_out.reshape(tok_rows, heads, HEAD_DIM),
        preferred_element_type=jnp.float32,
    )
    zero_rows = jnp.zeros((tok_rows, width), jnp.float32)

    def key_step(step, carry):
        block, sums, acc_query = carry
        d_query, d_keys, d_values = block_grads(
            q_heads,
            local_ids,
            grad_heads,
            log_total,
            delta,
            block[0].reshape(tok_rows, heads, HEAD_DIM),
            block[1].reshape(tok_rows, heads, HEAD_DIM),
            block[2],
            scale,
        )
        sums = (
            sums[0] + d_keys.reshape(tok_rows, width),
            sums[1] + d_values.reshape(tok_rows, width),
        )
        block = from_behind((block[0], block[1], block[2]), "ctx", 1)
        sums = (
            from_behind(sums[0].astype(jnp.bfloat16), "ctx", 1).astype(jnp.float32),
            from_behind(sums[1].astype(jnp.bfloat16), "ctx", 1).astype(jnp.float32),
        )
        return (block, sums, acc_query + d_query.reshape(tok_rows, width))

    block, sums, d_query_sum = lax.fori_loop(
        0, cycle, key_step, ((keys, values, local_ids), (zero_rows, zero_rows), zero_rows)
    )
    d_keys_sum, d_values_sum = sums
    grad_query = d_query_sum.astype(jnp.bfloat16)
    grad_keys = d_keys_sum.astype(jnp.bfloat16)
    grad_values = d_values_sum.astype(jnp.bfloat16)
    d_query_bias = jnp.sum(grad_query, axis=0, dtype=jnp.float32)
    d_value_bias = jnp.sum(grad_values, axis=0, dtype=jnp.float32)
    d_query_mat = matmul_tn(x_local, grad_query)
    d_key_mat = matmul_tn(x_local, grad_keys)
    d_value_mat = matmul_tn(x_local, grad_values)
    grad_input = (
        grad_first
        + matmul_nt(grad_query, query_mat)
        + matmul_nt(grad_keys, key_mat)
        + matmul_nt(grad_values, value_mat)
    )
    home_hidden, home_grad = (
        lax.all_to_all(
            layer_output.astype(jnp.bfloat16).reshape(share, cycle, width),
            "ctx",
            split_axis=1,
            concat_axis=1,
            tiled=True,
        ),
        lax.all_to_all(
            grad_input.astype(jnp.bfloat16).reshape(share, cycle, width),
            "ctx",
            split_axis=1,
            concat_axis=1,
            tiled=True,
        ),
    )
    hidden_out = home_hidden.reshape(tok_rows, width)[None]
    tokens_grad = home_grad.reshape(tok_rows, width)[None]
    shares = (
        lax.psum_scatter(
            d_query_mat.astype(jnp.bfloat16), "shard", scatter_dimension=0, tiled=True
        ).astype(jnp.float32),
        lax.psum_scatter(
            d_query_bias.astype(jnp.bfloat16), "shard", scatter_dimension=0, tiled=True
        ).astype(jnp.float32),
        lax.psum_scatter(
            d_key_mat.astype(jnp.bfloat16), "shard", scatter_dimension=0, tiled=True
        ).astype(jnp.float32),
        lax.psum_scatter(
            d_value_mat.astype(jnp.bfloat16), "shard", scatter_dimension=0, tiled=True
        ).astype(jnp.float32),
        lax.psum_scatter(
            d_value_bias.astype(jnp.bfloat16), "shard", scatter_dimension=0, tiled=True
        ).astype(jnp.float32),
        lax.psum_scatter(
            d_out_mat.astype(jnp.bfloat16), "shard", scatter_dimension=0, tiled=True
        ).astype(jnp.float32),
        lax.psum_scatter(
            d_out_bias.astype(jnp.bfloat16), "shard", scatter_dimension=0, tiled=True
        ).astype(jnp.float32),
        lax.psum_scatter(
            d_first_gain.astype(jnp.bfloat16), "shard", scatter_dimension=0, tiled=True
        ).astype(jnp.float32),
        lax.psum_scatter(
            d_first_shift.astype(jnp.bfloat16), "shard", scatter_dimension=0, tiled=True
        ).astype(jnp.float32),
        lax.psum_scatter(
            d_up_mat.astype(jnp.bfloat16), "shard", scatter_dimension=0, tiled=True
        ).astype(jnp.float32),
        lax.psum_scatter(
            d_up_bias.astype(jnp.bfloat16), "shard", scatter_dimension=0, tiled=True
        ).astype(jnp.float32),
        lax.psum_scatter(
            d_down_mat.astype(jnp.bfloat16), "shard", scatter_dimension=0, tiled=True
        ).astype(jnp.float32),
        lax.psum_scatter(
            d_down_bias.astype(jnp.bfloat16), "shard", scatter_dimension=0, tiled=True
        ).astype(jnp.float32),
        lax.psum_scatter(
            d_second_gain.astype(jnp.bfloat16), "shard", scatter_dimension=0, tiled=True
        ).astype(jnp.float32),
        lax.psum_scatter(
            d_second_shift.astype(jnp.bfloat16), "shard", scatter_dimension=0, tiled=True
        ).astype(jnp.float32),
    )
    totals = lax.psum(
        (
            shares[0],
            shares[1],
            shares[2],
            shares[3],
            shares[4],
            shares[5],
            shares[6],
            shares[7],
            shares[8],
            shares[9],
            shares[10],
            shares[11],
            shares[12],
            shares[13],
            shares[14],
        ),
        "ctx",
    )
    return (hidden_out, tokens_grad) + tuple(totals)


def ring_solution(mesh):
    return jax.shard_map(
        ring_local,
        mesh=mesh,
        in_specs=(
            P("shard", "ctx", None),
            P("shard", "ctx", None),
            P("shard", "ctx"),
            P("shard", None),
            P("shard"),
            P("shard", None),
            P("shard", None),
            P("shard"),
            P("shard", None),
            P("shard"),
            P("shard"),
            P("shard"),
            P("shard", None),
            P("shard"),
            P("shard", None),
            P("shard"),
            P("shard"),
            P("shard"),
        ),
        out_specs=(
            P("shard", "ctx", None),
            P("shard", "ctx", None),
            P("shard", None),
            P("shard"),
            P("shard", None),
            P("shard", None),
            P("shard"),
            P("shard", None),
            P("shard"),
            P("shard"),
            P("shard"),
            P("shard", None),
            P("shard"),
            P("shard", None),
            P("shard"),
            P("shard"),
            P("shard"),
        ),
        check_vma=False,
    )


AXES = ("q", "r", "x", "c")
ANY = pl.BlockSpec(memory_space=pl.ANY)
WHOLE = pl.BlockSpec(memory_space=pltpu.VMEM)
HBM = pl.BlockSpec(memory_space=pltpu.HBM)


def moved(block, move):
    sizes = [lax.axis_size(a) for a in AXES]

    def number(spot):
        place = 0
        for size, at in zip(sizes, spot):
            place = place * size + at
        return place

    spots = [
        (q, r, x, c)
        for q in range(sizes[0])
        for r in range(sizes[1])
        for x in range(sizes[2])
        for c in range(sizes[3])
    ]
    return lax.ppermute(block, AXES, [(number(s), number(move(*s))) for s in spots])


def swap_x(block):
    return moved(block, lambda q, r, x, c: (q, r, 1 - x, c))


def swap_c(block):
    return moved(block, lambda q, r, x, c: (q, r, x, 1 - c))


def swap_r(block):
    return moved(block, lambda q, r, x, c: (q, r ^ 1, x, c))


def swap_rc(block):
    return moved(block, lambda q, r, x, c: (q, r ^ 1, x, 1 - c))


def swap_near(block):
    return moved(block, lambda q, r, x, c: (q ^ 1, r, x, c))


def swap_far(block):
    return moved(block, lambda q, r, x, c: (q ^ 2, r, x, c))


def regroup(block):
    return moved(block, lambda q, r, x, c: (2 * c + x, r, q & 1, q >> 1))


def regroup_x(block):
    return moved(block, lambda q, r, x, c: (2 * c + x, r, 1 - (q & 1), q >> 1))


def swap_xc(block):
    return moved(block, lambda q, r, x, c: (q, r, 1 - x, 1 - c))


def beside(mine, got):
    return jnp.concatenate([mine, got])


def dot(left, right):
    return jnp.dot(left, right, preferred_element_type=jnp.float32)


def dot_nt(left, right):
    return lax.dot_general(
        left, right, (((1,), (1,)), ((), ())), preferred_element_type=jnp.float32
    )


def dot_tn(left, right):
    return lax.dot_general(
        left, right, (((0,), (0,)), ((), ())), preferred_element_type=jnp.float32
    )


class Copies:
    def __init__(self, sems):
        self.sems = sems
        self.count = 0
        self.held = []

    def start(self, source, target):
        copy = pltpu.make_async_copy(source, target, self.sems.at[self.count])
        copy.start()
        self.count += 1
        self.held.append(copy)

    def wait(self):
        for copy in self.held:
            copy.wait()
        self.held = []


def spot():
    return tuple(lax.axis_index(a) for a in AXES)


def fill_mask(ids, mask, own):
    blocks, rows = ids.shape
    mine = jnp.concatenate([ids[pl.ds(own, 1), :], ids[pl.ds(own + 1, 1), :]], axis=1)
    across = jnp.transpose(ids[...])
    for b in range(blocks):
        mask[rows * b : rows * (b + 1), :] = jnp.where(across[:, b : b + 1] == mine, 0.0, masked_fill)


def block_kernel(tokens, ids, block, line, sems):
    rows = tokens.shape[0]
    copies = Copies(sems)
    copies.start(tokens, block.at[pl.ds(0, rows)])
    copies.start(ids, line)
    block[rows:, :] = jnp.zeros((16, block.shape[1]), block.dtype)
    copies.wait()
    block[rows:, 0:rows] = jnp.broadcast_to(line[...].astype(jnp.float32), (16, rows)).astype(block.dtype)


def pack_kernel(w_q, w_k, w_v, *refs):
    vectors, b_up, theirs, mine = refs[:8], refs[8], refs[9], refs[10]
    lines, thin, thick, sems = refs[11], refs[12:20], refs[20], refs[21]
    q, r, x, c = spot()
    part, width = w_q.shape
    half = width // 2
    copies = Copies(sems)
    for t, w in enumerate((w_q, w_k, w_v)):
        rows = pl.ds(part * t, part)
        copies.start(w.at[:, pl.ds(pl.multiple_of(half * x, 128), half)], mine.at[rows])
        copies.start(w.at[:, pl.ds(pl.multiple_of(half * (1 - x), 128), half)], theirs.at[rows])
    for vector, held in zip(vectors, thin):
        copies.start(vector, held)
    copies.start(b_up, thick)
    lines[...] = jnp.zeros_like(lines)
    copies.wait()
    for i, vector in enumerate(thin):
        line = vector[...].astype(jnp.float32).reshape(1, part)
        none = jnp.zeros_like(line)
        first = jnp.concatenate([line, none], axis=1)
        second = jnp.concatenate([none, line], axis=1)
        lines[i : i + 1, :] = jnp.where(c == 0, first, second)
    wide = thick[...].astype(jnp.float32).reshape(1, width)
    lines[pl.ds(8 + 2 * c, 1), :] = wide[:, 0:half]
    lines[pl.ds(9 + 2 * c, 1), :] = wide[:, half:]
    low = lines[...].astype(jnp.bfloat16)
    mine[3 * part :, :] = low
    theirs[3 * part :, :] = low


def cut_kernel(w, theirs, mine, sems):
    q, r, x, c = spot()
    count = theirs.shape[1]
    copies = Copies(sems)
    copies.start(w.at[:, pl.ds(pl.multiple_of(count * (1 - x), 128), count)], theirs)
    copies.start(w.at[:, pl.ds(pl.multiple_of(count * x, 128), count)], mine)
    copies.wait()


def load_kernel(block, out, sems):
    copies = Copies(sems)
    copies.start(block, out)
    copies.wait()


def turn_kernel(keys, out):
    for p in range(keys.shape[0]):
        out[2 * p : 2 * p + 2] = jnp.transpose(keys[p]).reshape(2, 64, keys.shape[1])


def attend_kernel(
    b0, b1, b2, b3, b4, b5, b6, b7, w_q, w_k, w_v, w_x, w_m, w_mx, own_lines, w_o, w_om,
    a_low, x_out, w_out, wo_out, k_out, v_out, q_out, o_out, lse_out, ids_out, a_out, vecs, up_bias,
    xs, raw, w, wo, lines, k3, v3, vt, q3, ot, mask, sems, outs,
):
    q, r, x, c = spot()
    rows = xs.shape[0] // 8
    part = w.shape[0] // 4
    half = wo.shape[0]
    me, shard = 4 * r + 2 * c + x, 2 * x + c
    ins = Copies(sems)
    for j, block in enumerate((b0, b1, b2, b3, b4, b5, b6, b7)):
        at = me ^ j
        ins.start(block.at[pl.ds(0, rows)], xs.at[pl.ds(pl.multiple_of(rows * at, rows), rows)])
        ins.start(block.at[pl.ds(rows, 16)], raw.at[at])
    columns = pl.ds(pl.multiple_of(half * x, 128), half)
    for t, own in enumerate((w_q, w_k, w_v)):
        place = pl.ds(half * t, half)
        ins.start(own.at[:, columns], w.at[pl.ds(pl.multiple_of(part * shard, 64), part), place])
        for flip, piece in ((2, w_x), (1, w_m), (3, w_mx)):
            at = pl.ds(pl.multiple_of(part * (shard ^ flip), 64), part)
            ins.start(piece.at[pl.ds(part * t, part)], w.at[at, place])
    for i, piece in enumerate((own_lines, w_m, w_x, w_mx)):
        ins.start(piece.at[pl.ds(3 * part, 16)], lines.at[i])
    ins.start(w_o, wo.at[pl.ds(pl.multiple_of(part * c, 64), part)])
    ins.start(w_om, wo.at[pl.ds(pl.multiple_of(part * (1 - c), 64), part)])
    ins.wait()
    backs = Copies(outs)
    backs.start(xs, x_out)
    backs.start(w, w_out)
    backs.start(wo, wo_out)
    mine = lines[0].astype(jnp.float32) + lines[1].astype(jnp.float32)
    other = lines[2].astype(jnp.float32) + lines[3].astype(jnp.float32)
    vecs[:, columns] = mine[0:8, :]
    vecs[:, pl.ds(pl.multiple_of(half * (1 - x), 128), half)] = other[0:8, :]
    for i in range(4):
        up_bias[i] = jnp.broadcast_to(mine[8 + i : 9 + i, :], (8, half))
    for b in range(8):
        ids_out[b : b + 1, :] = raw[b, 0:1, 0:rows].astype(jnp.float32)
    fill_mask(ids_out, mask, 4 * r + 2 * c)
    keyed = dot(xs[...], w[:, half : 2 * half]).astype(jnp.bfloat16)
    valued = dot(xs[...], w[:, 2 * half : 3 * half]) + mine[1:2, :]
    own = pl.ds(pl.multiple_of(rows * (4 * r + 2 * c), rows), 2 * rows)
    asked = (dot(xs[own, :], w[:, 0:half]) + mine[0:1, :]).astype(jnp.bfloat16)
    valued = valued.astype(jnp.bfloat16)
    turned = jnp.transpose(valued)
    pairs = half // 128
    for p in range(pairs):
        k3[p] = keyed[:, 128 * p : 128 * (p + 1)]
        v3[p] = valued[:, 128 * p : 128 * (p + 1)]
        q3[p] = asked[:, 128 * p : 128 * (p + 1)]
    for h in range(2 * pairs):
        vt[h] = turned[64 * h : 64 * (h + 1), :]
    backs.start(k3, k_out)
    backs.start(v3, v_out)
    q_out[...] = q3[...]
    lane = lax.broadcasted_iota(jnp.int32, (2 * rows, 128), 1) // 64

    def head(h, carry):
        query = jnp.where(lane == h % 2, q3[h // 2], 0) * 0.125
        scores = dot_nt(k3[h // 2], query.astype(jnp.bfloat16)) + mask[...]
        top = jnp.max(scores, axis=0, keepdims=True)
        weights = jnp.exp(scores - top)
        total = jnp.sum(weights, axis=0, keepdims=True)
        ot[h] = dot(vt[h], weights.astype(jnp.bfloat16)) / total
        lse_out[pl.ds(h, 1), :] = top + jnp.log(total)
        return carry

    lax.fori_loop(0, 2 * pairs, head, 0)
    mixed = jnp.transpose(ot[...].reshape(half, 2 * rows)).astype(jnp.bfloat16)
    o_out[...] = mixed
    partial = dot(mixed, wo[...])
    a_out[...] = partial
    a_low[...] = partial.astype(jnp.bfloat16)
    backs.wait()


def load_feedforward(copies, up, down, u_own, u_x, u_m, u_mx, d_own, d_m):
    q, r, x, c = spot()
    part = up.shape[0] // 4
    count = up.shape[1]
    shard = 2 * x + c
    own = u_own.at[:, pl.ds(pl.multiple_of(count * x, 128), count)]
    for flip, piece in ((0, own), (2, u_x), (1, u_m), (3, u_mx)):
        rows = pl.ds(pl.multiple_of(part * (shard ^ flip), 64), part)
        copies.start(piece, up.at[rows])
    for side, piece in ((c, d_own), (1 - c, d_m)):
        copies.start(piece, down.at[pl.ds(pl.multiple_of(count // 2 * side, 128), count // 2)])


def norm_of(value):
    mean = jnp.mean(value, axis=-1, keepdims=True)
    centered = value - mean
    rstd = lax.rsqrt(jnp.mean(centered * centered, axis=-1, keepdims=True) + ln_eps)
    return centered * rstd, rstd


def norm_pull(scaled, normed, rstd):
    return rstd * (
        scaled
        - jnp.mean(scaled, axis=-1, keepdims=True)
        - normed * jnp.mean(scaled * normed, axis=-1, keepdims=True)
    )


def forward_kernel(
    a_own, a_got, xs, vecs, b_up, u_own, u_x, u_m, u_mx, d_own, d_m,
    y_low, h_out, z, n_out, r_out, slope, y_out,
    up, down, x_own, sems, more,
):
    q, r, x, c = spot()
    rows = x_own.shape[0]
    first = Copies(more)
    first.start(xs.at[pl.ds(pl.multiple_of(rows * (2 * r + c), rows), rows)], x_own)
    copies = Copies(sems)
    load_feedforward(copies, up, down, u_own, u_x, u_m, u_mx, d_own, d_m)
    first.wait()
    total = x_own[...].astype(jnp.float32) + (a_own[...] + a_got[...].astype(jnp.float32) + vecs[2:3, :])
    normed, rstd = norm_of(total)
    n_out[...] = normed
    r_out[...] = jnp.broadcast_to(rstd, r_out.shape)
    low = (normed * vecs[3:4, :] + vecs[4:5, :]).astype(jnp.bfloat16)
    h_out[...] = low
    copies.wait()
    wide = up.shape[1] // 4
    for j in range(4):
        at = slice(wide * j, wide * (j + 1))
        pre = dot(low, up[:, at]) + b_up[j, 0:1, :]
        cdf = 0.5 * (1.0 + lax.erf(pre * (1.0 / math.sqrt(2.0))))
        density = jnp.exp(-0.5 * pre * pre) * (1.0 / math.sqrt(2.0 * math.pi))
        z[:, at] = (pre * cdf).astype(jnp.bfloat16)
        slope[:, at] = cdf + pre * density
    result = dot(z[...], down[...])
    y_out[...] = result
    y_low[...] = result.astype(jnp.bfloat16)


def norm_back_kernel(
    y_own, y_got, normed1, g_own, g_x, vecs, low_out, hid_out, dy_out, sums, grad, hid, sems,
):
    q, r, x, c = spot()
    rows = grad.shape[0] // 2
    copies = Copies(sems)
    copies.start(g_own, grad.at[pl.ds(pl.multiple_of(rows * x, rows), rows)])
    copies.start(g_x, grad.at[pl.ds(pl.multiple_of(rows * (1 - x), rows), rows)])
    h1 = normed1[...] * vecs[3:4, :] + vecs[4:5, :]
    normed, rstd = norm_of(h1 + (y_own[...] + y_got[...].astype(jnp.float32) + vecs[5:6, :]))
    hid[...] = (normed * vecs[6:7, :] + vecs[7:8, :]).astype(jnp.bfloat16)
    hid_out[...] = hid[pl.ds(pl.multiple_of(rows * x, rows), rows), :]
    copies.wait()
    cot = grad[...].astype(jnp.float32)
    dy = norm_pull(cot * vecs[6:7, :], normed, rstd)
    low = dy.astype(jnp.bfloat16)
    dy_out[...] = dy
    low_out[...] = low
    sums[...] = jnp.zeros_like(sums)
    sums[0:1, :] = jnp.sum(low.astype(jnp.float32), axis=0, keepdims=True)
    sums[1:2, :] = jnp.sum(cot * normed, axis=0, keepdims=True)
    sums[2:3, :] = jnp.sum(cot, axis=0, keepdims=True)


def backward_kernel(
    dy, dy_low, slope, u_own, u_x, u_m, u_mx, d_own, d_m,
    p_low, s_out, du_out, up_sums, up, down, sems,
):
    copies = Copies(sems)
    load_feedforward(copies, up, down, u_own, u_x, u_m, u_mx, d_own, d_m)
    copies.wait()
    low = dy_low[...]
    wide = up.shape[1] // 4
    for j in range(4):
        at = slice(wide * j, wide * (j + 1))
        du = (dot_nt(low, down[at, :]) * slope[:, at]).astype(jnp.bfloat16)
        du_out[:, at] = du
        total = jnp.sum(du.astype(jnp.float32), axis=0, keepdims=True)
        up_sums[j] = jnp.broadcast_to(total, up_sums.shape[1:])
    result = dot_nt(du_out[...], up[...])
    s_out[...] = dy[...] + result
    p_low[...] = result.astype(jnp.bfloat16)


def attend_back_kernel(
    s_own, p_got, normed1, rstd1, vecs, wo, mixed, q3, k3, v3, kt, lse, ids,
    dkv_out, dq_out, dr_out, da_out, sums, qv_sums,
    mask, do3, delta, dk, dv, dqt, whole,
):
    q, r, x, c = spot()
    rows = dr_out.shape[0]
    pairs = q3.shape[0]
    half = 128 * pairs
    fill_mask(ids, mask, 4 * r + 2 * c)
    dh = s_own[...] + p_got[...].astype(jnp.float32)
    normed = normed1[...]
    dr = norm_pull(dh * vecs[3:4, :], normed, rstd1[:, 0:1])
    whole[...] = dr
    dr_out[...] = whole[pl.ds(pl.multiple_of(rows * x, rows), rows), :]
    low = dr.astype(jnp.bfloat16)
    da_out[...] = low
    sums[...] = jnp.zeros_like(sums)
    sums[0:1, :] = jnp.sum(low.astype(jnp.float32), axis=0, keepdims=True)
    sums[1:2, :] = jnp.sum(dh * normed, axis=0, keepdims=True)
    sums[2:3, :] = jnp.sum(dh, axis=0, keepdims=True)
    d_o = dot_nt(low, wo[...]).astype(jnp.bfloat16)
    products = jnp.transpose(d_o.astype(jnp.float32) * mixed[...].astype(jnp.float32))
    for h in range(2 * pairs):
        delta[h : h + 1, :] = jnp.sum(products[64 * h : 64 * (h + 1), :], axis=0, keepdims=True)
    for p in range(pairs):
        do3[p] = d_o[:, 128 * p : 128 * (p + 1)]
    dk[...] = jnp.zeros_like(dk)
    dv[...] = jnp.zeros_like(dv)
    lane = lax.broadcasted_iota(jnp.int32, (2 * rows, 128), 1) // 64

    def head(h, carry):
        p = h // 2
        here = lane == h % 2
        query = (jnp.where(here, q3[p], 0) * 0.125).astype(jnp.bfloat16)
        d_here = jnp.where(here, do3[p], 0).astype(jnp.bfloat16)
        probs = jnp.exp(dot_nt(k3[p], query) + mask[...] - lse[pl.ds(h, 1), :])
        d_probs = dot_nt(v3[p], d_here)
        d_scores = (probs * (d_probs - delta[pl.ds(h, 1), :])).astype(jnp.bfloat16)
        dv[p] += dot(probs.astype(jnp.bfloat16), d_here)
        dk[p] += dot(d_scores, query)
        dqt[h] = dot(kt[h], d_scores)
        return carry

    lax.fori_loop(0, 2 * pairs, head, 0)
    dq = (jnp.transpose(dqt[...].reshape(half, 2 * rows)) * 0.125).astype(jnp.bfloat16)
    dq_out[...] = dq
    qv_sums[...] = jnp.zeros_like(qv_sums)
    qv_sums[0:1, :] = jnp.sum(dq.astype(jnp.float32), axis=0, keepdims=True)
    for p in range(pairs):
        at = slice(128 * p, 128 * (p + 1))
        dkv_out[:, at] = dk[p].astype(jnp.bfloat16)
        value = dv[p].astype(jnp.bfloat16)
        dkv_out[:, half + 128 * p : half + 128 * (p + 1)] = value
        qv_sums[1:2, at] = jnp.sum(value.astype(jnp.float32), axis=0, keepdims=True)


def input_grad_kernel(dq, dkv, w, send, keep, whole):
    q, r, x, c = spot()
    half = dq.shape[1]
    rows = dq.shape[0] // 2
    whole[...] = dot_nt(dkv[...], w[:, half:])
    own = pl.ds(pl.multiple_of(rows * (4 * r + 2 * c), rows), 2 * rows)
    whole[own, :] += dot_nt(dq[...], w[:, 0:half])
    for b in range(2):
        for i in range(2):
            mine = pl.ds(pl.multiple_of(rows * (4 * i + 2 * c + b), rows), rows)
            keep[2 * rows * b + rows * i : 2 * rows * b + rows * (i + 1), :] = whole[mine, :]
            theirs = pl.ds(pl.multiple_of(rows * (4 * i + 2 * (1 - c) + b), rows), rows)
            send[2 * rows * b + rows * i : 2 * rows * b + rows * (i + 1), :] = whole[theirs, :].astype(jnp.bfloat16)


def octants():
    for at in range(8):
        r, q0, q1 = at >> 2, at >> 1 & 1, at & 1
        yield at, 4 * r + 2 * q1 + q0


def down_grad_kernel(z, dy, send, keep):
    q, r, x, c = spot()
    half = z.shape[1] // 2
    rows = half // 8
    for side, out in ((1 - c, send), (c, keep)):
        part = dot_tn(z[:, pl.ds(pl.multiple_of(half * side, 128), half)], dy[...])
        for at, within in octants():
            block = part[rows * within : rows * (within + 1), :]
            out[rows * at : rows * (at + 1), :] = block.astype(out.dtype)


def up_grad_kernel(h, du, send, keep, whole):
    q, r, x, c = spot()
    width = h.shape[1]
    thin = width // 32
    whole[...] = dot_tn(h[...], du[...])
    for side, out in ((1 - c, send), (c, keep)):
        for at, within in octants():
            pieces = []
            for xx in range(2):
                first = 8 * thin * (2 * xx + side) + thin * within
                rows = pl.ds(pl.multiple_of(first, 8), thin)
                pieces += [whole[rows, 0:width], whole[rows, width:]]
            block = jnp.concatenate(pieces)
            out[4 * thin * at : 4 * thin * (at + 1), :] = block.astype(out.dtype)


def join_kernel(*refs):
    out, at = refs[-1], 0
    for ref in refs[:-1]:
        count = ref.shape[0]
        out[at : at + count, :] = ref[...]
        at += count


def fold_kernel(bit, keep, got, send, kept):
    at = bit(*spot())
    send[...] = (keep[1 - at] + got[1 - at].astype(jnp.float32)).astype(send.dtype)
    kept[...] = keep[at] + got[at].astype(jnp.float32)


def copy_kernel(block, out):
    out[...] = block[...]


def sum_kernel(keep, got, out):
    out[...] = (keep[...] + got[...].astype(jnp.float32)).astype(out.dtype)


def total_kernel(keep, got, more, out):
    out[...] = (keep[...] + got[...].astype(jnp.float32) + more[...]).astype(out.dtype)


def share_kernel(keep, got, side, base):
    q, r, x, c = spot()
    side[...] = (keep[1 - x] + got[1 - x].astype(jnp.float32)).astype(side.dtype)
    base[...] = (keep[x] + got[x].astype(jnp.float32)).astype(base.dtype)


def weight_grad_kernel(
    xs, dkv, dq, mixed, da, sums1, sums2, qv_sums, up_sums, send, keep, packed, sems
):
    q, r, x, c = spot()
    width = xs.shape[1]
    own, half = dq.shape
    thin = width // 32
    for_c = 64 * thin
    own_rows = pl.ds(pl.multiple_of(own * (2 * r + c), own), own)
    asked = dot_tn(xs[own_rows, :], dq[...])
    kept = dot_tn(xs[...], dkv[...])
    outer = dot_tn(mixed[...], da[...])
    for cc in range(2):
        for rr in range(2):
            for q1 in range(2):
                for q0 in range(2):
                    at = ((4 * rr + 2 * q0 + q1) * 8) * thin
                    within = (4 * rr + 2 * q1 + q0) * thin
                    for xx in range(2):
                        rows = slice((16 * xx + 8 * cc) * thin + within, (16 * xx + 8 * cc + 1) * thin + within)
                        for t, piece in enumerate((asked, kept[:, 0:half], kept[:, half:])):
                            to = at + (3 * xx + t) * thin
                            packed[cc, to : to + thin, :] = piece[rows, :]
                    rows = slice(8 * cc * thin + within, (8 * cc + 1) * thin + within)
                    for t in range(2):
                        to = at + (6 + t) * thin
                        packed[cc, to : to + thin, :] = outer[rows, half * t : half * (t + 1)]
    columns = pl.ds(pl.multiple_of(half * x, 128), half)
    for cc in range(2):
        packed[cc, for_c : for_c + 16, :] = jnp.zeros((16, half), jnp.float32)
        packed[cc, for_c : for_c + 2, :] = qv_sums[0:2, :]
        for j in range(4):
            packed[cc, for_c + 2 + j : for_c + 3 + j, :] = up_sums[j, 0:1, :]
        packed[cc, for_c + 6 : for_c + 9, :] = sums1[0:3, columns]
        packed[cc, for_c + 9 : for_c + 12, :] = sums2[0:3, columns]
    send[...] = packed[1 - c].astype(jnp.bfloat16)
    copy = pltpu.make_async_copy(packed.at[c], keep, sems.at[0])
    copy.start()
    copy.wait()


def step_kernel(bit, keep, got, send, kept, whole):
    at = bit(*spot())
    count = send.shape[0] - 16
    whole[...] = keep[...] + got[...].astype(jnp.float32)
    theirs = pl.ds(pl.multiple_of(count * (1 - at), 64), count)
    mine = pl.ds(pl.multiple_of(count * at, 64), count)
    send[0:count, :] = whole[theirs, :].astype(jnp.bfloat16)
    send[count:, :] = whole[2 * count :, :].astype(jnp.bfloat16)
    kept[0:count, :] = whole[mine, :]
    kept[count:, :] = whole[2 * count :, :]


def last_step_kernel(keep, got, side, base, *refs):
    out, b_up, whole = refs[:8], refs[8], refs[9]
    q, r, x, c = spot()
    count = side.shape[0]
    part = out[0].shape[0]
    whole[...] = keep[...] + got[...].astype(jnp.float32)
    theirs = pl.ds(pl.multiple_of(count * (1 - x), 8), count)
    mine = pl.ds(pl.multiple_of(count * x, 8), count)
    side[...] = whole[theirs, :].astype(jnp.bfloat16)
    first = whole.shape[0] - 16
    base[...] = jnp.concatenate([whole[mine, :], whole[2 * count : first, :]]).astype(jnp.bfloat16)
    for i, one in enumerate(out):
        at = first + (i if i < 2 else i + 4)
        line = whole[at : at + 1, :]
        one[...] = jnp.where(c == 0, line[:, :part], line[:, part:]).reshape(part)
    line = jnp.concatenate([whole[pl.ds(first + 2 + 2 * c + i, 1), :] for i in range(2)], axis=1)
    b_up[...] = line.reshape(b_up.shape[0])


def down_out_kernel(near, far, out):
    q, r, x, c = spot()
    count = near.shape[0] // 4
    for d, piece in enumerate((near, far)):
        for k in range(4):
            at = 4 * (r ^ d) + 2 * ((q // 2) ^ (k & 1)) + ((q % 2) ^ (k >> 1))
            rows = pl.ds(pl.multiple_of(count * at, 32), count)
            out[rows, :] = piece[count * k : count * (k + 1), :].astype(jnp.float32)


def up_out_kernel(near, far, out, whole):
    q, r, x, c = spot()
    thin, width = near.shape[0] // 16, near.shape[1]
    for d, piece in enumerate((near, far)):
        whole[...] = piece[...].astype(jnp.float32)
        for k in range(4):
            at = 4 * (r ^ d) + 2 * ((q // 2) ^ (k & 1)) + ((q % 2) ^ (k >> 1))
            rows = pl.ds(pl.multiple_of(thin * at, 8), thin)
            for s in range(4):
                columns = pl.ds(pl.multiple_of(width * (2 * (x ^ (s >> 1)) + (s & 1)), 128), width)
                first = thin * (4 * k + s)
                out[rows, columns] = whole[first : first + thin, :]


def rest_out_kernel(near, far, hidden, total, out_q, out_k, out_v, out_o, out_h, out_t, whole):
    out_h[...] = hidden[...]
    out_t[...] = total[...]
    q, r, x, c = spot()
    half = near.shape[1]
    thin = near.shape[0] // 32
    ours = pl.ds(pl.multiple_of(half * x, 128), half)
    other = pl.ds(pl.multiple_of(half * (1 - x), 128), half)
    for d, piece in enumerate((near, far)):
        whole[...] = piece[...].astype(jnp.float32)
        for k in range(4):
            at = 4 * (r ^ d) + 2 * ((q // 2) ^ (k & 1)) + ((q % 2) ^ (k >> 1))
            rows = pl.ds(pl.multiple_of(thin * at, 8), thin)
            first = 8 * thin * k
            for t, out in enumerate((out_q, out_k, out_v)):
                out[rows, ours] = whole[first + thin * t : first + thin * (t + 1), :]
                out[rows, other] = whole[first + thin * (5 + t) : first + thin * (6 + t), :]
            for t in range(2):
                columns = slice(half * t, half * (t + 1))
                out_o[rows, columns] = whole[first + thin * (3 + t) : first + thin * (4 + t), :]


def kernel_call(body, name, ins, outs, scratch, args, after=(), room=2 << 20):
    count = len(args)

    def size(shape, dtype):
        return math.prod(shape) * jnp.dtype(dtype).itemsize

    used = sum(size(m.shape, m.dtype) for m in scratch if m.memory_space == pltpu.VMEM)

    args = [
        pltpu.with_memory_space_constraint(a, pltpu.HBM) if spec is HBM else a
        for a, spec in zip(args, ins)
    ]

    def run(*refs):
        body(*refs[:count], *refs[count + len(after) :])

    return pl.pallas_call(
        run,
        name=name,
        out_shape=[jax.ShapeDtypeStruct(shape, dtype) for shape, dtype, _ in outs],
        in_specs=list(ins) + [ANY] * len(after),
        out_specs=[spec for _, _, spec in outs],
        scratch_shapes=scratch,
        cost_estimate=pl.CostEstimate(flops=1, bytes_accessed=1, transcendentals=0),
        compiler_params=pltpu.CompilerParams(vmem_limit_bytes=used + room),
    )(*args, *after)


def once(value, *after):
    return pl.pallas_call(
        lambda *refs: None,
        name="once",
        out_shape=jax.ShapeDtypeStruct(value.shape, value.dtype),
        in_specs=[ANY] * (1 + len(after)),
        out_specs=ANY,
        input_output_aliases={0: 0},
        cost_estimate=pl.CostEstimate(flops=1, bytes_accessed=1, transcendentals=0),
        compiler_params=pltpu.CompilerParams(vmem_limit_bytes=1 << 18),
    )(value, *after)


def plane_local(
    tokens, cotangent, seq_ids, w_query, b_query, w_key, w_value, b_value, w_out, b_out,
    attn_gain, attn_shift, w_up, b_up, w_down, b_down, ffn_gain, ffn_shift,
):
    low, exact = jnp.bfloat16, jnp.float32
    rows, width = tokens.shape[1:]
    part = w_query.shape[0]
    half = width // 2
    inner = w_up.shape[1]
    wide = inner // 8
    keys = 8 * rows
    own = 2 * rows
    pairs = half // 128

    latest = []

    def call(body, name, ins, outs, scratch, args, after=(), **more):
        results = kernel_call(body, name, ins, outs, scratch, args, tuple(after) + tuple(latest), **more)
        if len(results) > 1 or not name.endswith("_out"):
            latest[:] = results[:1]
        return results

    (block,) = call(
        block_kernel, "block", [HBM] * 2, [((rows + 16, width), low, WHOLE)],
        [pltpu.VMEM((1, rows), jnp.int32), pltpu.SemaphoreType.DMA((2,))],
        (tokens[0], seq_ids),
    )
    block = regroup(block)
    theirs, mine = call(
        pack_kernel,
        "pack",
        [HBM] * 12,
        [((3 * part + 16, half), low, WHOLE)] * 2,
        [pltpu.VMEM((16, half), exact)]
        + [pltpu.VMEM((part,), low)] * 8
        + [pltpu.VMEM((width,), low), pltpu.SemaphoreType.DMA((15,))],
        (w_query, w_key, w_value, b_query, b_value, b_out, attn_gain, attn_shift, b_down, ffn_gain, ffn_shift, b_up),
    )
    qkv_x = swap_x(theirs)
    qkv_m = swap_c(mine)
    out_m = swap_c(w_out)
    blocks = [once(block, qkv_m, qkv_x, out_m)]
    beside_r = swap_r(blocks[0])
    blocks.append(once(swap_x(blocks[0]), beside_r))
    blocks.append(swap_c(blocks[0]))
    blocks.append(swap_c(blocks[1]))
    blocks.append(beside_r)
    blocks.append(swap_r(blocks[1]))
    blocks.append(swap_c(blocks[4]))
    blocks.append(swap_c(blocks[5]))
    qkv_mx = swap_c(qkv_x)
    up_theirs, up_mine = call(
        cut_kernel, "cut", [HBM], [((part, 4 * wide), low, WHOLE)] * 2, [pltpu.SemaphoreType.DMA((2,))],
        (w_up,), after=(blocks[3],),
    )
    up_x = swap_x(up_theirs)
    up_m = swap_c(up_mine)
    up_mx = swap_c(up_x)
    down_m = swap_c(w_down)
    (cot,) = call(
        load_kernel, "cotangent", [HBM], [((rows, width), low, WHOLE)], [pltpu.SemaphoreType.DMA((1,))],
        (cotangent[0],),
    )
    cot, cot_x = regroup(cot), regroup_x(cot)

    (
        a_low, x_all, w_all, wo_all, k3, v3, q3, mixed, lse, ids, a_own, vecs, up_bias
    ) = call(
        attend_kernel,
        "attend",
        [ANY] * 8 + [HBM] * 3 + [ANY] * 4 + [HBM, ANY],
        [
            ((own, width), low, WHOLE),
            ((keys, width), low, ANY),
            ((width, 3 * half), low, ANY),
            ((half, width), low, ANY),
            ((pairs, keys, 128), low, ANY),
            ((pairs, keys, 128), low, ANY),
            ((pairs, own, 128), low, WHOLE),
            ((own, half), low, WHOLE),
            ((8, own), exact, WHOLE),
            ((8, rows), exact, WHOLE),
            ((own, width), exact, WHOLE),
            ((8, width), exact, WHOLE),
            ((4, 8, wide), exact, WHOLE),
        ],
        [
            pltpu.VMEM((keys, width), low),
            pltpu.VMEM((8, 16, width), low),
            pltpu.VMEM((width, 3 * half), low),
            pltpu.VMEM((half, width), low),
            pltpu.VMEM((4, 16, half), low),
            pltpu.VMEM((pairs, keys, 128), low),
            pltpu.VMEM((pairs, keys, 128), low),
            pltpu.VMEM((2 * pairs, 64, keys), low),
            pltpu.VMEM((pairs, own, 128), low),
            pltpu.VMEM((2 * pairs, 64, own), exact),
            pltpu.VMEM((keys, own), exact),
            pltpu.SemaphoreType.DMA((34,)),
            pltpu.SemaphoreType.DMA((5,)),
        ],
        (*blocks, w_query, w_key, w_value, qkv_x, qkv_m, qkv_mx, mine, w_out, out_m),
        room=8 << 20,
    )
    a_got = swap_x(a_low)
    (kt,) = call(turn_kernel, "turn", [WHOLE], [((2 * pairs, 64, keys), low, WHOLE)], [], (k3,))

    inner_weights = (w_up, up_x, up_m, up_mx, w_down, down_m)
    inner_specs = [HBM, ANY, ANY, ANY, HBM, ANY]
    inner_scratch = [pltpu.VMEM((width, 4 * wide), low), pltpu.VMEM((4 * wide, width), low)]
    y_low, h_low, z, normed1, rstd1, slope, y_own = call(
        forward_kernel,
        "feedforward",
        [WHOLE, WHOLE, ANY, WHOLE, WHOLE] + inner_specs,
        [
            ((own, width), low, WHOLE),
            ((own, width), low, WHOLE),
            ((own, 4 * wide), low, WHOLE),
            ((own, width), exact, WHOLE),
            ((own, 128), exact, WHOLE),
            ((own, 4 * wide), exact, WHOLE),
            ((own, width), exact, WHOLE),
        ],
        inner_scratch
        + [pltpu.VMEM((own, width), low), pltpu.SemaphoreType.DMA((6,)), pltpu.SemaphoreType.DMA((1,))],
        (a_own, a_got, x_all, vecs, up_bias, *inner_weights),
        after=(cot, cot_x),
        room=8 << 20,
    )
    y_got = swap_x(y_low)
    dy_low, hidden, dy, sums2 = call(
        norm_back_kernel,
        "norm_back",
        [WHOLE, WHOLE, WHOLE, ANY, ANY, WHOLE],
        [
            ((own, width), low, WHOLE),
            ((rows, width), low, WHOLE),
            ((own, width), exact, WHOLE),
            ((8, width), exact, WHOLE),
        ],
        [
            pltpu.VMEM((own, width), low),
            pltpu.VMEM((own, width), low),
            pltpu.SemaphoreType.DMA((2,)),
        ],
        (y_own, y_got, normed1, cot, cot_x, vecs),
        room=6 << 20,
    )
    eighth = wide // 4
    down_send, down_keep = call(
        down_grad_kernel,
        "down_grad",
        [WHOLE] * 2,
        [((8 * eighth, width), low, WHOLE), ((8 * eighth, width), exact, WHOLE)],
        [],
        (z, dy_low),
        room=8 << 20,
    )
    down_got = swap_c(down_send)
    p_low, s_own, du, up_sums = call(
        backward_kernel,
        "feedforward_back",
        [WHOLE] * 3 + inner_specs,
        [
            ((own, width), low, WHOLE),
            ((own, width), exact, WHOLE),
            ((own, 4 * wide), low, WHOLE),
            ((4, 8, wide), exact, WHOLE),
        ],
        inner_scratch + [pltpu.SemaphoreType.DMA((6,))],
        (dy, dy_low, slope, *inner_weights),
        room=8 << 20,
    )
    p_got = swap_x(p_low)

    def fold(name, bit, keep, got):
        shape = (keep.shape[0] // 2, keep.shape[1])
        return call(
            lambda *refs: fold_kernel(bit, *refs),
            name,
            [WHOLE] * 2,
            [(shape, low, WHOLE), (shape, exact, WHOLE)],
            [],
            (keep.reshape(2, *shape), got.reshape(2, *shape)),
            room=4 << 20,
        )

    def bit_r(q, r, x, c):
        return r

    def bit_near(q, r, x, c):
        return q % 2

    def bit_far(q, r, x, c):
        return q // 2

    down_send, down_keep = fold("down_r", bit_r, down_keep, down_got)
    down_got = swap_r(down_send)
    up_send, up_keep = call(
        up_grad_kernel,
        "up_grad",
        [WHOLE] * 2,
        [((8 * eighth, width), low, WHOLE), ((8 * eighth, width), exact, WHOLE)],
        [pltpu.VMEM((width, 4 * wide), exact)],
        (h_low, du),
        room=8 << 20,
    )
    up_got = swap_c(up_send)

    dkv, dq, dr, da, sums1, qv_sums = call(
        attend_back_kernel,
        "attend_back",
        [WHOLE] * 13,
        [
            ((keys, 2 * half), low, WHOLE),
            ((own, half), low, WHOLE),
            ((rows, width), exact, WHOLE),
            ((own, width), low, WHOLE),
            ((8, width), exact, WHOLE),
            ((8, half), exact, WHOLE),
        ],
        [
            pltpu.VMEM((keys, own), exact),
            pltpu.VMEM((pairs, own, 128), low),
            pltpu.VMEM((8, own), exact),
            pltpu.VMEM((pairs, keys, 128), exact),
            pltpu.VMEM((pairs, keys, 128), exact),
            pltpu.VMEM((2 * pairs, 64, own), exact),
            pltpu.VMEM((own, width), exact),
        ],
        (s_own, p_got, normed1, rstd1, vecs, wo_all, mixed, q3, k3, v3, kt, lse, ids),
        room=8 << 20,
    )

    thin = part // 8
    count = 64 * thin

    def step(name, bit, keep, got, size):
        return call(
            lambda *refs: step_kernel(bit, *refs),
            name,
            [WHOLE] * 2,
            [((size + 16, half), low, WHOLE), ((size + 16, half), exact, WHOLE)],
            [pltpu.VMEM((2 * size + 16, half), exact)],
            (keep, got),
        )

    def join(name, *pieces):
        shape = (sum(p.shape[0] for p in pieces), pieces[0].shape[1])
        (out,) = call(join_kernel, name, [WHOLE] * len(pieces), [(shape, low, WHOLE)], [], pieces)
        return out

    up_send, up_keep = fold("up_r", bit_r, up_keep, up_got)
    up_got = swap_r(up_send)
    rest_send, rest_keep = call(
        weight_grad_kernel,
        "weight_grad",
        [WHOLE] * 9,
        [((count + 16, half), low, WHOLE), ((count + 16, half), exact, ANY)],
        [pltpu.VMEM((2, count + 16, half), exact), pltpu.SemaphoreType.DMA((1,))],
        (x_all, dkv, dq, mixed, da, sums1, sums2, qv_sums, up_sums),
        room=8 << 20,
    )
    rest_got = swap_c(rest_send)
    down_send, down_keep = fold("down_near", bit_near, down_keep, down_got)
    down_got = swap_near(down_send)
    x_send, x_keep = call(
        input_grad_kernel,
        "input_grad",
        [WHOLE] * 3,
        [((2 * own, width), low, WHOLE), ((2 * own, width), exact, WHOLE)],
        [pltpu.VMEM((keys, width), exact)],
        (dq, dkv, w_all),
        room=8 << 20,
    )
    x_got = swap_c(x_send)
    rest_send, rest_keep = step("rest_r", bit_r, rest_keep, rest_got, count // 2)
    rest_got = swap_r(rest_send)
    x_send, x_keep = fold("input_x", lambda q, r, x, c: x, x_keep, x_got)
    x_got = swap_x(x_send)
    down_send, down_keep = fold("down_far", bit_far, down_keep, down_got)
    down_got = swap_far(down_send)
    up_send, up_keep = fold("up_near", bit_near, up_keep, up_got)
    up_got = swap_near(up_send)
    x_send, x_keep = fold("input_r", bit_r, x_keep, x_got)
    x_got = swap_r(x_send)
    (down_sum,) = call(
        sum_kernel, "down_sum", [WHOLE] * 2, [((eighth, width), low, WHOLE)], [], (down_keep, down_got)
    )
    down_other = swap_far(down_sum)
    up_send, up_keep = fold("up_far", bit_far, up_keep, up_got)
    up_got = swap_far(up_send)
    rest_send, rest_keep = step("rest_near", bit_near, rest_keep, rest_got, count // 4)
    rest_got = swap_near(rest_send)
    (total,) = call(
        total_kernel, "input_sum", [WHOLE] * 3, [((rows, width), low, WHOLE)], [], (x_keep, x_got, dr)
    )
    total = regroup(total)
    down_sum = join("down_join", down_sum, down_other)
    down_other = swap_near(down_sum)
    side, base = call(
        share_kernel,
        "up_share",
        [WHOLE] * 2,
        [((eighth // 2, width), low, WHOLE)] * 2,
        [],
        (up_keep.reshape(2, eighth // 2, width), up_got.reshape(2, eighth // 2, width)),
    )
    side = swap_x(side)
    rest_send, rest_keep = step("rest_far", bit_far, rest_keep, rest_got, count // 8)
    rest_got = swap_far(rest_send)
    up_sum = join("up_join", base, side)
    up_other = swap_far(up_sum)
    down_near = join("down_join_near", down_sum, down_other)
    down_far = swap_r(down_near)
    side, base, *lines, b_up_grad = call(
        last_step_kernel,
        "rest_last",
        [WHOLE] * 2,
        [((3 * thin, half), low, WHOLE), ((5 * thin, half), low, WHOLE)]
        + [((part,), exact, WHOLE)] * 8
        + [((2 * wide,), exact, WHOLE)],
        [pltpu.VMEM((8 * thin + 16, half), exact)],
        (rest_keep, rest_got),
    )
    side = swap_x(side)
    hidden = regroup(hidden)
    up_sum = join("up_join_far", up_sum, up_other)
    up_other = swap_near(up_sum)
    rest_sum = join("rest_join", base, side)
    rest_other = swap_far(rest_sum)
    up_near = join("up_join_near", up_sum, up_other)
    up_far = swap_r(up_near)
    rest_sum = join("rest_join_far", rest_sum, rest_other)
    rest_other = swap_near(rest_sum)
    rest_near = join("rest_join_near", rest_sum, rest_other)
    rest_far = swap_r(rest_near)
    (w_down_grad,) = call(
        down_out_kernel, "down_out", [WHOLE] * 2, [((2 * wide, width), exact, WHOLE)], [], (down_near, down_far),
        room=6 << 20,
    )
    (w_up_grad,) = call(
        up_out_kernel, "up_out", [WHOLE] * 2, [((part, inner), exact, WHOLE)],
        [pltpu.VMEM((4 * eighth, width), exact)], (up_near, up_far),
        room=6 << 20,
    )
    w_query_grad, w_key_grad, w_value_grad, w_out_grad, hidden_out, tokens_grad = call(
        rest_out_kernel,
        "rest_out",
        [WHOLE] * 4,
        [((part, width), exact, WHOLE)] * 4 + [((rows, width), low, WHOLE)] * 2,
        [pltpu.VMEM((32 * thin, half), exact)],
        (rest_near, rest_far, hidden, total),
        room=6 << 20,
    )
    return (
        hidden_out[None],
        tokens_grad[None],
        w_query_grad,
        lines[0],
        w_key_grad,
        w_value_grad,
        lines[1],
        w_out_grad,
        lines[2],
        lines[3],
        lines[4],
        w_up_grad,
        b_up_grad,
        w_down_grad,
        lines[5],
        lines[6],
        lines[7],
    )


def plane_solution(mesh):
    planes, cycle = mesh.shape["shard"], mesh.shape["ctx"]
    grid = Mesh(mesh.devices.reshape(planes, cycle // planes, 2, 2), AXES)
    shard, ctx = ("x", "c"), ("q", "r")
    tokens, matrix, vector = P(shard, ctx, None), P(shard, None), P(shard)
    return jax.shard_map(
        plane_local,
        mesh=grid,
        in_specs=(
            tokens, tokens, P(shard, ctx), matrix, vector, matrix, matrix, vector, matrix, vector,
            vector, vector, matrix, vector, matrix, vector, vector, vector,
        ),
        out_specs=(
            tokens, tokens, matrix, vector, matrix, matrix, vector, matrix, vector,
            vector, vector, matrix, vector, matrix, vector, vector, vector,
        ),
        check_vma=False,
    )


def solution(mesh):
    if mesh.shape["shard"] == 4 and mesh.shape["ctx"] == 8:
        return plane_solution(mesh)
    return ring_solution(mesh)
```

```python
import math

import jax
import jax.numpy as jnp
from jax import lax
from jax.experimental import pallas as pl
from jax.experimental.pallas import tpu as pltpu
from jax.sharding import Mesh
from jax.sharding import PartitionSpec as P

HEAD_DIM = 64


ln_eps = 1e-12
masked_fill = -1e30


def from_behind(block, axis, distance):
    devices = range(lax.axis_size(axis))
    route = [((i - distance) % len(devices), i) for i in devices]
    return lax.ppermute(block, axis, route)


def matmul(left, right):
    return jnp.dot(left, right, preferred_element_type=jnp.float32)


def matmul_tn(left, right):
    return lax.dot_general(
        left, right, (((0,), (0,)), ((), ())), preferred_element_type=jnp.float32
    )


def matmul_nt(left, right):
    return lax.dot_general(
        left, right, (((1,), (1,)), ((), ())), preferred_element_type=jnp.float32
    )


def apply_layer_norm(value, gain, shift):
    mean = jnp.mean(value, axis=-1, keepdims=True)
    centered = value - mean
    rstd = lax.rsqrt(jnp.mean(centered * centered, axis=-1, keepdims=True) + ln_eps)
    normed = centered * rstd
    return (normed * gain + shift, normed, rstd)


def norm_back(grad, normed, rstd, gain):
    d_gain = jnp.sum(grad * normed, axis=0)
    d_shift = jnp.sum(grad, axis=0)
    scaled = grad * gain
    d_value = rstd * (
        scaled
        - jnp.mean(scaled, axis=-1, keepdims=True)
        - normed * jnp.mean(scaled * normed, axis=-1, keepdims=True)
    )
    return (d_value, d_gain, d_shift)


def gelu_slope(value):
    normal_cdf = 0.5 * (1.0 + lax.erf(value * (1.0 / math.sqrt(2.0))))
    density = jnp.exp(-0.5 * value * value) * (1.0 / math.sqrt(2.0 * math.pi))
    return normal_cdf + value * density


def scores_of(query, keys, q_ids, k_ids, scale):
    raw = jnp.einsum("qhd,khd->hqk", query, keys, preferred_element_type=jnp.float32) * scale
    match = (q_ids[:, None] == k_ids[None, :])[None, :, :]
    return (raw, match)


def attend(query, q_ids, keys, values, k_ids, stats, scale):
    top, total, accum = stats
    raw, match = scores_of(query, keys, q_ids, k_ids, scale)
    masked = jnp.where(match, raw, masked_fill)
    new_top = jnp.maximum(top, jnp.max(masked, axis=-1))
    weights = jnp.where(match, jnp.exp(masked - new_top[:, :, None]), 0.0)
    factor = jnp.exp(top - new_top)
    total = total * factor + jnp.sum(weights, axis=-1)
    accum = accum * factor[:, :, None] + jnp.einsum(
        "hqk,khd->hqd", weights.astype(jnp.bfloat16), values, preferred_element_type=jnp.float32
    )
    return (new_top, total, accum)


def block_grads(query, q_ids, d_out, log_total, delta, keys, values, k_ids, scale):
    raw, match = scores_of(query, keys, q_ids, k_ids, scale)
    probs = jnp.exp(jnp.where(match, raw - log_total[:, :, None], masked_fill))
    d_values = jnp.einsum(
        "hqk,qhd->khd", probs.astype(jnp.bfloat16), d_out, preferred_element_type=jnp.float32
    )
    d_probs = jnp.einsum("qhd,khd->hqk", d_out, values, preferred_element_type=jnp.float32)
    d_scores = (probs * (d_probs - delta[:, :, None])).astype(jnp.bfloat16)
    d_query = jnp.einsum("hqk,khd->qhd", d_scores, keys, preferred_element_type=jnp.float32) * scale
    d_keys = jnp.einsum("hqk,qhd->khd", d_scores, query, preferred_element_type=jnp.float32) * scale
    return (d_query, d_keys, d_values)


def ring_local(
    tokens,
    cotangent,
    seq_ids,
    w_query,
    b_query,
    w_key,
    w_value,
    b_value,
    w_out,
    b_out,
    attn_gain,
    attn_shift,
    w_up,
    b_up,
    w_down,
    b_down,
    ffn_gain,
    ffn_shift,
):
    cycle = lax.axis_size("ctx")
    tok_rows = tokens.shape[1]
    width = tokens.shape[2]
    heads = width // HEAD_DIM
    scale = 1.0 / math.sqrt(HEAD_DIM)
    share = tok_rows // cycle
    got_tokens, got_grads, got_ids = (
        lax.all_to_all(
            tokens[0].reshape(share, cycle, width), "ctx", split_axis=1, concat_axis=1, tiled=True
        ),
        lax.all_to_all(
            cotangent[0].reshape(share, cycle, width),
            "ctx",
            split_axis=1,
            concat_axis=1,
            tiled=True,
        ),
        lax.all_to_all(
            seq_ids[0].reshape(share, cycle), "ctx", split_axis=1, concat_axis=1, tiled=True
        ),
    )
    x_local = got_tokens.reshape(tok_rows, width)
    local_gradient = got_grads.reshape(tok_rows, width).astype(jnp.float32)
    local_ids = got_ids.reshape(tok_rows)
    (
        query_mat,
        query_bias,
        key_mat,
        value_mat,
        value_bias,
        out_mat,
        out_bias,
        attention_norm_gain,
        first_shift,
        up_mat,
        up_bias,
        down_mat,
        down_bias,
        feedforward_norm_gain,
        second_shift,
    ) = (
        lax.all_gather(w_query, "shard", axis=0, tiled=True),
        lax.all_gather(b_query, "shard", axis=0, tiled=True),
        lax.all_gather(w_key, "shard", axis=0, tiled=True),
        lax.all_gather(w_value, "shard", axis=0, tiled=True),
        lax.all_gather(b_value, "shard", axis=0, tiled=True),
        lax.all_gather(w_out, "shard", axis=0, tiled=True),
        lax.all_gather(b_out, "shard", axis=0, tiled=True),
        lax.all_gather(attn_gain, "shard", axis=0, tiled=True),
        lax.all_gather(attn_shift, "shard", axis=0, tiled=True),
        lax.all_gather(w_up, "shard", axis=0, tiled=True),
        lax.all_gather(b_up, "shard", axis=0, tiled=True),
        lax.all_gather(w_down, "shard", axis=0, tiled=True),
        lax.all_gather(b_down, "shard", axis=0, tiled=True),
        lax.all_gather(ffn_gain, "shard", axis=0, tiled=True),
        lax.all_gather(ffn_shift, "shard", axis=0, tiled=True),
    )
    query = (matmul(x_local, query_mat) + query_bias.astype(jnp.float32)).astype(jnp.bfloat16)
    keys = matmul(x_local, key_mat).astype(jnp.bfloat16)
    values = (matmul(x_local, value_mat) + value_bias.astype(jnp.float32)).astype(jnp.bfloat16)
    q_heads = query.reshape(tok_rows, heads, HEAD_DIM)
    start_stats = (
        jnp.full((heads, tok_rows), masked_fill, jnp.float32),
        jnp.zeros((heads, tok_rows), jnp.float32),
        jnp.zeros((heads, tok_rows, HEAD_DIM), jnp.float32),
    )

    def forward_step(step, carry):
        block, stats = carry
        stats = attend(
            q_heads,
            local_ids,
            block[0].reshape(tok_rows, heads, HEAD_DIM),
            block[1].reshape(tok_rows, heads, HEAD_DIM),
            block[2],
            stats,
            scale,
        )
        block = from_behind((block[0], block[1], block[2]), "ctx", 1)
        return (block, stats)

    block, stats = lax.fori_loop(
        0, cycle - 1, forward_step, ((keys, values, local_ids), start_stats)
    )
    top, total, accum = attend(
        q_heads,
        local_ids,
        block[0].reshape(tok_rows, heads, HEAD_DIM),
        block[1].reshape(tok_rows, heads, HEAD_DIM),
        block[2],
        stats,
        scale,
    )
    attn_out = (
        (accum / total[:, :, None]).transpose(1, 0, 2).reshape(tok_rows, width).astype(jnp.bfloat16)
    )
    log_total = top + jnp.log(total)
    attn_proj = matmul(attn_out, out_mat) + out_bias.astype(jnp.float32)
    first_sum = x_local.astype(jnp.float32) + attn_proj
    first_normalized_rows, first_centered_scaled, first_inverse_deviation = apply_layer_norm(
        first_sum, attention_norm_gain.astype(jnp.float32), first_shift.astype(jnp.float32)
    )
    normed_low = first_normalized_rows.astype(jnp.bfloat16)
    up_pre = matmul(normed_low, up_mat) + up_bias.astype(jnp.float32)
    up_act = jax.nn.gelu(up_pre, approximate=False).astype(jnp.bfloat16)
    down_pre = matmul(up_act, down_mat) + down_bias.astype(jnp.float32)
    layer_output, second_centered_scaled, second_inverse_deviation = apply_layer_norm(
        first_normalized_rows + down_pre,
        feedforward_norm_gain.astype(jnp.float32),
        second_shift.astype(jnp.float32),
    )
    (
        query_mat,
        key_mat,
        value_mat,
        out_mat,
        attention_norm_gain,
        up_mat,
        down_mat,
        feedforward_norm_gain,
    ) = (
        lax.all_gather(w_query, "shard", axis=0, tiled=True),
        lax.all_gather(w_key, "shard", axis=0, tiled=True),
        lax.all_gather(w_value, "shard", axis=0, tiled=True),
        lax.all_gather(w_out, "shard", axis=0, tiled=True),
        lax.all_gather(attn_gain, "shard", axis=0, tiled=True),
        lax.all_gather(w_up, "shard", axis=0, tiled=True),
        lax.all_gather(w_down, "shard", axis=0, tiled=True),
        lax.all_gather(ffn_gain, "shard", axis=0, tiled=True),
    )
    grad_two, d_second_gain, d_second_shift = norm_back(
        local_gradient,
        second_centered_scaled,
        second_inverse_deviation,
        feedforward_norm_gain.astype(jnp.float32),
    )
    grad_down = grad_two.astype(jnp.bfloat16)
    d_down_bias = jnp.sum(grad_down, axis=0, dtype=jnp.float32)
    d_down_mat = matmul_tn(up_act, grad_down)
    grad_up = (matmul_nt(grad_down, down_mat) * gelu_slope(up_pre)).astype(jnp.bfloat16)
    d_up_bias = jnp.sum(grad_up, axis=0, dtype=jnp.float32)
    d_up_mat = matmul_tn(normed_low, grad_up)
    first_norm_gradient = grad_two + matmul_nt(grad_up, up_mat)
    grad_first, d_first_gain, d_first_shift = norm_back(
        first_norm_gradient,
        first_centered_scaled,
        first_inverse_deviation,
        attention_norm_gain.astype(jnp.float32),
    )
    grad_proj = grad_first.astype(jnp.bfloat16)
    d_out_bias = jnp.sum(grad_proj, axis=0, dtype=jnp.float32)
    d_out_mat = matmul_tn(attn_out, grad_proj)
    grad_attn = matmul_nt(grad_proj, out_mat).astype(jnp.bfloat16)
    grad_heads = grad_attn.reshape(tok_rows, heads, HEAD_DIM)
    delta = jnp.einsum(
        "qhd,qhd->hq",
        grad_heads,
        attn_out.reshape(tok_rows, heads, HEAD_DIM),
        preferred_element_type=jnp.float32,
    )
    zero_rows = jnp.zeros((tok_rows, width), jnp.float32)

    def key_step(step, carry):
        block, sums, acc_query = carry
        d_query, d_keys, d_values = block_grads(
            q_heads,
            local_ids,
            grad_heads,
            log_total,
            delta,
            block[0].reshape(tok_rows, heads, HEAD_DIM),
            block[1].reshape(tok_rows, heads, HEAD_DIM),
            block[2],
            scale,
        )
        sums = (
            sums[0] + d_keys.reshape(tok_rows, width),
            sums[1] + d_values.reshape(tok_rows, width),
        )
        block = from_behind((block[0], block[1], block[2]), "ctx", 1)
        sums = (
            from_behind(sums[0].astype(jnp.bfloat16), "ctx", 1).astype(jnp.float32),
            from_behind(sums[1].astype(jnp.bfloat16), "ctx", 1).astype(jnp.float32),
        )
        return (block, sums, acc_query + d_query.reshape(tok_rows, width))

    block, sums, d_query_sum = lax.fori_loop(
        0, cycle, key_step, ((keys, values, local_ids), (zero_rows, zero_rows), zero_rows)
    )
    d_keys_sum, d_values_sum = sums
    grad_query = d_query_sum.astype(jnp.bfloat16)
    grad_keys = d_keys_sum.astype(jnp.bfloat16)
    grad_values = d_values_sum.astype(jnp.bfloat16)
    d_query_bias = jnp.sum(grad_query, axis=0, dtype=jnp.float32)
    d_value_bias = jnp.sum(grad_values, axis=0, dtype=jnp.float32)
    d_query_mat = matmul_tn(x_local, grad_query)
    d_key_mat = matmul_tn(x_local, grad_keys)
    d_value_mat = matmul_tn(x_local, grad_values)
    grad_input = (
        grad_first
        + matmul_nt(grad_query, query_mat)
        + matmul_nt(grad_keys, key_mat)
        + matmul_nt(grad_values, value_mat)
    )
    home_hidden, home_grad = (
        lax.all_to_all(
            layer_output.astype(jnp.bfloat16).reshape(share, cycle, width),
            "ctx",
            split_axis=1,
            concat_axis=1,
            tiled=True,
        ),
        lax.all_to_all(
            grad_input.astype(jnp.bfloat16).reshape(share, cycle, width),
            "ctx",
            split_axis=1,
            concat_axis=1,
            tiled=True,
        ),
    )
    hidden_out = home_hidden.reshape(tok_rows, width)[None]
    tokens_grad = home_grad.reshape(tok_rows, width)[None]
    shares = (
        lax.psum_scatter(
            d_query_mat.astype(jnp.bfloat16), "shard", scatter_dimension=0, tiled=True
        ).astype(jnp.float32),
        lax.psum_scatter(
            d_query_bias.astype(jnp.bfloat16), "shard", scatter_dimension=0, tiled=True
        ).astype(jnp.float32),
        lax.psum_scatter(
            d_key_mat.astype(jnp.bfloat16), "shard", scatter_dimension=0, tiled=True
        ).astype(jnp.float32),
        lax.psum_scatter(
            d_value_mat.astype(jnp.bfloat16), "shard", scatter_dimension=0, tiled=True
        ).astype(jnp.float32),
        lax.psum_scatter(
            d_value_bias.astype(jnp.bfloat16), "shard", scatter_dimension=0, tiled=True
        ).astype(jnp.float32),
        lax.psum_scatter(
            d_out_mat.astype(jnp.bfloat16), "shard", scatter_dimension=0, tiled=True
        ).astype(jnp.float32),
        lax.psum_scatter(
            d_out_bias.astype(jnp.bfloat16), "shard", scatter_dimension=0, tiled=True
        ).astype(jnp.float32),
        lax.psum_scatter(
            d_first_gain.astype(jnp.bfloat16), "shard", scatter_dimension=0, tiled=True
        ).astype(jnp.float32),
        lax.psum_scatter(
            d_first_shift.astype(jnp.bfloat16), "shard", scatter_dimension=0, tiled=True
        ).astype(jnp.float32),
        lax.psum_scatter(
            d_up_mat.astype(jnp.bfloat16), "shard", scatter_dimension=0, tiled=True
        ).astype(jnp.float32),
        lax.psum_scatter(
            d_up_bias.astype(jnp.bfloat16), "shard", scatter_dimension=0, tiled=True
        ).astype(jnp.float32),
        lax.psum_scatter(
            d_down_mat.astype(jnp.bfloat16), "shard", scatter_dimension=0, tiled=True
        ).astype(jnp.float32),
        lax.psum_scatter(
            d_down_bias.astype(jnp.bfloat16), "shard", scatter_dimension=0, tiled=True
        ).astype(jnp.float32),
        lax.psum_scatter(
            d_second_gain.astype(jnp.bfloat16), "shard", scatter_dimension=0, tiled=True
        ).astype(jnp.float32),
        lax.psum_scatter(
            d_second_shift.astype(jnp.bfloat16), "shard", scatter_dimension=0, tiled=True
        ).astype(jnp.float32),
    )
    totals = lax.psum(
        (
            shares[0],
            shares[1],
            shares[2],
            shares[3],
            shares[4],
            shares[5],
            shares[6],
            shares[7],
            shares[8],
            shares[9],
            shares[10],
            shares[11],
            shares[12],
            shares[13],
            shares[14],
        ),
        "ctx",
    )
    return (hidden_out, tokens_grad) + tuple(totals)


def ring_solution(mesh):
    return jax.shard_map(
        ring_local,
        mesh=mesh,
        in_specs=(
            P("shard", "ctx", None),
            P("shard", "ctx", None),
            P("shard", "ctx"),
            P("shard", None),
            P("shard"),
            P("shard", None),
            P("shard", None),
            P("shard"),
            P("shard", None),
            P("shard"),
            P("shard"),
            P("shard"),
            P("shard", None),
            P("shard"),
            P("shard", None),
            P("shard"),
            P("shard"),
            P("shard"),
        ),
        out_specs=(
            P("shard", "ctx", None),
            P("shard", "ctx", None),
            P("shard", None),
            P("shard"),
            P("shard", None),
            P("shard", None),
            P("shard"),
            P("shard", None),
            P("shard"),
            P("shard"),
            P("shard"),
            P("shard", None),
            P("shard"),
            P("shard", None),
            P("shard"),
            P("shard"),
            P("shard"),
        ),
        check_vma=False,
    )


AXES = ("q", "r", "x", "c")
ANY = pl.BlockSpec(memory_space=pl.ANY)
WHOLE = pl.BlockSpec(memory_space=pltpu.VMEM)
HBM = pl.BlockSpec(memory_space=pltpu.HBM)


def moved(block, move):
    sizes = [lax.axis_size(a) for a in AXES]

    def number(spot):
        place = 0
        for size, at in zip(sizes, spot):
            place = place * size + at
        return place

    spots = [
        (q, r, x, c)
        for q in range(sizes[0])
        for r in range(sizes[1])
        for x in range(sizes[2])
        for c in range(sizes[3])
    ]
    return lax.ppermute(block, AXES, [(number(s), number(move(*s))) for s in spots])


def swap_x(block):
    return moved(block, lambda q, r, x, c: (q, r, 1 - x, c))


def swap_c(block):
    return moved(block, lambda q, r, x, c: (q, r, x, 1 - c))


def swap_r(block):
    return moved(block, lambda q, r, x, c: (q, r ^ 1, x, c))


def swap_rc(block):
    return moved(block, lambda q, r, x, c: (q, r ^ 1, x, 1 - c))


def swap_near(block):
    return moved(block, lambda q, r, x, c: (q ^ 1, r, x, c))


def swap_far(block):
    return moved(block, lambda q, r, x, c: (q ^ 2, r, x, c))


def regroup(block):
    return moved(block, lambda q, r, x, c: (2 * c + x, r, q & 1, q >> 1))


def regroup_x(block):
    return moved(block, lambda q, r, x, c: (2 * c + x, r, 1 - (q & 1), q >> 1))


def swap_xc(block):
    return moved(block, lambda q, r, x, c: (q, r, 1 - x, 1 - c))


def beside(mine, got):
    return jnp.concatenate([mine, got])


def dot(left, right):
    return jnp.dot(left, right, preferred_element_type=jnp.float32)


def dot_nt(left, right):
    return lax.dot_general(
        left, right, (((1,), (1,)), ((), ())), preferred_element_type=jnp.float32
    )


def dot_tn(left, right):
    return lax.dot_general(
        left, right, (((0,), (0,)), ((), ())), preferred_element_type=jnp.float32
    )


class Copies:
    def __init__(self, sems):
        self.sems = sems
        self.count = 0
        self.held = []

    def start(self, source, target):
        copy = pltpu.make_async_copy(source, target, self.sems.at[self.count])
        copy.start()
        self.count += 1
        self.held.append(copy)

    def wait(self):
        for copy in self.held:
            copy.wait()
        self.held = []


def spot():
    return tuple(lax.axis_index(a) for a in AXES)


def fill_mask(ids, mask, own):
    blocks, rows = ids.shape
    mine = jnp.concatenate([ids[pl.ds(own, 1), :], ids[pl.ds(own + 1, 1), :]], axis=1)
    across = jnp.transpose(ids[...])
    for b in range(blocks):
        mask[rows * b : rows * (b + 1), :] = jnp.where(across[:, b : b + 1] == mine, 0.0, masked_fill)


def block_kernel(tokens, ids, block, line, sems):
    rows = tokens.shape[0]
    copies = Copies(sems)
    copies.start(tokens, block.at[pl.ds(0, rows)])
    copies.start(ids, line)
    block[rows:, :] = jnp.zeros((16, block.shape[1]), block.dtype)
    copies.wait()
    block[rows:, 0:rows] = jnp.broadcast_to(line[...].astype(jnp.float32), (16, rows)).astype(block.dtype)


def pack_kernel(w_q, w_k, w_v, *refs):
    vectors, b_up, theirs, mine = refs[:8], refs[8], refs[9], refs[10]
    lines, thin, thick, sems = refs[11], refs[12:20], refs[20], refs[21]
    q, r, x, c = spot()
    part, width = w_q.shape
    half = width // 2
    copies = Copies(sems)
    for t, w in enumerate((w_q, w_k, w_v)):
        rows = pl.ds(part * t, part)
        copies.start(w.at[:, pl.ds(pl.multiple_of(half * x, 128), half)], mine.at[rows])
        copies.start(w.at[:, pl.ds(pl.multiple_of(half * (1 - x), 128), half)], theirs.at[rows])
    for vector, held in zip(vectors, thin):
        copies.start(vector, held)
    copies.start(b_up, thick)
    lines[...] = jnp.zeros_like(lines)
    copies.wait()
    for i, vector in enumerate(thin):
        line = vector[...].astype(jnp.float32).reshape(1, part)
        none = jnp.zeros_like(line)
        first = jnp.concatenate([line, none], axis=1)
        second = jnp.concatenate([none, line], axis=1)
        lines[i : i + 1, :] = jnp.where(c == 0, first, second)
    wide = thick[...].astype(jnp.float32).reshape(1, width)
    lines[pl.ds(8 + 2 * c, 1), :] = wide[:, 0:half]
    lines[pl.ds(9 + 2 * c, 1), :] = wide[:, half:]
    low = lines[...].astype(jnp.bfloat16)
    mine[3 * part :, :] = low
    theirs[3 * part :, :] = low


def cut_kernel(w, theirs, mine, sems):
    q, r, x, c = spot()
    count = theirs.shape[1]
    copies = Copies(sems)
    copies.start(w.at[:, pl.ds(pl.multiple_of(count * (1 - x), 128), count)], theirs)
    copies.start(w.at[:, pl.ds(pl.multiple_of(count * x, 128), count)], mine)
    copies.wait()


def load_kernel(block, out, sems):
    copies = Copies(sems)
    copies.start(block, out)
    copies.wait()


def turn_kernel(keys, out):
    for p in range(keys.shape[0]):
        out[2 * p : 2 * p + 2] = jnp.transpose(keys[p]).reshape(2, 64, keys.shape[1])


def project_kernel(
    b0, b1, b2, b3, w_q, w_k, w_v, w_x, w_m, w_mx, own_lines,
    kv_out, q_out, w, vecs, up_bias, xs, sems,
):
    q, r, x, c = spot()
    rows = xs.shape[0] // 4
    part = w.shape[0] // 4
    half = w.shape[1] // 3
    me, shard = 2 * c + x, 2 * x + c
    columns = pl.ds(pl.multiple_of(half * x, 128), half)
    ins = Copies(sems)
    for t, own in enumerate((w_q, w_k, w_v)):
        at = pl.ds(pl.multiple_of(part * shard, 64), part)
        ins.start(own.at[:, columns], w.at[at, pl.ds(half * t, half)])
    for j, block in enumerate((b0, b1, b2, b3)):
        xs[pl.ds(pl.multiple_of(rows * (me ^ j), rows), rows), :] = block[0:rows, :]
    for flip, piece in ((2, w_x), (1, w_m), (3, w_mx)):
        at = pl.ds(pl.multiple_of(part * (shard ^ flip), 64), part)
        for t in range(3):
            w[at, half * t : half * (t + 1)] = piece[part * t : part * (t + 1), :]
    mine, other = (
        a[3 * part :, :].astype(jnp.float32) + b[3 * part :, :].astype(jnp.float32)
        for a, b in ((own_lines, w_m), (w_x, w_mx))
    )
    vecs[:, columns] = mine[0:8, :]
    vecs[:, pl.ds(pl.multiple_of(half * (1 - x), 128), half)] = other[0:8, :]
    for i in range(4):
        up_bias[i] = jnp.broadcast_to(mine[8 + i : 9 + i, :], (8, half))
    ins.wait()
    kv_out[:, 0:half] = dot(xs[...], w[:, half : 2 * half]).astype(jnp.bfloat16)
    kv_out[:, half:] = (dot(xs[...], w[:, 2 * half :]) + mine[1:2, :]).astype(jnp.bfloat16)
    own = pl.ds(pl.multiple_of(2 * rows * c, rows), 2 * rows)
    q_out[...] = (dot(xs[own, :], w[:, 0:half]) + mine[0:1, :]).astype(jnp.bfloat16)


def attend_kernel(
    b0, b1, b2, b3, b4, b5, b6, b7, kv_own, q_own, w, vecs, w_o, w_om,
    a_low, xs, wo, k3, v3, q3, o_out, lse_out, ids_out, a_out,
    vt, ot, mask, sems,
):
    q, r, x, c = spot()
    rows = xs.shape[0] // 8
    half = wo.shape[0]
    part = half // 2
    me = 4 * r + 2 * c + x
    ins = Copies(sems)
    ins.start(w_o, wo.at[pl.ds(pl.multiple_of(part * c, 64), part)])
    wo[pl.ds(pl.multiple_of(part * (1 - c), 64), part), :] = w_om[...]
    for j, block in enumerate((b0, b1, b2, b3, b4, b5, b6, b7)):
        at = me ^ j
        xs[pl.ds(pl.multiple_of(rows * at, rows), rows), :] = block[0:rows, :]
        ids_out[pl.ds(at, 1), :] = block[rows : rows + 16, 0:rows].astype(jnp.float32)[0:1, :]
    fill_mask(ids_out, mask, 4 * r + 2 * c)
    rest = pl.ds(pl.multiple_of(4 * rows * (1 - r), rows), 4 * rows)
    here = pl.ds(pl.multiple_of(4 * rows * r, rows), 4 * rows)
    bias = vecs[1:2, pl.ds(pl.multiple_of(half * x, 128), half)]
    keyed = dot(xs[rest, :], w[:, half : 2 * half]).astype(jnp.bfloat16)
    valued = (dot(xs[rest, :], w[:, 2 * half :]) + bias).astype(jnp.bfloat16)
    pairs = half // 128
    for p in range(pairs):
        at = slice(128 * p, 128 * (p + 1))
        k3[p, here, :] = kv_own[:, at]
        k3[p, rest, :] = keyed[:, at]
        v3[p, here, :] = kv_own[:, half + 128 * p : half + 128 * (p + 1)]
        v3[p, rest, :] = valued[:, at]
        q3[p] = q_own[:, at]
        vt[2 * p : 2 * p + 2] = jnp.transpose(v3[p]).reshape(2, 64, 8 * rows)
    lane = lax.broadcasted_iota(jnp.int32, (2 * rows, 128), 1) // 64

    def head(h, carry):
        query = jnp.where(lane == h % 2, q3[h // 2], 0) * 0.125
        scores = dot_nt(k3[h // 2], query.astype(jnp.bfloat16)) + mask[...]
        top = jnp.max(scores, axis=0, keepdims=True)
        weights = jnp.exp(scores - top)
        total = jnp.sum(weights, axis=0, keepdims=True)
        ot[h] = dot(vt[h], weights.astype(jnp.bfloat16)) / total
        lse_out[pl.ds(h, 1), :] = top + jnp.log(total)
        return carry

    lax.fori_loop(0, 2 * pairs, head, 0)
    mixed = jnp.transpose(ot[...].reshape(half, 2 * rows)).astype(jnp.bfloat16)
    o_out[...] = mixed
    ins.wait()
    partial = dot(mixed, wo[...])
    a_out[...] = partial
    a_low[...] = partial.astype(jnp.bfloat16)


def inner_kernel(u_own, u_x, u_m, u_mx, d_own, d_m, up, down, sems):
    q, r, x, c = spot()
    part = up.shape[0] // 4
    count = up.shape[1]
    shard = 2 * x + c
    ins = Copies(sems)
    own = u_own.at[:, pl.ds(pl.multiple_of(count * x, 128), count)]
    ins.start(own, up.at[pl.ds(pl.multiple_of(part * shard, 64), part)])
    ins.start(d_own, down.at[pl.ds(pl.multiple_of(count // 2 * c, 128), count // 2)])
    for flip, piece in ((2, u_x), (1, u_m), (3, u_mx)):
        up[pl.ds(pl.multiple_of(part * (shard ^ flip), 64), part), :] = piece[...]
    down[pl.ds(pl.multiple_of(count // 2 * (1 - c), 128), count // 2), :] = d_m[...]
    ins.wait()


def norm_of(value):
    mean = jnp.mean(value, axis=-1, keepdims=True)
    centered = value - mean
    rstd = lax.rsqrt(jnp.mean(centered * centered, axis=-1, keepdims=True) + ln_eps)
    return centered * rstd, rstd


def norm_pull(scaled, normed, rstd):
    return rstd * (
        scaled
        - jnp.mean(scaled, axis=-1, keepdims=True)
        - normed * jnp.mean(scaled * normed, axis=-1, keepdims=True)
    )


def forward_kernel(
    a_own, a_got, xs, vecs, b_up, up, down,
    y_low, y_more, h_out, z, n_out, r_out, slope, y_out,
):
    q, r, x, c = spot()
    rows = a_own.shape[0]
    x_own = xs[pl.ds(pl.multiple_of(rows * (2 * r + c), rows), rows), :]
    total = x_own.astype(jnp.float32) + (a_own[...] + a_got[...].astype(jnp.float32) + vecs[2:3, :])
    normed, rstd = norm_of(total)
    n_out[...] = normed
    r_out[...] = jnp.broadcast_to(rstd, r_out.shape)
    low = (normed * vecs[3:4, :] + vecs[4:5, :]).astype(jnp.bfloat16)
    h_out[...] = low
    wide = up.shape[1] // 4
    for j in range(4):
        at = slice(wide * j, wide * (j + 1))
        pre = dot(low, up[:, at]) + b_up[j, 0:1, :]
        cdf = 0.5 * (1.0 + lax.erf(pre * (1.0 / math.sqrt(2.0))))
        density = jnp.exp(-0.5 * pre * pre) * (1.0 / math.sqrt(2.0 * math.pi))
        z[:, at] = (pre * cdf).astype(jnp.bfloat16)
        slope[:, at] = cdf + pre * density
    result = dot(z[...], down[...])
    y_out[...] = result
    rows = y_low.shape[0]
    y_low[...] = result[0:rows, :].astype(jnp.bfloat16)
    y_more[...] = result[rows:, :].astype(jnp.bfloat16)


def norm_back_kernel(
    y_own, y_got, y_rest, normed1, g_own, g_x, vecs, low_out, hid_out, dy_out, sums, grad, hid,
):
    q, r, x, c = spot()
    rows = grad.shape[0] // 2
    grad[pl.ds(pl.multiple_of(rows * x, rows), rows), :] = g_own[...]
    grad[pl.ds(pl.multiple_of(rows * (1 - x), rows), rows), :] = g_x[...]
    got = jnp.concatenate([y_got[...], y_rest[...]]).astype(jnp.float32)
    h1 = normed1[...] * vecs[3:4, :] + vecs[4:5, :]
    normed, rstd = norm_of(h1 + (y_own[...] + got + vecs[5:6, :]))
    hid[...] = (normed * vecs[6:7, :] + vecs[7:8, :]).astype(jnp.bfloat16)
    hid_out[...] = hid[pl.ds(pl.multiple_of(rows * x, rows), rows), :]
    cot = grad[...].astype(jnp.float32)
    dy = norm_pull(cot * vecs[6:7, :], normed, rstd)
    low = dy.astype(jnp.bfloat16)
    dy_out[...] = dy
    low_out[...] = low
    sums[...] = jnp.zeros_like(sums)
    sums[0:1, :] = jnp.sum(low.astype(jnp.float32), axis=0, keepdims=True)
    sums[1:2, :] = jnp.sum(cot * normed, axis=0, keepdims=True)
    sums[2:3, :] = jnp.sum(cot, axis=0, keepdims=True)


def backward_kernel(dy, dy_low, slope, up, down, p_low, s_out, du_out, up_sums):
    low = dy_low[...]
    wide = up.shape[1] // 4
    for j in range(4):
        at = slice(wide * j, wide * (j + 1))
        du = (dot_nt(low, down[at, :]) * slope[:, at]).astype(jnp.bfloat16)
        du_out[:, at] = du
        total = jnp.sum(du.astype(jnp.float32), axis=0, keepdims=True)
        up_sums[j] = jnp.broadcast_to(total, up_sums.shape[1:])
    result = dot_nt(du_out[...], up[...])
    s_out[...] = dy[...] + result
    p_low[...] = result.astype(jnp.bfloat16)


def attend_back_kernel(
    s_own, p_got, normed1, rstd1, vecs, wo, mixed, q3, k3, v3, kt, lse, ids,
    dkv_out, dq_out, dr_out, da_out, sums, qv_sums,
    mask, do3, delta, dk, dv, dqt, whole,
):
    q, r, x, c = spot()
    rows = dr_out.shape[0]
    pairs = q3.shape[0]
    half = 128 * pairs
    fill_mask(ids, mask, 4 * r + 2 * c)
    dh = s_own[...] + p_got[...].astype(jnp.float32)
    normed = normed1[...]
    dr = norm_pull(dh * vecs[3:4, :], normed, rstd1[:, 0:1])
    whole[...] = dr
    dr_out[...] = whole[pl.ds(pl.multiple_of(rows * x, rows), rows), :]
    low = dr.astype(jnp.bfloat16)
    da_out[...] = low
    sums[...] = jnp.zeros_like(sums)
    sums[0:1, :] = jnp.sum(low.astype(jnp.float32), axis=0, keepdims=True)
    sums[1:2, :] = jnp.sum(dh * normed, axis=0, keepdims=True)
    sums[2:3, :] = jnp.sum(dh, axis=0, keepdims=True)
    d_o = dot_nt(low, wo[...]).astype(jnp.bfloat16)
    products = jnp.transpose(d_o.astype(jnp.float32) * mixed[...].astype(jnp.float32))
    for h in range(2 * pairs):
        delta[h : h + 1, :] = jnp.sum(products[64 * h : 64 * (h + 1), :], axis=0, keepdims=True)
    for p in range(pairs):
        do3[p] = d_o[:, 128 * p : 128 * (p + 1)]
    dk[...] = jnp.zeros_like(dk)
    dv[...] = jnp.zeros_like(dv)
    lane = lax.broadcasted_iota(jnp.int32, (2 * rows, 128), 1) // 64

    def head(h, carry):
        p = h // 2
        here = lane == h % 2
        query = (jnp.where(here, q3[p], 0) * 0.125).astype(jnp.bfloat16)
        d_here = jnp.where(here, do3[p], 0).astype(jnp.bfloat16)
        probs = jnp.exp(dot_nt(k3[p], query) + mask[...] - lse[pl.ds(h, 1), :])
        d_probs = dot_nt(v3[p], d_here)
        d_scores = (probs * (d_probs - delta[pl.ds(h, 1), :])).astype(jnp.bfloat16)
        dv[p] += dot(probs.astype(jnp.bfloat16), d_here)
        dk[p] += dot(d_scores, query)
        dqt[h] = dot(kt[h], d_scores)
        return carry

    lax.fori_loop(0, 2 * pairs, head, 0)
    dq = (jnp.transpose(dqt[...].reshape(half, 2 * rows)) * 0.125).astype(jnp.bfloat16)
    dq_out[...] = dq
    qv_sums[...] = jnp.zeros_like(qv_sums)
    qv_sums[0:1, :] = jnp.sum(dq.astype(jnp.float32), axis=0, keepdims=True)
    for p in range(pairs):
        at = slice(128 * p, 128 * (p + 1))
        dkv_out[:, at] = dk[p].astype(jnp.bfloat16)
        value = dv[p].astype(jnp.bfloat16)
        dkv_out[:, half + 128 * p : half + 128 * (p + 1)] = value
        qv_sums[1:2, at] = jnp.sum(value.astype(jnp.float32), axis=0, keepdims=True)


def input_grad_kernel(dq, dkv, w, *refs):
    sends, (keep, whole) = refs[:2], refs[2:]
    q, r, x, c = spot()
    half = dq.shape[1]
    rows = dq.shape[0] // 2
    whole[...] = dot_nt(dkv[...], w[:, half:])
    own = pl.ds(pl.multiple_of(rows * (4 * r + 2 * c), rows), 2 * rows)
    whole[own, :] += dot_nt(dq[...], w[:, 0:half])
    for b in range(2):
        for i in range(2):
            to = slice(2 * rows * b + rows * i, 2 * rows * b + rows * (i + 1))
            mine = pl.ds(pl.multiple_of(rows * (4 * i + 2 * c + b), rows), rows)
            keep[to, :] = whole[mine, :]
            theirs = pl.ds(pl.multiple_of(rows * (4 * i + 2 * (1 - c) + b), rows), rows)
            sends[b][rows * i : rows * (i + 1), :] = whole[theirs, :].astype(jnp.bfloat16)


def input_x_kernel(keep, got0, got1, send, kept):
    q, r, x, c = spot()
    half = send.shape[0]
    for side, got in enumerate((got0, got1)):
        total = keep[half * side : half * (side + 1), :] + got[...].astype(jnp.float32)

        @pl.when(x == side)
        def _():
            kept[...] = total

        @pl.when(x != side)
        def _():
            send[...] = total.astype(jnp.bfloat16)


def octants():
    for at in range(8):
        r, q0, q1 = at >> 2, at >> 1 & 1, at & 1
        yield 4 * r + 2 * q0 + 1 * q1, 1 * r + 4 * q0 + 2 * q1, 4 * r + 2 * q1 + q0


def down_grad_kernel(z, dy, send, keep):
    q, r, x, c = spot()
    half = z.shape[1] // 2
    rows = half // 8
    for side, out in ((1 - c, send), (c, keep)):
        part = dot_tn(z[:, pl.ds(pl.multiple_of(half * side, 128), half)], dy[...])
        for at, _, within in octants():
            block = part[rows * within : rows * (within + 1), :]
            out[rows * at : rows * (at + 1), :] = block.astype(out.dtype)


def up_grad_kernel(h, du, send, keep, whole):
    q, r, x, c = spot()
    width = h.shape[1]
    thin = width // 32
    whole[...] = dot_tn(h[...], du[...])
    for side, out in ((1 - c, send), (c, keep)):
        for _, at, within in octants():
            pieces = []
            for xx in range(2):
                first = 8 * thin * (2 * xx + side) + thin * within
                rows = pl.ds(pl.multiple_of(first, 8), thin)
                pieces += [whole[rows, 0:width], whole[rows, width:]]
            block = jnp.concatenate(pieces)
            out[4 * thin * at : 4 * thin * (at + 1), :] = block.astype(out.dtype)


def join_kernel(*refs):
    out, at = refs[-1], 0
    for ref in refs[:-1]:
        count = ref.shape[0]
        out[at : at + count, :] = ref[...]
        at += count


def fold_kernel(bit, keep, got, send, kept):
    at = bit(*spot())
    send[...] = (keep[1 - at] + got[1 - at].astype(jnp.float32)).astype(send.dtype)
    kept[...] = keep[at] + got[at].astype(jnp.float32)


def copy_kernel(block, out):
    out[...] = block[...]


def sum_kernel(keep, got, out):
    out[...] = (keep[...] + got[...].astype(jnp.float32)).astype(out.dtype)


def total_kernel(keep, got, more, out):
    out[...] = (keep[...] + got[...].astype(jnp.float32) + more[...]).astype(out.dtype)


def share_kernel(keep, got, side, base):
    q, r, x, c = spot()
    side[...] = (keep[1 - x] + got[1 - x].astype(jnp.float32)).astype(side.dtype)
    base[...] = (keep[x] + got[x].astype(jnp.float32)).astype(base.dtype)


def weight_grad_kernel(
    xs, dkv, dq, mixed, da, sums1, sums2, qv_sums, up_sums, *refs
):
    sends, (keep, packed) = refs[:-2], refs[-2:]
    q, r, x, c = spot()
    width = xs.shape[1]
    own, half = dq.shape
    thin = width // 32
    for_c = 64 * thin
    own_rows = pl.ds(pl.multiple_of(own * (2 * r + c), own), own)
    asked = dot_tn(xs[own_rows, :], dq[...])
    kept = dot_tn(xs[...], dkv[...])
    outer = dot_tn(mixed[...], da[...])
    for cc in range(2):
        for rr in range(2):
            for q1 in range(2):
                for q0 in range(2):
                    at = ((4 * rr + 2 * q0 + 1 * q1) * 8) * thin
                    within = (4 * rr + 2 * q1 + q0) * thin
                    for xx in range(2):
                        rows = slice((16 * xx + 8 * cc) * thin + within, (16 * xx + 8 * cc + 1) * thin + within)
                        for t, piece in enumerate((asked, kept[:, 0:half], kept[:, half:])):
                            to = at + (3 * xx + t) * thin
                            packed[cc, to : to + thin, :] = piece[rows, :]
                    rows = slice(8 * cc * thin + within, (8 * cc + 1) * thin + within)
                    for t in range(2):
                        to = at + (6 + t) * thin
                        packed[cc, to : to + thin, :] = outer[rows, half * t : half * (t + 1)]
    columns = pl.ds(pl.multiple_of(half * x, 128), half)
    for cc in range(2):
        packed[cc, for_c : for_c + 16, :] = jnp.zeros((16, half), jnp.float32)
        packed[cc, for_c : for_c + 2, :] = qv_sums[0:2, :]
        for j in range(4):
            packed[cc, for_c + 2 + j : for_c + 3 + j, :] = up_sums[j, 0:1, :]
        packed[cc, for_c + 6 : for_c + 9, :] = sums1[0:3, columns]
        packed[cc, for_c + 9 : for_c + 12, :] = sums2[0:3, columns]
    first = 0
    for send in sends:
        count = send.shape[0]
        send[...] = packed[1 - c, first : first + count, :].astype(jnp.bfloat16)
        first += count
    keep[...] = packed[c]


def step_kernel(bit, keep, *refs):
    gots, (send, kept, whole) = refs[:-3], refs[-3:]
    at = bit(*spot())
    count = send.shape[0] - 16
    first = 0
    for got in gots:
        rows = slice(first, first + got.shape[0])
        whole[rows, :] = keep[rows, :] + got[...].astype(jnp.float32)
        first += got.shape[0]
    theirs = pl.ds(pl.multiple_of(count * (1 - at), 64), count)
    mine = pl.ds(pl.multiple_of(count * at, 64), count)
    send[0:count, :] = whole[theirs, :].astype(jnp.bfloat16)
    send[count:, :] = whole[2 * count :, :].astype(jnp.bfloat16)
    kept[0:count, :] = whole[mine, :]
    kept[count:, :] = whole[2 * count :, :]


def last_step_kernel(keep, got, side, base, *refs):
    out, b_up, whole = refs[:8], refs[8], refs[9]
    q, r, x, c = spot()
    count = side.shape[0]
    part = out[0].shape[0]
    whole[...] = keep[...] + got[...].astype(jnp.float32)
    theirs = pl.ds(pl.multiple_of(count * (1 - x), 8), count)
    mine = pl.ds(pl.multiple_of(count * x, 8), count)
    side[...] = whole[theirs, :].astype(jnp.bfloat16)
    first = whole.shape[0] - 16
    base[...] = jnp.concatenate([whole[mine, :], whole[2 * count : first, :]]).astype(jnp.bfloat16)
    for i, one in enumerate(out):
        at = first + (i if i < 2 else i + 4)
        line = whole[at : at + 1, :]
        one[...] = jnp.where(c == 0, line[:, :part], line[:, part:]).reshape(part)
    line = jnp.concatenate([whole[pl.ds(first + 2 + 2 * c + i, 1), :] for i in range(2)], axis=1)
    b_up[...] = line.reshape(b_up.shape[0])


def down_out_kernel(near, far, out, mark):
    mark[...] = jnp.zeros_like(mark)
    q, r, x, c = spot()
    count = near.shape[0] // 4
    for d, piece in enumerate((near, far)):
        for k in range(4):
            at = 4 * (r ^ d) + 2 * ((q // 2) ^ (k & 1)) + ((q % 2) ^ (k >> 1))
            rows = pl.ds(pl.multiple_of(count * at, 32), count)
            out[rows, :] = piece[count * k : count * (k + 1), :].astype(jnp.float32)


def up_out_kernel(near, far, out, mark, whole):
    mark[...] = jnp.zeros_like(mark)
    q, r, x, c = spot()
    thin, width = near.shape[0] // 16, near.shape[1]
    for d, piece in enumerate((near, far)):
        whole[...] = piece[...].astype(jnp.float32)
        for k in range(4):
            at = 4 * (r ^ d) + 2 * ((q // 2) ^ (k & 1)) + ((q % 2) ^ (k >> 1))
            rows = pl.ds(pl.multiple_of(thin * at, 8), thin)
            for s in range(4):
                columns = pl.ds(pl.multiple_of(width * (2 * (x ^ (s >> 1)) + (s & 1)), 128), width)
                first = thin * (4 * k + s)
                out[rows, columns] = whole[first : first + thin, :]


def rest_out_kernel(near, far, hidden, total, out_q, out_k, out_v, out_o, out_h, out_t, whole):
    out_h[...] = hidden[...]
    out_t[...] = total[...]
    q, r, x, c = spot()
    half = near.shape[1]
    thin = near.shape[0] // 32
    ours = pl.ds(pl.multiple_of(half * x, 128), half)
    other = pl.ds(pl.multiple_of(half * (1 - x), 128), half)
    for d, piece in enumerate((near, far)):
        whole[...] = piece[...].astype(jnp.float32)
        for k in range(4):
            at = 4 * (r ^ d) + 2 * ((q // 2) ^ (k & 1)) + ((q % 2) ^ (k >> 1))
            rows = pl.ds(pl.multiple_of(thin * at, 8), thin)
            first = 8 * thin * k
            for t, out in enumerate((out_q, out_k, out_v)):
                out[rows, ours] = whole[first + thin * t : first + thin * (t + 1), :]
                out[rows, other] = whole[first + thin * (5 + t) : first + thin * (6 + t), :]
            for t in range(2):
                columns = slice(half * t, half * (t + 1))
                out_o[rows, columns] = whole[first + thin * (3 + t) : first + thin * (4 + t), :]


def kernel_call(body, name, ins, outs, scratch, args, after=(), room=2 << 20, cost=1):
    count = len(args)

    def size(shape, dtype):
        return math.prod(shape) * jnp.dtype(dtype).itemsize

    used = sum(size(m.shape, m.dtype) for m in scratch if m.memory_space == pltpu.VMEM)

    args = [
        pltpu.with_memory_space_constraint(a, pltpu.HBM) if spec is HBM else a
        for a, spec in zip(args, ins)
    ]

    def run(*refs):
        body(*refs[:count], *refs[count + len(after) :])

    return pl.pallas_call(
        run,
        name=name,
        out_shape=[jax.ShapeDtypeStruct(shape, dtype) for shape, dtype, _ in outs],
        in_specs=list(ins) + [ANY] * len(after),
        out_specs=[spec for _, _, spec in outs],
        scratch_shapes=scratch,
        cost_estimate=pl.CostEstimate(flops=cost, bytes_accessed=1, transcendentals=0),
        compiler_params=pltpu.CompilerParams(vmem_limit_bytes=used + room),
    )(*args, *after)


def once(value, *after):
    return pl.pallas_call(
        lambda *refs: None,
        name="once",
        out_shape=jax.ShapeDtypeStruct(value.shape, value.dtype),
        in_specs=[ANY] * (1 + len(after)),
        out_specs=ANY,
        input_output_aliases={0: 0},
        cost_estimate=pl.CostEstimate(flops=1, bytes_accessed=1, transcendentals=0),
        compiler_params=pltpu.CompilerParams(vmem_limit_bytes=1 << 18),
    )(value, *after)


HEAVY = ('attend_back', 'down_sum', 'project')


def plane_local(
    tokens, cotangent, seq_ids, w_query, b_query, w_key, w_value, b_value, w_out, b_out,
    attn_gain, attn_shift, w_up, b_up, w_down, b_down, ffn_gain, ffn_shift,
):
    low, exact = jnp.bfloat16, jnp.float32
    rows, width = tokens.shape[1:]
    part = w_query.shape[0]
    half = width // 2
    inner = w_up.shape[1]
    wide = inner // 8
    keys = 8 * rows
    own = 2 * rows
    pairs = half // 128

    latest = []

    def call(body, name, ins, outs, scratch, args, after=(), **more):
        cost = 10**10 if name in HEAVY else 1
        results = kernel_call(
            body, name, ins, outs, scratch, args, tuple(after) + tuple(latest), cost=cost, **more
        )
        latest[:] = results[-1:] if name.endswith("_out") else results[:1]
        return results

    (block,) = call(
        block_kernel, "block", [HBM] * 2, [((rows + 16, width), low, WHOLE)],
        [pltpu.VMEM((1, rows), jnp.int32), pltpu.SemaphoreType.DMA((2,))],
        (tokens[0], seq_ids),
    )
    block = regroup(block)
    theirs, mine = call(
        pack_kernel,
        "pack",
        [HBM] * 12,
        [((3 * part + 16, half), low, WHOLE)] * 2,
        [pltpu.VMEM((16, half), exact)]
        + [pltpu.VMEM((part,), low)] * 8
        + [pltpu.VMEM((width,), low), pltpu.SemaphoreType.DMA((15,))],
        (w_query, w_key, w_value, b_query, b_value, b_out, attn_gain, attn_shift, b_down, ffn_gain, ffn_shift, b_up),
    )
    qkv_x = swap_x(theirs)
    qkv_m = swap_c(mine)
    out_m = swap_c(w_out)
    blocks = [once(block, qkv_m, qkv_x, out_m)]
    beside_r = swap_r(blocks[0])
    blocks.append(once(swap_x(blocks[0]), beside_r))
    blocks.append(swap_c(blocks[0]))
    blocks.append(swap_c(blocks[1]))
    blocks.append(beside_r)
    blocks.append(swap_r(blocks[1]))
    qkv_mx = swap_c(qkv_x)
    up_theirs, up_mine = call(
        cut_kernel, "cut", [HBM], [((part, 4 * wide), low, WHOLE)] * 2, [pltpu.SemaphoreType.DMA((2,))],
        (w_up,), after=(blocks[1],),
    )
    up_x = swap_x(up_theirs)
    up_m = swap_c(up_mine)
    down_m = swap_c(w_down)
    (cot,) = call(
        load_kernel, "cotangent", [HBM], [((rows, width), low, WHOLE)], [pltpu.SemaphoreType.DMA((1,))],
        (cotangent[0],),
    )
    cot, cot_x = regroup(cot), regroup_x(cot)
    kv_own, q_own, w_all, vecs, up_bias = call(
        project_kernel,
        "project",
        [WHOLE] * 4 + [HBM] * 3 + [WHOLE] * 4,
        [
            ((4 * rows, width), low, WHOLE),
            ((own, half), low, WHOLE),
            ((width, 3 * half), low, WHOLE),
            ((8, width), exact, WHOLE),
            ((4, 8, wide), exact, WHOLE),
        ],
        [pltpu.VMEM((4 * rows, width), low), pltpu.SemaphoreType.DMA((3,))],
        (*blocks[:4], w_query, w_key, w_value, qkv_x, qkv_m, qkv_mx, mine),
        room=8 << 20,
    )
    blocks[5] = once(blocks[5], kv_own)
    blocks.append(swap_c(blocks[4]))
    blocks.append(swap_c(blocks[5]))
    a_low, x_all, wo_all, k3, v3, q3, mixed, lse, ids, a_own = call(
        attend_kernel,
        "attend",
        [WHOLE] * 12 + [HBM, WHOLE],
        [
            ((own, width), low, WHOLE),
            ((keys, width), low, WHOLE),
            ((half, width), low, WHOLE),
            ((pairs, keys, 128), low, WHOLE),
            ((pairs, keys, 128), low, WHOLE),
            ((pairs, own, 128), low, WHOLE),
            ((own, half), low, WHOLE),
            ((8, own), exact, WHOLE),
            ((8, rows), exact, WHOLE),
            ((own, width), exact, WHOLE),
        ],
        [
            pltpu.VMEM((2 * pairs, 64, keys), low),
            pltpu.VMEM((2 * pairs, 64, own), exact),
            pltpu.VMEM((keys, own), exact),
            pltpu.SemaphoreType.DMA((1,)),
        ],
        (*blocks, kv_own, q_own, w_all, vecs, w_out, out_m),
        after=(down_m,),
        room=8 << 20,
    )
    a_got = swap_x(a_low)
    up_x = once(up_x, a_low)
    up_mx = swap_c(up_x)
    (kt,) = call(turn_kernel, "turn", [WHOLE], [((2 * pairs, 64, keys), low, WHOLE)], [], (k3,),
        after=(up_m,))

    inner_weights = call(
        inner_kernel,
        "inner",
        [HBM, WHOLE, WHOLE, WHOLE, HBM, WHOLE],
        [((width, 4 * wide), low, WHOLE), ((4 * wide, width), low, WHOLE)],
        [pltpu.SemaphoreType.DMA((2,))],
        (w_up, up_x, up_m, up_mx, w_down, down_m),
    )
    y_low, y_more, h_low, z, normed1, rstd1, slope, y_own = call(
        forward_kernel,
        "feedforward",
        [WHOLE] * 7,
        [
            ((rows, width), low, WHOLE),
            ((rows, width), low, WHOLE),
            ((own, width), low, WHOLE),
            ((own, 4 * wide), low, WHOLE),
            ((own, width), exact, WHOLE),
            ((own, 128), exact, WHOLE),
            ((own, 4 * wide), exact, WHOLE),
            ((own, width), exact, WHOLE),
        ],
        [],
        (a_own, a_got, x_all, vecs, up_bias, *inner_weights),
        room=8 << 20,
    )
    y_got, y_rest = swap_x(y_low), swap_x(y_more)
    dy_low, hidden, dy, sums2 = call(
        norm_back_kernel,
        "norm_back",
        [WHOLE] * 7,
        [
            ((own, width), low, WHOLE),
            ((rows, width), low, WHOLE),
            ((own, width), exact, WHOLE),
            ((8, width), exact, WHOLE),
        ],
        [
            pltpu.VMEM((own, width), low),
            pltpu.VMEM((own, width), low),
        ],
        (y_own, y_got, y_rest, normed1, cot, cot_x, vecs),
        room=6 << 20,
    )
    eighth = wide // 4
    down_send, down_keep = call(
        down_grad_kernel,
        "down_grad",
        [WHOLE] * 2,
        [((8 * eighth, width), low, WHOLE), ((8 * eighth, width), exact, WHOLE)],
        [],
        (z, dy_low),
        room=8 << 20,
    )
    down_got = swap_c(down_send)
    p_low, s_own, du, up_sums = call(
        backward_kernel,
        "feedforward_back",
        [WHOLE] * 5,
        [
            ((own, width), low, WHOLE),
            ((own, width), exact, WHOLE),
            ((own, 4 * wide), low, WHOLE),
            ((4, 8, wide), exact, WHOLE),
        ],
        [],
        (dy, dy_low, slope, *inner_weights),
        room=8 << 20,
    )
    p_got = swap_x(p_low)
    hidden = regroup(hidden)

    def fold(name, bit, keep, got):
        shape = (keep.shape[0] // 2, keep.shape[1])
        return call(
            lambda *refs: fold_kernel(bit, *refs),
            name,
            [WHOLE] * 2,
            [(shape, low, WHOLE), (shape, exact, WHOLE)],
            [],
            (keep.reshape(2, *shape), got.reshape(2, *shape)),
            room=4 << 20,
        )

    def bit_r(q, r, x, c):
        return r

    def bit_near(q, r, x, c):
        return q % 2

    def bit_far(q, r, x, c):
        return q // 2

    thin = part // 8
    count = 64 * thin

    def step(name, bit, keep, size, *gots):
        return call(
            lambda *refs: step_kernel(bit, *refs),
            name,
            [WHOLE] * (1 + len(gots)),
            [((size + 16, half), low, WHOLE), ((size + 16, half), exact, WHOLE)],
            [pltpu.VMEM((2 * size + 16, half), exact)],
            (keep, *gots),
        )

    def join(name, *pieces):
        shape = (sum(p.shape[0] for p in pieces), pieces[0].shape[1])
        (out,) = call(join_kernel, name, [WHOLE] * len(pieces), [(shape, low, WHOLE)], [], pieces)
        return out

    cuts = (count // 3, count // 3, count - 2 * (count // 3) + 16)
    down_send, down_keep = fold("down_1", bit_r, down_keep, down_got)
    down_got = swap_r(down_send)
    up_send, up_keep = call(
        up_grad_kernel,
        "up_grad",
        [WHOLE] * 2,
        [((8 * eighth, width), low, WHOLE), ((8 * eighth, width), exact, WHOLE)],
        [pltpu.VMEM((width, 4 * wide), exact)],
        (h_low, du),
        room=8 << 20,
    )
    up_got = swap_c(up_send)
    up_send, up_keep = fold("up_1", bit_near, up_keep, up_got)
    up_got = swap_near(up_send)
    down_send, down_keep = fold("down_2", bit_near, down_keep, down_got)
    down_got = swap_near(down_send)
    dkv, dq, dr, da, sums1, qv_sums = call(
        attend_back_kernel,
        "attend_back",
        [WHOLE] * 13,
        [
            ((keys, 2 * half), low, WHOLE),
            ((own, half), low, WHOLE),
            ((rows, width), exact, WHOLE),
            ((own, width), low, WHOLE),
            ((8, width), exact, WHOLE),
            ((8, half), exact, WHOLE),
        ],
        [
            pltpu.VMEM((keys, own), exact),
            pltpu.VMEM((pairs, own, 128), low),
            pltpu.VMEM((8, own), exact),
            pltpu.VMEM((pairs, keys, 128), exact),
            pltpu.VMEM((pairs, keys, 128), exact),
            pltpu.VMEM((2 * pairs, 64, own), exact),
            pltpu.VMEM((own, width), exact),
        ],
        (s_own, p_got, normed1, rstd1, vecs, wo_all, mixed, q3, k3, v3, kt, lse, ids),
        room=8 << 20,
    )

    *rest_sends, rest_keep = call(
        weight_grad_kernel,
        "weight_grad",
        [WHOLE] * 9,
        [((n, half), low, WHOLE) for n in cuts] + [((count + 16, half), exact, WHOLE)],
        [pltpu.VMEM((2, count + 16, half), exact)],
        (x_all, dkv, dq, mixed, da, sums1, sums2, qv_sums, up_sums),
        after=(hidden,),
        room=8 << 20,
    )
    rest_gots = [swap_c(send) for send in rest_sends]
    up_send, up_keep = fold("up_2", bit_far, up_keep, up_got)
    up_got = swap_far(up_send)
    rest_send, rest_keep = step("rest_1", bit_r, rest_keep, count // 2, *rest_gots)
    rest_got = swap_r(rest_send)
    *x_sends, x_keep = call(
        input_grad_kernel,
        "input_grad",
        [WHOLE] * 3,
        [((own, width), low, WHOLE)] * 2 + [((2 * own, width), exact, WHOLE)],
        [pltpu.VMEM((keys, width), exact)],
        (dq, dkv, w_all),
        room=8 << 20,
    )
    x_gots = [swap_c(send) for send in x_sends]
    down_send, down_keep = fold("down_3", bit_far, down_keep, down_got)
    down_got = swap_far(down_send)
    x_send, x_keep = call(
        input_x_kernel,
        "input_x",
        [WHOLE] * 3,
        [((own, width), low, WHOLE), ((own, width), exact, WHOLE)],
        [],
        (x_keep, *x_gots),
        room=4 << 20,
    )
    x_got = swap_x(x_send)
    up_send, up_keep = fold("up_3", bit_r, up_keep, up_got)
    up_got = swap_r(up_send)
    (down_sum,) = call(
        sum_kernel, "down_sum", [WHOLE] * 2, [((eighth, width), low, WHOLE)], [], (down_keep, down_got)
    )
    down_other = swap_far(down_sum)
    rest_send, rest_keep = step("rest_2", bit_near, rest_keep, count // 4, rest_got)
    rest_got = swap_near(rest_send)
    x_send, x_keep = fold("input_r", bit_r, x_keep, x_got)
    x_got = swap_r(x_send)
    side, base = call(
        share_kernel,
        "up_share",
        [WHOLE] * 2,
        [((eighth // 2, width), low, WHOLE)] * 2,
        [],
        (up_keep.reshape(2, eighth // 2, width), up_got.reshape(2, eighth // 2, width)),
    )
    side = swap_x(side)
    down_sum = join("down_join", down_sum, down_other)
    down_other = swap_near(down_sum)
    rest_send, rest_keep = step("rest_3", bit_far, rest_keep, count // 8, rest_got)
    rest_got = swap_far(rest_send)
    up_sum = join("up_join", base, side)
    up_other = swap_far(up_sum)
    (total,) = call(
        total_kernel, "input_sum", [WHOLE] * 3, [((rows, width), low, WHOLE)], [], (x_keep, x_got, dr)
    )
    total = regroup(total)
    side, base, *lines, b_up_grad = call(
        last_step_kernel,
        "rest_last",
        [WHOLE] * 2,
        [((3 * thin, half), low, WHOLE), ((5 * thin, half), low, WHOLE)]
        + [((part,), exact, WHOLE)] * 8
        + [((2 * wide,), exact, WHOLE)],
        [pltpu.VMEM((8 * thin + 16, half), exact)],
        (rest_keep, rest_got),
    )
    side = swap_x(side)
    down_near = join("down_join_near", down_sum, down_other)
    down_far = swap_r(down_near)
    up_sum = join("up_join_far", up_sum, up_other)
    up_other = swap_near(up_sum)
    rest_sum = join("rest_join", base, side)
    rest_other = swap_far(rest_sum)
    up_near = join("up_join_near", up_sum, up_other)
    up_far = swap_r(up_near)
    w_down_grad, _ = call(
        down_out_kernel, "down_out", [WHOLE] * 2,
        [((2 * wide, width), exact, WHOLE), ((8, 128), exact, WHOLE)], [], (down_near, down_far),
        room=6 << 20,
    )
    rest_sum = join("rest_join_far", rest_sum, rest_other)
    rest_other = swap_near(rest_sum)
    rest_near = join("rest_join_near", rest_sum, rest_other)
    rest_far = swap_r(rest_near)
    w_up_grad, _ = call(
        up_out_kernel, "up_out", [WHOLE] * 2, [((part, inner), exact, WHOLE), ((8, 128), exact, WHOLE)],
        [pltpu.VMEM((4 * eighth, width), exact)], (up_near, up_far),
        room=6 << 20,
    )


    w_query_grad, w_key_grad, w_value_grad, w_out_grad, hidden_out, tokens_grad = call(
        rest_out_kernel,
        "rest_out",
        [WHOLE] * 4,
        [((part, width), exact, WHOLE)] * 4 + [((rows, width), low, WHOLE)] * 2,
        [pltpu.VMEM((32 * thin, half), exact)],
        (rest_near, rest_far, hidden, total),
        room=6 << 20,
    )

    return (
        hidden_out[None],
        tokens_grad[None],
        w_query_grad,
        lines[0],
        w_key_grad,
        w_value_grad,
        lines[1],
        w_out_grad,
        lines[2],
        lines[3],
        lines[4],
        w_up_grad,
        b_up_grad,
        w_down_grad,
        lines[5],
        lines[6],
        lines[7],
    )


def plane_solution(mesh):
    planes, cycle = mesh.shape["shard"], mesh.shape["ctx"]
    grid = Mesh(mesh.devices.reshape(planes, cycle // planes, 2, 2), AXES)
    shard, ctx = ("x", "c"), ("q", "r")
    tokens, matrix, vector = P(shard, ctx, None), P(shard, None), P(shard)
    return jax.shard_map(
        plane_local,
        mesh=grid,
        in_specs=(
            tokens, tokens, P(shard, ctx), matrix, vector, matrix, matrix, vector, matrix, vector,
            vector, vector, matrix, vector, matrix, vector, vector, vector,
        ),
        out_specs=(
            tokens, tokens, matrix, vector, matrix, matrix, vector, matrix, vector,
            vector, vector, matrix, vector, matrix, vector, vector, vector,
        ),
        check_vma=False,
    )


def solution(mesh):
    if mesh.shape["shard"] == 4 and mesh.shape["ctx"] == 8:
        return plane_solution(mesh)
    return ring_solution(mesh)
```

```python
import math

import jax
import jax.numpy as jnp
from jax import lax
from jax.experimental import pallas as pl
from jax.experimental.pallas import tpu as pltpu
from jax.sharding import Mesh
from jax.sharding import PartitionSpec as P

HEAD_DIM = 64


ln_eps = 1e-12
masked_fill = -1e30


def from_behind(block, axis, distance):
    devices = range(lax.axis_size(axis))
    route = [((i - distance) % len(devices), i) for i in devices]
    return lax.ppermute(block, axis, route)


def matmul(left, right):
    return jnp.dot(left, right, preferred_element_type=jnp.float32)


def matmul_tn(left, right):
    return lax.dot_general(
        left, right, (((0,), (0,)), ((), ())), preferred_element_type=jnp.float32
    )


def matmul_nt(left, right):
    return lax.dot_general(
        left, right, (((1,), (1,)), ((), ())), preferred_element_type=jnp.float32
    )


def apply_layer_norm(value, gain, shift):
    mean = jnp.mean(value, axis=-1, keepdims=True)
    centered = value - mean
    rstd = lax.rsqrt(jnp.mean(centered * centered, axis=-1, keepdims=True) + ln_eps)
    normed = centered * rstd
    return (normed * gain + shift, normed, rstd)


def norm_back(grad, normed, rstd, gain):
    d_gain = jnp.sum(grad * normed, axis=0)
    d_shift = jnp.sum(grad, axis=0)
    scaled = grad * gain
    d_value = rstd * (
        scaled
        - jnp.mean(scaled, axis=-1, keepdims=True)
        - normed * jnp.mean(scaled * normed, axis=-1, keepdims=True)
    )
    return (d_value, d_gain, d_shift)


def gelu_slope(value):
    normal_cdf = 0.5 * (1.0 + lax.erf(value * (1.0 / math.sqrt(2.0))))
    density = jnp.exp(-0.5 * value * value) * (1.0 / math.sqrt(2.0 * math.pi))
    return normal_cdf + value * density


def scores_of(query, keys, q_ids, k_ids, scale):
    raw = jnp.einsum("qhd,khd->hqk", query, keys, preferred_element_type=jnp.float32) * scale
    match = (q_ids[:, None] == k_ids[None, :])[None, :, :]
    return (raw, match)


def attend(query, q_ids, keys, values, k_ids, stats, scale):
    top, total, accum = stats
    raw, match = scores_of(query, keys, q_ids, k_ids, scale)
    masked = jnp.where(match, raw, masked_fill)
    new_top = jnp.maximum(top, jnp.max(masked, axis=-1))
    weights = jnp.where(match, jnp.exp(masked - new_top[:, :, None]), 0.0)
    factor = jnp.exp(top - new_top)
    total = total * factor + jnp.sum(weights, axis=-1)
    accum = accum * factor[:, :, None] + jnp.einsum(
        "hqk,khd->hqd", weights.astype(jnp.bfloat16), values, preferred_element_type=jnp.float32
    )
    return (new_top, total, accum)


def block_grads(query, q_ids, d_out, log_total, delta, keys, values, k_ids, scale):
    raw, match = scores_of(query, keys, q_ids, k_ids, scale)
    probs = jnp.exp(jnp.where(match, raw - log_total[:, :, None], masked_fill))
    d_values = jnp.einsum(
        "hqk,qhd->khd", probs.astype(jnp.bfloat16), d_out, preferred_element_type=jnp.float32
    )
    d_probs = jnp.einsum("qhd,khd->hqk", d_out, values, preferred_element_type=jnp.float32)
    d_scores = (probs * (d_probs - delta[:, :, None])).astype(jnp.bfloat16)
    d_query = jnp.einsum("hqk,khd->qhd", d_scores, keys, preferred_element_type=jnp.float32) * scale
    d_keys = jnp.einsum("hqk,qhd->khd", d_scores, query, preferred_element_type=jnp.float32) * scale
    return (d_query, d_keys, d_values)


def ring_local(
    tokens,
    cotangent,
    seq_ids,
    w_query,
    b_query,
    w_key,
    w_value,
    b_value,
    w_out,
    b_out,
    attn_gain,
    attn_shift,
    w_up,
    b_up,
    w_down,
    b_down,
    ffn_gain,
    ffn_shift,
):
    cycle = lax.axis_size("ctx")
    tok_rows = tokens.shape[1]
    width = tokens.shape[2]
    heads = width // HEAD_DIM
    scale = 1.0 / math.sqrt(HEAD_DIM)
    share = tok_rows // cycle
    got_tokens, got_grads, got_ids = (
        lax.all_to_all(
            tokens[0].reshape(share, cycle, width), "ctx", split_axis=1, concat_axis=1, tiled=True
        ),
        lax.all_to_all(
            cotangent[0].reshape(share, cycle, width),
            "ctx",
            split_axis=1,
            concat_axis=1,
            tiled=True,
        ),
        lax.all_to_all(
            seq_ids[0].reshape(share, cycle), "ctx", split_axis=1, concat_axis=1, tiled=True
        ),
    )
    x_local = got_tokens.reshape(tok_rows, width)
    local_gradient = got_grads.reshape(tok_rows, width).astype(jnp.float32)
    local_ids = got_ids.reshape(tok_rows)
    (
        query_mat,
        query_bias,
        key_mat,
        value_mat,
        value_bias,
        out_mat,
        out_bias,
        attention_norm_gain,
        first_shift,
        up_mat,
        up_bias,
        down_mat,
        down_bias,
        feedforward_norm_gain,
        second_shift,
    ) = (
        lax.all_gather(w_query, "shard", axis=0, tiled=True),
        lax.all_gather(b_query, "shard", axis=0, tiled=True),
        lax.all_gather(w_key, "shard", axis=0, tiled=True),
        lax.all_gather(w_value, "shard", axis=0, tiled=True),
        lax.all_gather(b_value, "shard", axis=0, tiled=True),
        lax.all_gather(w_out, "shard", axis=0, tiled=True),
        lax.all_gather(b_out, "shard", axis=0, tiled=True),
        lax.all_gather(attn_gain, "shard", axis=0, tiled=True),
        lax.all_gather(attn_shift, "shard", axis=0, tiled=True),
        lax.all_gather(w_up, "shard", axis=0, tiled=True),
        lax.all_gather(b_up, "shard", axis=0, tiled=True),
        lax.all_gather(w_down, "shard", axis=0, tiled=True),
        lax.all_gather(b_down, "shard", axis=0, tiled=True),
        lax.all_gather(ffn_gain, "shard", axis=0, tiled=True),
        lax.all_gather(ffn_shift, "shard", axis=0, tiled=True),
    )
    query = (matmul(x_local, query_mat) + query_bias.astype(jnp.float32)).astype(jnp.bfloat16)
    keys = matmul(x_local, key_mat).astype(jnp.bfloat16)
    values = (matmul(x_local, value_mat) + value_bias.astype(jnp.float32)).astype(jnp.bfloat16)
    q_heads = query.reshape(tok_rows, heads, HEAD_DIM)
    start_stats = (
        jnp.full((heads, tok_rows), masked_fill, jnp.float32),
        jnp.zeros((heads, tok_rows), jnp.float32),
        jnp.zeros((heads, tok_rows, HEAD_DIM), jnp.float32),
    )

    def forward_step(step, carry):
        block, stats = carry
        stats = attend(
            q_heads,
            local_ids,
            block[0].reshape(tok_rows, heads, HEAD_DIM),
            block[1].reshape(tok_rows, heads, HEAD_DIM),
            block[2],
            stats,
            scale,
        )
        block = from_behind((block[0], block[1], block[2]), "ctx", 1)
        return (block, stats)

    block, stats = lax.fori_loop(
        0, cycle - 1, forward_step, ((keys, values, local_ids), start_stats)
    )
    top, total, accum = attend(
        q_heads,
        local_ids,
        block[0].reshape(tok_rows, heads, HEAD_DIM),
        block[1].reshape(tok_rows, heads, HEAD_DIM),
        block[2],
        stats,
        scale,
    )
    attn_out = (
        (accum / total[:, :, None]).transpose(1, 0, 2).reshape(tok_rows, width).astype(jnp.bfloat16)
    )
    log_total = top + jnp.log(total)
    attn_proj = matmul(attn_out, out_mat) + out_bias.astype(jnp.float32)
    first_sum = x_local.astype(jnp.float32) + attn_proj
    first_normalized_rows, first_centered_scaled, first_inverse_deviation = apply_layer_norm(
        first_sum, attention_norm_gain.astype(jnp.float32), first_shift.astype(jnp.float32)
    )
    normed_low = first_normalized_rows.astype(jnp.bfloat16)
    up_pre = matmul(normed_low, up_mat) + up_bias.astype(jnp.float32)
    up_act = jax.nn.gelu(up_pre, approximate=False).astype(jnp.bfloat16)
    down_pre = matmul(up_act, down_mat) + down_bias.astype(jnp.float32)
    layer_output, second_centered_scaled, second_inverse_deviation = apply_layer_norm(
        first_normalized_rows + down_pre,
        feedforward_norm_gain.astype(jnp.float32),
        second_shift.astype(jnp.float32),
    )
    (
        query_mat,
        key_mat,
        value_mat,
        out_mat,
        attention_norm_gain,
        up_mat,
        down_mat,
        feedforward_norm_gain,
    ) = (
        lax.all_gather(w_query, "shard", axis=0, tiled=True),
        lax.all_gather(w_key, "shard", axis=0, tiled=True),
        lax.all_gather(w_value, "shard", axis=0, tiled=True),
        lax.all_gather(w_out, "shard", axis=0, tiled=True),
        lax.all_gather(attn_gain, "shard", axis=0, tiled=True),
        lax.all_gather(w_up, "shard", axis=0, tiled=True),
        lax.all_gather(w_down, "shard", axis=0, tiled=True),
        lax.all_gather(ffn_gain, "shard", axis=0, tiled=True),
    )
    grad_two, d_second_gain, d_second_shift = norm_back(
        local_gradient,
        second_centered_scaled,
        second_inverse_deviation,
        feedforward_norm_gain.astype(jnp.float32),
    )
    grad_down = grad_two.astype(jnp.bfloat16)
    d_down_bias = jnp.sum(grad_down, axis=0, dtype=jnp.float32)
    d_down_mat = matmul_tn(up_act, grad_down)
    grad_up = (matmul_nt(grad_down, down_mat) * gelu_slope(up_pre)).astype(jnp.bfloat16)
    d_up_bias = jnp.sum(grad_up, axis=0, dtype=jnp.float32)
    d_up_mat = matmul_tn(normed_low, grad_up)
    first_norm_gradient = grad_two + matmul_nt(grad_up, up_mat)
    grad_first, d_first_gain, d_first_shift = norm_back(
        first_norm_gradient,
        first_centered_scaled,
        first_inverse_deviation,
        attention_norm_gain.astype(jnp.float32),
    )
    grad_proj = grad_first.astype(jnp.bfloat16)
    d_out_bias = jnp.sum(grad_proj, axis=0, dtype=jnp.float32)
    d_out_mat = matmul_tn(attn_out, grad_proj)
    grad_attn = matmul_nt(grad_proj, out_mat).astype(jnp.bfloat16)
    grad_heads = grad_attn.reshape(tok_rows, heads, HEAD_DIM)
    delta = jnp.einsum(
        "qhd,qhd->hq",
        grad_heads,
        attn_out.reshape(tok_rows, heads, HEAD_DIM),
        preferred_element_type=jnp.float32,
    )
    zero_rows = jnp.zeros((tok_rows, width), jnp.float32)

    def key_step(step, carry):
        block, sums, acc_query = carry
        d_query, d_keys, d_values = block_grads(
            q_heads,
            local_ids,
            grad_heads,
            log_total,
            delta,
            block[0].reshape(tok_rows, heads, HEAD_DIM),
            block[1].reshape(tok_rows, heads, HEAD_DIM),
            block[2],
            scale,
        )
        sums = (
            sums[0] + d_keys.reshape(tok_rows, width),
            sums[1] + d_values.reshape(tok_rows, width),
        )
        block = from_behind((block[0], block[1], block[2]), "ctx", 1)
        sums = (
            from_behind(sums[0].astype(jnp.bfloat16), "ctx", 1).astype(jnp.float32),
            from_behind(sums[1].astype(jnp.bfloat16), "ctx", 1).astype(jnp.float32),
        )
        return (block, sums, acc_query + d_query.reshape(tok_rows, width))

    block, sums, d_query_sum = lax.fori_loop(
        0, cycle, key_step, ((keys, values, local_ids), (zero_rows, zero_rows), zero_rows)
    )
    d_keys_sum, d_values_sum = sums
    grad_query = d_query_sum.astype(jnp.bfloat16)
    grad_keys = d_keys_sum.astype(jnp.bfloat16)
    grad_values = d_values_sum.astype(jnp.bfloat16)
    d_query_bias = jnp.sum(grad_query, axis=0, dtype=jnp.float32)
    d_value_bias = jnp.sum(grad_values, axis=0, dtype=jnp.float32)
    d_query_mat = matmul_tn(x_local, grad_query)
    d_key_mat = matmul_tn(x_local, grad_keys)
    d_value_mat = matmul_tn(x_local, grad_values)
    grad_input = (
        grad_first
        + matmul_nt(grad_query, query_mat)
        + matmul_nt(grad_keys, key_mat)
        + matmul_nt(grad_values, value_mat)
    )
    home_hidden, home_grad = (
        lax.all_to_all(
            layer_output.astype(jnp.bfloat16).reshape(share, cycle, width),
            "ctx",
            split_axis=1,
            concat_axis=1,
            tiled=True,
        ),
        lax.all_to_all(
            grad_input.astype(jnp.bfloat16).reshape(share, cycle, width),
            "ctx",
            split_axis=1,
            concat_axis=1,
            tiled=True,
        ),
    )
    hidden_out = home_hidden.reshape(tok_rows, width)[None]
    tokens_grad = home_grad.reshape(tok_rows, width)[None]
    shares = (
        lax.psum_scatter(
            d_query_mat.astype(jnp.bfloat16), "shard", scatter_dimension=0, tiled=True
        ).astype(jnp.float32),
        lax.psum_scatter(
            d_query_bias.astype(jnp.bfloat16), "shard", scatter_dimension=0, tiled=True
        ).astype(jnp.float32),
        lax.psum_scatter(
            d_key_mat.astype(jnp.bfloat16), "shard", scatter_dimension=0, tiled=True
        ).astype(jnp.float32),
        lax.psum_scatter(
            d_value_mat.astype(jnp.bfloat16), "shard", scatter_dimension=0, tiled=True
        ).astype(jnp.float32),
        lax.psum_scatter(
            d_value_bias.astype(jnp.bfloat16), "shard", scatter_dimension=0, tiled=True
        ).astype(jnp.float32),
        lax.psum_scatter(
            d_out_mat.astype(jnp.bfloat16), "shard", scatter_dimension=0, tiled=True
        ).astype(jnp.float32),
        lax.psum_scatter(
            d_out_bias.astype(jnp.bfloat16), "shard", scatter_dimension=0, tiled=True
        ).astype(jnp.float32),
        lax.psum_scatter(
            d_first_gain.astype(jnp.bfloat16), "shard", scatter_dimension=0, tiled=True
        ).astype(jnp.float32),
        lax.psum_scatter(
            d_first_shift.astype(jnp.bfloat16), "shard", scatter_dimension=0, tiled=True
        ).astype(jnp.float32),
        lax.psum_scatter(
            d_up_mat.astype(jnp.bfloat16), "shard", scatter_dimension=0, tiled=True
        ).astype(jnp.float32),
        lax.psum_scatter(
            d_up_bias.astype(jnp.bfloat16), "shard", scatter_dimension=0, tiled=True
        ).astype(jnp.float32),
        lax.psum_scatter(
            d_down_mat.astype(jnp.bfloat16), "shard", scatter_dimension=0, tiled=True
        ).astype(jnp.float32),
        lax.psum_scatter(
            d_down_bias.astype(jnp.bfloat16), "shard", scatter_dimension=0, tiled=True
        ).astype(jnp.float32),
        lax.psum_scatter(
            d_second_gain.astype(jnp.bfloat16), "shard", scatter_dimension=0, tiled=True
        ).astype(jnp.float32),
        lax.psum_scatter(
            d_second_shift.astype(jnp.bfloat16), "shard", scatter_dimension=0, tiled=True
        ).astype(jnp.float32),
    )
    totals = lax.psum(
        (
            shares[0],
            shares[1],
            shares[2],
            shares[3],
            shares[4],
            shares[5],
            shares[6],
            shares[7],
            shares[8],
            shares[9],
            shares[10],
            shares[11],
            shares[12],
            shares[13],
            shares[14],
        ),
        "ctx",
    )
    return (hidden_out, tokens_grad) + tuple(totals)


def ring_solution(mesh):
    return jax.shard_map(
        ring_local,
        mesh=mesh,
        in_specs=(
            P("shard", "ctx", None),
            P("shard", "ctx", None),
            P("shard", "ctx"),
            P("shard", None),
            P("shard"),
            P("shard", None),
            P("shard", None),
            P("shard"),
            P("shard", None),
            P("shard"),
            P("shard"),
            P("shard"),
            P("shard", None),
            P("shard"),
            P("shard", None),
            P("shard"),
            P("shard"),
            P("shard"),
        ),
        out_specs=(
            P("shard", "ctx", None),
            P("shard", "ctx", None),
            P("shard", None),
            P("shard"),
            P("shard", None),
            P("shard", None),
            P("shard"),
            P("shard", None),
            P("shard"),
            P("shard"),
            P("shard"),
            P("shard", None),
            P("shard"),
            P("shard", None),
            P("shard"),
            P("shard"),
            P("shard"),
        ),
        check_vma=False,
    )


AXES = ("q", "r", "x", "c")
ANY = pl.BlockSpec(memory_space=pl.ANY)
WHOLE = pl.BlockSpec(memory_space=pltpu.VMEM)
HBM = pl.BlockSpec(memory_space=pltpu.HBM)


def moved(block, move):
    sizes = [lax.axis_size(a) for a in AXES]

    def number(spot):
        place = 0
        for size, at in zip(sizes, spot):
            place = place * size + at
        return place

    spots = [
        (q, r, x, c)
        for q in range(sizes[0])
        for r in range(sizes[1])
        for x in range(sizes[2])
        for c in range(sizes[3])
    ]
    return lax.ppermute(block, AXES, [(number(s), number(move(*s))) for s in spots])


def swap_x(block):
    return moved(block, lambda q, r, x, c: (q, r, 1 - x, c))


def swap_c(block):
    return moved(block, lambda q, r, x, c: (q, r, x, 1 - c))


def swap_r(block):
    return moved(block, lambda q, r, x, c: (q, r ^ 1, x, c))


def swap_rc(block):
    return moved(block, lambda q, r, x, c: (q, r ^ 1, x, 1 - c))


def swap_near(block):
    return moved(block, lambda q, r, x, c: (q ^ 1, r, x, c))


def swap_far(block):
    return moved(block, lambda q, r, x, c: (q ^ 2, r, x, c))


def regroup(block):
    return moved(block, lambda q, r, x, c: (2 * c + x, r, q & 1, q >> 1))


def regroup_x(block):
    return moved(block, lambda q, r, x, c: (2 * c + x, r, 1 - (q & 1), q >> 1))


def swap_xc(block):
    return moved(block, lambda q, r, x, c: (q, r, 1 - x, 1 - c))


def beside(mine, got):
    return jnp.concatenate([mine, got])


def dot(left, right):
    return jnp.dot(left, right, preferred_element_type=jnp.float32)


def dot_nt(left, right):
    return lax.dot_general(
        left, right, (((1,), (1,)), ((), ())), preferred_element_type=jnp.float32
    )


def dot_tn(left, right):
    return lax.dot_general(
        left, right, (((0,), (0,)), ((), ())), preferred_element_type=jnp.float32
    )


class Copies:
    def __init__(self, sems):
        self.sems = sems
        self.count = 0
        self.held = []

    def start(self, source, target):
        copy = pltpu.make_async_copy(source, target, self.sems.at[self.count])
        copy.start()
        self.count += 1
        self.held.append(copy)

    def wait(self):
        for copy in self.held:
            copy.wait()
        self.held = []


def spot():
    return tuple(lax.axis_index(a) for a in AXES)


def fill_mask(ids, mask, own):
    blocks, rows = ids.shape
    mine = jnp.concatenate([ids[pl.ds(own, 1), :], ids[pl.ds(own + 1, 1), :]], axis=1)
    across = jnp.transpose(ids[...])
    for b in range(blocks):
        mask[rows * b : rows * (b + 1), :] = jnp.where(across[:, b : b + 1] == mine, 0.0, masked_fill)


def block_kernel(tokens, ids, block, line, sems):
    rows = tokens.shape[0]
    copies = Copies(sems)
    copies.start(tokens, block.at[pl.ds(0, rows)])
    copies.start(ids, line)
    block[rows:, :] = jnp.zeros((16, block.shape[1]), block.dtype)
    copies.wait()
    block[rows:, 0:rows] = jnp.broadcast_to(line[...].astype(jnp.float32), (16, rows)).astype(block.dtype)


def pack_kernel(w_q, w_k, w_v, *refs):
    vectors, b_up, theirs, mine = refs[:8], refs[8], refs[9], refs[10]
    lines, thin, thick, sems = refs[11], refs[12:20], refs[20], refs[21]
    q, r, x, c = spot()
    part, width = w_q.shape
    half = width // 2
    copies = Copies(sems)
    for t, w in enumerate((w_q, w_k, w_v)):
        rows = pl.ds(part * t, part)
        copies.start(w.at[:, pl.ds(pl.multiple_of(half * x, 128), half)], mine.at[rows])
        copies.start(w.at[:, pl.ds(pl.multiple_of(half * (1 - x), 128), half)], theirs.at[rows])
    for vector, held in zip(vectors, thin):
        copies.start(vector, held)
    copies.start(b_up, thick)
    lines[...] = jnp.zeros_like(lines)
    copies.wait()
    for i, vector in enumerate(thin):
        line = vector[...].astype(jnp.float32).reshape(1, part)
        none = jnp.zeros_like(line)
        first = jnp.concatenate([line, none], axis=1)
        second = jnp.concatenate([none, line], axis=1)
        lines[i : i + 1, :] = jnp.where(c == 0, first, second)
    wide = thick[...].astype(jnp.float32).reshape(1, width)
    lines[pl.ds(8 + 2 * c, 1), :] = wide[:, 0:half]
    lines[pl.ds(9 + 2 * c, 1), :] = wide[:, half:]
    low = lines[...].astype(jnp.bfloat16)
    mine[3 * part :, :] = low
    theirs[3 * part :, :] = low


def cut_kernel(w, theirs, mine, sems):
    q, r, x, c = spot()
    count = theirs.shape[1]
    copies = Copies(sems)
    copies.start(w.at[:, pl.ds(pl.multiple_of(count * (1 - x), 128), count)], theirs)
    copies.start(w.at[:, pl.ds(pl.multiple_of(count * x, 128), count)], mine)
    copies.wait()


def load_kernel(block, out, sems):
    copies = Copies(sems)
    copies.start(block, out)
    copies.wait()


def turn_kernel(keys, out):
    for p in range(keys.shape[0]):
        out[2 * p : 2 * p + 2] = jnp.transpose(keys[p]).reshape(2, 64, keys.shape[1])


def project_kernel(
    b0, b1, b2, b3, w_q, w_k, w_v, w_x, w_m, w_mx, own_lines,
    kv_out, q_out, w, vecs, up_bias, xs, sems,
):
    q, r, x, c = spot()
    rows = xs.shape[0] // 4
    part = w.shape[0] // 4
    half = w.shape[1] // 3
    me, shard = 2 * c + x, 2 * x + c
    columns = pl.ds(pl.multiple_of(half * x, 128), half)
    ins = Copies(sems)
    for t, own in enumerate((w_q, w_k, w_v)):
        at = pl.ds(pl.multiple_of(part * shard, 64), part)
        ins.start(own.at[:, columns], w.at[at, pl.ds(half * t, half)])
    for j, block in enumerate((b0, b1, b2, b3)):
        xs[pl.ds(pl.multiple_of(rows * (me ^ j), rows), rows), :] = block[0:rows, :]
    for flip, piece in ((2, w_x), (1, w_m), (3, w_mx)):
        at = pl.ds(pl.multiple_of(part * (shard ^ flip), 64), part)
        for t in range(3):
            w[at, half * t : half * (t + 1)] = piece[part * t : part * (t + 1), :]
    mine, other = (
        a[3 * part :, :].astype(jnp.float32) + b[3 * part :, :].astype(jnp.float32)
        for a, b in ((own_lines, w_m), (w_x, w_mx))
    )
    vecs[:, columns] = mine[0:8, :]
    vecs[:, pl.ds(pl.multiple_of(half * (1 - x), 128), half)] = other[0:8, :]
    for i in range(4):
        up_bias[i] = jnp.broadcast_to(mine[8 + i : 9 + i, :], (8, half))
    ins.wait()
    kv_out[:, 0:half] = dot(xs[...], w[:, half : 2 * half]).astype(jnp.bfloat16)
    kv_out[:, half:] = (dot(xs[...], w[:, 2 * half :]) + mine[1:2, :]).astype(jnp.bfloat16)
    own = pl.ds(pl.multiple_of(2 * rows * c, rows), 2 * rows)
    q_out[...] = (dot(xs[own, :], w[:, 0:half]) + mine[0:1, :]).astype(jnp.bfloat16)


def attend_kernel(
    b0, b1, b2, b3, b4, b5, b6, b7, kv_own, q_own, w, vecs, w_o, w_om,
    a_low, xs, wo, k3, v3, q3, o_out, lse_out, ids_out, a_out,
    vt, ot, mask, sems,
):
    q, r, x, c = spot()
    rows = xs.shape[0] // 8
    half = wo.shape[0]
    part = half // 2
    me = 4 * r + 2 * c + x
    ins = Copies(sems)
    ins.start(w_o, wo.at[pl.ds(pl.multiple_of(part * c, 64), part)])
    wo[pl.ds(pl.multiple_of(part * (1 - c), 64), part), :] = w_om[...]
    for j, block in enumerate((b0, b1, b2, b3, b4, b5, b6, b7)):
        at = me ^ j
        xs[pl.ds(pl.multiple_of(rows * at, rows), rows), :] = block[0:rows, :]
        ids_out[pl.ds(at, 1), :] = block[rows : rows + 16, 0:rows].astype(jnp.float32)[0:1, :]
    fill_mask(ids_out, mask, 4 * r + 2 * c)
    rest = pl.ds(pl.multiple_of(4 * rows * (1 - r), rows), 4 * rows)
    here = pl.ds(pl.multiple_of(4 * rows * r, rows), 4 * rows)
    bias = vecs[1:2, pl.ds(pl.multiple_of(half * x, 128), half)]
    keyed = dot(xs[rest, :], w[:, half : 2 * half]).astype(jnp.bfloat16)
    valued = (dot(xs[rest, :], w[:, 2 * half :]) + bias).astype(jnp.bfloat16)
    pairs = half // 128
    for p in range(pairs):
        at = slice(128 * p, 128 * (p + 1))
        k3[p, here, :] = kv_own[:, at]
        k3[p, rest, :] = keyed[:, at]
        v3[p, here, :] = kv_own[:, half + 128 * p : half + 128 * (p + 1)]
        v3[p, rest, :] = valued[:, at]
        q3[p] = q_own[:, at]
        vt[2 * p : 2 * p + 2] = jnp.transpose(v3[p]).reshape(2, 64, 8 * rows)
    lane = lax.broadcasted_iota(jnp.int32, (2 * rows, 128), 1) // 64

    def head(h, carry):
        query = jnp.where(lane == h % 2, q3[h // 2], 0) * 0.125
        scores = dot_nt(k3[h // 2], query.astype(jnp.bfloat16)) + mask[...]
        top = jnp.max(scores, axis=0, keepdims=True)
        weights = jnp.exp(scores - top)
        total = jnp.sum(weights, axis=0, keepdims=True)
        ot[h] = dot(vt[h], weights.astype(jnp.bfloat16)) / total
        lse_out[pl.ds(h, 1), :] = top + jnp.log(total)
        return carry

    lax.fori_loop(0, 2 * pairs, head, 0)
    mixed = jnp.transpose(ot[...].reshape(half, 2 * rows)).astype(jnp.bfloat16)
    o_out[...] = mixed
    ins.wait()
    partial = dot(mixed, wo[...])
    a_out[...] = partial
    a_low[...] = partial.astype(jnp.bfloat16)


def inner_kernel(u_own, u_x, u_m, u_mx0, u_mx1, d_own, d_m, up, down, sems):
    q, r, x, c = spot()
    part = up.shape[0] // 4
    count = up.shape[1]
    shard = 2 * x + c
    ins = Copies(sems)
    own = u_own.at[:, pl.ds(pl.multiple_of(count * x, 128), count)]
    ins.start(own, up.at[pl.ds(pl.multiple_of(part * shard, 64), part)])
    ins.start(d_own, down.at[pl.ds(pl.multiple_of(count // 2 * c, 128), count // 2)])
    for flip, piece in ((2, u_x), (1, u_m)):
        up[pl.ds(pl.multiple_of(part * (shard ^ flip), 64), part), :] = piece[...]
    for i, piece in enumerate((u_mx0, u_mx1)):
        at = pl.multiple_of(part * (shard ^ 3) + part // 2 * i, 32)
        up[pl.ds(at, part // 2), :] = piece[...]
    down[pl.ds(pl.multiple_of(count // 2 * (1 - c), 128), count // 2), :] = d_m[...]
    ins.wait()


def norm_of(value):
    mean = jnp.mean(value, axis=-1, keepdims=True)
    centered = value - mean
    rstd = lax.rsqrt(jnp.mean(centered * centered, axis=-1, keepdims=True) + ln_eps)
    return centered * rstd, rstd


def norm_pull(scaled, normed, rstd):
    return rstd * (
        scaled
        - jnp.mean(scaled, axis=-1, keepdims=True)
        - normed * jnp.mean(scaled * normed, axis=-1, keepdims=True)
    )


def forward_kernel(
    a_own, a_got, xs, vecs, b_up, up, down,
    y_low, y_more, h_out, z, n_out, r_out, slope, y_out,
):
    q, r, x, c = spot()
    rows = a_own.shape[0]
    x_own = xs[pl.ds(pl.multiple_of(rows * (2 * r + c), rows), rows), :]
    total = x_own.astype(jnp.float32) + (a_own[...] + a_got[...].astype(jnp.float32) + vecs[2:3, :])
    normed, rstd = norm_of(total)
    n_out[...] = normed
    r_out[...] = jnp.broadcast_to(rstd, r_out.shape)
    low = (normed * vecs[3:4, :] + vecs[4:5, :]).astype(jnp.bfloat16)
    h_out[...] = low
    wide = up.shape[1] // 4
    for j in range(4):
        at = slice(wide * j, wide * (j + 1))
        pre = dot(low, up[:, at]) + b_up[j, 0:1, :]
        cdf = 0.5 * (1.0 + lax.erf(pre * (1.0 / math.sqrt(2.0))))
        density = jnp.exp(-0.5 * pre * pre) * (1.0 / math.sqrt(2.0 * math.pi))
        z[:, at] = (pre * cdf).astype(jnp.bfloat16)
        slope[:, at] = cdf + pre * density
    result = dot(z[...], down[...])
    y_out[...] = result
    rows = y_low.shape[0]
    y_low[...] = result[0:rows, :].astype(jnp.bfloat16)
    y_more[...] = result[rows:, :].astype(jnp.bfloat16)


def norm_back_kernel(
    y_own, y_got, y_rest, normed1, g_own, g_x, vecs, low_out, hid_out, dy_out, sums, grad, hid,
):
    q, r, x, c = spot()
    rows = grad.shape[0] // 2
    grad[pl.ds(pl.multiple_of(rows * x, rows), rows), :] = g_own[...]
    grad[pl.ds(pl.multiple_of(rows * (1 - x), rows), rows), :] = g_x[...]
    got = jnp.concatenate([y_got[...], y_rest[...]]).astype(jnp.float32)
    h1 = normed1[...] * vecs[3:4, :] + vecs[4:5, :]
    normed, rstd = norm_of(h1 + (y_own[...] + got + vecs[5:6, :]))
    hid[...] = (normed * vecs[6:7, :] + vecs[7:8, :]).astype(jnp.bfloat16)
    hid_out[...] = hid[pl.ds(pl.multiple_of(rows * x, rows), rows), :]
    cot = grad[...].astype(jnp.float32)
    dy = norm_pull(cot * vecs[6:7, :], normed, rstd)
    low = dy.astype(jnp.bfloat16)
    dy_out[...] = dy
    low_out[...] = low
    sums[...] = jnp.zeros_like(sums)
    sums[0:1, :] = jnp.sum(low.astype(jnp.float32), axis=0, keepdims=True)
    sums[1:2, :] = jnp.sum(cot * normed, axis=0, keepdims=True)
    sums[2:3, :] = jnp.sum(cot, axis=0, keepdims=True)


def backward_kernel(dy, dy_low, slope, up, down, p_low, s_out, du_out, up_sums):
    low = dy_low[...]
    wide = up.shape[1] // 4
    for j in range(4):
        at = slice(wide * j, wide * (j + 1))
        du = (dot_nt(low, down[at, :]) * slope[:, at]).astype(jnp.bfloat16)
        du_out[:, at] = du
        total = jnp.sum(du.astype(jnp.float32), axis=0, keepdims=True)
        up_sums[j] = jnp.broadcast_to(total, up_sums.shape[1:])
    result = dot_nt(du_out[...], up[...])
    s_out[...] = dy[...] + result
    p_low[...] = result.astype(jnp.bfloat16)


def attend_back_kernel(
    s_own, p_got, normed1, rstd1, vecs, wo, mixed, q3, k3, v3, kt, lse, ids,
    dkv_out, dq_out, dr_out, da_out, sums, qv_sums,
    mask, do3, delta, dk, dv, dqt, whole,
):
    q, r, x, c = spot()
    rows = dr_out.shape[0]
    pairs = q3.shape[0]
    half = 128 * pairs
    fill_mask(ids, mask, 4 * r + 2 * c)
    dh = s_own[...] + p_got[...].astype(jnp.float32)
    normed = normed1[...]
    dr = norm_pull(dh * vecs[3:4, :], normed, rstd1[:, 0:1])
    whole[...] = dr
    dr_out[...] = whole[pl.ds(pl.multiple_of(rows * x, rows), rows), :]
    low = dr.astype(jnp.bfloat16)
    da_out[...] = low
    sums[...] = jnp.zeros_like(sums)
    sums[0:1, :] = jnp.sum(low.astype(jnp.float32), axis=0, keepdims=True)
    sums[1:2, :] = jnp.sum(dh * normed, axis=0, keepdims=True)
    sums[2:3, :] = jnp.sum(dh, axis=0, keepdims=True)
    d_o = dot_nt(low, wo[...]).astype(jnp.bfloat16)
    products = jnp.transpose(d_o.astype(jnp.float32) * mixed[...].astype(jnp.float32))
    for h in range(2 * pairs):
        delta[h : h + 1, :] = jnp.sum(products[64 * h : 64 * (h + 1), :], axis=0, keepdims=True)
    for p in range(pairs):
        do3[p] = d_o[:, 128 * p : 128 * (p + 1)]
    dk[...] = jnp.zeros_like(dk)
    dv[...] = jnp.zeros_like(dv)
    lane = lax.broadcasted_iota(jnp.int32, (2 * rows, 128), 1) // 64

    def head(h, carry):
        p = h // 2
        here = lane == h % 2
        query = (jnp.where(here, q3[p], 0) * 0.125).astype(jnp.bfloat16)
        d_here = jnp.where(here, do3[p], 0).astype(jnp.bfloat16)
        probs = jnp.exp(dot_nt(k3[p], query) + mask[...] - lse[pl.ds(h, 1), :])
        d_probs = dot_nt(v3[p], d_here)
        d_scores = (probs * (d_probs - delta[pl.ds(h, 1), :])).astype(jnp.bfloat16)
        dv[p] += dot(probs.astype(jnp.bfloat16), d_here)
        dk[p] += dot(d_scores, query)
        dqt[h] = dot(kt[h], d_scores)
        return carry

    lax.fori_loop(0, 2 * pairs, head, 0)
    dq = (jnp.transpose(dqt[...].reshape(half, 2 * rows)) * 0.125).astype(jnp.bfloat16)
    dq_out[...] = dq
    qv_sums[...] = jnp.zeros_like(qv_sums)
    qv_sums[0:1, :] = jnp.sum(dq.astype(jnp.float32), axis=0, keepdims=True)
    for p in range(pairs):
        at = slice(128 * p, 128 * (p + 1))
        dkv_out[:, at] = dk[p].astype(jnp.bfloat16)
        value = dv[p].astype(jnp.bfloat16)
        dkv_out[:, half + 128 * p : half + 128 * (p + 1)] = value
        qv_sums[1:2, at] = jnp.sum(value.astype(jnp.float32), axis=0, keepdims=True)


def input_grad_kernel(dq, dkv, w, *refs):
    sends, (keep, whole) = refs[:2], refs[2:]
    q, r, x, c = spot()
    half = dq.shape[1]
    rows = dq.shape[0] // 2
    whole[...] = dot_nt(dkv[...], w[:, half:])
    own = pl.ds(pl.multiple_of(rows * (4 * r + 2 * c), rows), 2 * rows)
    whole[own, :] += dot_nt(dq[...], w[:, 0:half])
    for b in range(2):
        for i in range(2):
            to = slice(2 * rows * b + rows * i, 2 * rows * b + rows * (i + 1))
            mine = pl.ds(pl.multiple_of(rows * (4 * i + 2 * c + b), rows), rows)
            keep[to, :] = whole[mine, :]
            theirs = pl.ds(pl.multiple_of(rows * (4 * i + 2 * (1 - c) + b), rows), rows)
            sends[b][rows * i : rows * (i + 1), :] = whole[theirs, :].astype(jnp.bfloat16)


def input_x_kernel(keep, got0, got1, send, kept):
    q, r, x, c = spot()
    half = send.shape[0]
    for side, got in enumerate((got0, got1)):
        total = keep[half * side : half * (side + 1), :] + got[...].astype(jnp.float32)

        @pl.when(x == side)
        def _():
            kept[...] = total

        @pl.when(x != side)
        def _():
            send[...] = total.astype(jnp.bfloat16)


def octants():
    for at in range(8):
        r, q0, q1 = at >> 2, at >> 1 & 1, at & 1
        yield 4 * r + 2 * q0 + 1 * q1, 1 * r + 4 * q0 + 2 * q1, 4 * r + 2 * q1 + q0


def down_grad_kernel(z, dy, send, keep):
    q, r, x, c = spot()
    half = z.shape[1] // 2
    rows = half // 8
    for side, out in ((1 - c, send), (c, keep)):
        part = dot_tn(z[:, pl.ds(pl.multiple_of(half * side, 128), half)], dy[...])
        for at, _, within in octants():
            block = part[rows * within : rows * (within + 1), :]
            out[rows * at : rows * (at + 1), :] = block.astype(out.dtype)


def up_grad_kernel(h, du, *refs):
    q, r, x, c = spot()
    sends, (keep, whole) = refs[:4], refs[4:]
    width = h.shape[1]
    thin = width // 32
    whole[...] = dot_tn(h[...], du[...])
    for side in (1 - c, c):
        for _, at, within in octants():
            pieces = []
            for xx in range(2):
                first = 8 * thin * (2 * xx + side) + thin * within
                rows = pl.ds(pl.multiple_of(first, 8), thin)
                pieces += [whole[rows, 0:width], whole[rows, width:]]
            block = jnp.concatenate(pieces)
            if side is c:
                keep[4 * thin * at : 4 * thin * (at + 1), :] = block
            else:
                to = 4 * thin * (at % 2)
                sends[at // 2][to : to + 4 * thin, :] = block.astype(jnp.bfloat16)


def join_kernel(*refs):
    out, at = refs[-1], 0
    for ref in refs[:-1]:
        count = ref.shape[0]
        out[at : at + count, :] = ref[...]
        at += count


def fold_pieces_kernel(bit, count, keep, *refs):
    gots, sends, (kept, whole) = refs[: -2 - count], refs[-2 - count : -2], refs[-2:]
    at = bit(*spot())
    first = 0
    for got in gots:
        rows = slice(first, first + got.shape[0])
        whole[rows, :] = keep[rows, :] + got[...].astype(jnp.float32)
        first += got.shape[0]
    half = kept.shape[0]
    kept[...] = whole[pl.ds(pl.multiple_of(half * at, 64), half), :]
    for i, send in enumerate(sends):
        rows = pl.ds(pl.multiple_of(half * (1 - at) + half // count * i, 64), half // count)
        send[...] = whole[rows, :].astype(send.dtype)


def fold_kernel(bit, keep, got, send, kept):
    at = bit(*spot())
    send[...] = (keep[1 - at] + got[1 - at].astype(jnp.float32)).astype(send.dtype)
    kept[...] = keep[at] + got[at].astype(jnp.float32)


def copy_kernel(block, out):
    out[...] = block[...]


def sum_kernel(keep, got, out):
    out[...] = (keep[...] + got[...].astype(jnp.float32)).astype(out.dtype)


def total_kernel(keep, got, more, out):
    out[...] = (keep[...] + got[...].astype(jnp.float32) + more[...]).astype(out.dtype)


def share_kernel(keep, got, side, base):
    q, r, x, c = spot()
    side[...] = (keep[1 - x] + got[1 - x].astype(jnp.float32)).astype(side.dtype)
    base[...] = (keep[x] + got[x].astype(jnp.float32)).astype(base.dtype)


def weight_grad_kernel(
    xs, dkv, dq, mixed, da, sums1, sums2, qv_sums, up_sums, *refs
):
    sends, (keep, packed) = refs[:-2], refs[-2:]
    q, r, x, c = spot()
    width = xs.shape[1]
    own, half = dq.shape
    thin = width // 32
    for_c = 64 * thin
    own_rows = pl.ds(pl.multiple_of(own * (2 * r + c), own), own)
    asked = dot_tn(xs[own_rows, :], dq[...])
    kept = dot_tn(xs[...], dkv[...])
    outer = dot_tn(mixed[...], da[...])
    for cc in range(2):
        for rr in range(2):
            for q1 in range(2):
                for q0 in range(2):
                    at = ((4 * rr + 2 * q0 + 1 * q1) * 8) * thin
                    within = (4 * rr + 2 * q1 + q0) * thin
                    for xx in range(2):
                        rows = slice((16 * xx + 8 * cc) * thin + within, (16 * xx + 8 * cc + 1) * thin + within)
                        for t, piece in enumerate((asked, kept[:, 0:half], kept[:, half:])):
                            to = at + (3 * xx + t) * thin
                            packed[cc, to : to + thin, :] = piece[rows, :]
                    rows = slice(8 * cc * thin + within, (8 * cc + 1) * thin + within)
                    for t in range(2):
                        to = at + (6 + t) * thin
                        packed[cc, to : to + thin, :] = outer[rows, half * t : half * (t + 1)]
    columns = pl.ds(pl.multiple_of(half * x, 128), half)
    for cc in range(2):
        packed[cc, for_c : for_c + 16, :] = jnp.zeros((16, half), jnp.float32)
        packed[cc, for_c : for_c + 2, :] = qv_sums[0:2, :]
        for j in range(4):
            packed[cc, for_c + 2 + j : for_c + 3 + j, :] = up_sums[j, 0:1, :]
        packed[cc, for_c + 6 : for_c + 9, :] = sums1[0:3, columns]
        packed[cc, for_c + 9 : for_c + 12, :] = sums2[0:3, columns]
    first = 0
    for send in sends:
        count = send.shape[0]
        send[...] = packed[1 - c, first : first + count, :].astype(jnp.bfloat16)
        first += count
    keep[...] = packed[c]


def step_kernel(bit, keep, *refs):
    gots, (send, kept, whole) = refs[:-3], refs[-3:]
    at = bit(*spot())
    count = send.shape[0] - 16
    first = 0
    for got in gots:
        rows = slice(first, first + got.shape[0])
        whole[rows, :] = keep[rows, :] + got[...].astype(jnp.float32)
        first += got.shape[0]
    theirs = pl.ds(pl.multiple_of(count * (1 - at), 64), count)
    mine = pl.ds(pl.multiple_of(count * at, 64), count)
    send[0:count, :] = whole[theirs, :].astype(jnp.bfloat16)
    send[count:, :] = whole[2 * count :, :].astype(jnp.bfloat16)
    kept[0:count, :] = whole[mine, :]
    kept[count:, :] = whole[2 * count :, :]


def last_step_kernel(keep, got, side, base, *refs):
    out, b_up, whole = refs[:8], refs[8], refs[9]
    q, r, x, c = spot()
    count = side.shape[0]
    part = out[0].shape[0]
    whole[...] = keep[...] + got[...].astype(jnp.float32)
    theirs = pl.ds(pl.multiple_of(count * (1 - x), 8), count)
    mine = pl.ds(pl.multiple_of(count * x, 8), count)
    side[...] = whole[theirs, :].astype(jnp.bfloat16)
    first = whole.shape[0] - 16
    base[...] = jnp.concatenate([whole[mine, :], whole[2 * count : first, :]]).astype(jnp.bfloat16)
    for i, one in enumerate(out):
        at = first + (i if i < 2 else i + 4)
        line = whole[at : at + 1, :]
        one[...] = jnp.where(c == 0, line[:, :part], line[:, part:]).reshape(part)
    line = jnp.concatenate([whole[pl.ds(first + 2 + 2 * c + i, 1), :] for i in range(2)], axis=1)
    b_up[...] = line.reshape(b_up.shape[0])


def down_out_kernel(near, far, out, mark):
    mark[...] = jnp.zeros_like(mark)
    q, r, x, c = spot()
    count = near.shape[0] // 4
    for d, piece in enumerate((near, far)):
        for k in range(4):
            at = 4 * (r ^ d) + 2 * ((q // 2) ^ (k & 1)) + ((q % 2) ^ (k >> 1))
            rows = pl.ds(pl.multiple_of(count * at, 32), count)
            out[rows, :] = piece[count * k : count * (k + 1), :].astype(jnp.float32)


def up_out_kernel(near, far, out, mark, whole):
    mark[...] = jnp.zeros_like(mark)
    q, r, x, c = spot()
    thin, width = near.shape[0] // 16, near.shape[1]
    for d, piece in enumerate((near, far)):
        whole[...] = piece[...].astype(jnp.float32)
        for k in range(4):
            at = 4 * (r ^ d) + 2 * ((q // 2) ^ (k & 1)) + ((q % 2) ^ (k >> 1))
            rows = pl.ds(pl.multiple_of(thin * at, 8), thin)
            for s in range(4):
                columns = pl.ds(pl.multiple_of(width * (2 * (x ^ (s >> 1)) + (s & 1)), 128), width)
                first = thin * (4 * k + s)
                out[rows, columns] = whole[first : first + thin, :]


def rest_out_kernel(near, far, hidden, total, out_q, out_k, out_v, out_o, out_h, out_t, whole):
    out_h[...] = hidden[...]
    out_t[...] = total[...]
    q, r, x, c = spot()
    half = near.shape[1]
    thin = near.shape[0] // 32
    ours = pl.ds(pl.multiple_of(half * x, 128), half)
    other = pl.ds(pl.multiple_of(half * (1 - x), 128), half)
    for d, piece in enumerate((near, far)):
        whole[...] = piece[...].astype(jnp.float32)
        for k in range(4):
            at = 4 * (r ^ d) + 2 * ((q // 2) ^ (k & 1)) + ((q % 2) ^ (k >> 1))
            rows = pl.ds(pl.multiple_of(thin * at, 8), thin)
            first = 8 * thin * k
            for t, out in enumerate((out_q, out_k, out_v)):
                out[rows, ours] = whole[first + thin * t : first + thin * (t + 1), :]
                out[rows, other] = whole[first + thin * (5 + t) : first + thin * (6 + t), :]
            for t in range(2):
                columns = slice(half * t, half * (t + 1))
                out_o[rows, columns] = whole[first + thin * (3 + t) : first + thin * (4 + t), :]


def kernel_call(body, name, ins, outs, scratch, args, after=(), room=2 << 20, cost=1):
    count = len(args)

    def size(shape, dtype):
        return math.prod(shape) * jnp.dtype(dtype).itemsize

    used = sum(size(m.shape, m.dtype) for m in scratch if m.memory_space == pltpu.VMEM)

    args = [
        pltpu.with_memory_space_constraint(a, pltpu.HBM) if spec is HBM else a
        for a, spec in zip(args, ins)
    ]

    def run(*refs):
        body(*refs[:count], *refs[count + len(after) :])

    return pl.pallas_call(
        run,
        name=name,
        out_shape=[jax.ShapeDtypeStruct(shape, dtype) for shape, dtype, _ in outs],
        in_specs=list(ins) + [ANY] * len(after),
        out_specs=[spec for _, _, spec in outs],
        scratch_shapes=scratch,
        cost_estimate=pl.CostEstimate(flops=cost, bytes_accessed=1, transcendentals=0),
        compiler_params=pltpu.CompilerParams(vmem_limit_bytes=used + room),
    )(*args, *after)


def once(value, *after):
    return pl.pallas_call(
        lambda *refs: None,
        name="once",
        out_shape=jax.ShapeDtypeStruct(value.shape, value.dtype),
        in_specs=[ANY] * (1 + len(after)),
        out_specs=ANY,
        input_output_aliases={0: 0},
        cost_estimate=pl.CostEstimate(flops=1, bytes_accessed=1, transcendentals=0),
        compiler_params=pltpu.CompilerParams(vmem_limit_bytes=1 << 18),
    )(value, *after)


HEAVY = ('attend_back', 'down_sum', 'input_sum', 'project', 'rest_3')


def plane_local(
    tokens, cotangent, seq_ids, w_query, b_query, w_key, w_value, b_value, w_out, b_out,
    attn_gain, attn_shift, w_up, b_up, w_down, b_down, ffn_gain, ffn_shift,
):
    low, exact = jnp.bfloat16, jnp.float32
    rows, width = tokens.shape[1:]
    part = w_query.shape[0]
    half = width // 2
    inner = w_up.shape[1]
    wide = inner // 8
    keys = 8 * rows
    own = 2 * rows
    pairs = half // 128

    latest = []

    def call(body, name, ins, outs, scratch, args, after=(), **more):
        cost = 10**10 if name in HEAVY else 1
        results = kernel_call(
            body, name, ins, outs, scratch, args, tuple(after) + tuple(latest), cost=cost, **more
        )
        latest[:] = results[-1:] if name.endswith("_out") else results[:1]
        return results

    (block,) = call(
        block_kernel, "block", [HBM] * 2, [((rows + 16, width), low, WHOLE)],
        [pltpu.VMEM((1, rows), jnp.int32), pltpu.SemaphoreType.DMA((2,))],
        (tokens[0], seq_ids),
    )
    block = regroup(block)
    theirs, mine = call(
        pack_kernel,
        "pack",
        [HBM] * 12,
        [((3 * part + 16, half), low, WHOLE)] * 2,
        [pltpu.VMEM((16, half), exact)]
        + [pltpu.VMEM((part,), low)] * 8
        + [pltpu.VMEM((width,), low), pltpu.SemaphoreType.DMA((15,))],
        (w_query, w_key, w_value, b_query, b_value, b_out, attn_gain, attn_shift, b_down, ffn_gain, ffn_shift, b_up),
    )
    qkv_x = swap_x(theirs)
    qkv_m = swap_c(mine)
    out_m = swap_c(w_out)
    blocks = [once(block, qkv_m, qkv_x, out_m)]
    beside_r = swap_r(blocks[0])
    blocks.append(once(swap_x(blocks[0]), beside_r))
    blocks.append(swap_c(blocks[0]))
    blocks.append(swap_c(blocks[1]))
    blocks.append(beside_r)
    blocks.append(swap_r(blocks[1]))
    qkv_mx = swap_c(qkv_x)
    up_theirs, up_mine = call(
        cut_kernel, "cut", [HBM], [((part, 4 * wide), low, WHOLE)] * 2, [pltpu.SemaphoreType.DMA((2,))],
        (w_up,), after=(blocks[1],),
    )
    up_x = swap_x(up_theirs)
    up_m = swap_c(up_mine)
    down_m = swap_c(w_down)
    (cot,) = call(
        load_kernel, "cotangent", [HBM], [((rows, width), low, WHOLE)], [pltpu.SemaphoreType.DMA((1,))],
        (cotangent[0],),
    )
    kv_own, q_own, w_all, vecs, up_bias = call(
        project_kernel,
        "project",
        [WHOLE] * 4 + [HBM] * 3 + [WHOLE] * 4,
        [
            ((4 * rows, width), low, WHOLE),
            ((own, half), low, WHOLE),
            ((width, 3 * half), low, WHOLE),
            ((8, width), exact, WHOLE),
            ((4, 8, wide), exact, WHOLE),
        ],
        [pltpu.VMEM((4 * rows, width), low), pltpu.SemaphoreType.DMA((3,))],
        (*blocks[:4], w_query, w_key, w_value, qkv_x, qkv_m, qkv_mx, mine),
        room=8 << 20,
    )
    blocks[5] = once(blocks[5], kv_own)
    blocks.append(swap_c(blocks[4]))
    blocks.append(swap_c(blocks[5]))
    a_low, x_all, wo_all, k3, v3, q3, mixed, lse, ids, a_own = call(
        attend_kernel,
        "attend",
        [WHOLE] * 12 + [HBM, WHOLE],
        [
            ((own, width), low, WHOLE),
            ((keys, width), low, WHOLE),
            ((half, width), low, WHOLE),
            ((pairs, keys, 128), low, WHOLE),
            ((pairs, keys, 128), low, WHOLE),
            ((pairs, own, 128), low, WHOLE),
            ((own, half), low, WHOLE),
            ((8, own), exact, WHOLE),
            ((8, rows), exact, WHOLE),
            ((own, width), exact, WHOLE),
        ],
        [
            pltpu.VMEM((2 * pairs, 64, keys), low),
            pltpu.VMEM((2 * pairs, 64, own), exact),
            pltpu.VMEM((keys, own), exact),
            pltpu.SemaphoreType.DMA((1,)),
        ],
        (*blocks, kv_own, q_own, w_all, vecs, w_out, out_m),
        after=(down_m,),
        room=8 << 20,
    )
    a_got = swap_x(a_low)
    (kt,) = call(turn_kernel, "turn", [WHOLE], [((2 * pairs, 64, keys), low, WHOLE)], [], (k3,),
        after=(up_m,))

    up_x = once(up_x, kt)
    up_mx = [swap_c(piece) for piece in (up_x[: part // 2], up_x[part // 2 :])]
    inner_weights = call(
        inner_kernel,
        "inner",
        [HBM] + [WHOLE] * 4 + [HBM, WHOLE],
        [((width, 4 * wide), low, WHOLE), ((4 * wide, width), low, WHOLE)],
        [pltpu.SemaphoreType.DMA((2,))],
        (w_up, up_x, up_m, *up_mx, w_down, down_m),
    )
    cot = once(cot, inner_weights[0])
    cot, cot_x = regroup(cot), regroup_x(cot)
    y_low, y_more, h_low, z, normed1, rstd1, slope, y_own = call(
        forward_kernel,
        "feedforward",
        [WHOLE] * 7,
        [
            ((rows, width), low, WHOLE),
            ((rows, width), low, WHOLE),
            ((own, width), low, WHOLE),
            ((own, 4 * wide), low, WHOLE),
            ((own, width), exact, WHOLE),
            ((own, 128), exact, WHOLE),
            ((own, 4 * wide), exact, WHOLE),
            ((own, width), exact, WHOLE),
        ],
        [],
        (a_own, a_got, x_all, vecs, up_bias, *inner_weights),
        room=8 << 20,
    )
    y_got, y_rest = swap_x(y_low), swap_x(y_more)
    dy_low, hidden, dy, sums2 = call(
        norm_back_kernel,
        "norm_back",
        [WHOLE] * 7,
        [
            ((own, width), low, WHOLE),
            ((rows, width), low, WHOLE),
            ((own, width), exact, WHOLE),
            ((8, width), exact, WHOLE),
        ],
        [
            pltpu.VMEM((own, width), low),
            pltpu.VMEM((own, width), low),
        ],
        (y_own, y_got, y_rest, normed1, cot, cot_x, vecs),
        room=6 << 20,
    )
    eighth = wide // 4
    down_send, down_keep = call(
        down_grad_kernel,
        "down_grad",
        [WHOLE] * 2,
        [((8 * eighth, width), low, WHOLE), ((8 * eighth, width), exact, WHOLE)],
        [],
        (z, dy_low),
        room=8 << 20,
    )
    down_got = swap_c(down_send)
    p_low, s_own, du, up_sums = call(
        backward_kernel,
        "feedforward_back",
        [WHOLE] * 5,
        [
            ((own, width), low, WHOLE),
            ((own, width), exact, WHOLE),
            ((own, 4 * wide), low, WHOLE),
            ((4, 8, wide), exact, WHOLE),
        ],
        [],
        (dy, dy_low, slope, *inner_weights),
        room=8 << 20,
    )
    p_got = swap_x(p_low)
    hidden = regroup(hidden)

    def fold(name, bit, keep, got):
        shape = (keep.shape[0] // 2, keep.shape[1])
        return call(
            lambda *refs: fold_kernel(bit, *refs),
            name,
            [WHOLE] * 2,
            [(shape, low, WHOLE), (shape, exact, WHOLE)],
            [],
            (keep.reshape(2, *shape), got.reshape(2, *shape)),
            room=4 << 20,
        )

    def fold_into(count, name, bit, keep, gots):
        half_rows = keep.shape[0] // 2
        *sends, kept = call(
            lambda *refs: fold_pieces_kernel(bit, count, *refs),
            name,
            [WHOLE] * (1 + len(gots)),
            [((half_rows // count, width), low, WHOLE)] * count + [((half_rows, width), exact, WHOLE)],
            [pltpu.VMEM(keep.shape, exact)],
            (keep, *gots),
            room=4 << 20,
        )
        return sends, kept

    def bit_r(q, r, x, c):
        return r

    def bit_near(q, r, x, c):
        return q % 2

    def bit_far(q, r, x, c):
        return q // 2

    thin = part // 8
    count = 64 * thin

    def step(name, bit, keep, size, *gots):
        return call(
            lambda *refs: step_kernel(bit, *refs),
            name,
            [WHOLE] * (1 + len(gots)),
            [((size + 16, half), low, WHOLE), ((size + 16, half), exact, WHOLE)],
            [pltpu.VMEM((2 * size + 16, half), exact)],
            (keep, *gots),
        )

    def join(name, *pieces):
        shape = (sum(p.shape[0] for p in pieces), pieces[0].shape[1])
        (out,) = call(join_kernel, name, [WHOLE] * len(pieces), [(shape, low, WHOLE)], [], pieces)
        return out

    cuts = (count // 3, count // 3, count - 2 * (count // 3) + 16)
    down_sends, down_keep = fold_into(2, "down_1", bit_r, down_keep, (down_got,))
    down_gots = [swap_r(send) for send in down_sends]
    *up_sends, up_keep = call(
        up_grad_kernel,
        "up_grad",
        [WHOLE] * 2,
        [((2 * eighth, width), low, WHOLE)] * 4 + [((8 * eighth, width), exact, WHOLE)],
        [pltpu.VMEM((width, 4 * wide), exact)],
        (h_low, du),
        room=8 << 20,
    )
    up_gots = [swap_c(send) for send in up_sends]
    (up_send,), up_keep = fold_into(1, "up_1", bit_near, up_keep, up_gots)
    up_got = swap_near(up_send)
    dkv, dq, dr, da, sums1, qv_sums = call(
        attend_back_kernel,
        "attend_back",
        [WHOLE] * 13,
        [
            ((keys, 2 * half), low, WHOLE),
            ((own, half), low, WHOLE),
            ((rows, width), exact, WHOLE),
            ((own, width), low, WHOLE),
            ((8, width), exact, WHOLE),
            ((8, half), exact, WHOLE),
        ],
        [
            pltpu.VMEM((keys, own), exact),
            pltpu.VMEM((pairs, own, 128), low),
            pltpu.VMEM((8, own), exact),
            pltpu.VMEM((pairs, keys, 128), exact),
            pltpu.VMEM((pairs, keys, 128), exact),
            pltpu.VMEM((2 * pairs, 64, own), exact),
            pltpu.VMEM((own, width), exact),
        ],
        (s_own, p_got, normed1, rstd1, vecs, wo_all, mixed, q3, k3, v3, kt, lse, ids),
        room=8 << 20,
    )

    (down_send,), down_keep = fold_into(1, "down_2", bit_near, down_keep, down_gots)
    down_got = swap_near(down_send)
    *rest_sends, rest_keep = call(
        weight_grad_kernel,
        "weight_grad",
        [WHOLE] * 9,
        [((n, half), low, WHOLE) for n in cuts] + [((count + 16, half), exact, WHOLE)],
        [pltpu.VMEM((2, count + 16, half), exact)],
        (x_all, dkv, dq, mixed, da, sums1, sums2, qv_sums, up_sums),
        after=(hidden,),
        room=8 << 20,
    )
    rest_gots = [swap_c(send) for send in rest_sends]
    rest_send, rest_keep = step("rest_1", bit_r, rest_keep, count // 2, *rest_gots)
    rest_got = swap_r(rest_send)
    up_send, up_keep = fold("up_2", bit_far, up_keep, up_got)
    up_got = swap_far(up_send)
    *x_sends, x_keep = call(
        input_grad_kernel,
        "input_grad",
        [WHOLE] * 3,
        [((own, width), low, WHOLE)] * 2 + [((2 * own, width), exact, WHOLE)],
        [pltpu.VMEM((keys, width), exact)],
        (dq, dkv, w_all),
        room=8 << 20,
    )
    x_gots = [swap_c(send) for send in x_sends]
    down_send, down_keep = fold("down_3", bit_far, down_keep, down_got)
    down_got = swap_far(down_send)
    x_send, x_keep = call(
        input_x_kernel,
        "input_x",
        [WHOLE] * 3,
        [((own, width), low, WHOLE), ((own, width), exact, WHOLE)],
        [],
        (x_keep, *x_gots),
        room=4 << 20,
    )
    x_got = swap_x(x_send)
    up_send, up_keep = fold("up_3", bit_r, up_keep, up_got)
    up_got = swap_r(up_send)
    (down_sum,) = call(
        sum_kernel, "down_sum", [WHOLE] * 2, [((eighth, width), low, WHOLE)], [], (down_keep, down_got)
    )
    down_other = swap_far(down_sum)
    side, base = call(
        share_kernel,
        "up_share",
        [WHOLE] * 2,
        [((eighth // 2, width), low, WHOLE)] * 2,
        [],
        (up_keep.reshape(2, eighth // 2, width), up_got.reshape(2, eighth // 2, width)),
    )
    side = swap_x(side)
    rest_send, rest_keep = step("rest_2", bit_near, rest_keep, count // 4, rest_got)
    rest_got = swap_near(rest_send)
    x_send, x_keep = fold("input_r", bit_r, x_keep, x_got)
    x_got = swap_r(x_send)
    down_sum = join("down_join", down_sum, down_other)
    down_other = swap_near(down_sum)
    rest_send, rest_keep = step("rest_3", bit_far, rest_keep, count // 8, rest_got)
    rest_got = swap_far(rest_send)
    up_sum = join("up_join", base, side)
    up_other = swap_far(up_sum)
    (total,) = call(
        total_kernel, "input_sum", [WHOLE] * 3, [((rows, width), low, WHOLE)], [], (x_keep, x_got, dr)
    )
    total = regroup(total)
    rest_side, rest_base, *lines, b_up_grad = call(
        last_step_kernel,
        "rest_last",
        [WHOLE] * 2,
        [((3 * thin, half), low, WHOLE), ((5 * thin, half), low, WHOLE)]
        + [((part,), exact, WHOLE)] * 8
        + [((2 * wide,), exact, WHOLE)],
        [pltpu.VMEM((8 * thin + 16, half), exact)],
        (rest_keep, rest_got),
    )
    rest_side = swap_x(rest_side)
    down_near = join("down_join_near", down_sum, down_other)
    down_far = swap_r(down_near)
    up_sum = join("up_join_far", up_sum, up_other)
    up_other = swap_near(up_sum)
    rest_sum = join("rest_join", rest_base, rest_side)
    rest_other = swap_far(rest_sum)
    rest_sum = join("rest_join_far", rest_sum, rest_other)
    rest_other = swap_near(rest_sum)
    w_down_grad, _ = call(
        down_out_kernel, "down_out", [WHOLE] * 2,
        [((2 * wide, width), exact, WHOLE), ((8, 128), exact, WHOLE)], [], (down_near, down_far),
        room=6 << 20,
    )
    up_near = join("up_join_near", up_sum, up_other)
    up_far = swap_r(up_near)
    rest_near = join("rest_join_near", rest_sum, rest_other)
    rest_far = swap_r(rest_near)
    w_up_grad, _ = call(
        up_out_kernel, "up_out", [WHOLE] * 2, [((part, inner), exact, WHOLE), ((8, 128), exact, WHOLE)],
        [pltpu.VMEM((4 * eighth, width), exact)], (up_near, up_far),
        room=6 << 20,
    )


    w_query_grad, w_key_grad, w_value_grad, w_out_grad, hidden_out, tokens_grad = call(
        rest_out_kernel,
        "rest_out",
        [WHOLE] * 4,
        [((part, width), exact, WHOLE)] * 4 + [((rows, width), low, WHOLE)] * 2,
        [pltpu.VMEM((32 * thin, half), exact)],
        (rest_near, rest_far, hidden, total),
        room=6 << 20,
    )

    return (
        hidden_out[None],
        tokens_grad[None],
        w_query_grad,
        lines[0],
        w_key_grad,
        w_value_grad,
        lines[1],
        w_out_grad,
        lines[2],
        lines[3],
        lines[4],
        w_up_grad,
        b_up_grad,
        w_down_grad,
        lines[5],
        lines[6],
        lines[7],
    )


def plane_solution(mesh):
    planes, cycle = mesh.shape["shard"], mesh.shape["ctx"]
    grid = Mesh(mesh.devices.reshape(planes, cycle // planes, 2, 2), AXES)
    shard, ctx = ("x", "c"), ("q", "r")
    tokens, matrix, vector = P(shard, ctx, None), P(shard, None), P(shard)
    return jax.shard_map(
        plane_local,
        mesh=grid,
        in_specs=(
            tokens, tokens, P(shard, ctx), matrix, vector, matrix, matrix, vector, matrix, vector,
            vector, vector, matrix, vector, matrix, vector, vector, vector,
        ),
        out_specs=(
            tokens, tokens, matrix, vector, matrix, matrix, vector, matrix, vector,
            vector, vector, matrix, vector, matrix, vector, vector, vector,
        ),
        check_vma=False,
    )


def solution(mesh):
    if mesh.shape["shard"] == 4 and mesh.shape["ctx"] == 8:
        return plane_solution(mesh)
    return ring_solution(mesh)
```

```python
import math

import jax
import jax.numpy as jnp
from jax import lax
from jax.experimental import pallas as pl
from jax.experimental.pallas import tpu as pltpu
from jax.sharding import Mesh
from jax.sharding import PartitionSpec as P

HEAD_DIM = 64


ln_eps = 1e-12
masked_fill = -1e30


def from_behind(block, axis, distance):
    devices = range(lax.axis_size(axis))
    route = [((i - distance) % len(devices), i) for i in devices]
    return lax.ppermute(block, axis, route)


def matmul(left, right):
    return jnp.dot(left, right, preferred_element_type=jnp.float32)


def matmul_tn(left, right):
    return lax.dot_general(
        left, right, (((0,), (0,)), ((), ())), preferred_element_type=jnp.float32
    )


def matmul_nt(left, right):
    return lax.dot_general(
        left, right, (((1,), (1,)), ((), ())), preferred_element_type=jnp.float32
    )


def apply_layer_norm(value, gain, shift):
    mean = jnp.mean(value, axis=-1, keepdims=True)
    centered = value - mean
    rstd = lax.rsqrt(jnp.mean(centered * centered, axis=-1, keepdims=True) + ln_eps)
    normed = centered * rstd
    return (normed * gain + shift, normed, rstd)


def norm_back(grad, normed, rstd, gain):
    d_gain = jnp.sum(grad * normed, axis=0)
    d_shift = jnp.sum(grad, axis=0)
    scaled = grad * gain
    d_value = rstd * (
        scaled
        - jnp.mean(scaled, axis=-1, keepdims=True)
        - normed * jnp.mean(scaled * normed, axis=-1, keepdims=True)
    )
    return (d_value, d_gain, d_shift)


def gelu_slope(value):
    normal_cdf = 0.5 * (1.0 + lax.erf(value * (1.0 / math.sqrt(2.0))))
    density = jnp.exp(-0.5 * value * value) * (1.0 / math.sqrt(2.0 * math.pi))
    return normal_cdf + value * density


def scores_of(query, keys, q_ids, k_ids, scale):
    raw = jnp.einsum("qhd,khd->hqk", query, keys, preferred_element_type=jnp.float32) * scale
    match = (q_ids[:, None] == k_ids[None, :])[None, :, :]
    return (raw, match)


def attend(query, q_ids, keys, values, k_ids, stats, scale):
    top, total, accum = stats
    raw, match = scores_of(query, keys, q_ids, k_ids, scale)
    masked = jnp.where(match, raw, masked_fill)
    new_top = jnp.maximum(top, jnp.max(masked, axis=-1))
    weights = jnp.where(match, jnp.exp(masked - new_top[:, :, None]), 0.0)
    factor = jnp.exp(top - new_top)
    total = total * factor + jnp.sum(weights, axis=-1)
    accum = accum * factor[:, :, None] + jnp.einsum(
        "hqk,khd->hqd", weights.astype(jnp.bfloat16), values, preferred_element_type=jnp.float32
    )
    return (new_top, total, accum)


def block_grads(query, q_ids, d_out, log_total, delta, keys, values, k_ids, scale):
    raw, match = scores_of(query, keys, q_ids, k_ids, scale)
    probs = jnp.exp(jnp.where(match, raw - log_total[:, :, None], masked_fill))
    d_values = jnp.einsum(
        "hqk,qhd->khd", probs.astype(jnp.bfloat16), d_out, preferred_element_type=jnp.float32
    )
    d_probs = jnp.einsum("qhd,khd->hqk", d_out, values, preferred_element_type=jnp.float32)
    d_scores = (probs * (d_probs - delta[:, :, None])).astype(jnp.bfloat16)
    d_query = jnp.einsum("hqk,khd->qhd", d_scores, keys, preferred_element_type=jnp.float32) * scale
    d_keys = jnp.einsum("hqk,qhd->khd", d_scores, query, preferred_element_type=jnp.float32) * scale
    return (d_query, d_keys, d_values)


def ring_local(
    tokens,
    cotangent,
    seq_ids,
    w_query,
    b_query,
    w_key,
    w_value,
    b_value,
    w_out,
    b_out,
    attn_gain,
    attn_shift,
    w_up,
    b_up,
    w_down,
    b_down,
    ffn_gain,
    ffn_shift,
):
    cycle = lax.axis_size("ctx")
    tok_rows = tokens.shape[1]
    width = tokens.shape[2]
    heads = width // HEAD_DIM
    scale = 1.0 / math.sqrt(HEAD_DIM)
    share = tok_rows // cycle
    got_tokens, got_grads, got_ids = (
        lax.all_to_all(
            tokens[0].reshape(share, cycle, width), "ctx", split_axis=1, concat_axis=1, tiled=True
        ),
        lax.all_to_all(
            cotangent[0].reshape(share, cycle, width),
            "ctx",
            split_axis=1,
            concat_axis=1,
            tiled=True,
        ),
        lax.all_to_all(
            seq_ids[0].reshape(share, cycle), "ctx", split_axis=1, concat_axis=1, tiled=True
        ),
    )
    x_local = got_tokens.reshape(tok_rows, width)
    local_gradient = got_grads.reshape(tok_rows, width).astype(jnp.float32)
    local_ids = got_ids.reshape(tok_rows)
    (
        query_mat,
        query_bias,
        key_mat,
        value_mat,
        value_bias,
        out_mat,
        out_bias,
        attention_norm_gain,
        first_shift,
        up_mat,
        up_bias,
        down_mat,
        down_bias,
        feedforward_norm_gain,
        second_shift,
    ) = (
        lax.all_gather(w_query, "shard", axis=0, tiled=True),
        lax.all_gather(b_query, "shard", axis=0, tiled=True),
        lax.all_gather(w_key, "shard", axis=0, tiled=True),
        lax.all_gather(w_value, "shard", axis=0, tiled=True),
        lax.all_gather(b_value, "shard", axis=0, tiled=True),
        lax.all_gather(w_out, "shard", axis=0, tiled=True),
        lax.all_gather(b_out, "shard", axis=0, tiled=True),
        lax.all_gather(attn_gain, "shard", axis=0, tiled=True),
        lax.all_gather(attn_shift, "shard", axis=0, tiled=True),
        lax.all_gather(w_up, "shard", axis=0, tiled=True),
        lax.all_gather(b_up, "shard", axis=0, tiled=True),
        lax.all_gather(w_down, "shard", axis=0, tiled=True),
        lax.all_gather(b_down, "shard", axis=0, tiled=True),
        lax.all_gather(ffn_gain, "shard", axis=0, tiled=True),
        lax.all_gather(ffn_shift, "shard", axis=0, tiled=True),
    )
    query = (matmul(x_local, query_mat) + query_bias.astype(jnp.float32)).astype(jnp.bfloat16)
    keys = matmul(x_local, key_mat).astype(jnp.bfloat16)
    values = (matmul(x_local, value_mat) + value_bias.astype(jnp.float32)).astype(jnp.bfloat16)
    q_heads = query.reshape(tok_rows, heads, HEAD_DIM)
    start_stats = (
        jnp.full((heads, tok_rows), masked_fill, jnp.float32),
        jnp.zeros((heads, tok_rows), jnp.float32),
        jnp.zeros((heads, tok_rows, HEAD_DIM), jnp.float32),
    )

    def forward_step(step, carry):
        block, stats = carry
        stats = attend(
            q_heads,
            local_ids,
            block[0].reshape(tok_rows, heads, HEAD_DIM),
            block[1].reshape(tok_rows, heads, HEAD_DIM),
            block[2],
            stats,
            scale,
        )
        block = from_behind((block[0], block[1], block[2]), "ctx", 1)
        return (block, stats)

    block, stats = lax.fori_loop(
        0, cycle - 1, forward_step, ((keys, values, local_ids), start_stats)
    )
    top, total, accum = attend(
        q_heads,
        local_ids,
        block[0].reshape(tok_rows, heads, HEAD_DIM),
        block[1].reshape(tok_rows, heads, HEAD_DIM),
        block[2],
        stats,
        scale,
    )
    attn_out = (
        (accum / total[:, :, None]).transpose(1, 0, 2).reshape(tok_rows, width).astype(jnp.bfloat16)
    )
    log_total = top + jnp.log(total)
    attn_proj = matmul(attn_out, out_mat) + out_bias.astype(jnp.float32)
    first_sum = x_local.astype(jnp.float32) + attn_proj
    first_normalized_rows, first_centered_scaled, first_inverse_deviation = apply_layer_norm(
        first_sum, attention_norm_gain.astype(jnp.float32), first_shift.astype(jnp.float32)
    )
    normed_low = first_normalized_rows.astype(jnp.bfloat16)
    up_pre = matmul(normed_low, up_mat) + up_bias.astype(jnp.float32)
    up_act = jax.nn.gelu(up_pre, approximate=False).astype(jnp.bfloat16)
    down_pre = matmul(up_act, down_mat) + down_bias.astype(jnp.float32)
    layer_output, second_centered_scaled, second_inverse_deviation = apply_layer_norm(
        first_normalized_rows + down_pre,
        feedforward_norm_gain.astype(jnp.float32),
        second_shift.astype(jnp.float32),
    )
    (
        query_mat,
        key_mat,
        value_mat,
        out_mat,
        attention_norm_gain,
        up_mat,
        down_mat,
        feedforward_norm_gain,
    ) = (
        lax.all_gather(w_query, "shard", axis=0, tiled=True),
        lax.all_gather(w_key, "shard", axis=0, tiled=True),
        lax.all_gather(w_value, "shard", axis=0, tiled=True),
        lax.all_gather(w_out, "shard", axis=0, tiled=True),
        lax.all_gather(attn_gain, "shard", axis=0, tiled=True),
        lax.all_gather(w_up, "shard", axis=0, tiled=True),
        lax.all_gather(w_down, "shard", axis=0, tiled=True),
        lax.all_gather(ffn_gain, "shard", axis=0, tiled=True),
    )
    grad_two, d_second_gain, d_second_shift = norm_back(
        local_gradient,
        second_centered_scaled,
        second_inverse_deviation,
        feedforward_norm_gain.astype(jnp.float32),
    )
    grad_down = grad_two.astype(jnp.bfloat16)
    d_down_bias = jnp.sum(grad_down, axis=0, dtype=jnp.float32)
    d_down_mat = matmul_tn(up_act, grad_down)
    grad_up = (matmul_nt(grad_down, down_mat) * gelu_slope(up_pre)).astype(jnp.bfloat16)
    d_up_bias = jnp.sum(grad_up, axis=0, dtype=jnp.float32)
    d_up_mat = matmul_tn(normed_low, grad_up)
    first_norm_gradient = grad_two + matmul_nt(grad_up, up_mat)
    grad_first, d_first_gain, d_first_shift = norm_back(
        first_norm_gradient,
        first_centered_scaled,
        first_inverse_deviation,
        attention_norm_gain.astype(jnp.float32),
    )
    grad_proj = grad_first.astype(jnp.bfloat16)
    d_out_bias = jnp.sum(grad_proj, axis=0, dtype=jnp.float32)
    d_out_mat = matmul_tn(attn_out, grad_proj)
    grad_attn = matmul_nt(grad_proj, out_mat).astype(jnp.bfloat16)
    grad_heads = grad_attn.reshape(tok_rows, heads, HEAD_DIM)
    delta = jnp.einsum(
        "qhd,qhd->hq",
        grad_heads,
        attn_out.reshape(tok_rows, heads, HEAD_DIM),
        preferred_element_type=jnp.float32,
    )
    zero_rows = jnp.zeros((tok_rows, width), jnp.float32)

    def key_step(step, carry):
        block, sums, acc_query = carry
        d_query, d_keys, d_values = block_grads(
            q_heads,
            local_ids,
            grad_heads,
            log_total,
            delta,
            block[0].reshape(tok_rows, heads, HEAD_DIM),
            block[1].reshape(tok_rows, heads, HEAD_DIM),
            block[2],
            scale,
        )
        sums = (
            sums[0] + d_keys.reshape(tok_rows, width),
            sums[1] + d_values.reshape(tok_rows, width),
        )
        block = from_behind((block[0], block[1], block[2]), "ctx", 1)
        sums = (
            from_behind(sums[0].astype(jnp.bfloat16), "ctx", 1).astype(jnp.float32),
            from_behind(sums[1].astype(jnp.bfloat16), "ctx", 1).astype(jnp.float32),
        )
        return (block, sums, acc_query + d_query.reshape(tok_rows, width))

    block, sums, d_query_sum = lax.fori_loop(
        0, cycle, key_step, ((keys, values, local_ids), (zero_rows, zero_rows), zero_rows)
    )
    d_keys_sum, d_values_sum = sums
    grad_query = d_query_sum.astype(jnp.bfloat16)
    grad_keys = d_keys_sum.astype(jnp.bfloat16)
    grad_values = d_values_sum.astype(jnp.bfloat16)
    d_query_bias = jnp.sum(grad_query, axis=0, dtype=jnp.float32)
    d_value_bias = jnp.sum(grad_values, axis=0, dtype=jnp.float32)
    d_query_mat = matmul_tn(x_local, grad_query)
    d_key_mat = matmul_tn(x_local, grad_keys)
    d_value_mat = matmul_tn(x_local, grad_values)
    grad_input = (
        grad_first
        + matmul_nt(grad_query, query_mat)
        + matmul_nt(grad_keys, key_mat)
        + matmul_nt(grad_values, value_mat)
    )
    home_hidden, home_grad = (
        lax.all_to_all(
            layer_output.astype(jnp.bfloat16).reshape(share, cycle, width),
            "ctx",
            split_axis=1,
            concat_axis=1,
            tiled=True,
        ),
        lax.all_to_all(
            grad_input.astype(jnp.bfloat16).reshape(share, cycle, width),
            "ctx",
            split_axis=1,
            concat_axis=1,
            tiled=True,
        ),
    )
    hidden_out = home_hidden.reshape(tok_rows, width)[None]
    tokens_grad = home_grad.reshape(tok_rows, width)[None]
    shares = (
        lax.psum_scatter(
            d_query_mat.astype(jnp.bfloat16), "shard", scatter_dimension=0, tiled=True
        ).astype(jnp.float32),
        lax.psum_scatter(
            d_query_bias.astype(jnp.bfloat16), "shard", scatter_dimension=0, tiled=True
        ).astype(jnp.float32),
        lax.psum_scatter(
            d_key_mat.astype(jnp.bfloat16), "shard", scatter_dimension=0, tiled=True
        ).astype(jnp.float32),
        lax.psum_scatter(
            d_value_mat.astype(jnp.bfloat16), "shard", scatter_dimension=0, tiled=True
        ).astype(jnp.float32),
        lax.psum_scatter(
            d_value_bias.astype(jnp.bfloat16), "shard", scatter_dimension=0, tiled=True
        ).astype(jnp.float32),
        lax.psum_scatter(
            d_out_mat.astype(jnp.bfloat16), "shard", scatter_dimension=0, tiled=True
        ).astype(jnp.float32),
        lax.psum_scatter(
            d_out_bias.astype(jnp.bfloat16), "shard", scatter_dimension=0, tiled=True
        ).astype(jnp.float32),
        lax.psum_scatter(
            d_first_gain.astype(jnp.bfloat16), "shard", scatter_dimension=0, tiled=True
        ).astype(jnp.float32),
        lax.psum_scatter(
            d_first_shift.astype(jnp.bfloat16), "shard", scatter_dimension=0, tiled=True
        ).astype(jnp.float32),
        lax.psum_scatter(
            d_up_mat.astype(jnp.bfloat16), "shard", scatter_dimension=0, tiled=True
        ).astype(jnp.float32),
        lax.psum_scatter(
            d_up_bias.astype(jnp.bfloat16), "shard", scatter_dimension=0, tiled=True
        ).astype(jnp.float32),
        lax.psum_scatter(
            d_down_mat.astype(jnp.bfloat16), "shard", scatter_dimension=0, tiled=True
        ).astype(jnp.float32),
        lax.psum_scatter(
            d_down_bias.astype(jnp.bfloat16), "shard", scatter_dimension=0, tiled=True
        ).astype(jnp.float32),
        lax.psum_scatter(
            d_second_gain.astype(jnp.bfloat16), "shard", scatter_dimension=0, tiled=True
        ).astype(jnp.float32),
        lax.psum_scatter(
            d_second_shift.astype(jnp.bfloat16), "shard", scatter_dimension=0, tiled=True
        ).astype(jnp.float32),
    )
    totals = lax.psum(
        (
            shares[0],
            shares[1],
            shares[2],
            shares[3],
            shares[4],
            shares[5],
            shares[6],
            shares[7],
            shares[8],
            shares[9],
            shares[10],
            shares[11],
            shares[12],
            shares[13],
            shares[14],
        ),
        "ctx",
    )
    return (hidden_out, tokens_grad) + tuple(totals)


def ring_solution(mesh):
    return jax.shard_map(
        ring_local,
        mesh=mesh,
        in_specs=(
            P("shard", "ctx", None),
            P("shard", "ctx", None),
            P("shard", "ctx"),
            P("shard", None),
            P("shard"),
            P("shard", None),
            P("shard", None),
            P("shard"),
            P("shard", None),
            P("shard"),
            P("shard"),
            P("shard"),
            P("shard", None),
            P("shard"),
            P("shard", None),
            P("shard"),
            P("shard"),
            P("shard"),
        ),
        out_specs=(
            P("shard", "ctx", None),
            P("shard", "ctx", None),
            P("shard", None),
            P("shard"),
            P("shard", None),
            P("shard", None),
            P("shard"),
            P("shard", None),
            P("shard"),
            P("shard"),
            P("shard"),
            P("shard", None),
            P("shard"),
            P("shard", None),
            P("shard"),
            P("shard"),
            P("shard"),
        ),
        check_vma=False,
    )


AXES = ("q", "r", "x", "c")
ANY = pl.BlockSpec(memory_space=pl.ANY)
WHOLE = pl.BlockSpec(memory_space=pltpu.VMEM)
HBM = pl.BlockSpec(memory_space=pltpu.HBM)


def moved(block, move):
    sizes = [lax.axis_size(a) for a in AXES]

    def number(spot):
        place = 0
        for size, at in zip(sizes, spot):
            place = place * size + at
        return place

    spots = [
        (q, r, x, c)
        for q in range(sizes[0])
        for r in range(sizes[1])
        for x in range(sizes[2])
        for c in range(sizes[3])
    ]
    return lax.ppermute(block, AXES, [(number(s), number(move(*s))) for s in spots])


def swap_x(block):
    return moved(block, lambda q, r, x, c: (q, r, 1 - x, c))


def swap_c(block):
    return moved(block, lambda q, r, x, c: (q, r, x, 1 - c))


def swap_r(block):
    return moved(block, lambda q, r, x, c: (q, r ^ 1, x, c))


def swap_rc(block):
    return moved(block, lambda q, r, x, c: (q, r ^ 1, x, 1 - c))


def swap_near(block):
    return moved(block, lambda q, r, x, c: (q ^ 1, r, x, c))


def swap_far(block):
    return moved(block, lambda q, r, x, c: (q ^ 2, r, x, c))


def regroup(block):
    return moved(block, lambda q, r, x, c: (2 * c + x, r, q & 1, q >> 1))


def regroup_x(block):
    return moved(block, lambda q, r, x, c: (2 * c + x, r, 1 - (q & 1), q >> 1))


def swap_xc(block):
    return moved(block, lambda q, r, x, c: (q, r, 1 - x, 1 - c))


def beside(mine, got):
    return jnp.concatenate([mine, got])


def dot(left, right):
    return jnp.dot(left, right, preferred_element_type=jnp.float32)


def dot_nt(left, right):
    return lax.dot_general(
        left, right, (((1,), (1,)), ((), ())), preferred_element_type=jnp.float32
    )


def dot_tn(left, right):
    return lax.dot_general(
        left, right, (((0,), (0,)), ((), ())), preferred_element_type=jnp.float32
    )


class Copies:
    def __init__(self, sems):
        self.sems = sems
        self.count = 0
        self.held = []

    def start(self, source, target):
        copy = pltpu.make_async_copy(source, target, self.sems.at[self.count])
        copy.start()
        self.count += 1
        self.held.append(copy)

    def wait(self):
        for copy in self.held:
            copy.wait()
        self.held = []


def spot():
    return tuple(lax.axis_index(a) for a in AXES)


def fill_mask(ids, mask, own):
    blocks, rows = ids.shape
    mine = jnp.concatenate([ids[pl.ds(own, 1), :], ids[pl.ds(own + 1, 1), :]], axis=1)
    across = jnp.transpose(ids[...])
    for b in range(blocks):
        mask[rows * b : rows * (b + 1), :] = jnp.where(across[:, b : b + 1] == mine, 0.0, masked_fill)


def block_kernel(tokens, ids, block, line, sems):
    rows = tokens.shape[0]
    copies = Copies(sems)
    copies.start(tokens, block.at[pl.ds(0, rows)])
    copies.start(ids, line)
    block[rows:, :] = jnp.zeros((16, block.shape[1]), block.dtype)
    copies.wait()
    block[rows:, 0:rows] = jnp.broadcast_to(line[...].astype(jnp.float32), (16, rows)).astype(block.dtype)


def pack_kernel(w_q, w_k, w_v, *refs):
    vectors, b_up, theirs, mine = refs[:8], refs[8], refs[9], refs[10]
    lines, thin, thick, sems = refs[11], refs[12:20], refs[20], refs[21]
    q, r, x, c = spot()
    part, width = w_q.shape
    half = width // 2
    copies = Copies(sems)
    few = part // 2
    for t, w in enumerate((w_q, w_k, w_v)):
        copies.start(w.at[:, pl.ds(pl.multiple_of(half * x, 128), half)], mine.at[pl.ds(part * t, part)])
        copies.start(
            w.at[pl.ds(pl.multiple_of(few * r, 32), few), pl.ds(pl.multiple_of(half * (1 - x), 128), half)],
            theirs.at[pl.ds(few * t, few)],
        )
    for vector, held in zip(vectors, thin):
        copies.start(vector, held)
    copies.start(b_up, thick)
    lines[...] = jnp.zeros_like(lines)
    copies.wait()
    for i, vector in enumerate(thin):
        line = vector[...].astype(jnp.float32).reshape(1, part)
        none = jnp.zeros_like(line)
        first = jnp.concatenate([line, none], axis=1)
        second = jnp.concatenate([none, line], axis=1)
        lines[i : i + 1, :] = jnp.where(c == 0, first, second)
    wide = thick[...].astype(jnp.float32).reshape(1, width)
    lines[pl.ds(8 + 2 * c, 1), :] = wide[:, 0:half]
    lines[pl.ds(9 + 2 * c, 1), :] = wide[:, half:]
    low = lines[...].astype(jnp.bfloat16)
    mine[3 * part :, :] = low
    theirs[3 * few :, :] = low


def cut_kernel(w, theirs, mine, sems):
    q, r, x, c = spot()
    count = theirs.shape[1]
    copies = Copies(sems)
    copies.start(w.at[:, pl.ds(pl.multiple_of(count * (1 - x), 128), count)], theirs)
    copies.start(w.at[:, pl.ds(pl.multiple_of(count * x, 128), count)], mine)
    copies.wait()


def load_kernel(block, out, sems):
    copies = Copies(sems)
    copies.start(block, out)
    copies.wait()


def turn_kernel(keys, out):
    for p in range(keys.shape[0]):
        out[2 * p : 2 * p + 2] = jnp.transpose(keys[p]).reshape(2, 64, keys.shape[1])


def project_kernel(
    b0, b1, b2, b3, w_q, w_k, w_v, w_m, xa, xb, ma, mb, own_lines,
    kv_out, q_out, w, vecs, up_bias, xs, sems,
):
    q, r, x, c = spot()
    rows = xs.shape[0] // 4
    part = w.shape[0] // 4
    half = w.shape[1] // 3
    me, shard = 2 * c + x, 2 * x + c
    columns = pl.ds(pl.multiple_of(half * x, 128), half)
    ins = Copies(sems)
    for t, own in enumerate((w_q, w_k, w_v)):
        at = pl.ds(pl.multiple_of(part * shard, 64), part)
        ins.start(own.at[:, columns], w.at[at, pl.ds(half * t, half)])
    for j, block in enumerate((b0, b1, b2, b3)):
        xs[pl.ds(pl.multiple_of(rows * (me ^ j), rows), rows), :] = block[0:rows, :]
    few = part // 2
    for t in range(3):
        place = slice(half * t, half * (t + 1))
        at = pl.ds(pl.multiple_of(part * (shard ^ 1), 64), part)
        w[at, place] = w_m[part * t : part * (t + 1), :]
        for flip, side, piece in ((2, r, xa), (2, 1 - r, xb), (3, r, ma), (3, 1 - r, mb)):
            at = pl.ds(pl.multiple_of(part * (shard ^ flip) + few * side, 32), few)
            w[at, place] = piece[few * t : few * (t + 1), :]
    mine, other = (
        a[at:, :].astype(jnp.float32) + b[at:, :].astype(jnp.float32)
        for a, b, at in ((own_lines, w_m, 3 * part), (xa, ma, 3 * few))
    )
    vecs[:, columns] = mine[0:8, :]
    vecs[:, pl.ds(pl.multiple_of(half * (1 - x), 128), half)] = other[0:8, :]
    for i in range(4):
        up_bias[i] = jnp.broadcast_to(mine[8 + i : 9 + i, :], (8, half))
    ins.wait()
    kv_out[:, 0:half] = dot(xs[...], w[:, half : 2 * half]).astype(jnp.bfloat16)
    kv_out[:, half:] = (dot(xs[...], w[:, 2 * half :]) + mine[1:2, :]).astype(jnp.bfloat16)
    own = pl.ds(pl.multiple_of(2 * rows * c, rows), 2 * rows)
    q_out[...] = (dot(xs[own, :], w[:, 0:half]) + mine[0:1, :]).astype(jnp.bfloat16)


def attend_kernel(
    b0, b1, b2, b3, b4, b5, b6, b7, kv_own, q_own, w, vecs, w_o, w_om,
    a_low, xs, wo, k3, v3, q3, o_out, lse_out, ids_out, a_out,
    vt, ot, mask, sems,
):
    q, r, x, c = spot()
    rows = xs.shape[0] // 8
    half = wo.shape[0]
    part = half // 2
    me = 4 * r + 2 * c + x
    ins = Copies(sems)
    ins.start(w_o, wo.at[pl.ds(pl.multiple_of(part * c, 64), part)])
    wo[pl.ds(pl.multiple_of(part * (1 - c), 64), part), :] = w_om[...]
    for j, block in enumerate((b0, b1, b2, b3, b4, b5, b6, b7)):
        at = me ^ j
        xs[pl.ds(pl.multiple_of(rows * at, rows), rows), :] = block[0:rows, :]
        ids_out[pl.ds(at, 1), :] = block[rows : rows + 16, 0:rows].astype(jnp.float32)[0:1, :]
    fill_mask(ids_out, mask, 4 * r + 2 * c)
    rest = pl.ds(pl.multiple_of(4 * rows * (1 - r), rows), 4 * rows)
    here = pl.ds(pl.multiple_of(4 * rows * r, rows), 4 * rows)
    bias = vecs[1:2, pl.ds(pl.multiple_of(half * x, 128), half)]
    keyed = dot(xs[rest, :], w[:, half : 2 * half]).astype(jnp.bfloat16)
    valued = (dot(xs[rest, :], w[:, 2 * half :]) + bias).astype(jnp.bfloat16)
    pairs = half // 128
    for p in range(pairs):
        at = slice(128 * p, 128 * (p + 1))
        k3[p, here, :] = kv_own[:, at]
        k3[p, rest, :] = keyed[:, at]
        v3[p, here, :] = kv_own[:, half + 128 * p : half + 128 * (p + 1)]
        v3[p, rest, :] = valued[:, at]
        q3[p] = q_own[:, at]
        vt[2 * p : 2 * p + 2] = jnp.transpose(v3[p]).reshape(2, 64, 8 * rows)
    lane = lax.broadcasted_iota(jnp.int32, (2 * rows, 128), 1) // 64

    def head(h, carry):
        query = jnp.where(lane == h % 2, q3[h // 2], 0) * 0.125
        scores = dot_nt(k3[h // 2], query.astype(jnp.bfloat16)) + mask[...]
        top = jnp.max(scores, axis=0, keepdims=True)
        weights = jnp.exp(scores - top)
        total = jnp.sum(weights, axis=0, keepdims=True)
        ot[h] = dot(vt[h], weights.astype(jnp.bfloat16)) / total
        lse_out[pl.ds(h, 1), :] = top + jnp.log(total)
        return carry

    lax.fori_loop(0, 2 * pairs, head, 0)
    mixed = jnp.transpose(ot[...].reshape(half, 2 * rows)).astype(jnp.bfloat16)
    o_out[...] = mixed
    ins.wait()
    partial = dot(mixed, wo[...])
    a_out[...] = partial
    a_low[...] = partial.astype(jnp.bfloat16)


def inner_kernel(u_own, u_x, u_m, u_mx0, u_mx1, d_own, d_m, up, down, sems):
    q, r, x, c = spot()
    part = up.shape[0] // 4
    count = up.shape[1]
    shard = 2 * x + c
    ins = Copies(sems)
    own = u_own.at[:, pl.ds(pl.multiple_of(count * x, 128), count)]
    ins.start(own, up.at[pl.ds(pl.multiple_of(part * shard, 64), part)])
    ins.start(d_own, down.at[pl.ds(pl.multiple_of(count // 2 * c, 128), count // 2)])
    for flip, piece in ((2, u_x), (1, u_m)):
        up[pl.ds(pl.multiple_of(part * (shard ^ flip), 64), part), :] = piece[...]
    for i, piece in enumerate((u_mx0, u_mx1)):
        at = pl.multiple_of(part * (shard ^ 3) + part // 2 * i, 32)
        up[pl.ds(at, part // 2), :] = piece[...]
    down[pl.ds(pl.multiple_of(count // 2 * (1 - c), 128), count // 2), :] = d_m[...]
    ins.wait()


def norm_of(value):
    mean = jnp.mean(value, axis=-1, keepdims=True)
    centered = value - mean
    rstd = lax.rsqrt(jnp.mean(centered * centered, axis=-1, keepdims=True) + ln_eps)
    return centered * rstd, rstd


def norm_pull(scaled, normed, rstd):
    return rstd * (
        scaled
        - jnp.mean(scaled, axis=-1, keepdims=True)
        - normed * jnp.mean(scaled * normed, axis=-1, keepdims=True)
    )


def forward_kernel(
    a_own, a_got, xs, vecs, b_up, up, down,
    y_low, y_more, h_out, z, n_out, r_out, slope, y_out,
):
    q, r, x, c = spot()
    rows = a_own.shape[0]
    x_own = xs[pl.ds(pl.multiple_of(rows * (2 * r + c), rows), rows), :]
    total = x_own.astype(jnp.float32) + (a_own[...] + a_got[...].astype(jnp.float32) + vecs[2:3, :])
    normed, rstd = norm_of(total)
    n_out[...] = normed
    r_out[...] = jnp.broadcast_to(rstd, r_out.shape)
    low = (normed * vecs[3:4, :] + vecs[4:5, :]).astype(jnp.bfloat16)
    h_out[...] = low
    wide = up.shape[1] // 4
    for j in range(4):
        at = slice(wide * j, wide * (j + 1))
        pre = dot(low, up[:, at]) + b_up[j, 0:1, :]
        cdf = 0.5 * (1.0 + lax.erf(pre * (1.0 / math.sqrt(2.0))))
        density = jnp.exp(-0.5 * pre * pre) * (1.0 / math.sqrt(2.0 * math.pi))
        z[:, at] = (pre * cdf).astype(jnp.bfloat16)
        slope[:, at] = cdf + pre * density
    result = dot(z[...], down[...])
    y_out[...] = result
    rows = y_low.shape[0]
    y_low[...] = result[0:rows, :].astype(jnp.bfloat16)
    y_more[...] = result[rows:, :].astype(jnp.bfloat16)


def norm_back_kernel(
    y_own, y_got, y_rest, normed1, g_own, g_x, vecs, low_out, hid_out, dy_out, sums, grad, hid,
):
    q, r, x, c = spot()
    rows = grad.shape[0] // 2
    grad[pl.ds(pl.multiple_of(rows * x, rows), rows), :] = g_own[...]
    grad[pl.ds(pl.multiple_of(rows * (1 - x), rows), rows), :] = g_x[...]
    got = jnp.concatenate([y_got[...], y_rest[...]]).astype(jnp.float32)
    h1 = normed1[...] * vecs[3:4, :] + vecs[4:5, :]
    normed, rstd = norm_of(h1 + (y_own[...] + got + vecs[5:6, :]))
    hid[...] = (normed * vecs[6:7, :] + vecs[7:8, :]).astype(jnp.bfloat16)
    hid_out[...] = hid[pl.ds(pl.multiple_of(rows * x, rows), rows), :]
    cot = grad[...].astype(jnp.float32)
    dy = norm_pull(cot * vecs[6:7, :], normed, rstd)
    low = dy.astype(jnp.bfloat16)
    dy_out[...] = dy
    low_out[...] = low
    sums[...] = jnp.zeros_like(sums)
    sums[0:1, :] = jnp.sum(low.astype(jnp.float32), axis=0, keepdims=True)
    sums[1:2, :] = jnp.sum(cot * normed, axis=0, keepdims=True)
    sums[2:3, :] = jnp.sum(cot, axis=0, keepdims=True)


def backward_kernel(dy, dy_low, slope, up, down, p_low, s_out, du_out, up_sums):
    low = dy_low[...]
    wide = up.shape[1] // 4
    for j in range(4):
        at = slice(wide * j, wide * (j + 1))
        du = (dot_nt(low, down[at, :]) * slope[:, at]).astype(jnp.bfloat16)
        du_out[:, at] = du
        total = jnp.sum(du.astype(jnp.float32), axis=0, keepdims=True)
        up_sums[j] = jnp.broadcast_to(total, up_sums.shape[1:])
    result = dot_nt(du_out[...], up[...])
    s_out[...] = dy[...] + result
    p_low[...] = result.astype(jnp.bfloat16)


def attend_back_kernel(
    s_own, p_got, normed1, rstd1, vecs, wo, mixed, q3, k3, v3, kt, lse, ids,
    dkv_out, dq_out, dr_out, da_out, sums, qv_sums,
    mask, do3, delta, dk, dv, dqt, whole,
):
    q, r, x, c = spot()
    rows = dr_out.shape[0]
    pairs = q3.shape[0]
    half = 128 * pairs
    fill_mask(ids, mask, 4 * r + 2 * c)
    dh = s_own[...] + p_got[...].astype(jnp.float32)
    normed = normed1[...]
    dr = norm_pull(dh * vecs[3:4, :], normed, rstd1[:, 0:1])
    whole[...] = dr
    dr_out[...] = whole[pl.ds(pl.multiple_of(rows * x, rows), rows), :]
    low = dr.astype(jnp.bfloat16)
    da_out[...] = low
    sums[...] = jnp.zeros_like(sums)
    sums[0:1, :] = jnp.sum(low.astype(jnp.float32), axis=0, keepdims=True)
    sums[1:2, :] = jnp.sum(dh * normed, axis=0, keepdims=True)
    sums[2:3, :] = jnp.sum(dh, axis=0, keepdims=True)
    d_o = dot_nt(low, wo[...]).astype(jnp.bfloat16)
    products = jnp.transpose(d_o.astype(jnp.float32) * mixed[...].astype(jnp.float32))
    for h in range(2 * pairs):
        delta[h : h + 1, :] = jnp.sum(products[64 * h : 64 * (h + 1), :], axis=0, keepdims=True)
    for p in range(pairs):
        do3[p] = d_o[:, 128 * p : 128 * (p + 1)]
    dk[...] = jnp.zeros_like(dk)
    dv[...] = jnp.zeros_like(dv)
    lane = lax.broadcasted_iota(jnp.int32, (2 * rows, 128), 1) // 64

    def head(h, carry):
        p = h // 2
        here = lane == h % 2
        query = (jnp.where(here, q3[p], 0) * 0.125).astype(jnp.bfloat16)
        d_here = jnp.where(here, do3[p], 0).astype(jnp.bfloat16)
        probs = jnp.exp(dot_nt(k3[p], query) + mask[...] - lse[pl.ds(h, 1), :])
        d_probs = dot_nt(v3[p], d_here)
        d_scores = (probs * (d_probs - delta[pl.ds(h, 1), :])).astype(jnp.bfloat16)
        dv[p] += dot(probs.astype(jnp.bfloat16), d_here)
        dk[p] += dot(d_scores, query)
        dqt[h] = dot(kt[h], d_scores)
        return carry

    lax.fori_loop(0, 2 * pairs, head, 0)
    dq = (jnp.transpose(dqt[...].reshape(half, 2 * rows)) * 0.125).astype(jnp.bfloat16)
    dq_out[...] = dq
    qv_sums[...] = jnp.zeros_like(qv_sums)
    qv_sums[0:1, :] = jnp.sum(dq.astype(jnp.float32), axis=0, keepdims=True)
    for p in range(pairs):
        at = slice(128 * p, 128 * (p + 1))
        dkv_out[:, at] = dk[p].astype(jnp.bfloat16)
        value = dv[p].astype(jnp.bfloat16)
        dkv_out[:, half + 128 * p : half + 128 * (p + 1)] = value
        qv_sums[1:2, at] = jnp.sum(value.astype(jnp.float32), axis=0, keepdims=True)


def input_grad_kernel(dq, dkv, w, *refs):
    sends, (keep, whole) = refs[:2], refs[2:]
    q, r, x, c = spot()
    half = dq.shape[1]
    rows = dq.shape[0] // 2
    whole[...] = dot_nt(dkv[...], w[:, half:])
    own = pl.ds(pl.multiple_of(rows * (4 * r + 2 * c), rows), 2 * rows)
    whole[own, :] += dot_nt(dq[...], w[:, 0:half])
    for b in range(2):
        for i in range(2):
            to = slice(2 * rows * b + rows * i, 2 * rows * b + rows * (i + 1))
            mine = pl.ds(pl.multiple_of(rows * (4 * i + 2 * c + b), rows), rows)
            keep[to, :] = whole[mine, :]
            theirs = pl.ds(pl.multiple_of(rows * (4 * i + 2 * (1 - c) + b), rows), rows)
            sends[b][rows * i : rows * (i + 1), :] = whole[theirs, :].astype(jnp.bfloat16)


def input_x_kernel(keep, got0, got1, send, kept):
    q, r, x, c = spot()
    half = send.shape[0]
    for side, got in enumerate((got0, got1)):
        total = keep[half * side : half * (side + 1), :] + got[...].astype(jnp.float32)

        @pl.when(x == side)
        def _():
            kept[...] = total

        @pl.when(x != side)
        def _():
            send[...] = total.astype(jnp.bfloat16)


def octants():
    for at in range(8):
        r, q0, q1 = at >> 2, at >> 1 & 1, at & 1
        yield 4 * r + 2 * q0 + 1 * q1, 1 * r + 4 * q0 + 2 * q1, 4 * r + 2 * q1 + q0


def down_grad_kernel(z, dy, send, keep):
    q, r, x, c = spot()
    half = z.shape[1] // 2
    rows = half // 8
    for side, out in ((1 - c, send), (c, keep)):
        part = dot_tn(z[:, pl.ds(pl.multiple_of(half * side, 128), half)], dy[...])
        for at, _, within in octants():
            block = part[rows * within : rows * (within + 1), :]
            out[rows * at : rows * (at + 1), :] = block.astype(out.dtype)


def up_grad_kernel(h, du, *refs):
    q, r, x, c = spot()
    sends, (keep, whole) = refs[:4], refs[4:]
    width = h.shape[1]
    thin = width // 32
    whole[...] = dot_tn(h[...], du[...])
    for side in (1 - c, c):
        for _, at, within in octants():
            pieces = []
            for xx in range(2):
                first = 8 * thin * (2 * xx + side) + thin * within
                rows = pl.ds(pl.multiple_of(first, 8), thin)
                pieces += [whole[rows, 0:width], whole[rows, width:]]
            block = jnp.concatenate(pieces)
            if side is c:
                keep[4 * thin * at : 4 * thin * (at + 1), :] = block
            else:
                to = 4 * thin * (at % 2)
                sends[at // 2][to : to + 4 * thin, :] = block.astype(jnp.bfloat16)


def join_kernel(*refs):
    out, at = refs[-1], 0
    for ref in refs[:-1]:
        count = ref.shape[0]
        out[at : at + count, :] = ref[...]
        at += count


def fold_pieces_kernel(bit, count, keep, *refs):
    gots, sends, (kept, whole) = refs[: -2 - count], refs[-2 - count : -2], refs[-2:]
    at = bit(*spot())
    first = 0
    for got in gots:
        rows = slice(first, first + got.shape[0])
        whole[rows, :] = keep[rows, :] + got[...].astype(jnp.float32)
        first += got.shape[0]
    half = kept.shape[0]
    kept[...] = whole[pl.ds(pl.multiple_of(half * at, 64), half), :]
    for i, send in enumerate(sends):
        rows = pl.ds(pl.multiple_of(half * (1 - at) + half // count * i, 64), half // count)
        send[...] = whole[rows, :].astype(send.dtype)


def fold_kernel(bit, keep, got, send, kept):
    at = bit(*spot())
    send[...] = (keep[1 - at] + got[1 - at].astype(jnp.float32)).astype(send.dtype)
    kept[...] = keep[at] + got[at].astype(jnp.float32)


def copy_kernel(block, out):
    out[...] = block[...]


def sum_kernel(keep, got, out):
    out[...] = (keep[...] + got[...].astype(jnp.float32)).astype(out.dtype)


def total_kernel(keep, got, more, out):
    out[...] = (keep[...] + got[...].astype(jnp.float32) + more[...]).astype(out.dtype)


def share_kernel(keep, got, side, base):
    q, r, x, c = spot()
    side[...] = (keep[1 - x] + got[1 - x].astype(jnp.float32)).astype(side.dtype)
    base[...] = (keep[x] + got[x].astype(jnp.float32)).astype(base.dtype)


def weight_grad_kernel(
    xs, dkv, dq, mixed, da, sums1, sums2, qv_sums, up_sums, *refs
):
    sends, (keep, packed) = refs[:-2], refs[-2:]
    q, r, x, c = spot()
    width = xs.shape[1]
    own, half = dq.shape
    thin = width // 32
    for_c = 64 * thin
    own_rows = pl.ds(pl.multiple_of(own * (2 * r + c), own), own)
    asked = dot_tn(xs[own_rows, :], dq[...])
    kept = dot_tn(xs[...], dkv[...])
    outer = dot_tn(mixed[...], da[...])
    for cc in range(2):
        for rr in range(2):
            for q1 in range(2):
                for q0 in range(2):
                    at = ((4 * rr + 2 * q0 + 1 * q1) * 8) * thin
                    within = (4 * rr + 2 * q1 + q0) * thin
                    for xx in range(2):
                        rows = slice((16 * xx + 8 * cc) * thin + within, (16 * xx + 8 * cc + 1) * thin + within)
                        for t, piece in enumerate((asked, kept[:, 0:half], kept[:, half:])):
                            to = at + (3 * xx + t) * thin
                            packed[cc, to : to + thin, :] = piece[rows, :]
                    rows = slice(8 * cc * thin + within, (8 * cc + 1) * thin + within)
                    for t in range(2):
                        to = at + (6 + t) * thin
                        packed[cc, to : to + thin, :] = outer[rows, half * t : half * (t + 1)]
    columns = pl.ds(pl.multiple_of(half * x, 128), half)
    for cc in range(2):
        packed[cc, for_c : for_c + 16, :] = jnp.zeros((16, half), jnp.float32)
        packed[cc, for_c : for_c + 2, :] = qv_sums[0:2, :]
        for j in range(4):
            packed[cc, for_c + 2 + j : for_c + 3 + j, :] = up_sums[j, 0:1, :]
        packed[cc, for_c + 6 : for_c + 9, :] = sums1[0:3, columns]
        packed[cc, for_c + 9 : for_c + 12, :] = sums2[0:3, columns]
    first = 0
    for send in sends:
        count = send.shape[0]
        send[...] = packed[1 - c, first : first + count, :].astype(jnp.bfloat16)
        first += count
    keep[...] = packed[c]


def step_kernel(bit, keep, *refs):
    gots, (send, kept, whole) = refs[:-3], refs[-3:]
    at = bit(*spot())
    count = send.shape[0] - 16
    first = 0
    for got in gots:
        rows = slice(first, first + got.shape[0])
        whole[rows, :] = keep[rows, :] + got[...].astype(jnp.float32)
        first += got.shape[0]
    theirs = pl.ds(pl.multiple_of(count * (1 - at), 64), count)
    mine = pl.ds(pl.multiple_of(count * at, 64), count)
    send[0:count, :] = whole[theirs, :].astype(jnp.bfloat16)
    send[count:, :] = whole[2 * count :, :].astype(jnp.bfloat16)
    kept[0:count, :] = whole[mine, :]
    kept[count:, :] = whole[2 * count :, :]


def last_step_kernel(keep, got, side, base, *refs):
    out, b_up, whole = refs[:8], refs[8], refs[9]
    q, r, x, c = spot()
    count = side.shape[0]
    part = out[0].shape[0]
    whole[...] = keep[...] + got[...].astype(jnp.float32)
    theirs = pl.ds(pl.multiple_of(count * (1 - x), 8), count)
    mine = pl.ds(pl.multiple_of(count * x, 8), count)
    side[...] = whole[theirs, :].astype(jnp.bfloat16)
    first = whole.shape[0] - 16
    base[...] = jnp.concatenate([whole[mine, :], whole[2 * count : first, :]]).astype(jnp.bfloat16)
    for i, one in enumerate(out):
        at = first + (i if i < 2 else i + 4)
        line = whole[at : at + 1, :]
        one[...] = jnp.where(c == 0, line[:, :part], line[:, part:]).reshape(part)
    line = jnp.concatenate([whole[pl.ds(first + 2 + 2 * c + i, 1), :] for i in range(2)], axis=1)
    b_up[...] = line.reshape(b_up.shape[0])


def down_out_kernel(near, far, out, mark):
    mark[...] = jnp.zeros_like(mark)
    q, r, x, c = spot()
    count = near.shape[0] // 4
    for d, piece in enumerate((near, far)):
        for k in range(4):
            at = 4 * (r ^ d) + 2 * ((q // 2) ^ (k & 1)) + ((q % 2) ^ (k >> 1))
            rows = pl.ds(pl.multiple_of(count * at, 32), count)
            out[rows, :] = piece[count * k : count * (k + 1), :].astype(jnp.float32)


def up_out_kernel(near, far, out, mark, whole):
    mark[...] = jnp.zeros_like(mark)
    q, r, x, c = spot()
    thin, width = near.shape[0] // 16, near.shape[1]
    for d, piece in enumerate((near, far)):
        whole[...] = piece[...].astype(jnp.float32)
        for k in range(4):
            at = 4 * (r ^ d) + 2 * ((q // 2) ^ (k & 1)) + ((q % 2) ^ (k >> 1))
            rows = pl.ds(pl.multiple_of(thin * at, 8), thin)
            for s in range(4):
                columns = pl.ds(pl.multiple_of(width * (2 * (x ^ (s >> 1)) + (s & 1)), 128), width)
                first = thin * (4 * k + s)
                out[rows, columns] = whole[first : first + thin, :]


def rest_out_kernel(near, far, hidden, total, out_q, out_k, out_v, out_o, out_h, out_t, whole):
    out_h[...] = hidden[...]
    out_t[...] = total[...]
    q, r, x, c = spot()
    half = near.shape[1]
    thin = near.shape[0] // 32
    ours = pl.ds(pl.multiple_of(half * x, 128), half)
    other = pl.ds(pl.multiple_of(half * (1 - x), 128), half)
    for d, piece in enumerate((near, far)):
        whole[...] = piece[...].astype(jnp.float32)
        for k in range(4):
            at = 4 * (r ^ d) + 2 * ((q // 2) ^ (k & 1)) + ((q % 2) ^ (k >> 1))
            rows = pl.ds(pl.multiple_of(thin * at, 8), thin)
            first = 8 * thin * k
            for t, out in enumerate((out_q, out_k, out_v)):
                out[rows, ours] = whole[first + thin * t : first + thin * (t + 1), :]
                out[rows, other] = whole[first + thin * (5 + t) : first + thin * (6 + t), :]
            for t in range(2):
                columns = slice(half * t, half * (t + 1))
                out_o[rows, columns] = whole[first + thin * (3 + t) : first + thin * (4 + t), :]


def kernel_call(body, name, ins, outs, scratch, args, after=(), room=2 << 20, cost=1):
    count = len(args)

    def size(shape, dtype):
        return math.prod(shape) * jnp.dtype(dtype).itemsize

    used = sum(size(m.shape, m.dtype) for m in scratch if m.memory_space == pltpu.VMEM)

    args = [
        pltpu.with_memory_space_constraint(a, pltpu.HBM) if spec is HBM else a
        for a, spec in zip(args, ins)
    ]

    def run(*refs):
        body(*refs[:count], *refs[count + len(after) :])

    return pl.pallas_call(
        run,
        name=name,
        out_shape=[jax.ShapeDtypeStruct(shape, dtype) for shape, dtype, _ in outs],
        in_specs=list(ins) + [ANY] * len(after),
        out_specs=[spec for _, _, spec in outs],
        scratch_shapes=scratch,
        cost_estimate=pl.CostEstimate(flops=cost, bytes_accessed=1, transcendentals=0),
        compiler_params=pltpu.CompilerParams(vmem_limit_bytes=used + room),
    )(*args, *after)


def once(value, *after):
    return pl.pallas_call(
        lambda *refs: None,
        name="once",
        out_shape=jax.ShapeDtypeStruct(value.shape, value.dtype),
        in_specs=[ANY] * (1 + len(after)),
        out_specs=ANY,
        input_output_aliases={0: 0},
        cost_estimate=pl.CostEstimate(flops=1, bytes_accessed=1, transcendentals=0),
        compiler_params=pltpu.CompilerParams(vmem_limit_bytes=1 << 18),
    )(value, *after)


HEAVY = ('attend_back', 'down_sum', 'input_sum', 'project', 'rest_3', 'up_share')


def plane_local(
    tokens, cotangent, seq_ids, w_query, b_query, w_key, w_value, b_value, w_out, b_out,
    attn_gain, attn_shift, w_up, b_up, w_down, b_down, ffn_gain, ffn_shift,
):
    low, exact = jnp.bfloat16, jnp.float32
    rows, width = tokens.shape[1:]
    part = w_query.shape[0]
    half = width // 2
    inner = w_up.shape[1]
    wide = inner // 8
    keys = 8 * rows
    own = 2 * rows
    pairs = half // 128

    latest = []

    def call(body, name, ins, outs, scratch, args, after=(), **more):
        cost = 10**10 if name in HEAVY else 1
        results = kernel_call(
            body, name, ins, outs, scratch, args, tuple(after) + tuple(latest), cost=cost, **more
        )
        latest[:] = results[-1:] if name.endswith("_out") else results[:1]
        return results

    (block,) = call(
        block_kernel, "block", [HBM] * 2, [((rows + 16, width), low, WHOLE)],
        [pltpu.VMEM((1, rows), jnp.int32), pltpu.SemaphoreType.DMA((2,))],
        (tokens[0], seq_ids),
    )
    block = regroup(block)
    theirs, mine = call(
        pack_kernel,
        "pack",
        [HBM] * 12,
        [((3 * part // 2 + 16, half), low, WHOLE), ((3 * part + 16, half), low, WHOLE)],
        [pltpu.VMEM((16, half), exact)]
        + [pltpu.VMEM((part,), low)] * 8
        + [pltpu.VMEM((width,), low), pltpu.SemaphoreType.DMA((15,))],
        (w_query, w_key, w_value, b_query, b_value, b_out, attn_gain, attn_shift, b_down, ffn_gain, ffn_shift, b_up),
    )
    qkv_x = swap_x(theirs)
    qkv_m = swap_c(mine)
    out_m = swap_c(w_out)
    blocks = [once(block, qkv_m, out_m)]
    beside_r = swap_r(blocks[0])
    blocks.append(once(swap_x(blocks[0]), beside_r))
    blocks.append(swap_c(blocks[0]))
    blocks.append(swap_c(blocks[1]))
    blocks.append(beside_r)
    blocks.append(swap_r(blocks[1]))
    qkv_x = (qkv_x, swap_r(qkv_x))
    qkv_mx = [swap_c(piece) for piece in qkv_x]
    up_theirs, up_mine = call(
        cut_kernel, "cut", [HBM], [((part, 4 * wide), low, WHOLE)] * 2, [pltpu.SemaphoreType.DMA((2,))],
        (w_up,), after=(blocks[1],),
    )
    up_x = swap_x(up_theirs)
    up_m = swap_c(up_mine)
    down_m = swap_c(w_down)
    (cot,) = call(
        load_kernel, "cotangent", [HBM], [((rows, width), low, WHOLE)], [pltpu.SemaphoreType.DMA((1,))],
        (cotangent[0],),
    )
    kv_own, q_own, w_all, vecs, up_bias = call(
        project_kernel,
        "project",
        [WHOLE] * 4 + [HBM] * 3 + [WHOLE] * 6,
        [
            ((4 * rows, width), low, WHOLE),
            ((own, half), low, WHOLE),
            ((width, 3 * half), low, WHOLE),
            ((8, width), exact, WHOLE),
            ((4, 8, wide), exact, WHOLE),
        ],
        [pltpu.VMEM((4 * rows, width), low), pltpu.SemaphoreType.DMA((3,))],
        (*blocks[:4], w_query, w_key, w_value, qkv_m, *qkv_x, *qkv_mx, mine),
        room=8 << 20,
    )
    blocks[5] = once(blocks[5], kv_own)
    blocks.append(swap_c(blocks[4]))
    blocks.append(swap_c(blocks[5]))
    a_low, x_all, wo_all, k3, v3, q3, mixed, lse, ids, a_own = call(
        attend_kernel,
        "attend",
        [WHOLE] * 12 + [HBM, WHOLE],
        [
            ((own, width), low, WHOLE),
            ((keys, width), low, WHOLE),
            ((half, width), low, WHOLE),
            ((pairs, keys, 128), low, WHOLE),
            ((pairs, keys, 128), low, WHOLE),
            ((pairs, own, 128), low, WHOLE),
            ((own, half), low, WHOLE),
            ((8, own), exact, WHOLE),
            ((8, rows), exact, WHOLE),
            ((own, width), exact, WHOLE),
        ],
        [
            pltpu.VMEM((2 * pairs, 64, keys), low),
            pltpu.VMEM((2 * pairs, 64, own), exact),
            pltpu.VMEM((keys, own), exact),
            pltpu.SemaphoreType.DMA((1,)),
        ],
        (*blocks, kv_own, q_own, w_all, vecs, w_out, out_m),
        after=(down_m,),
        room=8 << 20,
    )
    a_got = swap_x(a_low)
    (kt,) = call(turn_kernel, "turn", [WHOLE], [((2 * pairs, 64, keys), low, WHOLE)], [], (k3,),
        after=(up_m,))

    up_x = once(up_x, kt)
    up_mx = [swap_c(piece) for piece in (up_x[: part // 2], up_x[part // 2 :])]
    inner_weights = call(
        inner_kernel,
        "inner",
        [HBM] + [WHOLE] * 4 + [HBM, WHOLE],
        [((width, 4 * wide), low, WHOLE), ((4 * wide, width), low, WHOLE)],
        [pltpu.SemaphoreType.DMA((2,))],
        (w_up, up_x, up_m, *up_mx, w_down, down_m),
    )
    cot = once(cot, inner_weights[0])
    cot, cot_x = regroup(cot), regroup_x(cot)
    y_low, y_more, h_low, z, normed1, rstd1, slope, y_own = call(
        forward_kernel,
        "feedforward",
        [WHOLE] * 7,
        [
            ((rows, width), low, WHOLE),
            ((rows, width), low, WHOLE),
            ((own, width), low, WHOLE),
            ((own, 4 * wide), low, WHOLE),
            ((own, width), exact, WHOLE),
            ((own, 128), exact, WHOLE),
            ((own, 4 * wide), exact, WHOLE),
            ((own, width), exact, WHOLE),
        ],
        [],
        (a_own, a_got, x_all, vecs, up_bias, *inner_weights),
        room=8 << 20,
    )
    y_got, y_rest = swap_x(y_low), swap_x(y_more)
    dy_low, hidden, dy, sums2 = call(
        norm_back_kernel,
        "norm_back",
        [WHOLE] * 7,
        [
            ((own, width), low, WHOLE),
            ((rows, width), low, WHOLE),
            ((own, width), exact, WHOLE),
            ((8, width), exact, WHOLE),
        ],
        [
            pltpu.VMEM((own, width), low),
            pltpu.VMEM((own, width), low),
        ],
        (y_own, y_got, y_rest, normed1, cot, cot_x, vecs),
        room=6 << 20,
    )
    eighth = wide // 4
    down_send, down_keep = call(
        down_grad_kernel,
        "down_grad",
        [WHOLE] * 2,
        [((8 * eighth, width), low, WHOLE), ((8 * eighth, width), exact, WHOLE)],
        [],
        (z, dy_low),
        room=8 << 20,
    )
    down_got = swap_c(down_send)
    p_low, s_own, du, up_sums = call(
        backward_kernel,
        "feedforward_back",
        [WHOLE] * 5,
        [
            ((own, width), low, WHOLE),
            ((own, width), exact, WHOLE),
            ((own, 4 * wide), low, WHOLE),
            ((4, 8, wide), exact, WHOLE),
        ],
        [],
        (dy, dy_low, slope, *inner_weights),
        room=8 << 20,
    )
    p_got = swap_x(p_low)
    hidden = regroup(hidden)

    def fold(name, bit, keep, got):
        shape = (keep.shape[0] // 2, keep.shape[1])
        return call(
            lambda *refs: fold_kernel(bit, *refs),
            name,
            [WHOLE] * 2,
            [(shape, low, WHOLE), (shape, exact, WHOLE)],
            [],
            (keep.reshape(2, *shape), got.reshape(2, *shape)),
            room=4 << 20,
        )

    def fold_into(count, name, bit, keep, gots):
        half_rows = keep.shape[0] // 2
        *sends, kept = call(
            lambda *refs: fold_pieces_kernel(bit, count, *refs),
            name,
            [WHOLE] * (1 + len(gots)),
            [((half_rows // count, width), low, WHOLE)] * count + [((half_rows, width), exact, WHOLE)],
            [pltpu.VMEM(keep.shape, exact)],
            (keep, *gots),
            room=4 << 20,
        )
        return sends, kept

    def bit_r(q, r, x, c):
        return r

    def bit_near(q, r, x, c):
        return q % 2

    def bit_far(q, r, x, c):
        return q // 2

    thin = part // 8
    count = 64 * thin

    def step(name, bit, keep, size, *gots):
        return call(
            lambda *refs: step_kernel(bit, *refs),
            name,
            [WHOLE] * (1 + len(gots)),
            [((size + 16, half), low, WHOLE), ((size + 16, half), exact, WHOLE)],
            [pltpu.VMEM((2 * size + 16, half), exact)],
            (keep, *gots),
        )

    def join(name, *pieces):
        shape = (sum(p.shape[0] for p in pieces), pieces[0].shape[1])
        (out,) = call(join_kernel, name, [WHOLE] * len(pieces), [(shape, low, WHOLE)], [], pieces)
        return out

    cuts = (count // 3, count // 3, count - 2 * (count // 3) + 16)
    *up_sends, up_keep = call(
        up_grad_kernel,
        "up_grad",
        [WHOLE] * 2,
        [((2 * eighth, width), low, WHOLE)] * 4 + [((8 * eighth, width), exact, WHOLE)],
        [pltpu.VMEM((width, 4 * wide), exact)],
        (h_low, du),
        room=8 << 20,
    )
    up_gots = [swap_c(send) for send in up_sends]
    down_sends, down_keep = fold_into(2, "down_1", bit_r, down_keep, (down_got,))
    down_gots = [swap_r(send) for send in down_sends]
    (up_send,), up_keep = fold_into(1, "up_1", bit_near, up_keep, up_gots)
    up_got = swap_near(up_send)
    dkv, dq, dr, da, sums1, qv_sums = call(
        attend_back_kernel,
        "attend_back",
        [WHOLE] * 13,
        [
            ((keys, 2 * half), low, WHOLE),
            ((own, half), low, WHOLE),
            ((rows, width), exact, WHOLE),
            ((own, width), low, WHOLE),
            ((8, width), exact, WHOLE),
            ((8, half), exact, WHOLE),
        ],
        [
            pltpu.VMEM((keys, own), exact),
            pltpu.VMEM((pairs, own, 128), low),
            pltpu.VMEM((8, own), exact),
            pltpu.VMEM((pairs, keys, 128), exact),
            pltpu.VMEM((pairs, keys, 128), exact),
            pltpu.VMEM((2 * pairs, 64, own), exact),
            pltpu.VMEM((own, width), exact),
        ],
        (s_own, p_got, normed1, rstd1, vecs, wo_all, mixed, q3, k3, v3, kt, lse, ids),
        room=8 << 20,
    )

    (down_send,), down_keep = fold_into(1, "down_2", bit_near, down_keep, down_gots)
    down_got = swap_near(down_send)
    *rest_sends, rest_keep = call(
        weight_grad_kernel,
        "weight_grad",
        [WHOLE] * 9,
        [((n, half), low, WHOLE) for n in cuts] + [((count + 16, half), exact, WHOLE)],
        [pltpu.VMEM((2, count + 16, half), exact)],
        (x_all, dkv, dq, mixed, da, sums1, sums2, qv_sums, up_sums),
        after=(hidden,),
        room=8 << 20,
    )
    rest_gots = [swap_c(send) for send in rest_sends]
    rest_send, rest_keep = step("rest_1", bit_r, rest_keep, count // 2, *rest_gots)
    rest_got = swap_r(rest_send)
    up_send, up_keep = fold("up_2", bit_far, up_keep, up_got)
    up_got = swap_far(up_send)
    *x_sends, x_keep = call(
        input_grad_kernel,
        "input_grad",
        [WHOLE] * 3,
        [((own, width), low, WHOLE)] * 2 + [((2 * own, width), exact, WHOLE)],
        [pltpu.VMEM((keys, width), exact)],
        (dq, dkv, w_all),
        room=8 << 20,
    )
    x_gots = [swap_c(send) for send in x_sends]
    down_send, down_keep = fold("down_3", bit_far, down_keep, down_got)
    down_got = swap_far(down_send)
    x_send, x_keep = call(
        input_x_kernel,
        "input_x",
        [WHOLE] * 3,
        [((own, width), low, WHOLE), ((own, width), exact, WHOLE)],
        [],
        (x_keep, *x_gots),
        room=4 << 20,
    )
    x_got = swap_x(x_send)
    up_send, up_keep = fold("up_3", bit_r, up_keep, up_got)
    up_got = swap_r(up_send)
    (down_sum,) = call(
        sum_kernel, "down_sum", [WHOLE] * 2, [((eighth, width), low, WHOLE)], [], (down_keep, down_got)
    )
    down_other = swap_far(down_sum)
    x_send, x_keep = fold("input_r", bit_r, x_keep, x_got)
    x_got = swap_r(x_send)
    side, base = call(
        share_kernel,
        "up_share",
        [WHOLE] * 2,
        [((eighth // 2, width), low, WHOLE)] * 2,
        [],
        (up_keep.reshape(2, eighth // 2, width), up_got.reshape(2, eighth // 2, width)),
    )
    side = swap_x(side)
    rest_send, rest_keep = step("rest_2", bit_near, rest_keep, count // 4, rest_got)
    rest_got = swap_near(rest_send)
    down_sum = join("down_join", down_sum, down_other)
    down_other = swap_near(down_sum)
    rest_send, rest_keep = step("rest_3", bit_far, rest_keep, count // 8, rest_got)
    rest_got = swap_far(rest_send)
    up_sum = join("up_join", base, side)
    up_other = swap_far(up_sum)
    down_near = join("down_join_near", down_sum, down_other)
    down_far = swap_r(down_near)
    rest_side, rest_base, *lines, b_up_grad = call(
        last_step_kernel,
        "rest_last",
        [WHOLE] * 2,
        [((3 * thin, half), low, WHOLE), ((5 * thin, half), low, WHOLE)]
        + [((part,), exact, WHOLE)] * 8
        + [((2 * wide,), exact, WHOLE)],
        [pltpu.VMEM((8 * thin + 16, half), exact)],
        (rest_keep, rest_got),
    )
    rest_side = swap_x(rest_side)
    up_sum = join("up_join_far", up_sum, up_other)
    up_other = swap_near(up_sum)
    (total,) = call(
        total_kernel, "input_sum", [WHOLE] * 3, [((rows, width), low, WHOLE)], [], (x_keep, x_got, dr)
    )
    total = regroup(total)
    rest_sum = join("rest_join", rest_base, rest_side)
    rest_other = swap_far(rest_sum)
    rest_sum = join("rest_join_far", rest_sum, rest_other)
    rest_other = swap_near(rest_sum)
    w_down_grad, _ = call(
        down_out_kernel, "down_out", [WHOLE] * 2,
        [((2 * wide, width), exact, WHOLE), ((8, 128), exact, WHOLE)], [], (down_near, down_far),
        room=6 << 20,
    )
    up_near = join("up_join_near", up_sum, up_other)
    up_far = swap_r(up_near)
    rest_near = join("rest_join_near", rest_sum, rest_other)
    rest_far = swap_r(rest_near)
    w_up_grad, _ = call(
        up_out_kernel, "up_out", [WHOLE] * 2, [((part, inner), exact, WHOLE), ((8, 128), exact, WHOLE)],
        [pltpu.VMEM((4 * eighth, width), exact)], (up_near, up_far),
        room=6 << 20,
    )


    w_query_grad, w_key_grad, w_value_grad, w_out_grad, hidden_out, tokens_grad = call(
        rest_out_kernel,
        "rest_out",
        [WHOLE] * 4,
        [((part, width), exact, WHOLE)] * 4 + [((rows, width), low, WHOLE)] * 2,
        [pltpu.VMEM((32 * thin, half), exact)],
        (rest_near, rest_far, hidden, total),
        room=6 << 20,
    )

    return (
        hidden_out[None],
        tokens_grad[None],
        w_query_grad,
        lines[0],
        w_key_grad,
        w_value_grad,
        lines[1],
        w_out_grad,
        lines[2],
        lines[3],
        lines[4],
        w_up_grad,
        b_up_grad,
        w_down_grad,
        lines[5],
        lines[6],
        lines[7],
    )


def plane_solution(mesh):
    planes, cycle = mesh.shape["shard"], mesh.shape["ctx"]
    grid = Mesh(mesh.devices.reshape(planes, cycle // planes, 2, 2), AXES)
    shard, ctx = ("x", "c"), ("q", "r")
    tokens, matrix, vector = P(shard, ctx, None), P(shard, None), P(shard)
    return jax.shard_map(
        plane_local,
        mesh=grid,
        in_specs=(
            tokens, tokens, P(shard, ctx), matrix, vector, matrix, matrix, vector, matrix, vector,
            vector, vector, matrix, vector, matrix, vector, vector, vector,
        ),
        out_specs=(
            tokens, tokens, matrix, vector, matrix, matrix, vector, matrix, vector,
            vector, vector, matrix, vector, matrix, vector, vector, vector,
        ),
        check_vma=False,
    )


def solution(mesh):
    if mesh.shape["shard"] == 4 and mesh.shape["ctx"] == 8:
        return plane_solution(mesh)
    return ring_solution(mesh)
```

```python
import math

import jax
import jax.numpy as jnp
from jax import lax
from jax.experimental import pallas as pl
from jax.experimental.pallas import tpu as pltpu
from jax.sharding import Mesh
from jax.sharding import PartitionSpec as P

HEAD_DIM = 64


ln_eps = 1e-12
masked_fill = -1e30


def from_behind(block, axis, distance):
    devices = range(lax.axis_size(axis))
    route = [((i - distance) % len(devices), i) for i in devices]
    return lax.ppermute(block, axis, route)


def matmul(left, right):
    return jnp.dot(left, right, preferred_element_type=jnp.float32)


def matmul_tn(left, right):
    return lax.dot_general(
        left, right, (((0,), (0,)), ((), ())), preferred_element_type=jnp.float32
    )


def matmul_nt(left, right):
    return lax.dot_general(
        left, right, (((1,), (1,)), ((), ())), preferred_element_type=jnp.float32
    )


def apply_layer_norm(value, gain, shift):
    mean = jnp.mean(value, axis=-1, keepdims=True)
    centered = value - mean
    rstd = lax.rsqrt(jnp.mean(centered * centered, axis=-1, keepdims=True) + ln_eps)
    normed = centered * rstd
    return (normed * gain + shift, normed, rstd)


def norm_back(grad, normed, rstd, gain):
    d_gain = jnp.sum(grad * normed, axis=0)
    d_shift = jnp.sum(grad, axis=0)
    scaled = grad * gain
    d_value = rstd * (
        scaled
        - jnp.mean(scaled, axis=-1, keepdims=True)
        - normed * jnp.mean(scaled * normed, axis=-1, keepdims=True)
    )
    return (d_value, d_gain, d_shift)


def gelu_slope(value):
    normal_cdf = 0.5 * (1.0 + lax.erf(value * (1.0 / math.sqrt(2.0))))
    density = jnp.exp(-0.5 * value * value) * (1.0 / math.sqrt(2.0 * math.pi))
    return normal_cdf + value * density


def scores_of(query, keys, q_ids, k_ids, scale):
    raw = jnp.einsum("qhd,khd->hqk", query, keys, preferred_element_type=jnp.float32) * scale
    match = (q_ids[:, None] == k_ids[None, :])[None, :, :]
    return (raw, match)


def attend(query, q_ids, keys, values, k_ids, stats, scale):
    top, total, accum = stats
    raw, match = scores_of(query, keys, q_ids, k_ids, scale)
    masked = jnp.where(match, raw, masked_fill)
    new_top = jnp.maximum(top, jnp.max(masked, axis=-1))
    weights = jnp.where(match, jnp.exp(masked - new_top[:, :, None]), 0.0)
    factor = jnp.exp(top - new_top)
    total = total * factor + jnp.sum(weights, axis=-1)
    accum = accum * factor[:, :, None] + jnp.einsum(
        "hqk,khd->hqd", weights.astype(jnp.bfloat16), values, preferred_element_type=jnp.float32
    )
    return (new_top, total, accum)


def block_grads(query, q_ids, d_out, log_total, delta, keys, values, k_ids, scale):
    raw, match = scores_of(query, keys, q_ids, k_ids, scale)
    probs = jnp.exp(jnp.where(match, raw - log_total[:, :, None], masked_fill))
    d_values = jnp.einsum(
        "hqk,qhd->khd", probs.astype(jnp.bfloat16), d_out, preferred_element_type=jnp.float32
    )
    d_probs = jnp.einsum("qhd,khd->hqk", d_out, values, preferred_element_type=jnp.float32)
    d_scores = (probs * (d_probs - delta[:, :, None])).astype(jnp.bfloat16)
    d_query = jnp.einsum("hqk,khd->qhd", d_scores, keys, preferred_element_type=jnp.float32) * scale
    d_keys = jnp.einsum("hqk,qhd->khd", d_scores, query, preferred_element_type=jnp.float32) * scale
    return (d_query, d_keys, d_values)


def ring_local(
    tokens,
    cotangent,
    seq_ids,
    w_query,
    b_query,
    w_key,
    w_value,
    b_value,
    w_out,
    b_out,
    attn_gain,
    attn_shift,
    w_up,
    b_up,
    w_down,
    b_down,
    ffn_gain,
    ffn_shift,
):
    cycle = lax.axis_size("ctx")
    tok_rows = tokens.shape[1]
    width = tokens.shape[2]
    heads = width // HEAD_DIM
    scale = 1.0 / math.sqrt(HEAD_DIM)
    share = tok_rows // cycle
    got_tokens, got_grads, got_ids = (
        lax.all_to_all(
            tokens[0].reshape(share, cycle, width), "ctx", split_axis=1, concat_axis=1, tiled=True
        ),
        lax.all_to_all(
            cotangent[0].reshape(share, cycle, width),
            "ctx",
            split_axis=1,
            concat_axis=1,
            tiled=True,
        ),
        lax.all_to_all(
            seq_ids[0].reshape(share, cycle), "ctx", split_axis=1, concat_axis=1, tiled=True
        ),
    )
    x_local = got_tokens.reshape(tok_rows, width)
    local_gradient = got_grads.reshape(tok_rows, width).astype(jnp.float32)
    local_ids = got_ids.reshape(tok_rows)
    (
        query_mat,
        query_bias,
        key_mat,
        value_mat,
        value_bias,
        out_mat,
        out_bias,
        attention_norm_gain,
        first_shift,
        up_mat,
        up_bias,
        down_mat,
        down_bias,
        feedforward_norm_gain,
        second_shift,
    ) = (
        lax.all_gather(w_query, "shard", axis=0, tiled=True),
        lax.all_gather(b_query, "shard", axis=0, tiled=True),
        lax.all_gather(w_key, "shard", axis=0, tiled=True),
        lax.all_gather(w_value, "shard", axis=0, tiled=True),
        lax.all_gather(b_value, "shard", axis=0, tiled=True),
        lax.all_gather(w_out, "shard", axis=0, tiled=True),
        lax.all_gather(b_out, "shard", axis=0, tiled=True),
        lax.all_gather(attn_gain, "shard", axis=0, tiled=True),
        lax.all_gather(attn_shift, "shard", axis=0, tiled=True),
        lax.all_gather(w_up, "shard", axis=0, tiled=True),
        lax.all_gather(b_up, "shard", axis=0, tiled=True),
        lax.all_gather(w_down, "shard", axis=0, tiled=True),
        lax.all_gather(b_down, "shard", axis=0, tiled=True),
        lax.all_gather(ffn_gain, "shard", axis=0, tiled=True),
        lax.all_gather(ffn_shift, "shard", axis=0, tiled=True),
    )
    query = (matmul(x_local, query_mat) + query_bias.astype(jnp.float32)).astype(jnp.bfloat16)
    keys = matmul(x_local, key_mat).astype(jnp.bfloat16)
    values = (matmul(x_local, value_mat) + value_bias.astype(jnp.float32)).astype(jnp.bfloat16)
    q_heads = query.reshape(tok_rows, heads, HEAD_DIM)
    start_stats = (
        jnp.full((heads, tok_rows), masked_fill, jnp.float32),
        jnp.zeros((heads, tok_rows), jnp.float32),
        jnp.zeros((heads, tok_rows, HEAD_DIM), jnp.float32),
    )

    def forward_step(step, carry):
        block, stats = carry
        stats = attend(
            q_heads,
            local_ids,
            block[0].reshape(tok_rows, heads, HEAD_DIM),
            block[1].reshape(tok_rows, heads, HEAD_DIM),
            block[2],
            stats,
            scale,
        )
        block = from_behind((block[0], block[1], block[2]), "ctx", 1)
        return (block, stats)

    block, stats = lax.fori_loop(
        0, cycle - 1, forward_step, ((keys, values, local_ids), start_stats)
    )
    top, total, accum = attend(
        q_heads,
        local_ids,
        block[0].reshape(tok_rows, heads, HEAD_DIM),
        block[1].reshape(tok_rows, heads, HEAD_DIM),
        block[2],
        stats,
        scale,
    )
    attn_out = (
        (accum / total[:, :, None]).transpose(1, 0, 2).reshape(tok_rows, width).astype(jnp.bfloat16)
    )
    log_total = top + jnp.log(total)
    attn_proj = matmul(attn_out, out_mat) + out_bias.astype(jnp.float32)
    first_sum = x_local.astype(jnp.float32) + attn_proj
    first_normalized_rows, first_centered_scaled, first_inverse_deviation = apply_layer_norm(
        first_sum, attention_norm_gain.astype(jnp.float32), first_shift.astype(jnp.float32)
    )
    normed_low = first_normalized_rows.astype(jnp.bfloat16)
    up_pre = matmul(normed_low, up_mat) + up_bias.astype(jnp.float32)
    up_act = jax.nn.gelu(up_pre, approximate=False).astype(jnp.bfloat16)
    down_pre = matmul(up_act, down_mat) + down_bias.astype(jnp.float32)
    layer_output, second_centered_scaled, second_inverse_deviation = apply_layer_norm(
        first_normalized_rows + down_pre,
        feedforward_norm_gain.astype(jnp.float32),
        second_shift.astype(jnp.float32),
    )
    (
        query_mat,
        key_mat,
        value_mat,
        out_mat,
        attention_norm_gain,
        up_mat,
        down_mat,
        feedforward_norm_gain,
    ) = (
        lax.all_gather(w_query, "shard", axis=0, tiled=True),
        lax.all_gather(w_key, "shard", axis=0, tiled=True),
        lax.all_gather(w_value, "shard", axis=0, tiled=True),
        lax.all_gather(w_out, "shard", axis=0, tiled=True),
        lax.all_gather(attn_gain, "shard", axis=0, tiled=True),
        lax.all_gather(w_up, "shard", axis=0, tiled=True),
        lax.all_gather(w_down, "shard", axis=0, tiled=True),
        lax.all_gather(ffn_gain, "shard", axis=0, tiled=True),
    )
    grad_two, d_second_gain, d_second_shift = norm_back(
        local_gradient,
        second_centered_scaled,
        second_inverse_deviation,
        feedforward_norm_gain.astype(jnp.float32),
    )
    grad_down = grad_two.astype(jnp.bfloat16)
    d_down_bias = jnp.sum(grad_down, axis=0, dtype=jnp.float32)
    d_down_mat = matmul_tn(up_act, grad_down)
    grad_up = (matmul_nt(grad_down, down_mat) * gelu_slope(up_pre)).astype(jnp.bfloat16)
    d_up_bias = jnp.sum(grad_up, axis=0, dtype=jnp.float32)
    d_up_mat = matmul_tn(normed_low, grad_up)
    first_norm_gradient = grad_two + matmul_nt(grad_up, up_mat)
    grad_first, d_first_gain, d_first_shift = norm_back(
        first_norm_gradient,
        first_centered_scaled,
        first_inverse_deviation,
        attention_norm_gain.astype(jnp.float32),
    )
    grad_proj = grad_first.astype(jnp.bfloat16)
    d_out_bias = jnp.sum(grad_proj, axis=0, dtype=jnp.float32)
    d_out_mat = matmul_tn(attn_out, grad_proj)
    grad_attn = matmul_nt(grad_proj, out_mat).astype(jnp.bfloat16)
    grad_heads = grad_attn.reshape(tok_rows, heads, HEAD_DIM)
    delta = jnp.einsum(
        "qhd,qhd->hq",
        grad_heads,
        attn_out.reshape(tok_rows, heads, HEAD_DIM),
        preferred_element_type=jnp.float32,
    )
    zero_rows = jnp.zeros((tok_rows, width), jnp.float32)

    def key_step(step, carry):
        block, sums, acc_query = carry
        d_query, d_keys, d_values = block_grads(
            q_heads,
            local_ids,
            grad_heads,
            log_total,
            delta,
            block[0].reshape(tok_rows, heads, HEAD_DIM),
            block[1].reshape(tok_rows, heads, HEAD_DIM),
            block[2],
            scale,
        )
        sums = (
            sums[0] + d_keys.reshape(tok_rows, width),
            sums[1] + d_values.reshape(tok_rows, width),
        )
        block = from_behind((block[0], block[1], block[2]), "ctx", 1)
        sums = (
            from_behind(sums[0].astype(jnp.bfloat16), "ctx", 1).astype(jnp.float32),
            from_behind(sums[1].astype(jnp.bfloat16), "ctx", 1).astype(jnp.float32),
        )
        return (block, sums, acc_query + d_query.reshape(tok_rows, width))

    block, sums, d_query_sum = lax.fori_loop(
        0, cycle, key_step, ((keys, values, local_ids), (zero_rows, zero_rows), zero_rows)
    )
    d_keys_sum, d_values_sum = sums
    grad_query = d_query_sum.astype(jnp.bfloat16)
    grad_keys = d_keys_sum.astype(jnp.bfloat16)
    grad_values = d_values_sum.astype(jnp.bfloat16)
    d_query_bias = jnp.sum(grad_query, axis=0, dtype=jnp.float32)
    d_value_bias = jnp.sum(grad_values, axis=0, dtype=jnp.float32)
    d_query_mat = matmul_tn(x_local, grad_query)
    d_key_mat = matmul_tn(x_local, grad_keys)
    d_value_mat = matmul_tn(x_local, grad_values)
    grad_input = (
        grad_first
        + matmul_nt(grad_query, query_mat)
        + matmul_nt(grad_keys, key_mat)
        + matmul_nt(grad_values, value_mat)
    )
    home_hidden, home_grad = (
        lax.all_to_all(
            layer_output.astype(jnp.bfloat16).reshape(share, cycle, width),
            "ctx",
            split_axis=1,
            concat_axis=1,
            tiled=True,
        ),
        lax.all_to_all(
            grad_input.astype(jnp.bfloat16).reshape(share, cycle, width),
            "ctx",
            split_axis=1,
            concat_axis=1,
            tiled=True,
        ),
    )
    hidden_out = home_hidden.reshape(tok_rows, width)[None]
    tokens_grad = home_grad.reshape(tok_rows, width)[None]
    shares = (
        lax.psum_scatter(
            d_query_mat.astype(jnp.bfloat16), "shard", scatter_dimension=0, tiled=True
        ).astype(jnp.float32),
        lax.psum_scatter(
            d_query_bias.astype(jnp.bfloat16), "shard", scatter_dimension=0, tiled=True
        ).astype(jnp.float32),
        lax.psum_scatter(
            d_key_mat.astype(jnp.bfloat16), "shard", scatter_dimension=0, tiled=True
        ).astype(jnp.float32),
        lax.psum_scatter(
            d_value_mat.astype(jnp.bfloat16), "shard", scatter_dimension=0, tiled=True
        ).astype(jnp.float32),
        lax.psum_scatter(
            d_value_bias.astype(jnp.bfloat16), "shard", scatter_dimension=0, tiled=True
        ).astype(jnp.float32),
        lax.psum_scatter(
            d_out_mat.astype(jnp.bfloat16), "shard", scatter_dimension=0, tiled=True
        ).astype(jnp.float32),
        lax.psum_scatter(
            d_out_bias.astype(jnp.bfloat16), "shard", scatter_dimension=0, tiled=True
        ).astype(jnp.float32),
        lax.psum_scatter(
            d_first_gain.astype(jnp.bfloat16), "shard", scatter_dimension=0, tiled=True
        ).astype(jnp.float32),
        lax.psum_scatter(
            d_first_shift.astype(jnp.bfloat16), "shard", scatter_dimension=0, tiled=True
        ).astype(jnp.float32),
        lax.psum_scatter(
            d_up_mat.astype(jnp.bfloat16), "shard", scatter_dimension=0, tiled=True
        ).astype(jnp.float32),
        lax.psum_scatter(
            d_up_bias.astype(jnp.bfloat16), "shard", scatter_dimension=0, tiled=True
        ).astype(jnp.float32),
        lax.psum_scatter(
            d_down_mat.astype(jnp.bfloat16), "shard", scatter_dimension=0, tiled=True
        ).astype(jnp.float32),
        lax.psum_scatter(
            d_down_bias.astype(jnp.bfloat16), "shard", scatter_dimension=0, tiled=True
        ).astype(jnp.float32),
        lax.psum_scatter(
            d_second_gain.astype(jnp.bfloat16), "shard", scatter_dimension=0, tiled=True
        ).astype(jnp.float32),
        lax.psum_scatter(
            d_second_shift.astype(jnp.bfloat16), "shard", scatter_dimension=0, tiled=True
        ).astype(jnp.float32),
    )
    totals = lax.psum(
        (
            shares[0],
            shares[1],
            shares[2],
            shares[3],
            shares[4],
            shares[5],
            shares[6],
            shares[7],
            shares[8],
            shares[9],
            shares[10],
            shares[11],
            shares[12],
            shares[13],
            shares[14],
        ),
        "ctx",
    )
    return (hidden_out, tokens_grad) + tuple(totals)


def ring_solution(mesh):
    return jax.shard_map(
        ring_local,
        mesh=mesh,
        in_specs=(
            P("shard", "ctx", None),
            P("shard", "ctx", None),
            P("shard", "ctx"),
            P("shard", None),
            P("shard"),
            P("shard", None),
            P("shard", None),
            P("shard"),
            P("shard", None),
            P("shard"),
            P("shard"),
            P("shard"),
            P("shard", None),
            P("shard"),
            P("shard", None),
            P("shard"),
            P("shard"),
            P("shard"),
        ),
        out_specs=(
            P("shard", "ctx", None),
            P("shard", "ctx", None),
            P("shard", None),
            P("shard"),
            P("shard", None),
            P("shard", None),
            P("shard"),
            P("shard", None),
            P("shard"),
            P("shard"),
            P("shard"),
            P("shard", None),
            P("shard"),
            P("shard", None),
            P("shard"),
            P("shard"),
            P("shard"),
        ),
        check_vma=False,
    )


AXES = ("q", "r", "x", "c")
ANY = pl.BlockSpec(memory_space=pl.ANY)
WHOLE = pl.BlockSpec(memory_space=pltpu.VMEM)
HBM = pl.BlockSpec(memory_space=pltpu.HBM)


def moved(block, move):
    sizes = [lax.axis_size(a) for a in AXES]

    def number(spot):
        place = 0
        for size, at in zip(sizes, spot):
            place = place * size + at
        return place

    spots = [
        (q, r, x, c)
        for q in range(sizes[0])
        for r in range(sizes[1])
        for x in range(sizes[2])
        for c in range(sizes[3])
    ]
    return lax.ppermute(block, AXES, [(number(s), number(move(*s))) for s in spots])


def swap_x(block):
    return moved(block, lambda q, r, x, c: (q, r, 1 - x, c))


def swap_c(block):
    return moved(block, lambda q, r, x, c: (q, r, x, 1 - c))


def swap_r(block):
    return moved(block, lambda q, r, x, c: (q, r ^ 1, x, c))


def swap_rc(block):
    return moved(block, lambda q, r, x, c: (q, r ^ 1, x, 1 - c))


def swap_near(block):
    return moved(block, lambda q, r, x, c: (q ^ 1, r, x, c))


def swap_far(block):
    return moved(block, lambda q, r, x, c: (q ^ 2, r, x, c))


def regroup(block):
    return moved(block, lambda q, r, x, c: (2 * c + x, r, q & 1, q >> 1))


def regroup_x(block):
    return moved(block, lambda q, r, x, c: (2 * c + x, r, 1 - (q & 1), q >> 1))


def swap_xc(block):
    return moved(block, lambda q, r, x, c: (q, r, 1 - x, 1 - c))


def beside(mine, got):
    return jnp.concatenate([mine, got])


def dot(left, right):
    return jnp.dot(left, right, preferred_element_type=jnp.float32)


def dot_nt(left, right):
    return lax.dot_general(
        left, right, (((1,), (1,)), ((), ())), preferred_element_type=jnp.float32
    )


def dot_tn(left, right):
    return lax.dot_general(
        left, right, (((0,), (0,)), ((), ())), preferred_element_type=jnp.float32
    )


class Copies:
    def __init__(self, sems):
        self.sems = sems
        self.count = 0
        self.held = []

    def start(self, source, target):
        copy = pltpu.make_async_copy(source, target, self.sems.at[self.count])
        copy.start()
        self.count += 1
        self.held.append(copy)

    def wait(self):
        for copy in self.held:
            copy.wait()
        self.held = []


def spot():
    return tuple(lax.axis_index(a) for a in AXES)


def fill_mask(ids, mask, own):
    blocks, rows = ids.shape
    mine = jnp.concatenate([ids[pl.ds(own, 1), :], ids[pl.ds(own + 1, 1), :]], axis=1)
    across = jnp.transpose(ids[...])
    for b in range(blocks):
        mask[rows * b : rows * (b + 1), :] = jnp.where(across[:, b : b + 1] == mine, 0.0, masked_fill)


def block_kernel(tokens, ids, block, line, sems):
    rows = tokens.shape[0]
    copies = Copies(sems)
    copies.start(tokens, block.at[pl.ds(0, rows)])
    copies.start(ids, line)
    block[rows:, :] = jnp.zeros((16, block.shape[1]), block.dtype)
    copies.wait()
    block[rows:, 0:rows] = jnp.broadcast_to(line[...].astype(jnp.float32), (16, rows)).astype(block.dtype)


def pack_kernel(w_q, w_k, w_v, *refs):
    vectors, b_up, theirs, mine = refs[:8], refs[8], refs[9], refs[10]
    lines, thin, thick, sems = refs[11], refs[12:20], refs[20], refs[21]
    q, r, x, c = spot()
    part, width = w_q.shape
    half = width // 2
    copies = Copies(sems)
    few = part // 2
    for t, w in enumerate((w_q, w_k, w_v)):
        copies.start(w.at[:, pl.ds(pl.multiple_of(half * x, 128), half)], mine.at[pl.ds(part * t, part)])
        copies.start(
            w.at[pl.ds(pl.multiple_of(few * r, 32), few), pl.ds(pl.multiple_of(half * (1 - x), 128), half)],
            theirs.at[pl.ds(few * t, few)],
        )
    for vector, held in zip(vectors, thin):
        copies.start(vector, held)
    copies.start(b_up, thick)
    lines[...] = jnp.zeros_like(lines)
    copies.wait()
    for i, vector in enumerate(thin):
        line = vector[...].astype(jnp.float32).reshape(1, part)
        none = jnp.zeros_like(line)
        first = jnp.concatenate([line, none], axis=1)
        second = jnp.concatenate([none, line], axis=1)
        lines[i : i + 1, :] = jnp.where(c == 0, first, second)
    wide = thick[...].astype(jnp.float32).reshape(1, width)
    lines[pl.ds(8 + 2 * c, 1), :] = wide[:, 0:half]
    lines[pl.ds(9 + 2 * c, 1), :] = wide[:, half:]
    low = lines[...].astype(jnp.bfloat16)
    mine[3 * part :, :] = low
    theirs[3 * few :, :] = low


def cut_kernel(w, theirs, mine, sems):
    q, r, x, c = spot()
    count = theirs.shape[1]
    copies = Copies(sems)
    copies.start(w.at[:, pl.ds(pl.multiple_of(count * (1 - x), 128), count)], theirs)
    copies.start(w.at[:, pl.ds(pl.multiple_of(count * x, 128), count)], mine)
    copies.wait()


def load_kernel(block, out, sems):
    copies = Copies(sems)
    copies.start(block, out)
    copies.wait()


def turn_kernel(keys, out):
    for p in range(keys.shape[0]):
        out[2 * p : 2 * p + 2] = jnp.transpose(keys[p]).reshape(2, 64, keys.shape[1])


def project_kernel(
    b0, b1, b2, b3, w_q, w_k, w_v, w_m, xa, xb, ma, mb, own_lines,
    kv_out, q_out, w, vecs, up_bias, xs, sems,
):
    q, r, x, c = spot()
    rows = xs.shape[0] // 4
    part = w.shape[0] // 4
    half = w.shape[1] // 3
    me, shard = 2 * c + x, 2 * x + c
    columns = pl.ds(pl.multiple_of(half * x, 128), half)
    ins = Copies(sems)
    for t, own in enumerate((w_q, w_k, w_v)):
        at = pl.ds(pl.multiple_of(part * shard, 64), part)
        ins.start(own.at[:, columns], w.at[at, pl.ds(half * t, half)])
    for j, block in enumerate((b0, b1, b2, b3)):
        xs[pl.ds(pl.multiple_of(rows * (me ^ j), rows), rows), :] = block[0:rows, :]
    few = part // 2
    for t in range(3):
        place = slice(half * t, half * (t + 1))
        at = pl.ds(pl.multiple_of(part * (shard ^ 1), 64), part)
        w[at, place] = w_m[part * t : part * (t + 1), :]
        for flip, side, piece in ((2, r, xa), (2, 1 - r, xb), (3, r, ma), (3, 1 - r, mb)):
            at = pl.ds(pl.multiple_of(part * (shard ^ flip) + few * side, 32), few)
            w[at, place] = piece[few * t : few * (t + 1), :]
    mine, other = (
        a[at:, :].astype(jnp.float32) + b[at:, :].astype(jnp.float32)
        for a, b, at in ((own_lines, w_m, 3 * part), (xa, ma, 3 * few))
    )
    vecs[:, columns] = mine[0:8, :]
    vecs[:, pl.ds(pl.multiple_of(half * (1 - x), 128), half)] = other[0:8, :]
    for i in range(4):
        up_bias[i] = jnp.broadcast_to(mine[8 + i : 9 + i, :], (8, half))
    ins.wait()
    kv_out[:, 0:half] = dot(xs[...], w[:, half : 2 * half]).astype(jnp.bfloat16)
    kv_out[:, half:] = (dot(xs[...], w[:, 2 * half :]) + mine[1:2, :]).astype(jnp.bfloat16)
    own = pl.ds(pl.multiple_of(2 * rows * c, rows), 2 * rows)
    q_out[...] = (dot(xs[own, :], w[:, 0:half]) + mine[0:1, :]).astype(jnp.bfloat16)


def attend_kernel(
    b0, b1, b2, b3, b4, b5, b6, b7, kv_own, q_own, w, vecs, w_o, w_om,
    a_low, xs, wo, k3, v3, q3, o_out, lse_out, ids_out, a_out,
    vt, ot, mask, sems,
):
    q, r, x, c = spot()
    rows = xs.shape[0] // 8
    half = wo.shape[0]
    part = half // 2
    me = 4 * r + 2 * c + x
    ins = Copies(sems)
    ins.start(w_o, wo.at[pl.ds(pl.multiple_of(part * c, 64), part)])
    wo[pl.ds(pl.multiple_of(part * (1 - c), 64), part), :] = w_om[...]
    for j, block in enumerate((b0, b1, b2, b3, b4, b5, b6, b7)):
        at = me ^ j
        xs[pl.ds(pl.multiple_of(rows * at, rows), rows), :] = block[0:rows, :]
        ids_out[pl.ds(at, 1), :] = block[rows : rows + 16, 0:rows].astype(jnp.float32)[0:1, :]
    fill_mask(ids_out, mask, 4 * r + 2 * c)
    rest = pl.ds(pl.multiple_of(4 * rows * (1 - r), rows), 4 * rows)
    here = pl.ds(pl.multiple_of(4 * rows * r, rows), 4 * rows)
    bias = vecs[1:2, pl.ds(pl.multiple_of(half * x, 128), half)]
    keyed = dot(xs[rest, :], w[:, half : 2 * half]).astype(jnp.bfloat16)
    valued = (dot(xs[rest, :], w[:, 2 * half :]) + bias).astype(jnp.bfloat16)
    pairs = half // 128
    for p in range(pairs):
        at = slice(128 * p, 128 * (p + 1))
        k3[p, here, :] = kv_own[:, at]
        k3[p, rest, :] = keyed[:, at]
        v3[p, here, :] = kv_own[:, half + 128 * p : half + 128 * (p + 1)]
        v3[p, rest, :] = valued[:, at]
        q3[p] = q_own[:, at]
        vt[2 * p : 2 * p + 2] = jnp.transpose(v3[p]).reshape(2, 64, 8 * rows)
    lane = lax.broadcasted_iota(jnp.int32, (2 * rows, 128), 1) // 64

    def head(h, carry):
        query = jnp.where(lane == h % 2, q3[h // 2], 0) * 0.125
        scores = dot_nt(k3[h // 2], query.astype(jnp.bfloat16)) + mask[...]
        top = jnp.max(scores, axis=0, keepdims=True)
        weights = jnp.exp(scores - top)
        total = jnp.sum(weights, axis=0, keepdims=True)
        ot[h] = dot(vt[h], weights.astype(jnp.bfloat16)) / total
        lse_out[pl.ds(h, 1), :] = top + jnp.log(total)
        return carry

    lax.fori_loop(0, 2 * pairs, head, 0, unroll=3)
    mixed = jnp.transpose(ot[...].reshape(half, 2 * rows)).astype(jnp.bfloat16)
    o_out[...] = mixed
    ins.wait()
    partial = dot(mixed, wo[...])
    a_out[...] = partial
    a_low[...] = partial.astype(jnp.bfloat16)


def inner_kernel(u_own, u_x, u_m, u_mx0, u_mx1, d_own, d_m, up, down, sems):
    q, r, x, c = spot()
    part = up.shape[0] // 4
    count = up.shape[1]
    shard = 2 * x + c
    ins = Copies(sems)
    own = u_own.at[:, pl.ds(pl.multiple_of(count * x, 128), count)]
    ins.start(own, up.at[pl.ds(pl.multiple_of(part * shard, 64), part)])
    ins.start(d_own, down.at[pl.ds(pl.multiple_of(count // 2 * c, 128), count // 2)])
    for flip, piece in ((2, u_x), (1, u_m)):
        up[pl.ds(pl.multiple_of(part * (shard ^ flip), 64), part), :] = piece[...]
    for i, piece in enumerate((u_mx0, u_mx1)):
        at = pl.multiple_of(part * (shard ^ 3) + part // 2 * i, 32)
        up[pl.ds(at, part // 2), :] = piece[...]
    down[pl.ds(pl.multiple_of(count // 2 * (1 - c), 128), count // 2), :] = d_m[...]
    ins.wait()


def norm_of(value):
    mean = jnp.mean(value, axis=-1, keepdims=True)
    centered = value - mean
    rstd = lax.rsqrt(jnp.mean(centered * centered, axis=-1, keepdims=True) + ln_eps)
    return centered * rstd, rstd


def norm_pull(scaled, normed, rstd):
    return rstd * (
        scaled
        - jnp.mean(scaled, axis=-1, keepdims=True)
        - normed * jnp.mean(scaled * normed, axis=-1, keepdims=True)
    )


def forward_kernel(
    a_own, a_got, xs, vecs, b_up, up, down,
    y_low, y_more, h_out, z, n_out, r_out, slope, y_out,
):
    q, r, x, c = spot()
    rows = a_own.shape[0]
    x_own = xs[pl.ds(pl.multiple_of(rows * (2 * r + c), rows), rows), :]
    total = x_own.astype(jnp.float32) + (a_own[...] + a_got[...].astype(jnp.float32) + vecs[2:3, :])
    normed, rstd = norm_of(total)
    n_out[...] = normed
    r_out[...] = jnp.broadcast_to(rstd, r_out.shape)
    low = (normed * vecs[3:4, :] + vecs[4:5, :]).astype(jnp.bfloat16)
    h_out[...] = low
    wide = up.shape[1] // 4
    for j in range(4):
        at = slice(wide * j, wide * (j + 1))
        pre = dot(low, up[:, at]) + b_up[j, 0:1, :]
        cdf = 0.5 * (1.0 + lax.erf(pre * (1.0 / math.sqrt(2.0))))
        density = jnp.exp(-0.5 * pre * pre) * (1.0 / math.sqrt(2.0 * math.pi))
        z[:, at] = (pre * cdf).astype(jnp.bfloat16)
        slope[:, at] = cdf + pre * density
    result = dot(z[...], down[...])
    y_out[...] = result
    rows = y_low.shape[0]
    y_low[...] = result[0:rows, :].astype(jnp.bfloat16)
    y_more[...] = result[rows:, :].astype(jnp.bfloat16)


def norm_back_kernel(
    y_own, y_got, y_rest, normed1, g_own, g_x, vecs, low_out, hid_out, dy_out, sums, grad, hid,
):
    q, r, x, c = spot()
    rows = grad.shape[0] // 2
    grad[pl.ds(pl.multiple_of(rows * x, rows), rows), :] = g_own[...]
    grad[pl.ds(pl.multiple_of(rows * (1 - x), rows), rows), :] = g_x[...]
    got = jnp.concatenate([y_got[...], y_rest[...]]).astype(jnp.float32)
    h1 = normed1[...] * vecs[3:4, :] + vecs[4:5, :]
    normed, rstd = norm_of(h1 + (y_own[...] + got + vecs[5:6, :]))
    hid[...] = (normed * vecs[6:7, :] + vecs[7:8, :]).astype(jnp.bfloat16)
    hid_out[...] = hid[pl.ds(pl.multiple_of(rows * x, rows), rows), :]
    cot = grad[...].astype(jnp.float32)
    dy = norm_pull(cot * vecs[6:7, :], normed, rstd)
    low = dy.astype(jnp.bfloat16)
    dy_out[...] = dy
    low_out[...] = low
    sums[...] = jnp.zeros_like(sums)
    sums[0:1, :] = jnp.sum(low.astype(jnp.float32), axis=0, keepdims=True)
    sums[1:2, :] = jnp.sum(cot * normed, axis=0, keepdims=True)
    sums[2:3, :] = jnp.sum(cot, axis=0, keepdims=True)


def backward_kernel(dy, dy_low, slope, up, down, p_low, s_out, du_out, up_sums):
    low = dy_low[...]
    wide = up.shape[1] // 4
    for j in range(4):
        at = slice(wide * j, wide * (j + 1))
        du = (dot_nt(low, down[at, :]) * slope[:, at]).astype(jnp.bfloat16)
        du_out[:, at] = du
        total = jnp.sum(du.astype(jnp.float32), axis=0, keepdims=True)
        up_sums[j] = jnp.broadcast_to(total, up_sums.shape[1:])
    result = dot_nt(du_out[...], up[...])
    s_out[...] = dy[...] + result
    p_low[...] = result.astype(jnp.bfloat16)


def attend_back_kernel(
    s_own, p_got, normed1, rstd1, vecs, wo, mixed, q3, k3, v3, kt, lse, ids,
    dkv_out, dq_out, dr_out, da_out, sums, qv_sums,
    mask, do3, delta, dk, dv, dqt, whole,
):
    q, r, x, c = spot()
    rows = dr_out.shape[0]
    pairs = q3.shape[0]
    half = 128 * pairs
    fill_mask(ids, mask, 4 * r + 2 * c)
    dh = s_own[...] + p_got[...].astype(jnp.float32)
    normed = normed1[...]
    dr = norm_pull(dh * vecs[3:4, :], normed, rstd1[:, 0:1])
    whole[...] = dr
    dr_out[...] = whole[pl.ds(pl.multiple_of(rows * x, rows), rows), :]
    low = dr.astype(jnp.bfloat16)
    da_out[...] = low
    sums[...] = jnp.zeros_like(sums)
    sums[0:1, :] = jnp.sum(low.astype(jnp.float32), axis=0, keepdims=True)
    sums[1:2, :] = jnp.sum(dh * normed, axis=0, keepdims=True)
    sums[2:3, :] = jnp.sum(dh, axis=0, keepdims=True)
    d_o = dot_nt(low, wo[...]).astype(jnp.bfloat16)
    products = jnp.transpose(d_o.astype(jnp.float32) * mixed[...].astype(jnp.float32))
    for h in range(2 * pairs):
        delta[h : h + 1, :] = jnp.sum(products[64 * h : 64 * (h + 1), :], axis=0, keepdims=True)
    for p in range(pairs):
        do3[p] = d_o[:, 128 * p : 128 * (p + 1)]
    dk[...] = jnp.zeros_like(dk)
    dv[...] = jnp.zeros_like(dv)
    lane = lax.broadcasted_iota(jnp.int32, (2 * rows, 128), 1) // 64

    def head(h, carry):
        p = h // 2
        here = lane == h % 2
        query = (jnp.where(here, q3[p], 0) * 0.125).astype(jnp.bfloat16)
        d_here = jnp.where(here, do3[p], 0).astype(jnp.bfloat16)
        probs = jnp.exp(dot_nt(k3[p], query) + mask[...] - lse[pl.ds(h, 1), :])
        d_probs = dot_nt(v3[p], d_here)
        d_scores = (probs * (d_probs - delta[pl.ds(h, 1), :])).astype(jnp.bfloat16)
        dv[p] += dot(probs.astype(jnp.bfloat16), d_here)
        dk[p] += dot(d_scores, query)
        dqt[h] = dot(kt[h], d_scores)
        return carry

    lax.fori_loop(0, 2 * pairs, head, 0, unroll=3)
    dq = (jnp.transpose(dqt[...].reshape(half, 2 * rows)) * 0.125).astype(jnp.bfloat16)
    dq_out[...] = dq
    qv_sums[...] = jnp.zeros_like(qv_sums)
    qv_sums[0:1, :] = jnp.sum(dq.astype(jnp.float32), axis=0, keepdims=True)
    for p in range(pairs):
        at = slice(128 * p, 128 * (p + 1))
        dkv_out[:, at] = dk[p].astype(jnp.bfloat16)
        value = dv[p].astype(jnp.bfloat16)
        dkv_out[:, half + 128 * p : half + 128 * (p + 1)] = value
        qv_sums[1:2, at] = jnp.sum(value.astype(jnp.float32), axis=0, keepdims=True)


def input_grad_kernel(dq, dkv, w, *refs):
    sends, (keep, whole) = refs[:2], refs[2:]
    q, r, x, c = spot()
    half = dq.shape[1]
    rows = dq.shape[0] // 2
    whole[...] = dot_nt(dkv[...], w[:, half:])
    own = pl.ds(pl.multiple_of(rows * (4 * r + 2 * c), rows), 2 * rows)
    whole[own, :] += dot_nt(dq[...], w[:, 0:half])
    for b in range(2):
        for i in range(2):
            to = slice(2 * rows * b + rows * i, 2 * rows * b + rows * (i + 1))
            mine = pl.ds(pl.multiple_of(rows * (4 * i + 2 * c + b), rows), rows)
            keep[to, :] = whole[mine, :]
            theirs = pl.ds(pl.multiple_of(rows * (4 * i + 2 * (1 - c) + b), rows), rows)
            sends[b][rows * i : rows * (i + 1), :] = whole[theirs, :].astype(jnp.bfloat16)


def input_x_kernel(keep, got0, got1, send, kept):
    q, r, x, c = spot()
    half = send.shape[0]
    for side, got in enumerate((got0, got1)):
        total = keep[half * side : half * (side + 1), :] + got[...].astype(jnp.float32)

        @pl.when(x == side)
        def _():
            kept[...] = total

        @pl.when(x != side)
        def _():
            send[...] = total.astype(jnp.bfloat16)


def octants():
    for at in range(8):
        r, q0, q1 = at >> 2, at >> 1 & 1, at & 1
        yield 4 * r + 2 * q0 + 1 * q1, 1 * r + 4 * q0 + 2 * q1, 4 * r + 2 * q1 + q0


def down_grad_kernel(z, dy, send, keep):
    q, r, x, c = spot()
    half = z.shape[1] // 2
    rows = half // 8
    for side, out in ((1 - c, send), (c, keep)):
        part = dot_tn(z[:, pl.ds(pl.multiple_of(half * side, 128), half)], dy[...])
        for at, _, within in octants():
            block = part[rows * within : rows * (within + 1), :]
            out[rows * at : rows * (at + 1), :] = block.astype(out.dtype)


def up_grad_kernel(h, du, *refs):
    q, r, x, c = spot()
    sends, (keep, whole) = refs[:4], refs[4:]
    width = h.shape[1]
    thin = width // 32
    whole[...] = dot_tn(h[...], du[...])
    for side in (1 - c, c):
        for _, at, within in octants():
            pieces = []
            for xx in range(2):
                first = 8 * thin * (2 * xx + side) + thin * within
                rows = pl.ds(pl.multiple_of(first, 8), thin)
                pieces += [whole[rows, 0:width], whole[rows, width:]]
            block = jnp.concatenate(pieces)
            if side is c:
                keep[4 * thin * at : 4 * thin * (at + 1), :] = block
            else:
                to = 4 * thin * (at % 2)
                sends[at // 2][to : to + 4 * thin, :] = block.astype(jnp.bfloat16)


def join_kernel(*refs):
    out, at = refs[-1], 0
    for ref in refs[:-1]:
        count = ref.shape[0]
        out[at : at + count, :] = ref[...]
        at += count


def fold_pieces_kernel(bit, count, keep, *refs):
    gots, sends, (kept, whole) = refs[: -2 - count], refs[-2 - count : -2], refs[-2:]
    at = bit(*spot())
    first = 0
    for got in gots:
        rows = slice(first, first + got.shape[0])
        whole[rows, :] = keep[rows, :] + got[...].astype(jnp.float32)
        first += got.shape[0]
    half = kept.shape[0]
    kept[...] = whole[pl.ds(pl.multiple_of(half * at, 64), half), :]
    for i, send in enumerate(sends):
        rows = pl.ds(pl.multiple_of(half * (1 - at) + half // count * i, 64), half // count)
        send[...] = whole[rows, :].astype(send.dtype)


def fold_kernel(bit, keep, got, send, kept):
    at = bit(*spot())
    send[...] = (keep[1 - at] + got[1 - at].astype(jnp.float32)).astype(send.dtype)
    kept[...] = keep[at] + got[at].astype(jnp.float32)


def copy_kernel(block, out):
    out[...] = block[...]


def sum_kernel(keep, got, out):
    out[...] = (keep[...] + got[...].astype(jnp.float32)).astype(out.dtype)


def total_kernel(keep, got, more, out):
    out[...] = (keep[...] + got[...].astype(jnp.float32) + more[...]).astype(out.dtype)


def share_kernel(keep, got, side, base):
    q, r, x, c = spot()
    side[...] = (keep[1 - x] + got[1 - x].astype(jnp.float32)).astype(side.dtype)
    base[...] = (keep[x] + got[x].astype(jnp.float32)).astype(base.dtype)


def weight_grad_kernel(
    xs, dkv, dq, mixed, da, sums1, sums2, qv_sums, up_sums, *refs
):
    sends, (keep, packed) = refs[:-2], refs[-2:]
    q, r, x, c = spot()
    width = xs.shape[1]
    own, half = dq.shape
    thin = width // 32
    for_c = 64 * thin
    own_rows = pl.ds(pl.multiple_of(own * (2 * r + c), own), own)
    asked = dot_tn(xs[own_rows, :], dq[...])
    kept = dot_tn(xs[...], dkv[...])
    outer = dot_tn(mixed[...], da[...])
    for cc in range(2):
        for rr in range(2):
            for q1 in range(2):
                for q0 in range(2):
                    at = ((4 * rr + 2 * q0 + 1 * q1) * 8) * thin
                    within = (4 * rr + 2 * q1 + q0) * thin
                    for xx in range(2):
                        rows = slice((16 * xx + 8 * cc) * thin + within, (16 * xx + 8 * cc + 1) * thin + within)
                        for t, piece in enumerate((asked, kept[:, 0:half], kept[:, half:])):
                            to = at + (3 * xx + t) * thin
                            packed[cc, to : to + thin, :] = piece[rows, :]
                    rows = slice(8 * cc * thin + within, (8 * cc + 1) * thin + within)
                    for t in range(2):
                        to = at + (6 + t) * thin
                        packed[cc, to : to + thin, :] = outer[rows, half * t : half * (t + 1)]
    columns = pl.ds(pl.multiple_of(half * x, 128), half)
    for cc in range(2):
        packed[cc, for_c : for_c + 16, :] = jnp.zeros((16, half), jnp.float32)
        packed[cc, for_c : for_c + 2, :] = qv_sums[0:2, :]
        for j in range(4):
            packed[cc, for_c + 2 + j : for_c + 3 + j, :] = up_sums[j, 0:1, :]
        packed[cc, for_c + 6 : for_c + 9, :] = sums1[0:3, columns]
        packed[cc, for_c + 9 : for_c + 12, :] = sums2[0:3, columns]
    first = 0
    for send in sends:
        count = send.shape[0]
        send[...] = packed[1 - c, first : first + count, :].astype(jnp.bfloat16)
        first += count
    keep[...] = packed[c]


def step_kernel(bit, keep, *refs):
    gots, (send, kept, whole) = refs[:-3], refs[-3:]
    at = bit(*spot())
    count = send.shape[0] - 16
    first = 0
    for got in gots:
        rows = slice(first, first + got.shape[0])
        whole[rows, :] = keep[rows, :] + got[...].astype(jnp.float32)
        first += got.shape[0]
    theirs = pl.ds(pl.multiple_of(count * (1 - at), 64), count)
    mine = pl.ds(pl.multiple_of(count * at, 64), count)
    send[0:count, :] = whole[theirs, :].astype(jnp.bfloat16)
    send[count:, :] = whole[2 * count :, :].astype(jnp.bfloat16)
    kept[0:count, :] = whole[mine, :]
    kept[count:, :] = whole[2 * count :, :]


def last_step_kernel(keep, got, side, base, *refs):
    out, b_up, whole = refs[:8], refs[8], refs[9]
    q, r, x, c = spot()
    count = side.shape[0]
    part = out[0].shape[0]
    whole[...] = keep[...] + got[...].astype(jnp.float32)
    theirs = pl.ds(pl.multiple_of(count * (1 - x), 8), count)
    mine = pl.ds(pl.multiple_of(count * x, 8), count)
    side[...] = whole[theirs, :].astype(jnp.bfloat16)
    first = whole.shape[0] - 16
    base[...] = jnp.concatenate([whole[mine, :], whole[2 * count : first, :]]).astype(jnp.bfloat16)
    for i, one in enumerate(out):
        at = first + (i if i < 2 else i + 4)
        line = whole[at : at + 1, :]
        one[...] = jnp.where(c == 0, line[:, :part], line[:, part:]).reshape(part)
    line = jnp.concatenate([whole[pl.ds(first + 2 + 2 * c + i, 1), :] for i in range(2)], axis=1)
    b_up[...] = line.reshape(b_up.shape[0])


def down_out_kernel(near, far, out, mark):
    mark[...] = jnp.zeros_like(mark)
    q, r, x, c = spot()
    count = near.shape[0] // 4
    for d, piece in enumerate((near, far)):
        for k in range(4):
            at = 4 * (r ^ d) + 2 * ((q // 2) ^ (k & 1)) + ((q % 2) ^ (k >> 1))
            rows = pl.ds(pl.multiple_of(count * at, 32), count)
            out[rows, :] = piece[count * k : count * (k + 1), :].astype(jnp.float32)


def up_out_kernel(near, far, out, mark, whole):
    mark[...] = jnp.zeros_like(mark)
    q, r, x, c = spot()
    thin, width = near.shape[0] // 16, near.shape[1]
    for d, piece in enumerate((near, far)):
        whole[...] = piece[...].astype(jnp.float32)
        for k in range(4):
            at = 4 * (r ^ d) + 2 * ((q // 2) ^ (k & 1)) + ((q % 2) ^ (k >> 1))
            rows = pl.ds(pl.multiple_of(thin * at, 8), thin)
            for s in range(4):
                columns = pl.ds(pl.multiple_of(width * (2 * (x ^ (s >> 1)) + (s & 1)), 128), width)
                first = thin * (4 * k + s)
                out[rows, columns] = whole[first : first + thin, :]


def rest_out_kernel(near, far, hidden, total, out_q, out_k, out_v, out_o, out_h, out_t, whole):
    out_h[...] = hidden[...]
    out_t[...] = total[...]
    q, r, x, c = spot()
    half = near.shape[1]
    thin = near.shape[0] // 32
    ours = pl.ds(pl.multiple_of(half * x, 128), half)
    other = pl.ds(pl.multiple_of(half * (1 - x), 128), half)
    for d, piece in enumerate((near, far)):
        whole[...] = piece[...].astype(jnp.float32)
        for k in range(4):
            at = 4 * (r ^ d) + 2 * ((q // 2) ^ (k & 1)) + ((q % 2) ^ (k >> 1))
            rows = pl.ds(pl.multiple_of(thin * at, 8), thin)
            first = 8 * thin * k
            for t, out in enumerate((out_q, out_k, out_v)):
                out[rows, ours] = whole[first + thin * t : first + thin * (t + 1), :]
                out[rows, other] = whole[first + thin * (5 + t) : first + thin * (6 + t), :]
            for t in range(2):
                columns = slice(half * t, half * (t + 1))
                out_o[rows, columns] = whole[first + thin * (3 + t) : first + thin * (4 + t), :]


def kernel_call(body, name, ins, outs, scratch, args, after=(), room=2 << 20, cost=1):
    count = len(args)

    def size(shape, dtype):
        return math.prod(shape) * jnp.dtype(dtype).itemsize

    used = sum(size(m.shape, m.dtype) for m in scratch if m.memory_space == pltpu.VMEM)

    args = [
        pltpu.with_memory_space_constraint(a, pltpu.HBM) if spec is HBM else a
        for a, spec in zip(args, ins)
    ]

    def run(*refs):
        body(*refs[:count], *refs[count + len(after) :])

    return pl.pallas_call(
        run,
        name=name,
        out_shape=[jax.ShapeDtypeStruct(shape, dtype) for shape, dtype, _ in outs],
        in_specs=list(ins) + [ANY] * len(after),
        out_specs=[spec for _, _, spec in outs],
        scratch_shapes=scratch,
        cost_estimate=pl.CostEstimate(flops=cost, bytes_accessed=1, transcendentals=0),
        compiler_params=pltpu.CompilerParams(vmem_limit_bytes=used + room),
    )(*args, *after)


def once(value, *after):
    return pl.pallas_call(
        lambda *refs: None,
        name="once",
        out_shape=jax.ShapeDtypeStruct(value.shape, value.dtype),
        in_specs=[ANY] * (1 + len(after)),
        out_specs=ANY,
        input_output_aliases={0: 0},
        cost_estimate=pl.CostEstimate(flops=1, bytes_accessed=1, transcendentals=0),
        compiler_params=pltpu.CompilerParams(vmem_limit_bytes=1 << 18),
    )(value, *after)


HEAVY = ('attend_back', 'down_sum', 'input_sum', 'project', 'rest_3', 'up_share')


def plane_local(
    tokens, cotangent, seq_ids, w_query, b_query, w_key, w_value, b_value, w_out, b_out,
    attn_gain, attn_shift, w_up, b_up, w_down, b_down, ffn_gain, ffn_shift,
):
    low, exact = jnp.bfloat16, jnp.float32
    rows, width = tokens.shape[1:]
    part = w_query.shape[0]
    half = width // 2
    inner = w_up.shape[1]
    wide = inner // 8
    keys = 8 * rows
    own = 2 * rows
    pairs = half // 128

    latest = []

    def call(body, name, ins, outs, scratch, args, after=(), **more):
        cost = 10**10 if name in HEAVY else 1
        results = kernel_call(
            body, name, ins, outs, scratch, args, tuple(after) + tuple(latest), cost=cost, **more
        )
        latest[:] = results[-1:] if name.endswith("_out") else results[:1]
        return results

    (block,) = call(
        block_kernel, "block", [HBM] * 2, [((rows + 16, width), low, WHOLE)],
        [pltpu.VMEM((1, rows), jnp.int32), pltpu.SemaphoreType.DMA((2,))],
        (tokens[0], seq_ids),
    )
    block = regroup(block)
    theirs, mine = call(
        pack_kernel,
        "pack",
        [HBM] * 12,
        [((3 * part // 2 + 16, half), low, WHOLE), ((3 * part + 16, half), low, WHOLE)],
        [pltpu.VMEM((16, half), exact)]
        + [pltpu.VMEM((part,), low)] * 8
        + [pltpu.VMEM((width,), low), pltpu.SemaphoreType.DMA((15,))],
        (w_query, w_key, w_value, b_query, b_value, b_out, attn_gain, attn_shift, b_down, ffn_gain, ffn_shift, b_up),
    )
    qkv_x = swap_x(theirs)
    qkv_m = swap_c(mine)
    out_m = swap_c(w_out)
    blocks = [once(block, qkv_m, out_m)]
    beside_r = swap_r(blocks[0])
    blocks.append(once(swap_x(blocks[0]), beside_r))
    blocks.append(swap_c(blocks[0]))
    blocks.append(swap_c(blocks[1]))
    blocks.append(beside_r)
    blocks.append(swap_r(blocks[1]))
    qkv_x = (qkv_x, swap_r(qkv_x))
    qkv_mx = [swap_c(piece) for piece in qkv_x]
    up_theirs, up_mine = call(
        cut_kernel, "cut", [HBM], [((part, 4 * wide), low, WHOLE)] * 2, [pltpu.SemaphoreType.DMA((2,))],
        (w_up,), after=(blocks[1],),
    )
    up_x = swap_x(up_theirs)
    up_m = swap_c(up_mine)
    down_m = swap_c(w_down)
    (cot,) = call(
        load_kernel, "cotangent", [HBM], [((rows, width), low, WHOLE)], [pltpu.SemaphoreType.DMA((1,))],
        (cotangent[0],),
    )
    kv_own, q_own, w_all, vecs, up_bias = call(
        project_kernel,
        "project",
        [WHOLE] * 4 + [HBM] * 3 + [WHOLE] * 6,
        [
            ((4 * rows, width), low, WHOLE),
            ((own, half), low, WHOLE),
            ((width, 3 * half), low, WHOLE),
            ((8, width), exact, WHOLE),
            ((4, 8, wide), exact, WHOLE),
        ],
        [pltpu.VMEM((4 * rows, width), low), pltpu.SemaphoreType.DMA((3,))],
        (*blocks[:4], w_query, w_key, w_value, qkv_m, *qkv_x, *qkv_mx, mine),
        room=8 << 20,
    )
    blocks[5] = once(blocks[5], kv_own)
    blocks.append(swap_c(blocks[4]))
    blocks.append(swap_c(blocks[5]))
    a_low, x_all, wo_all, k3, v3, q3, mixed, lse, ids, a_own = call(
        attend_kernel,
        "attend",
        [WHOLE] * 12 + [HBM, WHOLE],
        [
            ((own, width), low, WHOLE),
            ((keys, width), low, WHOLE),
            ((half, width), low, WHOLE),
            ((pairs, keys, 128), low, WHOLE),
            ((pairs, keys, 128), low, WHOLE),
            ((pairs, own, 128), low, WHOLE),
            ((own, half), low, WHOLE),
            ((8, own), exact, WHOLE),
            ((8, rows), exact, WHOLE),
            ((own, width), exact, WHOLE),
        ],
        [
            pltpu.VMEM((2 * pairs, 64, keys), low),
            pltpu.VMEM((2 * pairs, 64, own), exact),
            pltpu.VMEM((keys, own), exact),
            pltpu.SemaphoreType.DMA((1,)),
        ],
        (*blocks, kv_own, q_own, w_all, vecs, w_out, out_m),
        after=(down_m,),
        room=8 << 20,
    )
    a_got = swap_x(a_low)
    (kt,) = call(turn_kernel, "turn", [WHOLE], [((2 * pairs, 64, keys), low, WHOLE)], [], (k3,),
        after=(up_m,))

    up_x = once(up_x, kt)
    up_mx = [swap_c(piece) for piece in (up_x[: part // 2], up_x[part // 2 :])]
    inner_weights = call(
        inner_kernel,
        "inner",
        [HBM] + [WHOLE] * 4 + [HBM, WHOLE],
        [((width, 4 * wide), low, WHOLE), ((4 * wide, width), low, WHOLE)],
        [pltpu.SemaphoreType.DMA((2,))],
        (w_up, up_x, up_m, *up_mx, w_down, down_m),
    )
    cot = once(cot, inner_weights[0])
    cot, cot_x = regroup(cot), regroup_x(cot)
    y_low, y_more, h_low, z, normed1, rstd1, slope, y_own = call(
        forward_kernel,
        "feedforward",
        [WHOLE] * 7,
        [
            ((rows, width), low, WHOLE),
            ((rows, width), low, WHOLE),
            ((own, width), low, WHOLE),
            ((own, 4 * wide), low, WHOLE),
            ((own, width), exact, WHOLE),
            ((own, 128), exact, WHOLE),
            ((own, 4 * wide), exact, WHOLE),
            ((own, width), exact, WHOLE),
        ],
        [],
        (a_own, a_got, x_all, vecs, up_bias, *inner_weights),
        room=8 << 20,
    )
    y_got, y_rest = swap_x(y_low), swap_x(y_more)
    dy_low, hidden, dy, sums2 = call(
        norm_back_kernel,
        "norm_back",
        [WHOLE] * 7,
        [
            ((own, width), low, WHOLE),
            ((rows, width), low, WHOLE),
            ((own, width), exact, WHOLE),
            ((8, width), exact, WHOLE),
        ],
        [
            pltpu.VMEM((own, width), low),
            pltpu.VMEM((own, width), low),
        ],
        (y_own, y_got, y_rest, normed1, cot, cot_x, vecs),
        room=6 << 20,
    )
    eighth = wide // 4
    down_send, down_keep = call(
        down_grad_kernel,
        "down_grad",
        [WHOLE] * 2,
        [((8 * eighth, width), low, WHOLE), ((8 * eighth, width), exact, WHOLE)],
        [],
        (z, dy_low),
        room=8 << 20,
    )
    down_got = swap_c(down_send)
    p_low, s_own, du, up_sums = call(
        backward_kernel,
        "feedforward_back",
        [WHOLE] * 5,
        [
            ((own, width), low, WHOLE),
            ((own, width), exact, WHOLE),
            ((own, 4 * wide), low, WHOLE),
            ((4, 8, wide), exact, WHOLE),
        ],
        [],
        (dy, dy_low, slope, *inner_weights),
        room=8 << 20,
    )
    p_got = swap_x(p_low)
    hidden = regroup(hidden)

    def fold(name, bit, keep, got):
        shape = (keep.shape[0] // 2, keep.shape[1])
        return call(
            lambda *refs: fold_kernel(bit, *refs),
            name,
            [WHOLE] * 2,
            [(shape, low, WHOLE), (shape, exact, WHOLE)],
            [],
            (keep.reshape(2, *shape), got.reshape(2, *shape)),
            room=4 << 20,
        )

    def fold_into(count, name, bit, keep, gots):
        half_rows = keep.shape[0] // 2
        *sends, kept = call(
            lambda *refs: fold_pieces_kernel(bit, count, *refs),
            name,
            [WHOLE] * (1 + len(gots)),
            [((half_rows // count, width), low, WHOLE)] * count + [((half_rows, width), exact, WHOLE)],
            [pltpu.VMEM(keep.shape, exact)],
            (keep, *gots),
            room=4 << 20,
        )
        return sends, kept

    def bit_r(q, r, x, c):
        return r

    def bit_near(q, r, x, c):
        return q % 2

    def bit_far(q, r, x, c):
        return q // 2

    thin = part // 8
    count = 64 * thin

    def step(name, bit, keep, size, *gots):
        return call(
            lambda *refs: step_kernel(bit, *refs),
            name,
            [WHOLE] * (1 + len(gots)),
            [((size + 16, half), low, WHOLE), ((size + 16, half), exact, WHOLE)],
            [pltpu.VMEM((2 * size + 16, half), exact)],
            (keep, *gots),
        )

    def join(name, *pieces):
        shape = (sum(p.shape[0] for p in pieces), pieces[0].shape[1])
        (out,) = call(join_kernel, name, [WHOLE] * len(pieces), [(shape, low, WHOLE)], [], pieces)
        return out

    cuts = (count // 3, count // 3, count - 2 * (count // 3) + 16)
    *up_sends, up_keep = call(
        up_grad_kernel,
        "up_grad",
        [WHOLE] * 2,
        [((2 * eighth, width), low, WHOLE)] * 4 + [((8 * eighth, width), exact, WHOLE)],
        [pltpu.VMEM((width, 4 * wide), exact)],
        (h_low, du),
        room=8 << 20,
    )
    up_gots = [swap_c(send) for send in up_sends]
    down_sends, down_keep = fold_into(2, "down_1", bit_r, down_keep, (down_got,))
    down_gots = [swap_r(send) for send in down_sends]
    (up_send,), up_keep = fold_into(1, "up_1", bit_near, up_keep, up_gots)
    up_got = swap_near(up_send)
    dkv, dq, dr, da, sums1, qv_sums = call(
        attend_back_kernel,
        "attend_back",
        [WHOLE] * 13,
        [
            ((keys, 2 * half), low, WHOLE),
            ((own, half), low, WHOLE),
            ((rows, width), exact, WHOLE),
            ((own, width), low, WHOLE),
            ((8, width), exact, WHOLE),
            ((8, half), exact, WHOLE),
        ],
        [
            pltpu.VMEM((keys, own), exact),
            pltpu.VMEM((pairs, own, 128), low),
            pltpu.VMEM((8, own), exact),
            pltpu.VMEM((pairs, keys, 128), exact),
            pltpu.VMEM((pairs, keys, 128), exact),
            pltpu.VMEM((2 * pairs, 64, own), exact),
            pltpu.VMEM((own, width), exact),
        ],
        (s_own, p_got, normed1, rstd1, vecs, wo_all, mixed, q3, k3, v3, kt, lse, ids),
        room=8 << 20,
    )

    (down_send,), down_keep = fold_into(1, "down_2", bit_near, down_keep, down_gots)
    down_got = swap_near(down_send)
    *rest_sends, rest_keep = call(
        weight_grad_kernel,
        "weight_grad",
        [WHOLE] * 9,
        [((n, half), low, WHOLE) for n in cuts] + [((count + 16, half), exact, WHOLE)],
        [pltpu.VMEM((2, count + 16, half), exact)],
        (x_all, dkv, dq, mixed, da, sums1, sums2, qv_sums, up_sums),
        after=(hidden,),
        room=8 << 20,
    )
    rest_gots = [swap_c(send) for send in rest_sends]
    rest_send, rest_keep = step("rest_1", bit_r, rest_keep, count // 2, *rest_gots)
    rest_got = swap_r(rest_send)
    up_send, up_keep = fold("up_2", bit_far, up_keep, up_got)
    up_got = swap_far(up_send)
    *x_sends, x_keep = call(
        input_grad_kernel,
        "input_grad",
        [WHOLE] * 3,
        [((own, width), low, WHOLE)] * 2 + [((2 * own, width), exact, WHOLE)],
        [pltpu.VMEM((keys, width), exact)],
        (dq, dkv, w_all),
        room=8 << 20,
    )
    x_gots = [swap_c(send) for send in x_sends]
    down_send, down_keep = fold("down_3", bit_far, down_keep, down_got)
    down_got = swap_far(down_send)
    x_send, x_keep = call(
        input_x_kernel,
        "input_x",
        [WHOLE] * 3,
        [((own, width), low, WHOLE), ((own, width), exact, WHOLE)],
        [],
        (x_keep, *x_gots),
        room=4 << 20,
    )
    x_got = swap_x(x_send)
    up_send, up_keep = fold("up_3", bit_r, up_keep, up_got)
    up_got = swap_r(up_send)
    (down_sum,) = call(
        sum_kernel, "down_sum", [WHOLE] * 2, [((eighth, width), low, WHOLE)], [], (down_keep, down_got)
    )
    down_other = swap_far(down_sum)
    x_send, x_keep = fold("input_r", bit_r, x_keep, x_got)
    x_got = swap_r(x_send)
    side, base = call(
        share_kernel,
        "up_share",
        [WHOLE] * 2,
        [((eighth // 2, width), low, WHOLE)] * 2,
        [],
        (up_keep.reshape(2, eighth // 2, width), up_got.reshape(2, eighth // 2, width)),
    )
    side = swap_x(side)
    rest_send, rest_keep = step("rest_2", bit_near, rest_keep, count // 4, rest_got)
    rest_got = swap_near(rest_send)
    down_sum = join("down_join", down_sum, down_other)
    down_other = swap_near(down_sum)
    rest_send, rest_keep = step("rest_3", bit_far, rest_keep, count // 8, rest_got)
    rest_got = swap_far(rest_send)
    up_sum = join("up_join", base, side)
    up_other = swap_far(up_sum)
    down_near = join("down_join_near", down_sum, down_other)
    down_far = swap_r(down_near)
    rest_side, rest_base, *lines, b_up_grad = call(
        last_step_kernel,
        "rest_last",
        [WHOLE] * 2,
        [((3 * thin, half), low, WHOLE), ((5 * thin, half), low, WHOLE)]
        + [((part,), exact, WHOLE)] * 8
        + [((2 * wide,), exact, WHOLE)],
        [pltpu.VMEM((8 * thin + 16, half), exact)],
        (rest_keep, rest_got),
    )
    rest_side = swap_x(rest_side)
    up_sum = join("up_join_far", up_sum, up_other)
    up_other = swap_near(up_sum)
    (total,) = call(
        total_kernel, "input_sum", [WHOLE] * 3, [((rows, width), low, WHOLE)], [], (x_keep, x_got, dr)
    )
    total = regroup(total)
    rest_sum = join("rest_join", rest_base, rest_side)
    rest_other = swap_far(rest_sum)
    rest_sum = join("rest_join_far", rest_sum, rest_other)
    rest_other = swap_near(rest_sum)
    w_down_grad, _ = call(
        down_out_kernel, "down_out", [WHOLE] * 2,
        [((2 * wide, width), exact, WHOLE), ((8, 128), exact, WHOLE)], [], (down_near, down_far),
        room=6 << 20,
    )
    up_near = join("up_join_near", up_sum, up_other)
    up_far = swap_r(up_near)
    rest_near = join("rest_join_near", rest_sum, rest_other)
    rest_far = swap_r(rest_near)
    w_up_grad, _ = call(
        up_out_kernel, "up_out", [WHOLE] * 2, [((part, inner), exact, WHOLE), ((8, 128), exact, WHOLE)],
        [pltpu.VMEM((4 * eighth, width), exact)], (up_near, up_far),
        room=6 << 20,
    )


    w_query_grad, w_key_grad, w_value_grad, w_out_grad, hidden_out, tokens_grad = call(
        rest_out_kernel,
        "rest_out",
        [WHOLE] * 4,
        [((part, width), exact, WHOLE)] * 4 + [((rows, width), low, WHOLE)] * 2,
        [pltpu.VMEM((32 * thin, half), exact)],
        (rest_near, rest_far, hidden, total),
        room=6 << 20,
    )

    return (
        hidden_out[None],
        tokens_grad[None],
        w_query_grad,
        lines[0],
        w_key_grad,
        w_value_grad,
        lines[1],
        w_out_grad,
        lines[2],
        lines[3],
        lines[4],
        w_up_grad,
        b_up_grad,
        w_down_grad,
        lines[5],
        lines[6],
        lines[7],
    )


def plane_solution(mesh):
    planes, cycle = mesh.shape["shard"], mesh.shape["ctx"]
    grid = Mesh(mesh.devices.reshape(planes, cycle // planes, 2, 2), AXES)
    shard, ctx = ("x", "c"), ("q", "r")
    tokens, matrix, vector = P(shard, ctx, None), P(shard, None), P(shard)
    return jax.shard_map(
        plane_local,
        mesh=grid,
        in_specs=(
            tokens, tokens, P(shard, ctx), matrix, vector, matrix, matrix, vector, matrix, vector,
            vector, vector, matrix, vector, matrix, vector, vector, vector,
        ),
        out_specs=(
            tokens, tokens, matrix, vector, matrix, matrix, vector, matrix, vector,
            vector, vector, matrix, vector, matrix, vector, vector, vector,
        ),
        check_vma=False,
    )


def solution(mesh):
    if mesh.shape["shard"] == 4 and mesh.shape["ctx"] == 8:
        return plane_solution(mesh)
    return ring_solution(mesh)
```

```python
import math

import jax
import jax.numpy as jnp
from jax import lax
from jax.experimental import pallas as pl
from jax.experimental.pallas import tpu as pltpu
from jax.sharding import Mesh
from jax.sharding import PartitionSpec as P

HEAD_DIM = 64


ln_eps = 1e-12
masked_fill = -1e30


def from_behind(block, axis, distance):
    devices = range(lax.axis_size(axis))
    route = [((i - distance) % len(devices), i) for i in devices]
    return lax.ppermute(block, axis, route)


def matmul(left, right):
    return jnp.dot(left, right, preferred_element_type=jnp.float32)


def matmul_tn(left, right):
    return lax.dot_general(
        left, right, (((0,), (0,)), ((), ())), preferred_element_type=jnp.float32
    )


def matmul_nt(left, right):
    return lax.dot_general(
        left, right, (((1,), (1,)), ((), ())), preferred_element_type=jnp.float32
    )


def apply_layer_norm(value, gain, shift):
    mean = jnp.mean(value, axis=-1, keepdims=True)
    centered = value - mean
    rstd = lax.rsqrt(jnp.mean(centered * centered, axis=-1, keepdims=True) + ln_eps)
    normed = centered * rstd
    return (normed * gain + shift, normed, rstd)


def norm_back(grad, normed, rstd, gain):
    d_gain = jnp.sum(grad * normed, axis=0)
    d_shift = jnp.sum(grad, axis=0)
    scaled = grad * gain
    d_value = rstd * (
        scaled
        - jnp.mean(scaled, axis=-1, keepdims=True)
        - normed * jnp.mean(scaled * normed, axis=-1, keepdims=True)
    )
    return (d_value, d_gain, d_shift)


def gelu_slope(value):
    normal_cdf = 0.5 * (1.0 + lax.erf(value * (1.0 / math.sqrt(2.0))))
    density = jnp.exp(-0.5 * value * value) * (1.0 / math.sqrt(2.0 * math.pi))
    return normal_cdf + value * density


def scores_of(query, keys, q_ids, k_ids, scale):
    raw = jnp.einsum("qhd,khd->hqk", query, keys, preferred_element_type=jnp.float32) * scale
    match = (q_ids[:, None] == k_ids[None, :])[None, :, :]
    return (raw, match)


def attend(query, q_ids, keys, values, k_ids, stats, scale):
    top, total, accum = stats
    raw, match = scores_of(query, keys, q_ids, k_ids, scale)
    masked = jnp.where(match, raw, masked_fill)
    new_top = jnp.maximum(top, jnp.max(masked, axis=-1))
    weights = jnp.where(match, jnp.exp(masked - new_top[:, :, None]), 0.0)
    factor = jnp.exp(top - new_top)
    total = total * factor + jnp.sum(weights, axis=-1)
    accum = accum * factor[:, :, None] + jnp.einsum(
        "hqk,khd->hqd", weights.astype(jnp.bfloat16), values, preferred_element_type=jnp.float32
    )
    return (new_top, total, accum)


def block_grads(query, q_ids, d_out, log_total, delta, keys, values, k_ids, scale):
    raw, match = scores_of(query, keys, q_ids, k_ids, scale)
    probs = jnp.exp(jnp.where(match, raw - log_total[:, :, None], masked_fill))
    d_values = jnp.einsum(
        "hqk,qhd->khd", probs.astype(jnp.bfloat16), d_out, preferred_element_type=jnp.float32
    )
    d_probs = jnp.einsum("qhd,khd->hqk", d_out, values, preferred_element_type=jnp.float32)
    d_scores = (probs * (d_probs - delta[:, :, None])).astype(jnp.bfloat16)
    d_query = jnp.einsum("hqk,khd->qhd", d_scores, keys, preferred_element_type=jnp.float32) * scale
    d_keys = jnp.einsum("hqk,qhd->khd", d_scores, query, preferred_element_type=jnp.float32) * scale
    return (d_query, d_keys, d_values)


def ring_local(
    tokens,
    cotangent,
    seq_ids,
    w_query,
    b_query,
    w_key,
    w_value,
    b_value,
    w_out,
    b_out,
    attn_gain,
    attn_shift,
    w_up,
    b_up,
    w_down,
    b_down,
    ffn_gain,
    ffn_shift,
):
    cycle = lax.axis_size("ctx")
    tok_rows = tokens.shape[1]
    width = tokens.shape[2]
    heads = width // HEAD_DIM
    scale = 1.0 / math.sqrt(HEAD_DIM)
    share = tok_rows // cycle
    got_tokens, got_grads, got_ids = (
        lax.all_to_all(
            tokens[0].reshape(share, cycle, width), "ctx", split_axis=1, concat_axis=1, tiled=True
        ),
        lax.all_to_all(
            cotangent[0].reshape(share, cycle, width),
            "ctx",
            split_axis=1,
            concat_axis=1,
            tiled=True,
        ),
        lax.all_to_all(
            seq_ids[0].reshape(share, cycle), "ctx", split_axis=1, concat_axis=1, tiled=True
        ),
    )
    x_local = got_tokens.reshape(tok_rows, width)
    local_gradient = got_grads.reshape(tok_rows, width).astype(jnp.float32)
    local_ids = got_ids.reshape(tok_rows)
    (
        query_mat,
        query_bias,
        key_mat,
        value_mat,
        value_bias,
        out_mat,
        out_bias,
        attention_norm_gain,
        first_shift,
        up_mat,
        up_bias,
        down_mat,
        down_bias,
        feedforward_norm_gain,
        second_shift,
    ) = (
        lax.all_gather(w_query, "shard", axis=0, tiled=True),
        lax.all_gather(b_query, "shard", axis=0, tiled=True),
        lax.all_gather(w_key, "shard", axis=0, tiled=True),
        lax.all_gather(w_value, "shard", axis=0, tiled=True),
        lax.all_gather(b_value, "shard", axis=0, tiled=True),
        lax.all_gather(w_out, "shard", axis=0, tiled=True),
        lax.all_gather(b_out, "shard", axis=0, tiled=True),
        lax.all_gather(attn_gain, "shard", axis=0, tiled=True),
        lax.all_gather(attn_shift, "shard", axis=0, tiled=True),
        lax.all_gather(w_up, "shard", axis=0, tiled=True),
        lax.all_gather(b_up, "shard", axis=0, tiled=True),
        lax.all_gather(w_down, "shard", axis=0, tiled=True),
        lax.all_gather(b_down, "shard", axis=0, tiled=True),
        lax.all_gather(ffn_gain, "shard", axis=0, tiled=True),
        lax.all_gather(ffn_shift, "shard", axis=0, tiled=True),
    )
    query = (matmul(x_local, query_mat) + query_bias.astype(jnp.float32)).astype(jnp.bfloat16)
    keys = matmul(x_local, key_mat).astype(jnp.bfloat16)
    values = (matmul(x_local, value_mat) + value_bias.astype(jnp.float32)).astype(jnp.bfloat16)
    q_heads = query.reshape(tok_rows, heads, HEAD_DIM)
    start_stats = (
        jnp.full((heads, tok_rows), masked_fill, jnp.float32),
        jnp.zeros((heads, tok_rows), jnp.float32),
        jnp.zeros((heads, tok_rows, HEAD_DIM), jnp.float32),
    )

    def forward_step(step, carry):
        block, stats = carry
        stats = attend(
            q_heads,
            local_ids,
            block[0].reshape(tok_rows, heads, HEAD_DIM),
            block[1].reshape(tok_rows, heads, HEAD_DIM),
            block[2],
            stats,
            scale,
        )
        block = from_behind((block[0], block[1], block[2]), "ctx", 1)
        return (block, stats)

    block, stats = lax.fori_loop(
        0, cycle - 1, forward_step, ((keys, values, local_ids), start_stats)
    )
    top, total, accum = attend(
        q_heads,
        local_ids,
        block[0].reshape(tok_rows, heads, HEAD_DIM),
        block[1].reshape(tok_rows, heads, HEAD_DIM),
        block[2],
        stats,
        scale,
    )
    attn_out = (
        (accum / total[:, :, None]).transpose(1, 0, 2).reshape(tok_rows, width).astype(jnp.bfloat16)
    )
    log_total = top + jnp.log(total)
    attn_proj = matmul(attn_out, out_mat) + out_bias.astype(jnp.float32)
    first_sum = x_local.astype(jnp.float32) + attn_proj
    first_normalized_rows, first_centered_scaled, first_inverse_deviation = apply_layer_norm(
        first_sum, attention_norm_gain.astype(jnp.float32), first_shift.astype(jnp.float32)
    )
    normed_low = first_normalized_rows.astype(jnp.bfloat16)
    up_pre = matmul(normed_low, up_mat) + up_bias.astype(jnp.float32)
    up_act = jax.nn.gelu(up_pre, approximate=False).astype(jnp.bfloat16)
    down_pre = matmul(up_act, down_mat) + down_bias.astype(jnp.float32)
    layer_output, second_centered_scaled, second_inverse_deviation = apply_layer_norm(
        first_normalized_rows + down_pre,
        feedforward_norm_gain.astype(jnp.float32),
        second_shift.astype(jnp.float32),
    )
    (
        query_mat,
        key_mat,
        value_mat,
        out_mat,
        attention_norm_gain,
        up_mat,
        down_mat,
        feedforward_norm_gain,
    ) = (
        lax.all_gather(w_query, "shard", axis=0, tiled=True),
        lax.all_gather(w_key, "shard", axis=0, tiled=True),
        lax.all_gather(w_value, "shard", axis=0, tiled=True),
        lax.all_gather(w_out, "shard", axis=0, tiled=True),
        lax.all_gather(attn_gain, "shard", axis=0, tiled=True),
        lax.all_gather(w_up, "shard", axis=0, tiled=True),
        lax.all_gather(w_down, "shard", axis=0, tiled=True),
        lax.all_gather(ffn_gain, "shard", axis=0, tiled=True),
    )
    grad_two, d_second_gain, d_second_shift = norm_back(
        local_gradient,
        second_centered_scaled,
        second_inverse_deviation,
        feedforward_norm_gain.astype(jnp.float32),
    )
    grad_down = grad_two.astype(jnp.bfloat16)
    d_down_bias = jnp.sum(grad_down, axis=0, dtype=jnp.float32)
    d_down_mat = matmul_tn(up_act, grad_down)
    grad_up = (matmul_nt(grad_down, down_mat) * gelu_slope(up_pre)).astype(jnp.bfloat16)
    d_up_bias = jnp.sum(grad_up, axis=0, dtype=jnp.float32)
    d_up_mat = matmul_tn(normed_low, grad_up)
    first_norm_gradient = grad_two + matmul_nt(grad_up, up_mat)
    grad_first, d_first_gain, d_first_shift = norm_back(
        first_norm_gradient,
        first_centered_scaled,
        first_inverse_deviation,
        attention_norm_gain.astype(jnp.float32),
    )
    grad_proj = grad_first.astype(jnp.bfloat16)
    d_out_bias = jnp.sum(grad_proj, axis=0, dtype=jnp.float32)
    d_out_mat = matmul_tn(attn_out, grad_proj)
    grad_attn = matmul_nt(grad_proj, out_mat).astype(jnp.bfloat16)
    grad_heads = grad_attn.reshape(tok_rows, heads, HEAD_DIM)
    delta = jnp.einsum(
        "qhd,qhd->hq",
        grad_heads,
        attn_out.reshape(tok_rows, heads, HEAD_DIM),
        preferred_element_type=jnp.float32,
    )
    zero_rows = jnp.zeros((tok_rows, width), jnp.float32)

    def key_step(step, carry):
        block, sums, acc_query = carry
        d_query, d_keys, d_values = block_grads(
            q_heads,
            local_ids,
            grad_heads,
            log_total,
            delta,
            block[0].reshape(tok_rows, heads, HEAD_DIM),
            block[1].reshape(tok_rows, heads, HEAD_DIM),
            block[2],
            scale,
        )
        sums = (
            sums[0] + d_keys.reshape(tok_rows, width),
            sums[1] + d_values.reshape(tok_rows, width),
        )
        block = from_behind((block[0], block[1], block[2]), "ctx", 1)
        sums = (
            from_behind(sums[0].astype(jnp.bfloat16), "ctx", 1).astype(jnp.float32),
            from_behind(sums[1].astype(jnp.bfloat16), "ctx", 1).astype(jnp.float32),
        )
        return (block, sums, acc_query + d_query.reshape(tok_rows, width))

    block, sums, d_query_sum = lax.fori_loop(
        0, cycle, key_step, ((keys, values, local_ids), (zero_rows, zero_rows), zero_rows)
    )
    d_keys_sum, d_values_sum = sums
    grad_query = d_query_sum.astype(jnp.bfloat16)
    grad_keys = d_keys_sum.astype(jnp.bfloat16)
    grad_values = d_values_sum.astype(jnp.bfloat16)
    d_query_bias = jnp.sum(grad_query, axis=0, dtype=jnp.float32)
    d_value_bias = jnp.sum(grad_values, axis=0, dtype=jnp.float32)
    d_query_mat = matmul_tn(x_local, grad_query)
    d_key_mat = matmul_tn(x_local, grad_keys)
    d_value_mat = matmul_tn(x_local, grad_values)
    grad_input = (
        grad_first
        + matmul_nt(grad_query, query_mat)
        + matmul_nt(grad_keys, key_mat)
        + matmul_nt(grad_values, value_mat)
    )
    home_hidden, home_grad = (
        lax.all_to_all(
            layer_output.astype(jnp.bfloat16).reshape(share, cycle, width),
            "ctx",
            split_axis=1,
            concat_axis=1,
            tiled=True,
        ),
        lax.all_to_all(
            grad_input.astype(jnp.bfloat16).reshape(share, cycle, width),
            "ctx",
            split_axis=1,
            concat_axis=1,
            tiled=True,
        ),
    )
    hidden_out = home_hidden.reshape(tok_rows, width)[None]
    tokens_grad = home_grad.reshape(tok_rows, width)[None]
    shares = (
        lax.psum_scatter(
            d_query_mat.astype(jnp.bfloat16), "shard", scatter_dimension=0, tiled=True
        ).astype(jnp.float32),
        lax.psum_scatter(
            d_query_bias.astype(jnp.bfloat16), "shard", scatter_dimension=0, tiled=True
        ).astype(jnp.float32),
        lax.psum_scatter(
            d_key_mat.astype(jnp.bfloat16), "shard", scatter_dimension=0, tiled=True
        ).astype(jnp.float32),
        lax.psum_scatter(
            d_value_mat.astype(jnp.bfloat16), "shard", scatter_dimension=0, tiled=True
        ).astype(jnp.float32),
        lax.psum_scatter(
            d_value_bias.astype(jnp.bfloat16), "shard", scatter_dimension=0, tiled=True
        ).astype(jnp.float32),
        lax.psum_scatter(
            d_out_mat.astype(jnp.bfloat16), "shard", scatter_dimension=0, tiled=True
        ).astype(jnp.float32),
        lax.psum_scatter(
            d_out_bias.astype(jnp.bfloat16), "shard", scatter_dimension=0, tiled=True
        ).astype(jnp.float32),
        lax.psum_scatter(
            d_first_gain.astype(jnp.bfloat16), "shard", scatter_dimension=0, tiled=True
        ).astype(jnp.float32),
        lax.psum_scatter(
            d_first_shift.astype(jnp.bfloat16), "shard", scatter_dimension=0, tiled=True
        ).astype(jnp.float32),
        lax.psum_scatter(
            d_up_mat.astype(jnp.bfloat16), "shard", scatter_dimension=0, tiled=True
        ).astype(jnp.float32),
        lax.psum_scatter(
            d_up_bias.astype(jnp.bfloat16), "shard", scatter_dimension=0, tiled=True
        ).astype(jnp.float32),
        lax.psum_scatter(
            d_down_mat.astype(jnp.bfloat16), "shard", scatter_dimension=0, tiled=True
        ).astype(jnp.float32),
        lax.psum_scatter(
            d_down_bias.astype(jnp.bfloat16), "shard", scatter_dimension=0, tiled=True
        ).astype(jnp.float32),
        lax.psum_scatter(
            d_second_gain.astype(jnp.bfloat16), "shard", scatter_dimension=0, tiled=True
        ).astype(jnp.float32),
        lax.psum_scatter(
            d_second_shift.astype(jnp.bfloat16), "shard", scatter_dimension=0, tiled=True
        ).astype(jnp.float32),
    )
    totals = lax.psum(
        (
            shares[0],
            shares[1],
            shares[2],
            shares[3],
            shares[4],
            shares[5],
            shares[6],
            shares[7],
            shares[8],
            shares[9],
            shares[10],
            shares[11],
            shares[12],
            shares[13],
            shares[14],
        ),
        "ctx",
    )
    return (hidden_out, tokens_grad) + tuple(totals)


def ring_solution(mesh):
    return jax.shard_map(
        ring_local,
        mesh=mesh,
        in_specs=(
            P("shard", "ctx", None),
            P("shard", "ctx", None),
            P("shard", "ctx"),
            P("shard", None),
            P("shard"),
            P("shard", None),
            P("shard", None),
            P("shard"),
            P("shard", None),
            P("shard"),
            P("shard"),
            P("shard"),
            P("shard", None),
            P("shard"),
            P("shard", None),
            P("shard"),
            P("shard"),
            P("shard"),
        ),
        out_specs=(
            P("shard", "ctx", None),
            P("shard", "ctx", None),
            P("shard", None),
            P("shard"),
            P("shard", None),
            P("shard", None),
            P("shard"),
            P("shard", None),
            P("shard"),
            P("shard"),
            P("shard"),
            P("shard", None),
            P("shard"),
            P("shard", None),
            P("shard"),
            P("shard"),
            P("shard"),
        ),
        check_vma=False,
    )


AXES = ("q", "r", "x", "c")
ANY = pl.BlockSpec(memory_space=pl.ANY)
WHOLE = pl.BlockSpec(memory_space=pltpu.VMEM)
HBM = pl.BlockSpec(memory_space=pltpu.HBM)


def moved(block, move):
    sizes = [lax.axis_size(a) for a in AXES]

    def number(spot):
        place = 0
        for size, at in zip(sizes, spot):
            place = place * size + at
        return place

    spots = [
        (q, r, x, c)
        for q in range(sizes[0])
        for r in range(sizes[1])
        for x in range(sizes[2])
        for c in range(sizes[3])
    ]
    return lax.ppermute(block, AXES, [(number(s), number(move(*s))) for s in spots])


def swap_x(block):
    return moved(block, lambda q, r, x, c: (q, r, 1 - x, c))


def swap_c(block):
    return moved(block, lambda q, r, x, c: (q, r, x, 1 - c))


def swap_r(block):
    return moved(block, lambda q, r, x, c: (q, r ^ 1, x, c))


def swap_rc(block):
    return moved(block, lambda q, r, x, c: (q, r ^ 1, x, 1 - c))


def swap_near(block):
    return moved(block, lambda q, r, x, c: (q ^ 1, r, x, c))


def swap_far(block):
    return moved(block, lambda q, r, x, c: (q ^ 2, r, x, c))


def regroup(block):
    return moved(block, lambda q, r, x, c: (2 * c + x, r, q & 1, q >> 1))


def regroup_x(block):
    return moved(block, lambda q, r, x, c: (2 * c + x, r, 1 - (q & 1), q >> 1))


def swap_xc(block):
    return moved(block, lambda q, r, x, c: (q, r, 1 - x, 1 - c))


def beside(mine, got):
    return jnp.concatenate([mine, got])


def dot(left, right):
    return jnp.dot(left, right, preferred_element_type=jnp.float32)


def dot_nt(left, right):
    return lax.dot_general(
        left, right, (((1,), (1,)), ((), ())), preferred_element_type=jnp.float32
    )


def dot_tn(left, right):
    return lax.dot_general(
        left, right, (((0,), (0,)), ((), ())), preferred_element_type=jnp.float32
    )


class Copies:
    def __init__(self, sems):
        self.sems = sems
        self.count = 0
        self.held = []

    def start(self, source, target):
        copy = pltpu.make_async_copy(source, target, self.sems.at[self.count])
        copy.start()
        self.count += 1
        self.held.append(copy)

    def wait(self):
        for copy in self.held:
            copy.wait()
        self.held = []


def spot():
    return tuple(lax.axis_index(a) for a in AXES)


def fill_mask(ids, mask, own):
    blocks, rows = ids.shape
    mine = jnp.concatenate([ids[pl.ds(own, 1), :], ids[pl.ds(own + 1, 1), :]], axis=1)
    across = jnp.transpose(ids[...])
    for b in range(blocks):
        mask[rows * b : rows * (b + 1), :] = jnp.where(across[:, b : b + 1] == mine, 0.0, masked_fill)


def block_kernel(tokens, ids, block, line, sems):
    rows = tokens.shape[0]
    copies = Copies(sems)
    copies.start(tokens, block.at[pl.ds(0, rows)])
    copies.start(ids, line)
    block[rows:, :] = jnp.zeros((16, block.shape[1]), block.dtype)
    copies.wait()
    block[rows:, 0:rows] = jnp.broadcast_to(line[...].astype(jnp.float32), (16, rows)).astype(block.dtype)


def pack_kernel(w_q, w_k, w_v, *refs):
    vectors, b_up, theirs, mine = refs[:8], refs[8], refs[9], refs[10]
    lines, thin, thick, sems = refs[11], refs[12:20], refs[20], refs[21]
    q, r, x, c = spot()
    part, width = w_q.shape
    half = width // 2
    copies = Copies(sems)
    few = part // 2
    for t, w in enumerate((w_q, w_k, w_v)):
        copies.start(w.at[:, pl.ds(pl.multiple_of(half * x, 128), half)], mine.at[pl.ds(part * t, part)])
        copies.start(
            w.at[pl.ds(pl.multiple_of(few * r, 32), few), pl.ds(pl.multiple_of(half * (1 - x), 128), half)],
            theirs.at[pl.ds(few * t, few)],
        )
    for vector, held in zip(vectors, thin):
        copies.start(vector, held)
    copies.start(b_up, thick)
    lines[...] = jnp.zeros_like(lines)
    copies.wait()
    for i, vector in enumerate(thin):
        line = vector[...].astype(jnp.float32).reshape(1, part)
        none = jnp.zeros_like(line)
        first = jnp.concatenate([line, none], axis=1)
        second = jnp.concatenate([none, line], axis=1)
        lines[i : i + 1, :] = jnp.where(c == 0, first, second)
    wide = thick[...].astype(jnp.float32).reshape(1, width)
    lines[pl.ds(8 + 2 * c, 1), :] = wide[:, 0:half]
    lines[pl.ds(9 + 2 * c, 1), :] = wide[:, half:]
    low = lines[...].astype(jnp.bfloat16)
    mine[3 * part :, :] = low
    theirs[3 * few :, :] = low


def cut_kernel(w, theirs, mine, sems):
    q, r, x, c = spot()
    count = theirs.shape[1]
    copies = Copies(sems)
    copies.start(w.at[:, pl.ds(pl.multiple_of(count * (1 - x), 128), count)], theirs)
    copies.start(w.at[:, pl.ds(pl.multiple_of(count * x, 128), count)], mine)
    copies.wait()


def load_kernel(block, out, sems):
    copies = Copies(sems)
    copies.start(block, out)
    copies.wait()


def turn_kernel(keys, out):
    for p in range(keys.shape[0]):
        out[2 * p : 2 * p + 2] = jnp.transpose(keys[p]).reshape(2, 64, keys.shape[1])


def project_kernel(
    b0, b1, b2, b3, w_q, w_k, w_v, w_m, xa, xb, ma, mb, own_lines,
    kv_out, q_out, w, vecs, up_bias, xs, sems,
):
    q, r, x, c = spot()
    rows = xs.shape[0] // 4
    part = w.shape[0] // 4
    half = w.shape[1] // 3
    me, shard = 2 * c + x, 2 * x + c
    columns = pl.ds(pl.multiple_of(half * x, 128), half)
    ins = Copies(sems)
    for t, own in enumerate((w_q, w_k, w_v)):
        at = pl.ds(pl.multiple_of(part * shard, 64), part)
        ins.start(own.at[:, columns], w.at[at, pl.ds(half * t, half)])
    for j, block in enumerate((b0, b1, b2, b3)):
        xs[pl.ds(pl.multiple_of(rows * (me ^ j), rows), rows), :] = block[0:rows, :]
    few = part // 2
    for t in range(3):
        place = slice(half * t, half * (t + 1))
        at = pl.ds(pl.multiple_of(part * (shard ^ 1), 64), part)
        w[at, place] = w_m[part * t : part * (t + 1), :]
        for flip, side, piece in ((2, r, xa), (2, 1 - r, xb), (3, r, ma), (3, 1 - r, mb)):
            at = pl.ds(pl.multiple_of(part * (shard ^ flip) + few * side, 32), few)
            w[at, place] = piece[few * t : few * (t + 1), :]
    mine, other = (
        a[at:, :].astype(jnp.float32) + b[at:, :].astype(jnp.float32)
        for a, b, at in ((own_lines, w_m, 3 * part), (xa, ma, 3 * few))
    )
    vecs[:, columns] = mine[0:8, :]
    vecs[:, pl.ds(pl.multiple_of(half * (1 - x), 128), half)] = other[0:8, :]
    for i in range(4):
        up_bias[i] = jnp.broadcast_to(mine[8 + i : 9 + i, :], (8, half))
    ins.wait()
    kv_out[:, 0:half] = dot(xs[...], w[:, half : 2 * half]).astype(jnp.bfloat16)
    kv_out[:, half:] = (dot(xs[...], w[:, 2 * half :]) + mine[1:2, :]).astype(jnp.bfloat16)
    own = pl.ds(pl.multiple_of(2 * rows * c, rows), 2 * rows)
    q_out[...] = (dot(xs[own, :], w[:, 0:half]) + mine[0:1, :]).astype(jnp.bfloat16)


def attend_kernel(
    b0, b1, b2, b3, b4, b5, b6, b7, kv_own, q_own, w, vecs, w_o, w_om,
    a_low, xs, wo, k3, v3, q3, o_out, lse_out, ids_out, a_out,
    vt, ot, mask, sems,
):
    q, r, x, c = spot()
    rows = xs.shape[0] // 8
    half = wo.shape[0]
    part = half // 2
    me = 4 * r + 2 * c + x
    ins = Copies(sems)
    ins.start(w_o, wo.at[pl.ds(pl.multiple_of(part * c, 64), part)])
    wo[pl.ds(pl.multiple_of(part * (1 - c), 64), part), :] = w_om[...]
    for j, block in enumerate((b0, b1, b2, b3, b4, b5, b6, b7)):
        at = me ^ j
        xs[pl.ds(pl.multiple_of(rows * at, rows), rows), :] = block[0:rows, :]
        ids_out[pl.ds(at, 1), :] = block[rows : rows + 16, 0:rows].astype(jnp.float32)[0:1, :]
    fill_mask(ids_out, mask, 4 * r + 2 * c)
    rest = pl.ds(pl.multiple_of(4 * rows * (1 - r), rows), 4 * rows)
    here = pl.ds(pl.multiple_of(4 * rows * r, rows), 4 * rows)
    bias = vecs[1:2, pl.ds(pl.multiple_of(half * x, 128), half)]
    keyed = dot(xs[rest, :], w[:, half : 2 * half]).astype(jnp.bfloat16)
    valued = (dot(xs[rest, :], w[:, 2 * half :]) + bias).astype(jnp.bfloat16)
    pairs = half // 128
    for p in range(pairs):
        at = slice(128 * p, 128 * (p + 1))
        k3[p, here, :] = kv_own[:, at]
        k3[p, rest, :] = keyed[:, at]
        v3[p, here, :] = kv_own[:, half + 128 * p : half + 128 * (p + 1)]
        v3[p, rest, :] = valued[:, at]
        q3[p] = q_own[:, at]
        vt[2 * p : 2 * p + 2] = jnp.transpose(v3[p]).reshape(2, 64, 8 * rows)
    lane = lax.broadcasted_iota(jnp.int32, (2 * rows, 128), 1) // 64

    def head(h, carry):
        query = jnp.where(lane == h % 2, q3[h // 2], 0) * 0.125
        scores = dot_nt(k3[h // 2], query.astype(jnp.bfloat16)) + mask[...]
        top = jnp.max(scores, axis=0, keepdims=True)
        weights = jnp.exp(scores - top)
        total = jnp.sum(weights, axis=0, keepdims=True)
        ot[h] = dot(vt[h], weights.astype(jnp.bfloat16)) / total
        lse_out[pl.ds(h, 1), :] = top + jnp.log(total)
        return carry

    lax.fori_loop(0, 2 * pairs, head, 0, unroll=6)
    mixed = jnp.transpose(ot[...].reshape(half, 2 * rows)).astype(jnp.bfloat16)
    o_out[...] = mixed
    ins.wait()
    partial = dot(mixed, wo[...])
    a_out[...] = partial
    a_low[...] = partial.astype(jnp.bfloat16)


def inner_kernel(u_own, u_x, u_m, u_mx0, u_mx1, d_own, d_m, up, down, sems):
    q, r, x, c = spot()
    part = up.shape[0] // 4
    count = up.shape[1]
    shard = 2 * x + c
    ins = Copies(sems)
    own = u_own.at[:, pl.ds(pl.multiple_of(count * x, 128), count)]
    ins.start(own, up.at[pl.ds(pl.multiple_of(part * shard, 64), part)])
    ins.start(d_own, down.at[pl.ds(pl.multiple_of(count // 2 * c, 128), count // 2)])
    for flip, piece in ((2, u_x), (1, u_m)):
        up[pl.ds(pl.multiple_of(part * (shard ^ flip), 64), part), :] = piece[...]
    for i, piece in enumerate((u_mx0, u_mx1)):
        at = pl.multiple_of(part * (shard ^ 3) + part // 2 * i, 32)
        up[pl.ds(at, part // 2), :] = piece[...]
    down[pl.ds(pl.multiple_of(count // 2 * (1 - c), 128), count // 2), :] = d_m[...]
    ins.wait()


def norm_of(value):
    mean = jnp.mean(value, axis=-1, keepdims=True)
    centered = value - mean
    rstd = lax.rsqrt(jnp.mean(centered * centered, axis=-1, keepdims=True) + ln_eps)
    return centered * rstd, rstd


def norm_pull(scaled, normed, rstd):
    return rstd * (
        scaled
        - jnp.mean(scaled, axis=-1, keepdims=True)
        - normed * jnp.mean(scaled * normed, axis=-1, keepdims=True)
    )


def forward_kernel(
    a_own, a_got, xs, vecs, b_up, up, down,
    y_low, y_more, h_out, z, n_out, r_out, slope, y_out,
):
    q, r, x, c = spot()
    rows = a_own.shape[0]
    x_own = xs[pl.ds(pl.multiple_of(rows * (2 * r + c), rows), rows), :]
    total = x_own.astype(jnp.float32) + (a_own[...] + a_got[...].astype(jnp.float32) + vecs[2:3, :])
    normed, rstd = norm_of(total)
    n_out[...] = normed
    r_out[...] = jnp.broadcast_to(rstd, r_out.shape)
    low = (normed * vecs[3:4, :] + vecs[4:5, :]).astype(jnp.bfloat16)
    h_out[...] = low
    wide = up.shape[1] // 4
    for j in range(4):
        at = slice(wide * j, wide * (j + 1))
        pre = dot(low, up[:, at]) + b_up[j, 0:1, :]
        cdf = 0.5 * (1.0 + lax.erf(pre * (1.0 / math.sqrt(2.0))))
        density = jnp.exp(-0.5 * pre * pre) * (1.0 / math.sqrt(2.0 * math.pi))
        z[:, at] = (pre * cdf).astype(jnp.bfloat16)
        slope[:, at] = cdf + pre * density
    result = dot(z[...], down[...])
    y_out[...] = result
    rows = y_low.shape[0]
    y_low[...] = result[0:rows, :].astype(jnp.bfloat16)
    y_more[...] = result[rows:, :].astype(jnp.bfloat16)


def norm_back_kernel(
    y_own, y_got, y_rest, normed1, g_own, g_x, vecs, low_out, hid_out, dy_out, sums, grad, hid,
):
    q, r, x, c = spot()
    rows = grad.shape[0] // 2
    grad[pl.ds(pl.multiple_of(rows * x, rows), rows), :] = g_own[...]
    grad[pl.ds(pl.multiple_of(rows * (1 - x), rows), rows), :] = g_x[...]
    got = jnp.concatenate([y_got[...], y_rest[...]]).astype(jnp.float32)
    h1 = normed1[...] * vecs[3:4, :] + vecs[4:5, :]
    normed, rstd = norm_of(h1 + (y_own[...] + got + vecs[5:6, :]))
    hid[...] = (normed * vecs[6:7, :] + vecs[7:8, :]).astype(jnp.bfloat16)
    hid_out[...] = hid[pl.ds(pl.multiple_of(rows * x, rows), rows), :]
    cot = grad[...].astype(jnp.float32)
    dy = norm_pull(cot * vecs[6:7, :], normed, rstd)
    low = dy.astype(jnp.bfloat16)
    dy_out[...] = dy
    low_out[...] = low
    sums[...] = jnp.zeros_like(sums)
    sums[0:1, :] = jnp.sum(low.astype(jnp.float32), axis=0, keepdims=True)
    sums[1:2, :] = jnp.sum(cot * normed, axis=0, keepdims=True)
    sums[2:3, :] = jnp.sum(cot, axis=0, keepdims=True)


def backward_kernel(dy, dy_low, slope, up, down, p_low, s_out, du_out, up_sums):
    low = dy_low[...]
    wide = up.shape[1] // 4
    for j in range(4):
        at = slice(wide * j, wide * (j + 1))
        du = (dot_nt(low, down[at, :]) * slope[:, at]).astype(jnp.bfloat16)
        du_out[:, at] = du
        total = jnp.sum(du.astype(jnp.float32), axis=0, keepdims=True)
        up_sums[j] = jnp.broadcast_to(total, up_sums.shape[1:])
    result = dot_nt(du_out[...], up[...])
    s_out[...] = dy[...] + result
    p_low[...] = result.astype(jnp.bfloat16)


def attend_back_kernel(
    s_own, p_got, normed1, rstd1, vecs, wo, mixed, q3, k3, v3, kt, lse, ids,
    dkv_out, dq_out, dr_out, da_out, sums, qv_sums,
    mask, do3, delta, dk, dv, dqt, whole,
):
    q, r, x, c = spot()
    rows = dr_out.shape[0]
    pairs = q3.shape[0]
    half = 128 * pairs
    fill_mask(ids, mask, 4 * r + 2 * c)
    dh = s_own[...] + p_got[...].astype(jnp.float32)
    normed = normed1[...]
    dr = norm_pull(dh * vecs[3:4, :], normed, rstd1[:, 0:1])
    whole[...] = dr
    dr_out[...] = whole[pl.ds(pl.multiple_of(rows * x, rows), rows), :]
    low = dr.astype(jnp.bfloat16)
    da_out[...] = low
    sums[...] = jnp.zeros_like(sums)
    sums[0:1, :] = jnp.sum(low.astype(jnp.float32), axis=0, keepdims=True)
    sums[1:2, :] = jnp.sum(dh * normed, axis=0, keepdims=True)
    sums[2:3, :] = jnp.sum(dh, axis=0, keepdims=True)
    d_o = dot_nt(low, wo[...]).astype(jnp.bfloat16)
    products = jnp.transpose(d_o.astype(jnp.float32) * mixed[...].astype(jnp.float32))
    for h in range(2 * pairs):
        delta[h : h + 1, :] = jnp.sum(products[64 * h : 64 * (h + 1), :], axis=0, keepdims=True)
    for p in range(pairs):
        do3[p] = d_o[:, 128 * p : 128 * (p + 1)]
    dk[...] = jnp.zeros_like(dk)
    dv[...] = jnp.zeros_like(dv)
    lane = lax.broadcasted_iota(jnp.int32, (2 * rows, 128), 1) // 64

    def head(h, carry):
        p = h // 2
        here = lane == h % 2
        query = (jnp.where(here, q3[p], 0) * 0.125).astype(jnp.bfloat16)
        d_here = jnp.where(here, do3[p], 0).astype(jnp.bfloat16)
        probs = jnp.exp(dot_nt(k3[p], query) + mask[...] - lse[pl.ds(h, 1), :])
        d_probs = dot_nt(v3[p], d_here)
        d_scores = (probs * (d_probs - delta[pl.ds(h, 1), :])).astype(jnp.bfloat16)
        dv[p] += dot(probs.astype(jnp.bfloat16), d_here)
        dk[p] += dot(d_scores, query)
        dqt[h] = dot(kt[h], d_scores)
        return carry

    lax.fori_loop(0, 2 * pairs, head, 0, unroll=6)
    dq = (jnp.transpose(dqt[...].reshape(half, 2 * rows)) * 0.125).astype(jnp.bfloat16)
    dq_out[...] = dq
    qv_sums[...] = jnp.zeros_like(qv_sums)
    qv_sums[0:1, :] = jnp.sum(dq.astype(jnp.float32), axis=0, keepdims=True)
    for p in range(pairs):
        at = slice(128 * p, 128 * (p + 1))
        dkv_out[:, at] = dk[p].astype(jnp.bfloat16)
        value = dv[p].astype(jnp.bfloat16)
        dkv_out[:, half + 128 * p : half + 128 * (p + 1)] = value
        qv_sums[1:2, at] = jnp.sum(value.astype(jnp.float32), axis=0, keepdims=True)


def input_grad_kernel(dq, dkv, w, *refs):
    sends, (keep, whole) = refs[:2], refs[2:]
    q, r, x, c = spot()
    half = dq.shape[1]
    rows = dq.shape[0] // 2
    whole[...] = dot_nt(dkv[...], w[:, half:])
    own = pl.ds(pl.multiple_of(rows * (4 * r + 2 * c), rows), 2 * rows)
    whole[own, :] += dot_nt(dq[...], w[:, 0:half])
    for b in range(2):
        for i in range(2):
            to = slice(2 * rows * b + rows * i, 2 * rows * b + rows * (i + 1))
            mine = pl.ds(pl.multiple_of(rows * (4 * i + 2 * c + b), rows), rows)
            keep[to, :] = whole[mine, :]
            theirs = pl.ds(pl.multiple_of(rows * (4 * i + 2 * (1 - c) + b), rows), rows)
            sends[b][rows * i : rows * (i + 1), :] = whole[theirs, :].astype(jnp.bfloat16)


def input_x_kernel(keep, got0, got1, send, kept):
    q, r, x, c = spot()
    half = send.shape[0]
    for side, got in enumerate((got0, got1)):
        total = keep[half * side : half * (side + 1), :] + got[...].astype(jnp.float32)

        @pl.when(x == side)
        def _():
            kept[...] = total

        @pl.when(x != side)
        def _():
            send[...] = total.astype(jnp.bfloat16)


def octants():
    for at in range(8):
        r, q0, q1 = at >> 2, at >> 1 & 1, at & 1
        yield 4 * r + 2 * q0 + 1 * q1, 1 * r + 4 * q0 + 2 * q1, 4 * r + 2 * q1 + q0


def down_grad_kernel(z, dy, send, keep):
    q, r, x, c = spot()
    half = z.shape[1] // 2
    rows = half // 8
    for side, out in ((1 - c, send), (c, keep)):
        part = dot_tn(z[:, pl.ds(pl.multiple_of(half * side, 128), half)], dy[...])
        for at, _, within in octants():
            block = part[rows * within : rows * (within + 1), :]
            out[rows * at : rows * (at + 1), :] = block.astype(out.dtype)


def up_grad_kernel(h, du, *refs):
    q, r, x, c = spot()
    sends, (keep, whole) = refs[:4], refs[4:]
    width = h.shape[1]
    thin = width // 32
    whole[...] = dot_tn(h[...], du[...])
    for side in (1 - c, c):
        for _, at, within in octants():
            pieces = []
            for xx in range(2):
                first = 8 * thin * (2 * xx + side) + thin * within
                rows = pl.ds(pl.multiple_of(first, 8), thin)
                pieces += [whole[rows, 0:width], whole[rows, width:]]
            block = jnp.concatenate(pieces)
            if side is c:
                keep[4 * thin * at : 4 * thin * (at + 1), :] = block
            else:
                to = 4 * thin * (at % 2)
                sends[at // 2][to : to + 4 * thin, :] = block.astype(jnp.bfloat16)


def join_kernel(*refs):
    out, at = refs[-1], 0
    for ref in refs[:-1]:
        count = ref.shape[0]
        out[at : at + count, :] = ref[...]
        at += count


def fold_pieces_kernel(bit, count, keep, *refs):
    gots, sends, (kept, whole) = refs[: -2 - count], refs[-2 - count : -2], refs[-2:]
    at = bit(*spot())
    first = 0
    for got in gots:
        rows = slice(first, first + got.shape[0])
        whole[rows, :] = keep[rows, :] + got[...].astype(jnp.float32)
        first += got.shape[0]
    half = kept.shape[0]
    kept[...] = whole[pl.ds(pl.multiple_of(half * at, 64), half), :]
    for i, send in enumerate(sends):
        rows = pl.ds(pl.multiple_of(half * (1 - at) + half // count * i, 64), half // count)
        send[...] = whole[rows, :].astype(send.dtype)


def fold_kernel(bit, keep, got, send, kept):
    at = bit(*spot())
    send[...] = (keep[1 - at] + got[1 - at].astype(jnp.float32)).astype(send.dtype)
    kept[...] = keep[at] + got[at].astype(jnp.float32)


def copy_kernel(block, out):
    out[...] = block[...]


def sum_kernel(keep, got, out):
    out[...] = (keep[...] + got[...].astype(jnp.float32)).astype(out.dtype)


def total_kernel(keep, got, more, out):
    out[...] = (keep[...] + got[...].astype(jnp.float32) + more[...]).astype(out.dtype)


def share_kernel(keep, got, side, base):
    q, r, x, c = spot()
    side[...] = (keep[1 - x] + got[1 - x].astype(jnp.float32)).astype(side.dtype)
    base[...] = (keep[x] + got[x].astype(jnp.float32)).astype(base.dtype)


def weight_grad_kernel(
    xs, dkv, dq, mixed, da, sums1, sums2, qv_sums, up_sums, *refs
):
    sends, (keep, packed) = refs[:-2], refs[-2:]
    q, r, x, c = spot()
    width = xs.shape[1]
    own, half = dq.shape
    thin = width // 32
    for_c = 64 * thin
    own_rows = pl.ds(pl.multiple_of(own * (2 * r + c), own), own)
    asked = dot_tn(xs[own_rows, :], dq[...])
    kept = dot_tn(xs[...], dkv[...])
    outer = dot_tn(mixed[...], da[...])
    for cc in range(2):
        for rr in range(2):
            for q1 in range(2):
                for q0 in range(2):
                    at = ((4 * rr + 2 * q0 + 1 * q1) * 8) * thin
                    within = (4 * rr + 2 * q1 + q0) * thin
                    for xx in range(2):
                        rows = slice((16 * xx + 8 * cc) * thin + within, (16 * xx + 8 * cc + 1) * thin + within)
                        for t, piece in enumerate((asked, kept[:, 0:half], kept[:, half:])):
                            to = at + (3 * xx + t) * thin
                            packed[cc, to : to + thin, :] = piece[rows, :]
                    rows = slice(8 * cc * thin + within, (8 * cc + 1) * thin + within)
                    for t in range(2):
                        to = at + (6 + t) * thin
                        packed[cc, to : to + thin, :] = outer[rows, half * t : half * (t + 1)]
    columns = pl.ds(pl.multiple_of(half * x, 128), half)
    for cc in range(2):
        packed[cc, for_c : for_c + 16, :] = jnp.zeros((16, half), jnp.float32)
        packed[cc, for_c : for_c + 2, :] = qv_sums[0:2, :]
        for j in range(4):
            packed[cc, for_c + 2 + j : for_c + 3 + j, :] = up_sums[j, 0:1, :]
        packed[cc, for_c + 6 : for_c + 9, :] = sums1[0:3, columns]
        packed[cc, for_c + 9 : for_c + 12, :] = sums2[0:3, columns]
    first = 0
    for send in sends:
        count = send.shape[0]
        send[...] = packed[1 - c, first : first + count, :].astype(jnp.bfloat16)
        first += count
    keep[...] = packed[c]


def step_kernel(bit, keep, *refs):
    gots, (send, kept, whole) = refs[:-3], refs[-3:]
    at = bit(*spot())
    count = send.shape[0] - 16
    first = 0
    for got in gots:
        rows = slice(first, first + got.shape[0])
        whole[rows, :] = keep[rows, :] + got[...].astype(jnp.float32)
        first += got.shape[0]
    theirs = pl.ds(pl.multiple_of(count * (1 - at), 64), count)
    mine = pl.ds(pl.multiple_of(count * at, 64), count)
    send[0:count, :] = whole[theirs, :].astype(jnp.bfloat16)
    send[count:, :] = whole[2 * count :, :].astype(jnp.bfloat16)
    kept[0:count, :] = whole[mine, :]
    kept[count:, :] = whole[2 * count :, :]


def last_step_kernel(keep, got, side, base, *refs):
    out, b_up, whole = refs[:8], refs[8], refs[9]
    q, r, x, c = spot()
    count = side.shape[0]
    part = out[0].shape[0]
    whole[...] = keep[...] + got[...].astype(jnp.float32)
    theirs = pl.ds(pl.multiple_of(count * (1 - x), 8), count)
    mine = pl.ds(pl.multiple_of(count * x, 8), count)
    side[...] = whole[theirs, :].astype(jnp.bfloat16)
    first = whole.shape[0] - 16
    base[...] = jnp.concatenate([whole[mine, :], whole[2 * count : first, :]]).astype(jnp.bfloat16)
    for i, one in enumerate(out):
        at = first + (i if i < 2 else i + 4)
        line = whole[at : at + 1, :]
        one[...] = jnp.where(c == 0, line[:, :part], line[:, part:]).reshape(part)
    line = jnp.concatenate([whole[pl.ds(first + 2 + 2 * c + i, 1), :] for i in range(2)], axis=1)
    b_up[...] = line.reshape(b_up.shape[0])


def down_out_kernel(near, far, out, mark):
    mark[...] = jnp.zeros_like(mark)
    q, r, x, c = spot()
    count = near.shape[0] // 4
    for d, piece in enumerate((near, far)):
        for k in range(4):
            at = 4 * (r ^ d) + 2 * ((q // 2) ^ (k & 1)) + ((q % 2) ^ (k >> 1))
            rows = pl.ds(pl.multiple_of(count * at, 32), count)
            out[rows, :] = piece[count * k : count * (k + 1), :].astype(jnp.float32)


def up_out_kernel(near, far, out, mark, whole):
    mark[...] = jnp.zeros_like(mark)
    q, r, x, c = spot()
    thin, width = near.shape[0] // 16, near.shape[1]
    for d, piece in enumerate((near, far)):
        whole[...] = piece[...].astype(jnp.float32)
        for k in range(4):
            at = 4 * (r ^ d) + 2 * ((q // 2) ^ (k & 1)) + ((q % 2) ^ (k >> 1))
            rows = pl.ds(pl.multiple_of(thin * at, 8), thin)
            for s in range(4):
                columns = pl.ds(pl.multiple_of(width * (2 * (x ^ (s >> 1)) + (s & 1)), 128), width)
                first = thin * (4 * k + s)
                out[rows, columns] = whole[first : first + thin, :]


def rest_out_kernel(near, far, hidden, total, out_q, out_k, out_v, out_o, out_h, out_t, whole):
    out_h[...] = hidden[...]
    out_t[...] = total[...]
    q, r, x, c = spot()
    half = near.shape[1]
    thin = near.shape[0] // 32
    ours = pl.ds(pl.multiple_of(half * x, 128), half)
    other = pl.ds(pl.multiple_of(half * (1 - x), 128), half)
    for d, piece in enumerate((near, far)):
        whole[...] = piece[...].astype(jnp.float32)
        for k in range(4):
            at = 4 * (r ^ d) + 2 * ((q // 2) ^ (k & 1)) + ((q % 2) ^ (k >> 1))
            rows = pl.ds(pl.multiple_of(thin * at, 8), thin)
            first = 8 * thin * k
            for t, out in enumerate((out_q, out_k, out_v)):
                out[rows, ours] = whole[first + thin * t : first + thin * (t + 1), :]
                out[rows, other] = whole[first + thin * (5 + t) : first + thin * (6 + t), :]
            for t in range(2):
                columns = slice(half * t, half * (t + 1))
                out_o[rows, columns] = whole[first + thin * (3 + t) : first + thin * (4 + t), :]


def kernel_call(body, name, ins, outs, scratch, args, after=(), room=2 << 20, cost=1):
    count = len(args)

    def size(shape, dtype):
        return math.prod(shape) * jnp.dtype(dtype).itemsize

    used = sum(size(m.shape, m.dtype) for m in scratch if m.memory_space == pltpu.VMEM)

    args = [
        pltpu.with_memory_space_constraint(a, pltpu.HBM) if spec is HBM else a
        for a, spec in zip(args, ins)
    ]

    def run(*refs):
        body(*refs[:count], *refs[count + len(after) :])

    return pl.pallas_call(
        run,
        name=name,
        out_shape=[jax.ShapeDtypeStruct(shape, dtype) for shape, dtype, _ in outs],
        in_specs=list(ins) + [ANY] * len(after),
        out_specs=[spec for _, _, spec in outs],
        scratch_shapes=scratch,
        cost_estimate=pl.CostEstimate(flops=cost, bytes_accessed=1, transcendentals=0),
        compiler_params=pltpu.CompilerParams(vmem_limit_bytes=used + room),
    )(*args, *after)


def once(value, *after):
    return pl.pallas_call(
        lambda *refs: None,
        name="once",
        out_shape=jax.ShapeDtypeStruct(value.shape, value.dtype),
        in_specs=[ANY] * (1 + len(after)),
        out_specs=ANY,
        input_output_aliases={0: 0},
        cost_estimate=pl.CostEstimate(flops=1, bytes_accessed=1, transcendentals=0),
        compiler_params=pltpu.CompilerParams(vmem_limit_bytes=1 << 18),
    )(value, *after)


HEAVY = ('attend_back', 'down_sum', 'input_sum', 'project', 'rest_3', 'up_share')


def plane_local(
    tokens, cotangent, seq_ids, w_query, b_query, w_key, w_value, b_value, w_out, b_out,
    attn_gain, attn_shift, w_up, b_up, w_down, b_down, ffn_gain, ffn_shift,
):
    low, exact = jnp.bfloat16, jnp.float32
    rows, width = tokens.shape[1:]
    part = w_query.shape[0]
    half = width // 2
    inner = w_up.shape[1]
    wide = inner // 8
    keys = 8 * rows
    own = 2 * rows
    pairs = half // 128

    latest = []

    def call(body, name, ins, outs, scratch, args, after=(), **more):
        cost = 10**10 if name in HEAVY else 1
        results = kernel_call(
            body, name, ins, outs, scratch, args, tuple(after) + tuple(latest), cost=cost, **more
        )
        latest[:] = results[-1:] if name.endswith("_out") else results[:1]
        return results

    (block,) = call(
        block_kernel, "block", [HBM] * 2, [((rows + 16, width), low, WHOLE)],
        [pltpu.VMEM((1, rows), jnp.int32), pltpu.SemaphoreType.DMA((2,))],
        (tokens[0], seq_ids),
    )
    block = regroup(block)
    theirs, mine = call(
        pack_kernel,
        "pack",
        [HBM] * 12,
        [((3 * part // 2 + 16, half), low, WHOLE), ((3 * part + 16, half), low, WHOLE)],
        [pltpu.VMEM((16, half), exact)]
        + [pltpu.VMEM((part,), low)] * 8
        + [pltpu.VMEM((width,), low), pltpu.SemaphoreType.DMA((15,))],
        (w_query, w_key, w_value, b_query, b_value, b_out, attn_gain, attn_shift, b_down, ffn_gain, ffn_shift, b_up),
    )
    qkv_x = swap_x(theirs)
    qkv_m = swap_c(mine)
    out_m = swap_c(w_out)
    blocks = [once(block, qkv_m, out_m)]
    beside_r = swap_r(blocks[0])
    blocks.append(once(swap_x(blocks[0]), beside_r))
    blocks.append(swap_c(blocks[0]))
    blocks.append(swap_c(blocks[1]))
    blocks.append(beside_r)
    blocks.append(swap_r(blocks[1]))
    qkv_x = (qkv_x, swap_r(qkv_x))
    qkv_mx = [swap_c(piece) for piece in qkv_x]
    up_theirs, up_mine = call(
        cut_kernel, "cut", [HBM], [((part, 4 * wide), low, WHOLE)] * 2, [pltpu.SemaphoreType.DMA((2,))],
        (w_up,), after=(blocks[1],),
    )
    up_x = swap_x(up_theirs)
    up_m = swap_c(up_mine)
    down_m = swap_c(w_down)
    (cot,) = call(
        load_kernel, "cotangent", [HBM], [((rows, width), low, WHOLE)], [pltpu.SemaphoreType.DMA((1,))],
        (cotangent[0],),
    )
    kv_own, q_own, w_all, vecs, up_bias = call(
        project_kernel,
        "project",
        [WHOLE] * 4 + [HBM] * 3 + [WHOLE] * 6,
        [
            ((4 * rows, width), low, WHOLE),
            ((own, half), low, WHOLE),
            ((width, 3 * half), low, WHOLE),
            ((8, width), exact, WHOLE),
            ((4, 8, wide), exact, WHOLE),
        ],
        [pltpu.VMEM((4 * rows, width), low), pltpu.SemaphoreType.DMA((3,))],
        (*blocks[:4], w_query, w_key, w_value, qkv_m, *qkv_x, *qkv_mx, mine),
        room=8 << 20,
    )
    blocks[5] = once(blocks[5], kv_own)
    blocks.append(swap_c(blocks[4]))
    blocks.append(swap_c(blocks[5]))
    a_low, x_all, wo_all, k3, v3, q3, mixed, lse, ids, a_own = call(
        attend_kernel,
        "attend",
        [WHOLE] * 12 + [HBM, WHOLE],
        [
            ((own, width), low, WHOLE),
            ((keys, width), low, WHOLE),
            ((half, width), low, WHOLE),
            ((pairs, keys, 128), low, WHOLE),
            ((pairs, keys, 128), low, WHOLE),
            ((pairs, own, 128), low, WHOLE),
            ((own, half), low, WHOLE),
            ((8, own), exact, WHOLE),
            ((8, rows), exact, WHOLE),
            ((own, width), exact, WHOLE),
        ],
        [
            pltpu.VMEM((2 * pairs, 64, keys), low),
            pltpu.VMEM((2 * pairs, 64, own), exact),
            pltpu.VMEM((keys, own), exact),
            pltpu.SemaphoreType.DMA((1,)),
        ],
        (*blocks, kv_own, q_own, w_all, vecs, w_out, out_m),
        after=(down_m,),
        room=8 << 20,
    )
    a_got = swap_x(a_low)
    (kt,) = call(turn_kernel, "turn", [WHOLE], [((2 * pairs, 64, keys), low, WHOLE)], [], (k3,),
        after=(up_m,))

    up_x = once(up_x, kt)
    up_mx = [swap_c(piece) for piece in (up_x[: part // 2], up_x[part // 2 :])]
    inner_weights = call(
        inner_kernel,
        "inner",
        [HBM] + [WHOLE] * 4 + [HBM, WHOLE],
        [((width, 4 * wide), low, WHOLE), ((4 * wide, width), low, WHOLE)],
        [pltpu.SemaphoreType.DMA((2,))],
        (w_up, up_x, up_m, *up_mx, w_down, down_m),
    )
    cot = once(cot, inner_weights[0])
    cot, cot_x = regroup(cot), regroup_x(cot)
    y_low, y_more, h_low, z, normed1, rstd1, slope, y_own = call(
        forward_kernel,
        "feedforward",
        [WHOLE] * 7,
        [
            ((rows, width), low, WHOLE),
            ((rows, width), low, WHOLE),
            ((own, width), low, WHOLE),
            ((own, 4 * wide), low, WHOLE),
            ((own, width), exact, WHOLE),
            ((own, 128), exact, WHOLE),
            ((own, 4 * wide), exact, WHOLE),
            ((own, width), exact, WHOLE),
        ],
        [],
        (a_own, a_got, x_all, vecs, up_bias, *inner_weights),
        room=8 << 20,
    )
    y_got, y_rest = swap_x(y_low), swap_x(y_more)
    dy_low, hidden, dy, sums2 = call(
        norm_back_kernel,
        "norm_back",
        [WHOLE] * 7,
        [
            ((own, width), low, WHOLE),
            ((rows, width), low, WHOLE),
            ((own, width), exact, WHOLE),
            ((8, width), exact, WHOLE),
        ],
        [
            pltpu.VMEM((own, width), low),
            pltpu.VMEM((own, width), low),
        ],
        (y_own, y_got, y_rest, normed1, cot, cot_x, vecs),
        room=6 << 20,
    )
    eighth = wide // 4
    down_send, down_keep = call(
        down_grad_kernel,
        "down_grad",
        [WHOLE] * 2,
        [((8 * eighth, width), low, WHOLE), ((8 * eighth, width), exact, WHOLE)],
        [],
        (z, dy_low),
        room=8 << 20,
    )
    down_got = swap_c(down_send)
    p_low, s_own, du, up_sums = call(
        backward_kernel,
        "feedforward_back",
        [WHOLE] * 5,
        [
            ((own, width), low, WHOLE),
            ((own, width), exact, WHOLE),
            ((own, 4 * wide), low, WHOLE),
            ((4, 8, wide), exact, WHOLE),
        ],
        [],
        (dy, dy_low, slope, *inner_weights),
        room=8 << 20,
    )
    p_got = swap_x(p_low)
    hidden = regroup(hidden)

    def fold(name, bit, keep, got):
        shape = (keep.shape[0] // 2, keep.shape[1])
        return call(
            lambda *refs: fold_kernel(bit, *refs),
            name,
            [WHOLE] * 2,
            [(shape, low, WHOLE), (shape, exact, WHOLE)],
            [],
            (keep.reshape(2, *shape), got.reshape(2, *shape)),
            room=4 << 20,
        )

    def fold_into(count, name, bit, keep, gots):
        half_rows = keep.shape[0] // 2
        *sends, kept = call(
            lambda *refs: fold_pieces_kernel(bit, count, *refs),
            name,
            [WHOLE] * (1 + len(gots)),
            [((half_rows // count, width), low, WHOLE)] * count + [((half_rows, width), exact, WHOLE)],
            [pltpu.VMEM(keep.shape, exact)],
            (keep, *gots),
            room=4 << 20,
        )
        return sends, kept

    def bit_r(q, r, x, c):
        return r

    def bit_near(q, r, x, c):
        return q % 2

    def bit_far(q, r, x, c):
        return q // 2

    thin = part // 8
    count = 64 * thin

    def step(name, bit, keep, size, *gots):
        return call(
            lambda *refs: step_kernel(bit, *refs),
            name,
            [WHOLE] * (1 + len(gots)),
            [((size + 16, half), low, WHOLE), ((size + 16, half), exact, WHOLE)],
            [pltpu.VMEM((2 * size + 16, half), exact)],
            (keep, *gots),
        )

    def join(name, *pieces):
        shape = (sum(p.shape[0] for p in pieces), pieces[0].shape[1])
        (out,) = call(join_kernel, name, [WHOLE] * len(pieces), [(shape, low, WHOLE)], [], pieces)
        return out

    cuts = (count // 3, count // 3, count - 2 * (count // 3) + 16)
    *up_sends, up_keep = call(
        up_grad_kernel,
        "up_grad",
        [WHOLE] * 2,
        [((2 * eighth, width), low, WHOLE)] * 4 + [((8 * eighth, width), exact, WHOLE)],
        [pltpu.VMEM((width, 4 * wide), exact)],
        (h_low, du),
        room=8 << 20,
    )
    up_gots = [swap_c(send) for send in up_sends]
    down_sends, down_keep = fold_into(2, "down_1", bit_r, down_keep, (down_got,))
    down_gots = [swap_r(send) for send in down_sends]
    (up_send,), up_keep = fold_into(1, "up_1", bit_near, up_keep, up_gots)
    up_got = swap_near(up_send)
    dkv, dq, dr, da, sums1, qv_sums = call(
        attend_back_kernel,
        "attend_back",
        [WHOLE] * 13,
        [
            ((keys, 2 * half), low, WHOLE),
            ((own, half), low, WHOLE),
            ((rows, width), exact, WHOLE),
            ((own, width), low, WHOLE),
            ((8, width), exact, WHOLE),
            ((8, half), exact, WHOLE),
        ],
        [
            pltpu.VMEM((keys, own), exact),
            pltpu.VMEM((pairs, own, 128), low),
            pltpu.VMEM((8, own), exact),
            pltpu.VMEM((pairs, keys, 128), exact),
            pltpu.VMEM((pairs, keys, 128), exact),
            pltpu.VMEM((2 * pairs, 64, own), exact),
            pltpu.VMEM((own, width), exact),
        ],
        (s_own, p_got, normed1, rstd1, vecs, wo_all, mixed, q3, k3, v3, kt, lse, ids),
        room=8 << 20,
    )

    (down_send,), down_keep = fold_into(1, "down_2", bit_near, down_keep, down_gots)
    down_got = swap_near(down_send)
    *rest_sends, rest_keep = call(
        weight_grad_kernel,
        "weight_grad",
        [WHOLE] * 9,
        [((n, half), low, WHOLE) for n in cuts] + [((count + 16, half), exact, WHOLE)],
        [pltpu.VMEM((2, count + 16, half), exact)],
        (x_all, dkv, dq, mixed, da, sums1, sums2, qv_sums, up_sums),
        after=(hidden,),
        room=8 << 20,
    )
    rest_gots = [swap_c(send) for send in rest_sends]
    rest_send, rest_keep = step("rest_1", bit_r, rest_keep, count // 2, *rest_gots)
    rest_got = swap_r(rest_send)
    up_send, up_keep = fold("up_2", bit_far, up_keep, up_got)
    up_got = swap_far(up_send)
    *x_sends, x_keep = call(
        input_grad_kernel,
        "input_grad",
        [WHOLE] * 3,
        [((own, width), low, WHOLE)] * 2 + [((2 * own, width), exact, WHOLE)],
        [pltpu.VMEM((keys, width), exact)],
        (dq, dkv, w_all),
        room=8 << 20,
    )
    x_gots = [swap_c(send) for send in x_sends]
    down_send, down_keep = fold("down_3", bit_far, down_keep, down_got)
    down_got = swap_far(down_send)
    x_send, x_keep = call(
        input_x_kernel,
        "input_x",
        [WHOLE] * 3,
        [((own, width), low, WHOLE), ((own, width), exact, WHOLE)],
        [],
        (x_keep, *x_gots),
        room=4 << 20,
    )
    x_got = swap_x(x_send)
    up_send, up_keep = fold("up_3", bit_r, up_keep, up_got)
    up_got = swap_r(up_send)
    (down_sum,) = call(
        sum_kernel, "down_sum", [WHOLE] * 2, [((eighth, width), low, WHOLE)], [], (down_keep, down_got)
    )
    down_other = swap_far(down_sum)
    x_send, x_keep = fold("input_r", bit_r, x_keep, x_got)
    x_got = swap_r(x_send)
    side, base = call(
        share_kernel,
        "up_share",
        [WHOLE] * 2,
        [((eighth // 2, width), low, WHOLE)] * 2,
        [],
        (up_keep.reshape(2, eighth // 2, width), up_got.reshape(2, eighth // 2, width)),
    )
    side = swap_x(side)
    rest_send, rest_keep = step("rest_2", bit_near, rest_keep, count // 4, rest_got)
    rest_got = swap_near(rest_send)
    down_sum = join("down_join", down_sum, down_other)
    down_other = swap_near(down_sum)
    rest_send, rest_keep = step("rest_3", bit_far, rest_keep, count // 8, rest_got)
    rest_got = swap_far(rest_send)
    up_sum = join("up_join", base, side)
    up_other = swap_far(up_sum)
    down_near = join("down_join_near", down_sum, down_other)
    down_far = swap_r(down_near)
    rest_side, rest_base, *lines, b_up_grad = call(
        last_step_kernel,
        "rest_last",
        [WHOLE] * 2,
        [((3 * thin, half), low, WHOLE), ((5 * thin, half), low, WHOLE)]
        + [((part,), exact, WHOLE)] * 8
        + [((2 * wide,), exact, WHOLE)],
        [pltpu.VMEM((8 * thin + 16, half), exact)],
        (rest_keep, rest_got),
    )
    rest_side = swap_x(rest_side)
    up_sum = join("up_join_far", up_sum, up_other)
    up_other = swap_near(up_sum)
    (total,) = call(
        total_kernel, "input_sum", [WHOLE] * 3, [((rows, width), low, WHOLE)], [], (x_keep, x_got, dr)
    )
    total = regroup(total)
    rest_sum = join("rest_join", rest_base, rest_side)
    rest_other = swap_far(rest_sum)
    rest_sum = join("rest_join_far", rest_sum, rest_other)
    rest_other = swap_near(rest_sum)
    w_down_grad, _ = call(
        down_out_kernel, "down_out", [WHOLE] * 2,
        [((2 * wide, width), exact, WHOLE), ((8, 128), exact, WHOLE)], [], (down_near, down_far),
        room=6 << 20,
    )
    up_near = join("up_join_near", up_sum, up_other)
    up_far = swap_r(up_near)
    rest_near = join("rest_join_near", rest_sum, rest_other)
    rest_far = swap_r(rest_near)
    w_up_grad, _ = call(
        up_out_kernel, "up_out", [WHOLE] * 2, [((part, inner), exact, WHOLE), ((8, 128), exact, WHOLE)],
        [pltpu.VMEM((4 * eighth, width), exact)], (up_near, up_far),
        room=6 << 20,
    )


    w_query_grad, w_key_grad, w_value_grad, w_out_grad, hidden_out, tokens_grad = call(
        rest_out_kernel,
        "rest_out",
        [WHOLE] * 4,
        [((part, width), exact, WHOLE)] * 4 + [((rows, width), low, WHOLE)] * 2,
        [pltpu.VMEM((32 * thin, half), exact)],
        (rest_near, rest_far, hidden, total),
        room=6 << 20,
    )

    return (
        hidden_out[None],
        tokens_grad[None],
        w_query_grad,
        lines[0],
        w_key_grad,
        w_value_grad,
        lines[1],
        w_out_grad,
        lines[2],
        lines[3],
        lines[4],
        w_up_grad,
        b_up_grad,
        w_down_grad,
        lines[5],
        lines[6],
        lines[7],
    )


def plane_solution(mesh):
    planes, cycle = mesh.shape["shard"], mesh.shape["ctx"]
    grid = Mesh(mesh.devices.reshape(planes, cycle // planes, 2, 2), AXES)
    shard, ctx = ("x", "c"), ("q", "r")
    tokens, matrix, vector = P(shard, ctx, None), P(shard, None), P(shard)
    return jax.shard_map(
        plane_local,
        mesh=grid,
        in_specs=(
            tokens, tokens, P(shard, ctx), matrix, vector, matrix, matrix, vector, matrix, vector,
            vector, vector, matrix, vector, matrix, vector, vector, vector,
        ),
        out_specs=(
            tokens, tokens, matrix, vector, matrix, matrix, vector, matrix, vector,
            vector, vector, matrix, vector, matrix, vector, vector, vector,
        ),
        check_vma=False,
    )


def solution(mesh):
    if mesh.shape["shard"] == 4 and mesh.shape["ctx"] == 8:
        return plane_solution(mesh)
    return ring_solution(mesh)
```
